32 devices in a mesh: dp: 8 (over z, y), tensor: 4 (over x, core).
Axes of the slice: x: 2, y: 2, z: 4, core: 2. Of those that a mesh axis runs over, the one named last changes fastest.
Arguments:
- stream_in: float32 [20480, 1024], P(('dp', 'tensor')), may hold values from -27 to 27
- segment_ids: int32 [20480], P('dp'), may hold values from 0 to 103, as said below
- parent_ids: int32 [20480], P('dp'), may hold values from 0 to 95, as said below
- norm_gain_attn: float32 [1024], replicated, may hold values from 0.5 to 1.5
- norm_shift_attn: float32 [1024], replicated, may hold values from -1 to 1
- norm_gain_mlp: float32 [1024], replicated, may hold values from 0.5 to 1.5
- norm_shift_mlp: float32 [1024], replicated, may hold values from -1 to 1
- qkv_weight: float32 [1024, 3072], P('dp', 'tensor'), may hold values from -0.1875 to 0.1875
- qkv_bias: float32 [3072], replicated, may hold values from -1 to 1
- dense_weight: float32 [1024, 1024], P('tensor', 'dp'), may hold values from -3 to 3
- dense_bias: float32 [1024], replicated, may hold values from -1 to 1
- fc_weight: float32 [1024, 4096], P('dp', 'tensor'), may hold values from -0.1875 to 0.1875
- fc_bias: float32 [4096], replicated, may hold values from -1 to 1
- out_weight: float32 [4096, 1024], P('tensor', 'dp'), may hold values from -0.125 to 0.125
- out_bias: float32 [1024], replicated, may hold values from -1 to 1
- out_grad: bfloat16 [20480, 1024], P(('dp', 'tensor')), may hold values from -6 to 6
Outputs:
- output: float32 [20480, 1024], P(('dp', 'tensor'))
- stream_grad: float32 [20480, 1024], P(('dp', 'tensor'))
- gain_attn_grad: float32 [1024], replicated
- shift_attn_grad: float32 [1024], replicated
- gain_mlp_grad: float32 [1024], replicated
- shift_mlp_grad: float32 [1024], replicated
- qkv_weight_grad: float32 [1024, 3072], P('dp', 'tensor')
- qkv_bias_grad: float32 [3072], replicated
- dense_weight_grad: float32 [1024, 1024], P('tensor', 'dp')
- dense_bias_grad: float32 [1024], replicated
- fc_weight_grad: float32 [1024, 4096], P('dp', 'tensor')
- fc_bias_grad: float32 [4096], replicated
- out_weight_grad: float32 [4096, 1024], P('tensor', 'dp')
- out_bias_grad: float32 [1024], replicated
- root_squares: float32 [3], replicated
The draws below stay inside these ranges and needn't reach their ends.
Inputs may be any that keep to these rules, and one draw needn't show every extreme that they name: `segment_ids`: each tree is 2560 consecutive tokens: its trunk of 1024 tokens first, then 128-token branches and leaves in an order that varies; 4 branches with 2 leaves each; segment numbers are distinct across trees. `parent_ids`: A branch's parent is its tree's trunk, a leaf's parent a branch of the same tree.
All inputs are finite; a program needn't handle non-finite values.
Results may differ from the reference program's by a relative error of at most 0.012.
The reference program's roundings to bfloat16 on the way count: a program that leaves them out, or rounds other values in their place, can miss the bound.
Values may be sent and summed in bfloat16 or wider, within the bound.
No kernel may reach another device: no remote copies, remote signals or barrier semaphores. Data moves between devices by JAX's collectives and lax.ppermute only.
A program may use at most 320 MiB of HBM per device.

```python
import jax
import jax.numpy as jnp
from jax import lax

D = 1024
H = 16
HD = 64
ROT = 16
FF = 4096
TRUNK = 1024
SEG = 128
BRANCHES = 4
LEAVES = 2
TREE = 2560
NSEG = 13
TOKENS = 20480
TREES = 8
N_TENSOR = 4


def tree_layout(key):
    base_key = jax.random.fold_in(key, 11)
    tree_keys = jax.random.split(base_key, TREES)
    short_count = BRANCHES * (1 + LEAVES)

    def one_tree(tree_key, tree_number):
        order_key, leaf_key = jax.random.split(tree_key)
        order = jax.random.permutation(order_key, short_count).astype(jnp.int32)
        leaf_owner = (jax.random.permutation(leaf_key, BRANCHES * LEAVES) // LEAVES).astype(jnp.int32)
        parent_local = jnp.concatenate([jnp.zeros((BRANCHES,), jnp.int32), 1 + leaf_owner])
        segment_tokens = jnp.concatenate([jnp.zeros((TRUNK,), jnp.int32), jnp.repeat(1 + order, SEG)])
        parent_tokens = jnp.concatenate([jnp.zeros((TRUNK,), jnp.int32), jnp.repeat(parent_local[order], SEG)])
        offset = tree_number * NSEG
        return (segment_tokens + offset, parent_tokens + offset)
    seg_all, parent_all = jax.vmap(one_tree)(tree_keys, jnp.arange(TREES, dtype=jnp.int32))
    return (seg_all.reshape(-1), parent_all.reshape(-1))


def draw_segment_ids(key, part):
    return tree_layout(key)[0]


def draw_parent_ids(key, part):
    return tree_layout(key)[1]


def draw_stream_in(key, part):
    noise_key, scale_key = jax.random.split(jax.random.fold_in(key, 3))
    base_values = jnp.clip(jax.random.normal(noise_key, (TOKENS, D), jnp.float32), -6.0, 6.0)
    rough = jnp.exp(jax.random.uniform(scale_key, (TOKENS, 1), jnp.float32, -0.4, 0.4))
    ramp = jnp.exp(jnp.log(3.0) * jnp.arange(TOKENS, dtype=jnp.float32)[:, None] / TOKENS)
    return base_values * rough * ramp


def steps_of(key, dims, cuts, low, high):
    factor_of, own = 1.0, jax.random.fold_in(key, 6)
    for axis_at, blocks in cuts:
        draws = jnp.exp(jax.random.uniform(jax.random.fold_in(own, axis_at), (blocks,), jnp.float32, low / len(cuts), high / len(cuts)))
        factor_of = factor_of * jnp.repeat(draws, dims[axis_at] // blocks).reshape([-1 if axis == axis_at else 1 for axis in range(len(dims))])
    return factor_of


def bell_draw(own_key, dims, width, most, cuts=(), held_as=jnp.bfloat16):
    entries = jax.random.normal(own_key, dims, jnp.float32) * width
    if len(cuts) > 0:
        entries = steps_of(own_key, dims, cuts, -0.22, 0.18) * entries
    return jnp.clip(entries, min=-most, max=most).astype(held_as)


def setup_inputs(seed: int = 0) -> dict:
    key_of = jax.random.split(jax.random.key(seed), 17)
    return {
        "stream_in": draw_stream_in(jax.random.fold_in(key_of[16], 71), 0),
        "segment_ids": draw_segment_ids(jax.random.fold_in(key_of[16], 71), 0),
        "parent_ids": draw_parent_ids(jax.random.fold_in(key_of[16], 71), 0),
        "norm_gain_attn": jnp.clip(1.0 + 0.1 * jax.random.normal(key_of[3], (D,), jnp.float32), 0.5, 1.5),
        "norm_shift_attn": bell_draw(key_of[4], (D,), 0.2, 1.0, (), jnp.float32),
        "norm_gain_mlp": jnp.clip(1.0 + 0.1 * jax.random.normal(key_of[5], (D,), jnp.float32), 0.5, 1.5),
        "norm_shift_mlp": bell_draw(key_of[6], (D,), 0.2, 1.0, (), jnp.float32),
        "qkv_weight": bell_draw(key_of[7], (D, 3 * D), D ** -0.5, 0.1875, ((0, 8), (1, 4)), jnp.float32),
        "qkv_bias": bell_draw(key_of[8], (3 * D,), 0.2, 1.0, (), jnp.float32),
        "dense_weight": bell_draw(key_of[9], (D, D), (max(1, D // 256)) ** -0.5, 3.0, ((0, 4), (1, 8)), jnp.float32),
        "dense_bias": bell_draw(key_of[10], (D,), 0.2, 1.0, (), jnp.float32),
        "fc_weight": bell_draw(key_of[11], (D, FF), D ** -0.5, 0.1875, ((0, 8), (1, 4)), jnp.float32),
        "fc_bias": bell_draw(key_of[12], (FF,), 0.2, 1.0, (), jnp.float32),
        "out_weight": bell_draw(key_of[13], (FF, D), (FF // 2) ** -0.5, 0.125, ((0, 4), (1, 8)), jnp.float32),
        "out_bias": bell_draw(key_of[14], (D,), 0.2, 1.0, (), jnp.float32),
        "out_grad": bell_draw(key_of[15], (TOKENS, D), 1.0, 6.0, ((0, 32),)),
    }


@jax.custom_vjp
def low(v):
    return lax.optimization_barrier(v.astype(jnp.bfloat16)).astype(jnp.float32)

@jax.custom_vjp
def low_back(v):
    return v

def low_keep(v):
    return (low(v), None)

def low_pass(kept, grad):
    return (grad,)

def back_keep(v):
    return (v, None)

def back_low(kept, grad):
    return (low(grad),)
low.defvjp(low_keep, low_pass)
low_back.defvjp(back_keep, back_low)
eps_norm = 1e-05
masked_score = -1e+30

def matmul(left, right):
    return jnp.dot(left, right, precision=lax.Precision.HIGHEST, preferred_element_type=jnp.float32)

def position_tables(segments, parents):
    token_count = segments.shape[0]
    index_all = jnp.arange(token_count, dtype=jnp.int32) % TREE
    root_ids = jnp.repeat(segments.reshape(token_count // TREE, TREE)[:, 0], TREE)
    depth_shift = jnp.where(parents == root_ids, 0, SEG)
    places = jnp.where(index_all < TRUNK, index_all, TRUNK + (index_all - TRUNK) % SEG + depth_shift)
    half_rot = ROT // 2
    inverse_freq = 10000.0 ** (-(jnp.arange(half_rot, dtype=jnp.float32) * 2.0 / ROT))
    angles = places.astype(jnp.float32)[:, None] * inverse_freq[None, :]
    cosine_table = jnp.concatenate([jnp.cos(angles), jnp.cos(angles)], axis=1)
    sine_table = jnp.concatenate([jnp.sin(angles), jnp.sin(angles)], axis=1)
    return (cosine_table, sine_table, root_ids)

def rotate_forward(field, cosine_table, sine_table):
    half_rot = ROT // 2
    turned_part = field[..., :ROT]
    first_half = turned_part[..., :half_rot]
    second_half = turned_part[..., half_rot:]
    swapped = jnp.concatenate([-second_half, first_half], axis=-1)
    turned = turned_part * cosine_table[:, None, :] + swapped * sine_table[:, None, :]
    return jnp.concatenate([turned, field[..., ROT:]], axis=-1)

def visible(seg_rows, parent_rows, root_rows, index_rows, seg_cols, index_cols):
    same_seg = (seg_cols[None, :] == seg_rows[:, None]) & (index_cols[None, :] <= index_rows[:, None])
    upper_seg = (seg_cols[None, :] == parent_rows[:, None]) & (parent_rows != seg_rows)[:, None]
    rooted_seg = (seg_cols[None, :] == root_rows[:, None]) & (root_rows != seg_rows)[:, None]
    return same_seg | upper_seg | rooted_seg

def tree_attention(pieces):
    queries, key_rows, values, seg_tree, parent_tree, root_tree = pieces
    index_tree = jnp.arange(TREE, dtype=jnp.int32)
    allowed = visible(seg_tree, parent_tree, root_tree, index_tree, seg_tree, index_tree)
    raw_scores = jnp.einsum('qhd,khd->hqk', queries, key_rows, precision=lax.Precision.HIGHEST)
    scores = low_back(raw_scores) * HD ** (-0.5)
    scores = jnp.where(allowed[None], scores, masked_score)
    soft_low = low(jax.nn.softmax(scores, axis=-1))
    return jnp.einsum('hqk,khd->qhd', soft_low, values, precision=lax.Precision.HIGHEST)

def layer_forward(stream, gain_attn, shift_attn, gain_mlp, shift_mlp, qkv_w, qkv_b, dense_w, dense_b, fc_w, fc_b, out_w, out_b, cosine_table, sine_table, segments, parents, root_ids):
    row_mean = lax.optimization_barrier(jnp.mean(stream, axis=-1, keepdims=True))
    centred = stream - row_mean
    row_var = lax.optimization_barrier(jnp.mean(centred * centred, axis=-1, keepdims=True))
    normalized = centred * lax.rsqrt(row_var + eps_norm)
    sent_norm = low(normalized)
    heads_group = H // N_TENSOR
    qkv_width = heads_group * 3 * HD
    ctx_width = heads_group * HD
    ff_group = FF // N_TENSOR
    tree_count = TOKENS // TREE
    seg_trees = segments.reshape(tree_count, TREE)
    parent_trees = parents.reshape(tree_count, TREE)
    root_trees = root_ids.reshape(tree_count, TREE)
    attn_total = jnp.zeros((TOKENS, D), jnp.float32)
    mlp_total = jnp.zeros((TOKENS, D), jnp.float32)
    for group in range(N_TENSOR):
        own_copy = low_back(sent_norm)
        normed_attn = low(own_copy * gain_attn + shift_attn)
        normed_mlp = low(own_copy * gain_mlp + shift_mlp)
        qkv_cols = slice(group * qkv_width, (group + 1) * qkv_width)
        qkv = low_back(matmul(normed_attn, low(qkv_w[:, qkv_cols])) + qkv_b[qkv_cols])
        qkv = qkv.reshape(TOKENS, heads_group, 3, HD)
        queries = low(rotate_forward(qkv[:, :, 0], cosine_table, sine_table))
        key_rows = low(rotate_forward(qkv[:, :, 1], cosine_table, sine_table))
        values = low(qkv[:, :, 2])
        context = lax.map(jax.checkpoint(tree_attention), (queries.reshape(tree_count, TREE, heads_group, HD), key_rows.reshape(tree_count, TREE, heads_group, HD), values.reshape(tree_count, TREE, heads_group, HD), seg_trees, parent_trees, root_trees))
        context = low(low_back(context.reshape(TOKENS, ctx_width)))
        ctx_rows = slice(group * ctx_width, (group + 1) * ctx_width)
        attn_total = attn_total + low(matmul(context, low(dense_w[ctx_rows])))
        ff_cols = slice(group * ff_group, (group + 1) * ff_group)
        hidden = low_back(matmul(normed_mlp, low(fc_w[:, ff_cols])) + fc_b[ff_cols])
        activated = low(jax.nn.gelu(hidden, approximate=False))
        mlp_total = mlp_total + low(matmul(activated, low(out_w[ff_cols])))
    attn_out = attn_total + dense_b
    mlp_out = mlp_total + out_b
    return (stream + attn_out + mlp_out, (attn_out, mlp_out))

def reference(stream_in, segment_ids, parent_ids, norm_gain_attn, norm_shift_attn, norm_gain_mlp, norm_shift_mlp, qkv_weight, qkv_bias, dense_weight, dense_bias, fc_weight, fc_bias, out_weight, out_bias, out_grad):
    cosine_table, sine_table, root_ids = position_tables(segment_ids, parent_ids)

    def forward_only(*params):
        return layer_forward(*params, cosine_table, sine_table, segment_ids, parent_ids, root_ids)
    output, pullback, branches = jax.vjp(forward_only, stream_in, norm_gain_attn, norm_shift_attn, norm_gain_mlp, norm_shift_mlp, qkv_weight, qkv_bias, dense_weight, dense_bias, fc_weight, fc_bias, out_weight, out_bias, has_aux=True)
    grads = pullback(out_grad.astype(jnp.float32))
    attn_out, mlp_out = branches
    count_all = TOKENS * D
    root_squares = jnp.sqrt(jnp.stack([jnp.sum(output * output), jnp.sum(attn_out * attn_out), jnp.sum(mlp_out * mlp_out)]) / count_all)
    return (output, grads[0], grads[1], grads[2], grads[3], grads[4], grads[5], grads[6], grads[7], grads[8], grads[9], grads[10], grads[11], grads[12], root_squares)
```

```python
import jax
import jax.numpy as jnp
from jax import lax
from jax.experimental import pallas as pl
from jax.experimental.pallas import tpu as pltpu
from jax.sharding import PartitionSpec as P

HD = 64
ROT = 16
TRUNK = 1024
SEG = 128
TREE = 2560
NB = TREE // SEG
NT = TRUNK // SEG

f32 = jnp.float32
bf16 = jnp.bfloat16
eps_norm = 1e-05
masked_score = -1e30
VMEM_MOST = 62 << 20

TAIL_SLOPE = 0.3
TAIL_COEFS = (
    0.11968663334846497,
    0.11957288533449173,
    0.11022695899009705,
    0.07842729985713959,
    0.09605274349451065,
    -0.07923758029937744,
    0.191569522023201,
    -0.22805799543857574,
    0.1123715341091156,
    -0.02061200700700283,
)


def dot_nn(left, right):
    return lax.dot_general(left, right, (((1,), (0,)), ((), ())), preferred_element_type=f32)


def dot_nt(left, right):
    return lax.dot_general(left, right, (((1,), (1,)), ((), ())), preferred_element_type=f32)


def dot_tn(left, right):
    return lax.dot_general(left, right, (((0,), (0,)), ((), ())), preferred_element_type=f32)


def bits_of(size):
    bits = []
    bit = 1
    while bit < size:
        bits.append(bit)
        bit *= 2
    return bits


def swap(block, axis, bit):
    size = lax.axis_size(axis)
    return lax.ppermute(block, axis, [(i, i ^ bit) for i in range(size)])


def gather_pieces(block, axis, bits):
    pieces = {0: block}
    for bit in bits:
        for j in list(pieces):
            pieces[j | bit] = swap(pieces[j], axis, bit)
    return [pieces[j] for j in range(len(pieces))]


def halving_order(bits):
    if not bits:
        return [0]
    rest = halving_order(bits[1:])
    return [bits[0] ^ j for j in rest] + rest


def scatter_halves(send, keep, axis, bits):
    terms = [keep]
    for at, bit in enumerate(bits):
        got = swap(send, axis, bit)
        terms = [t.astype(f32) for t in terms] + [got.astype(f32)]
        total = sum(terms)
        if at == len(bits) - 1:
            return total[0]
        half = total.shape[0] // 2
        send = total[:half].astype(bf16)
        terms = [total[half:]]
    return terms[0][0].astype(f32)


def scatter_parts(parts, axis, bits):
    parts = dict(enumerate(parts))
    for at, bit in enumerate(bits):
        last = at == len(bits) - 1
        kept = {}
        for j in sorted(parts):
            if not j & bit:
                got = swap(parts[j | bit], axis, bit)
                total = parts[j].astype(f32) + got.astype(f32)
                kept[j] = total if last or j == 0 else total.astype(bf16)
        parts = kept
    return parts[0].astype(f32)


def sum_everywhere(value, axes):
    for axis in axes:
        for bit in bits_of(lax.axis_size(axis)):
            value = value + swap(value, axis, bit)
    return value


def resident(shape):
    zeros = (0,) * len(shape)
    return pl.BlockSpec(shape, lambda *_: zeros, pipeline_mode=pl.Buffered(1))


def own_block(rows, columns):
    return pl.BlockSpec((rows, columns), lambda i, ids, *_: (ids[0] ^ i, 0))


def step_block(rows, columns):
    return pl.BlockSpec((rows, columns), lambda i, *_: (i, 0))


def place_pieces(pieces, where, number):
    rows = pieces[0].shape[0]
    for j, piece in enumerate(pieces):
        where[pl.ds(pl.multiple_of((number ^ j) * rows, rows), rows), :] = piece[...]


def pick_piece(pieces, where, step):
    for j, piece in enumerate(pieces):

        @pl.when(step == j)
        def _(piece=piece):
            where[...] = piece[...]


def store_part(parts, value, step, rows):
    if len(parts) == 1:
        parts[0][pl.ds(pl.multiple_of(step * rows, rows), rows), :] = value
        return
    for j, part in enumerate(parts):

        @pl.when(step == j)
        def _(part=part):
            part[...] = value


def store_halves(send, keep, total, number, order):
    half, rows = send.shape[0], send.shape[1]
    for at, j in enumerate(order):
        where = send if at < half else keep
        block = total[pl.ds(pl.multiple_of((number ^ j) * rows, rows), rows), :]
        where[at % half] = block.astype(bf16)


def halves_shape(size, rows, columns):
    return jax.ShapeDtypeStruct((max(size // 2, 1), rows, columns), bf16)


def call(kernel, name, grid, prefetch, operands, specs, outs, out_specs, scratch, flops, extra=0):
    size = sum(x.size * x.dtype.itemsize for x in list(operands) + list(outs))
    return pl.pallas_call(
        kernel,
        grid_spec=pltpu.PrefetchScalarGridSpec(
            num_scalar_prefetch=len(prefetch),
            grid=grid,
            in_specs=specs,
            out_specs=out_specs,
            scratch_shapes=scratch,
        ),
        out_shape=outs,
        compiler_params=pltpu.CompilerParams(
            dimension_semantics=("arbitrary",) * len(grid), vmem_limit_bytes=VMEM_MOST
        ),
        cost_estimate=pl.CostEstimate(
            flops=int(flops), bytes_accessed=int(size), transcendentals=int(extra)
        ),
        name=name,
    )(*prefetch, *operands)


def shaped(*shape, dtype=bf16):
    return jax.ShapeDtypeStruct(shape, dtype)


def shift_gain(block, gain, shift):
    return (block.astype(f32) * gain[...] + shift[...]).astype(bf16)


def turn(block, cosine, low_sine, high_sine, sign):
    width = block.shape[1]
    step = min(width, 128)
    done = []
    for start in range(0, width, step):
        part = block[:, start : start + step]
        if step == 128:
            left = pltpu.roll(part, step - ROT // 2, 1)
            right = pltpu.roll(part, ROT // 2, 1)
        else:
            left = jnp.concatenate([part[:, ROT // 2 :], part[:, : ROT // 2]], axis=1)
            right = jnp.concatenate([part[:, -ROT // 2 :], part[:, : -ROT // 2]], axis=1)
        moved = left * low_sine[:, :step] + right * high_sine[:, :step]
        done.append(part * cosine[:, :step] + moved * sign)
    return done[0] if len(done) == 1 else jnp.concatenate(done, axis=1)


def project_qkv(ids, info, sent, gain, shift, weight, bias, tables, width):
    groups, pieces = len(sent), len(weight)
    rows, model = sent[0].shape

    def kernel(ids, info, *refs):
        sent_refs, refs = refs[:groups], refs[groups:]
        weight_refs, refs = refs[:pieces], refs[pieces:]
        gain, shift, bias, cos, low, high, q_out, k_out, v_out, whole, block = refs
        step = pl.program_id(0)

        @pl.when(step == 0)
        def _():
            place_pieces(weight_refs, whole, ids[1])

        pick_piece(sent_refs, block, step)
        qkv = dot_nn(shift_gain(block[...], gain, shift), whole[...]) + bias[...]
        first = (ids[0] ^ step) * (rows // SEG)
        for at in range(rows // SEG):
            number = first + at
            table = pl.ds(pl.multiple_of(info[number // NB, number % NB, 4] * SEG, SEG), SEG)
            tabs = (cos[table, :], low[table, :], high[table, :])
            own = slice(at * SEG, (at + 1) * SEG)
            q_out[own, :] = (turn(qkv[own, :width], *tabs, 1.0) * HD**-0.5).astype(bf16)
            k_out[own, :] = turn(qkv[own, width : 2 * width], *tabs, 1.0).astype(bf16)
        v_out[...] = qkv[:, 2 * width :].astype(bf16)

    operands = [*sent, *weight, gain, shift, bias, *tables]
    out = shaped(groups * rows, width)
    return call(
        kernel,
        "project_qkv",
        (groups,),
        [ids, info],
        operands,
        [resident(x.shape) for x in operands],
        [out] * 3,
        [own_block(rows, width)] * 3,
        [pltpu.VMEM((model, 3 * width), bf16), pltpu.VMEM((rows, model), bf16)],
        2 * groups * rows * model * 3 * width,
    )


def project_grad(ids, grad, weight):
    groups, pieces = len(grad), len(weight)
    rows, model = grad[0].shape
    width = weight[0].shape[1]

    def kernel(ids, *refs):
        grad_refs, refs = refs[:groups], refs[groups:]
        weight_refs, (out, whole, block) = refs[:pieces], refs[pieces:]
        step = pl.program_id(0)

        @pl.when(step == 0)
        def _():
            place_pieces(weight_refs, whole, ids[1])

        pick_piece(grad_refs, block, step)
        out[...] = dot_nn(block[...], whole[...]).astype(bf16)

    operands = [*grad, *weight]
    return call(
        kernel,
        "project_grad",
        (groups,),
        [ids],
        operands,
        [resident(x.shape) for x in operands],
        [shaped(groups * rows, width)],
        [own_block(rows, width)],
        [pltpu.VMEM((model, width), bf16), pltpu.VMEM((rows, model), bf16)],
        2 * groups * rows * model * width,
    )[0]


def attention_kernel(
    info, q_ref, do_ref, k_ref, v_ref, cos, low, high, ctx_ref, dq_ref, dk_ref, dv_ref, dk_sum, dv_sum
):
    tree, step = pl.program_id(0), pl.program_id(1)
    width = q_ref.shape[1]
    heads = width // HD
    lane_head = lax.broadcasted_iota(jnp.int32, (SEG, width), 1) // HD

    @pl.when(step == 0)
    def _():
        dk_sum[...] = jnp.zeros_like(dk_sum)
        dv_sum[...] = jnp.zeros_like(dv_sum)

    first, second = info[tree, step, 0], info[tree, step, 1]
    first_rows = pl.ds(pl.multiple_of(first * SEG, SEG), SEG)
    second_rows = pl.ds(pl.multiple_of(second * SEG, SEG), SEG)
    queries, grads = q_ref[...], do_ref[...]
    zero = jnp.zeros_like(queries)
    q_rows = jnp.concatenate([jnp.where(lane_head == h, queries, zero) for h in range(heads)], axis=0)
    g_rows = jnp.concatenate([jnp.where(lane_head == h, grads, zero) for h in range(heads)], axis=0)
    q_turned, g_turned = queries.T, grads.T
    ahead = lax.broadcasted_iota(jnp.int32, (SEG, SEG), 1) - lax.broadcasted_iota(
        jnp.int32, (SEG, SEG), 0
    )
    seen = jnp.concatenate([ahead <= info[tree, step, 2], ahead <= info[tree, step, 3]], axis=1)
    seen = jnp.concatenate([seen] * heads, axis=0)
    k_near = jnp.concatenate([k_ref[first_rows, :], k_ref[second_rows, :]], axis=0)
    v_near = jnp.concatenate([v_ref[first_rows, :], v_ref[second_rows, :]], axis=0)

    def work(pairs):
        count = pairs * 2 * SEG
        near = jnp.where(seen, dot_nt(q_rows, k_near), masked_score)
        most = jnp.max(near, axis=1, keepdims=True)
        if count:
            k_far, v_far = k_ref[0:count, :], v_ref[0:count, :]
            far = dot_nt(q_rows, k_far)
            most = jnp.maximum(most, jnp.max(far, axis=1, keepdims=True))
        near = jnp.exp(near - most)
        total = jnp.sum(near, axis=1, keepdims=True)
        if count:
            far = jnp.exp(far - most)
            total = total + jnp.sum(far, axis=1, keepdims=True)
        scale = 1.0 / total
        near = near * scale
        near_low = near.astype(bf16)
        context = dot_nn(near_low, v_near)
        if count:
            far = far * scale
            far_low = far.astype(bf16)
            context = context + dot_nn(far_low, v_far)
        delta = jnp.sum(context * g_rows.astype(f32), axis=1, keepdims=True)
        near = (near * (dot_nt(g_rows, v_near) - delta)).astype(bf16)
        dq = dot_nn(near, k_near)
        if count:
            far = (far * (dot_nt(g_rows, v_far) - delta)).astype(bf16)
            dq = dq + dot_nn(far, k_far)
        ctx_own, dq_own = context[0:SEG], dq[0:SEG]
        for h in range(1, heads):
            ctx_own = jnp.where(lane_head == h, context[h * SEG : (h + 1) * SEG], ctx_own)
            dq_own = jnp.where(lane_head == h, dq[h * SEG : (h + 1) * SEG], dq_own)
        ctx_ref[...] = ctx_own.astype(bf16)
        dq_ref[...] = turn(dq_own * HD**-0.5, cos, low, high, -1.0).astype(bf16)
        for h in range(heads):
            own = slice(h * SEG, (h + 1) * SEG)
            part = slice(h * HD, (h + 1) * HD)
            dk = dot_nn(q_turned[part], near[own])
            dv = dot_nn(g_turned[part], near_low[own])
            dk_sum[first, part, :] += dk[:, :SEG]
            dv_sum[first, part, :] += dv[:, :SEG]
            dk_sum[second, part, :] += dk[:, SEG:]
            dv_sum[second, part, :] += dv[:, SEG:]
            if count:
                dk = dot_nn(q_turned[part], far[own])
                dv = dot_nn(g_turned[part], far_low[own])
                for j in range(2 * pairs):
                    dk_sum[j, part, :] += dk[:, j * SEG : (j + 1) * SEG]
                    dv_sum[j, part, :] += dv[:, j * SEG : (j + 1) * SEG]

    for pairs in range(NT // 2):

        @pl.when(step // 2 == pairs)
        def _(pairs=pairs):
            work(pairs)

    @pl.when(step >= NT)
    def _():
        work(NT // 2)

    @pl.when(step == NB - 1)
    def _():
        def finish(j, carry):
            rows = pl.ds(pl.multiple_of(j * SEG, SEG), SEG)
            dv_ref[rows, :] = dv_sum[j].T.astype(bf16)
            dk_ref[rows, :] = dk_sum[j].T.astype(bf16)
            return carry

        lax.fori_loop(0, NB, finish, 0)


def attention(info, tables, queries, keys, values, grads):
    total, width = queries.shape
    trees = total // TREE
    table_width = tables[0].shape[1]
    block = pl.BlockSpec((SEG, width), lambda t, b, info: (t * NB + b, 0))
    whole = pl.BlockSpec((TREE, width), lambda t, b, info: (t, 0))
    table = pl.BlockSpec((SEG, table_width), lambda t, b, info: (info[t, b, 4], 0))
    scores = trees * (TREE - TRUNK) * (TRUNK + 2 * SEG) * (width // HD)
    return call(
        attention_kernel,
        "attention",
        (trees, NB),
        [info],
        [queries, grads, keys, values, *tables],
        [block, block, whole, whole, table, table, table],
        [shaped(total, width)] * 4,
        [block, block, whole, whole],
        [pltpu.VMEM((NB, width, SEG), f32), pltpu.VMEM((NB, width, SEG), f32)],
        scores * width * 2 * 6 * 1.3,
        scores,
    )


def project_context(ids, context, grad, weight, order):
    groups, pieces = len(grad), len(weight)
    rows, model = grad[0].shape
    width = context.shape[1]
    parts = groups if groups <= 4 else 1

    def kernel(ids, ctx, *refs):
        grad_refs, refs = refs[:groups], refs[groups:]
        weight_refs, refs = refs[:pieces], refs[pieces:]
        part_refs, refs = refs[:parts], refs[parts:]
        send, keep, whole, block, total = refs
        step = pl.program_id(0)

        @pl.when(step == 0)
        def _():
            place_pieces(weight_refs, whole, ids[1])
            total[...] = jnp.zeros_like(total)

        pick_piece(grad_refs, block, step)
        store_part(part_refs, dot_nt(ctx[...], whole[...]).astype(bf16), step, rows)
        total[...] += dot_tn(block[...], ctx[...])

        @pl.when(step == groups - 1)
        def _():
            store_halves(send, keep, total, ids[1], order)

    operands = [context, *grad, *weight]
    part = shaped(groups * rows // parts, model)
    halves = halves_shape(pieces, model // pieces, width)
    outs = [part] * parts + [halves] * 2
    out = call(
        kernel,
        "project_context",
        (groups,),
        [ids],
        operands,
        [own_block(rows, width)] + [resident(x.shape) for x in operands[1:]],
        outs,
        [resident(x.shape) for x in outs],
        [
            pltpu.VMEM((model, width), bf16),
            pltpu.VMEM((rows, model), bf16),
            pltpu.VMEM((model, width), f32),
        ],
        4 * groups * rows * model * width,
    )
    return split_parts(out[:parts], groups), out[parts], out[parts + 1]


def split_parts(parts, groups):
    if len(parts) == groups:
        return list(parts)
    rows = parts[0].shape[0] // groups
    return [parts[0][j * rows : (j + 1) * rows] for j in range(groups)]


def mlp_forward(ids, sent, gain, shift, fc, bias, out):
    groups, pieces = len(sent), len(fc)
    rows, model = sent[0].shape
    units = fc[0].shape[1]
    parts = groups if groups <= 4 else 1

    def kernel(ids, *refs):
        sent_refs, refs = refs[:groups], refs[groups:]
        fc_refs, refs = refs[:pieces], refs[pieces:]
        out_refs, refs = refs[:pieces], refs[pieces:]
        gain, shift, bias, act_ref, slope_ref = refs[:5]
        part_refs, (fc_whole, out_whole, block) = refs[5 : 5 + parts], refs[5 + parts :]
        step = pl.program_id(0)

        @pl.when(step == 0)
        def _():
            place_pieces(fc_refs, fc_whole, ids[1])
            place_pieces(out_refs, out_whole, ids[1])

        pick_piece(sent_refs, block, step)
        hidden = dot_nn(shift_gain(block[...], gain, shift), fc_whole[...]) + bias[...]
        size = jnp.abs(hidden)
        ratio = 1.0 / (1.0 + TAIL_SLOPE * size)
        tail = jnp.full_like(ratio, TAIL_COEFS[-1])
        for coef in TAIL_COEFS[-2::-1]:
            tail = tail * ratio + coef
        bell = jnp.exp(hidden * hidden * -0.5)
        tail = tail * ratio * bell
        chance = jnp.where(hidden < 0, tail, 1.0 - tail)
        active = (hidden * chance).astype(bf16)
        act_ref[...] = active
        slope_ref[...] = chance + hidden * bell * 0.3989422804014327
        store_part(part_refs, dot_nt(active, out_whole[...]).astype(bf16), step, rows)

    operands = [*sent, *fc, *out, gain, shift, bias]
    part = shaped(groups * rows // parts, model)
    outs = [shaped(groups * rows, units), shaped(groups * rows, units, dtype=f32)] + [part] * parts
    done = call(
        kernel,
        "mlp_forward",
        (groups,),
        [ids],
        operands,
        [resident(x.shape) for x in operands],
        outs,
        [step_block(rows, units)] * 2 + [resident(part.shape)] * parts,
        [
            pltpu.VMEM((model, units), bf16),
            pltpu.VMEM((model, units), bf16),
            pltpu.VMEM((rows, model), bf16),
        ],
        4 * groups * rows * model * units,
    )
    return done[0], done[1], split_parts(done[2:], groups)


def mlp_backward(ids, sent, grad, active, slope, gain, shift, fc, out, fc_order, out_order):
    groups, pieces = len(sent), len(fc)
    rows, model = sent[0].shape
    units = fc[0].shape[1]

    def kernel(ids, act_ref, slope_ref, *refs):
        sent_refs, refs = refs[:groups], refs[groups:]
        grad_refs, refs = refs[:groups], refs[groups:]
        fc_refs, refs = refs[:pieces], refs[pieces:]
        out_refs, refs = refs[:pieces], refs[pieces:]
        gain, shift, back_ref, bias_ref, sums_ref, fc_send, fc_keep, out_send, out_keep = refs[:9]
        fc_whole, out_whole, block, grad_block, fc_total, out_total = refs[9:]
        step = pl.program_id(0)

        @pl.when(step == 0)
        def _():
            place_pieces(fc_refs, fc_whole, ids[1])
            place_pieces(out_refs, out_whole, ids[1])
            fc_total[...] = jnp.zeros_like(fc_total)
            out_total[...] = jnp.zeros_like(out_total)
            bias_ref[...] = jnp.zeros_like(bias_ref)
            sums_ref[...] = jnp.zeros_like(sums_ref)

        pick_piece(sent_refs, block, step)
        pick_piece(grad_refs, grad_block, step)
        hidden = (dot_nn(grad_block[...], out_whole[...]) * slope_ref[...]).astype(bf16)
        bias_ref[0:1, :] += jnp.sum(hidden.astype(f32), axis=0, keepdims=True)
        back = dot_nt(hidden, fc_whole[...])
        back_ref[...] = back
        token = block[...]
        sums_ref[0:1, :] += jnp.sum(back * token.astype(f32), axis=0, keepdims=True)
        sums_ref[1:2, :] += jnp.sum(back, axis=0, keepdims=True)
        fc_total[...] += dot_tn(shift_gain(token, gain, shift), hidden)
        out_total[...] += dot_tn(grad_block[...], act_ref[...])

        @pl.when(step == groups - 1)
        def _():
            store_halves(fc_send, fc_keep, fc_total, ids[1], fc_order)
            store_halves(out_send, out_keep, out_total, ids[1], out_order)

    operands = [active, slope, *sent, *grad, *fc, *out, gain, shift]
    halves = halves_shape(pieces, model // pieces, units)
    outs = [
        shaped(groups * rows, model, dtype=f32),
        shaped(8, units, dtype=f32),
        shaped(8, model, dtype=f32),
    ] + [halves] * 4
    return call(
        kernel,
        "mlp_backward",
        (groups,),
        [ids],
        operands,
        [step_block(rows, units)] * 2 + [resident(x.shape) for x in operands[2:]],
        outs,
        [step_block(rows, model)] + [resident(x.shape) for x in outs[1:]],
        [
            pltpu.VMEM((model, units), bf16),
            pltpu.VMEM((model, units), bf16),
            pltpu.VMEM((rows, model), bf16),
            pltpu.VMEM((rows, model), bf16),
            pltpu.VMEM((model, units), f32),
            pltpu.VMEM((model, units), f32),
        ],
        8 * groups * rows * model * units,
    )


def qkv_backward(ids, info, tables, dq, dk, dv, sent, back_mlp, gain, shift, gain_mlp, weight, order):
    groups, pieces = len(sent), len(weight)
    rows, model = sent[0].shape
    width = dq.shape[1]
    parts = groups if groups <= 4 else 1

    def kernel(ids, info, dq_ref, dk_ref, dv_ref, mlp_ref, *refs):
        sent_refs, refs = refs[:groups], refs[groups:]
        weight_refs, refs = refs[:pieces], refs[pieces:]
        gain, shift, gain_mlp, cos, low, high = refs[:6]
        part_refs, refs = refs[6 : 6 + parts], refs[6 + parts :]
        bias_ref, sums_ref, send, keep, whole, block, total, grads = refs
        step = pl.program_id(0)

        @pl.when(step == 0)
        def _():
            place_pieces(weight_refs, whole, ids[1])
            total[...] = jnp.zeros_like(total)
            bias_ref[...] = jnp.zeros_like(bias_ref)
            sums_ref[...] = jnp.zeros_like(sums_ref)

        pick_piece(sent_refs, block, step)
        grads[:, :width] = dq_ref[...]
        first = (ids[0] ^ step) * (rows // SEG)
        for at in range(rows // SEG):
            number = first + at
            table = pl.ds(pl.multiple_of(info[number // NB, number % NB, 4] * SEG, SEG), SEG)
            own = slice(at * SEG, (at + 1) * SEG)
            turned = turn(dk_ref[own, :], cos[table, :], low[table, :], high[table, :], -1.0)
            grads[own, width : 2 * width] = turned.astype(bf16)
        grads[:, 2 * width :] = dv_ref[...]
        bias_ref[0:1, :] += jnp.sum(grads[...].astype(f32), axis=0, keepdims=True)
        back = dot_nt(grads[...], whole[...])
        token = block[...]
        sums_ref[0:1, :] += jnp.sum(back * token.astype(f32), axis=0, keepdims=True)
        sums_ref[1:2, :] += jnp.sum(back, axis=0, keepdims=True)
        part = (back * gain[...] + mlp_ref[...] * gain_mlp[...]).astype(bf16)
        store_part(part_refs, part, step, rows)
        total[...] += dot_tn(shift_gain(token, gain, shift), grads[...])

        @pl.when(step == groups - 1)
        def _():
            store_halves(send, keep, total, ids[1], order)

    operands = [dq, dk, dv, back_mlp, *sent, *weight, gain, shift, gain_mlp, *tables]
    part = shaped(groups * rows // parts, model)
    halves = halves_shape(pieces, model // pieces, 3 * width)
    outs = (
        [part] * parts
        + [shaped(8, 3 * width, dtype=f32), shaped(8, model, dtype=f32)]
        + [halves] * 2
    )
    done = call(
        kernel,
        "qkv_backward",
        (groups,),
        [ids, info],
        operands,
        [own_block(rows, width)] * 3
        + [step_block(rows, model)]
        + [resident(x.shape) for x in operands[4:]],
        outs,
        [resident(x.shape) for x in outs],
        [
            pltpu.VMEM((model, 3 * width), bf16),
            pltpu.VMEM((rows, model), bf16),
            pltpu.VMEM((model, 3 * width), f32),
            pltpu.VMEM((rows, 3 * width), bf16),
        ],
        4 * groups * rows * model * 3 * width,
    )
    return (split_parts(done[:parts], groups), *done[parts:])


def tree_table(segment_ids, parent_ids):
    trees = segment_ids.shape[0] // TREE
    segment = segment_ids.reshape(trees, NB, SEG)[:, :, 0]
    parent = parent_ids.reshape(trees, NB, SEG)[:, :, 0]
    block = lax.broadcasted_iota(jnp.int32, (trees, NB), 1)
    trunk = block < NT
    leaf = (parent != segment[:, :1]) & ~trunk
    at = lax.broadcasted_iota(jnp.int32, (trees, NB, NB), 2)
    owner = jnp.sum(jnp.where(segment[:, None, :] == parent[:, :, None], at, 0), axis=2)
    odd = block % 2 == 1
    first = jnp.where(trunk, block // 2 * 2, block)
    second = jnp.where(trunk, block // 2 * 2 + 1, jnp.where(leaf, owner, block))
    first_most = jnp.where(trunk & odd, SEG, 0)
    second_most = jnp.where(trunk, jnp.where(odd, 0, -SEG), jnp.where(leaf, SEG, -SEG))
    table = jnp.where(trunk, block, jnp.where(leaf, NT + 1, NT))
    return jnp.stack([first, second, first_most, second_most, table], axis=2).astype(jnp.int32)


def angle_tables():
    places = TRUNK + 2 * SEG
    place = lax.broadcasted_iota(jnp.int32, (places, 2 * HD), 0).astype(f32)
    lane = lax.broadcasted_iota(jnp.int32, (places, 2 * HD), 1) % HD
    half = ROT // 2
    frequency = 10000.0 ** (-((lane % half).astype(f32) * 2.0 / ROT))
    angle = place * frequency
    cosine = jnp.where(lane < ROT, jnp.cos(angle), 1.0)
    sine = jnp.sin(angle)
    low = jnp.where(lane < half, -sine, 0.0)
    high = jnp.where((lane >= half) & (lane < ROT), sine, 0.0)
    return cosine, low, high


def by_kind(array, heads):
    shape = array.shape[:-1]
    array = array.reshape(*shape, heads, 3, HD)
    return jnp.swapaxes(array, -3, -2).reshape(*shape, 3 * heads * HD)


def by_head(array, heads):
    shape = array.shape[:-1]
    array = array.reshape(*shape, 3, heads, HD)
    return jnp.swapaxes(array, -3, -2).reshape(*shape, 3 * heads * HD)


def local(
    stream_in,
    segment_ids,
    parent_ids,
    norm_gain_attn,
    norm_shift_attn,
    norm_gain_mlp,
    norm_shift_mlp,
    qkv_weight,
    qkv_bias,
    dense_weight,
    dense_bias,
    fc_weight,
    fc_bias,
    out_weight,
    out_bias,
    out_grad,
):
    tensor_rank = lax.axis_index("tensor")
    data_rank = lax.axis_index("dp")
    ids = jnp.stack([tensor_rank, data_rank]).astype(jnp.int32)
    rows_local = stream_in.shape[0]
    model = stream_in.shape[1]
    qkv_width = qkv_weight.shape[1]
    heads = qkv_width // (3 * HD)
    width = heads * HD
    units = fc_weight.shape[1]
    tensor_bits = bits_of(lax.axis_size("tensor"))
    far_first = tensor_bits[:0:-1] + tensor_bits[:1]
    data_bits = bits_of(lax.axis_size("dp"))
    rows_first = data_bits[:0:-1] + data_bits[:1]
    columns_first = data_bits[:1] + data_bits[:0:-1]

    row_mean = jnp.mean(stream_in, axis=-1, keepdims=True)
    centred = stream_in - row_mean
    row_var = jnp.mean(centred * centred, axis=-1, keepdims=True)
    inv_std = lax.rsqrt(row_var + eps_norm)
    normalized = centred * inv_std
    sent_norm = normalized.astype(bf16)

    qkv_pieces = gather_pieces(by_kind(qkv_weight.astype(bf16), heads), "dp", rows_first)
    dense_pieces = gather_pieces(dense_weight.astype(bf16).T, "dp", columns_first)
    fc_pieces = gather_pieces(fc_weight.astype(bf16), "dp", rows_first)
    out_pieces = gather_pieces(out_weight.astype(bf16).T, "dp", columns_first)
    sent = gather_pieces(sent_norm, "tensor", far_first)
    first_grad = lax.optimization_barrier((out_grad, sent[-1]))[0]
    grad = gather_pieces(first_grad, "tensor", far_first)

    info = tree_table(segment_ids, parent_ids)
    tables = angle_tables()
    gain_attn, shift_attn = norm_gain_attn[None, :], norm_shift_attn[None, :]
    gain_mlp, shift_mlp = norm_gain_mlp[None, :], norm_shift_mlp[None, :]
    qkv_bias_own = by_kind(
        lax.dynamic_slice_in_dim(qkv_bias, tensor_rank * qkv_width, qkv_width), heads
    )[None, :]
    fc_bias_own = lax.dynamic_slice_in_dim(fc_bias, tensor_rank * units, units)[None, :]

    queries, keys, values = project_qkv(
        ids, info, sent, gain_attn, shift_attn, qkv_pieces, qkv_bias_own, tables, width
    )
    active, slope, mlp_parts = mlp_forward(
        ids, sent, gain_mlp, shift_mlp, fc_pieces, fc_bias_own, out_pieces
    )
    mlp_sum = scatter_parts(mlp_parts, "tensor", tensor_bits)
    grad_context = project_grad(ids, grad, dense_pieces)
    context, dq, dk, dv = attention(info, tables, queries, keys, values, grad_context)
    out_bits, fc_bits = columns_first[::-1], rows_first[::-1]
    attn_parts, dense_send, dense_keep = project_context(
        ids, context, grad, dense_pieces, halving_order(out_bits)
    )
    attn_sum = scatter_parts(attn_parts, "tensor", tensor_bits)
    back_mlp, fc_bias_sums, mlp_sums, fc_send, fc_keep, out_send, out_keep = mlp_backward(
        ids,
        sent,
        grad,
        active,
        slope,
        gain_mlp,
        shift_mlp,
        fc_pieces,
        out_pieces,
        halving_order(fc_bits),
        halving_order(out_bits),
    )
    back_parts, qkv_bias_sums, attn_sums, qkv_send, qkv_keep = qkv_backward(
        ids,
        info,
        tables,
        dq,
        dk,
        dv,
        sent,
        back_mlp,
        gain_attn,
        shift_attn,
        gain_mlp,
        qkv_pieces,
        halving_order(fc_bits),
    )
    grad_sent = scatter_parts(back_parts, "tensor", tensor_bits)

    fc_weight_grad = scatter_halves(fc_send, fc_keep, "dp", fc_bits)
    out_weight_grad = scatter_halves(out_send, out_keep, "dp", out_bits).T
    dense_weight_grad = scatter_halves(dense_send, dense_keep, "dp", out_bits).T
    qkv_weight_grad = by_head(scatter_halves(qkv_send, qkv_keep, "dp", fc_bits), heads)

    attn_out = attn_sum + dense_bias
    mlp_out = mlp_sum + out_bias
    output = stream_in + attn_out + mlp_out

    mean_grad = jnp.mean(grad_sent, axis=-1, keepdims=True)
    mean_cross = jnp.mean(grad_sent * normalized, axis=-1, keepdims=True)
    stream_grad = out_grad.astype(f32) + inv_std * (
        grad_sent - mean_grad - normalized * mean_cross
    )

    residual_part = jnp.sum(out_grad.astype(f32), axis=0)
    squares = jnp.stack([jnp.sum(output * output), jnp.sum(attn_out * attn_out), jnp.sum(mlp_out * mlp_out)])
    count_all = float(rows_local * lax.axis_size("dp") * lax.axis_size("tensor") * model)

    fc_bias_spread = lax.dynamic_update_slice(
        jnp.zeros(fc_bias.shape, f32), fc_bias_sums[0], (tensor_rank * units,)
    )
    early = jnp.concatenate(
        [residual_part, mlp_sums[0], mlp_sums[1], fc_bias_spread, jnp.pad(squares, (0, 125))]
    )
    early = sum_everywhere(early, ("tensor", "dp"))
    qkv_bias_spread = lax.dynamic_update_slice(
        jnp.zeros(qkv_bias.shape, f32), by_head(qkv_bias_sums[0], heads), (tensor_rank * qkv_width,)
    )
    late = jnp.concatenate([attn_sums[0], attn_sums[1], qkv_bias_spread])
    late = sum_everywhere(late, ("tensor", "dp"))

    residual_grad = early[:model]
    gain_mlp_grad = early[model : 2 * model]
    shift_mlp_grad = early[2 * model : 3 * model]
    fc_bias_grad = early[3 * model : 3 * model + fc_bias.shape[0]]
    squares = early[3 * model + fc_bias.shape[0] :][:3]
    gain_attn_grad = late[:model]
    shift_attn_grad = late[model : 2 * model]
    qkv_bias_grad = late[2 * model :]
    root_squares = jnp.sqrt(squares / count_all)
    return (
        output,
        stream_grad,
        gain_attn_grad,
        shift_attn_grad,
        gain_mlp_grad,
        shift_mlp_grad,
        qkv_weight_grad,
        qkv_bias_grad,
        dense_weight_grad,
        residual_grad,
        fc_weight_grad,
        fc_bias_grad,
        out_weight_grad,
        residual_grad,
        root_squares,
    )


def solution(mesh):
    tokens, weights, rows, whole = (
        P(("dp", "tensor"), None),
        P("dp", "tensor"),
        P("tensor", "dp"),
        P(),
    )
    return jax.shard_map(
        local,
        mesh=mesh,
        in_specs=(
            tokens,
            P("dp"),
            P("dp"),
            whole,
            whole,
            whole,
            whole,
            weights,
            whole,
            rows,
            whole,
            weights,
            whole,
            rows,
            whole,
            tokens,
        ),
        out_specs=(
            tokens,
            tokens,
            whole,
            whole,
            whole,
            whole,
            weights,
            whole,
            rows,
            whole,
            weights,
            whole,
            rows,
            whole,
            whole,
        ),
        check_vma=False,
    )
```

```python
import jax
import jax.numpy as jnp
from jax import lax
from jax.experimental import pallas as pl
from jax.experimental.pallas import tpu as pltpu
from jax.sharding import PartitionSpec as P

HD = 64
ROT = 16
TRUNK = 1024
SEG = 128
TREE = 2560
NB = TREE // SEG
NT = TRUNK // SEG

f32 = jnp.float32
bf16 = jnp.bfloat16
eps_norm = 1e-05
masked_score = -1e30
VMEM_MOST = 62 << 20

TAIL_SLOPE = 0.3
TAIL_COEFS = (
    0.11968663334846497,
    0.11957288533449173,
    0.11022695899009705,
    0.07842729985713959,
    0.09605274349451065,
    -0.07923758029937744,
    0.191569522023201,
    -0.22805799543857574,
    0.1123715341091156,
    -0.02061200700700283,
)


def dot_nn(left, right):
    return lax.dot_general(left, right, (((1,), (0,)), ((), ())), preferred_element_type=f32)


def dot_nt(left, right):
    return lax.dot_general(left, right, (((1,), (1,)), ((), ())), preferred_element_type=f32)


def dot_tn(left, right):
    return lax.dot_general(left, right, (((0,), (0,)), ((), ())), preferred_element_type=f32)


def bits_of(size):
    bits = []
    bit = 1
    while bit < size:
        bits.append(bit)
        bit *= 2
    return bits


def swap(block, axis, bit):
    size = lax.axis_size(axis)
    return lax.ppermute(block, axis, [(i, i ^ bit) for i in range(size)])


def tie(*values):
    return lax.optimization_barrier(values)


def gather_far(block, axis, bits):
    pieces = [block]
    for bit in bits[1:]:
        pieces = pieces + [swap(piece, axis, bit) for piece in pieces]
    return pieces


def gather_near(pieces, axis):
    pieces = [x for piece in pieces for x in (piece, swap(piece, axis, 1))]
    return pieces


class Pack:
    def __init__(self, block, axis, bits):
        self.rows, self.axis, self.bits = block.shape[0], axis, list(bits)
        self.arrays, self.owners = [block], [[0]]

    def double(self):
        bit = self.bits.pop(0)
        held = self.arrays[0] if len(self.arrays) == 1 else jnp.concatenate(self.arrays, axis=0)
        self.owners.append([j ^ bit for owners in self.owners for j in owners])
        self.arrays.append(swap(held, self.axis, bit))

    def place(self, refs, where, number, columns):
        for ref, owners in zip(refs, self.owners):
            for at, j in enumerate(owners):
                rows = pl.ds(pl.multiple_of((number ^ j) * self.rows, self.rows), self.rows)
                where[rows, :] = ref[at * self.rows : (at + 1) * self.rows, columns]


def tie_packs(*packs, beside=()):
    flat = tie(*beside, *[x for pack in packs for x in pack.arrays])
    at = len(beside)
    for pack in packs:
        pack.arrays = list(flat[at : at + len(pack.arrays)])
        at += len(pack.arrays)
    return list(flat[: len(beside)])


def halving_order(bits):
    if not bits:
        return [0]
    rest = halving_order(bits[1:])
    return [bits[0] ^ j for j in rest] + rest


class Halving:
    def __init__(self, send, keep, axis, bits):
        self.send, self.terms, self.axis, self.bits = send, [keep], axis, list(bits)

    def swap(self):
        self.got = swap(self.send, self.axis, self.bits.pop(0))

    def add(self):
        total = sum([x.astype(f32) for x in self.terms] + [self.got.astype(f32)])
        if self.bits:
            half = total.shape[0] // 2
            self.send = total[:half].astype(bf16)
            self.terms = [total[half:]]
        else:
            self.total = total[0]

    def most(self):
        while len(self.bits) > 1:
            self.swap()
            self.add()

    def finish(self):
        while self.bits:
            self.swap()
            self.add()
        return self.total


def tie_halves(values, *halvings):
    flat = tie(*values, *[x.got for x in halvings])
    for x, got in zip(halvings, flat[len(values) :]):
        x.got = got
    return flat[: len(values)]


def sum_everywhere(value, axes):
    for axis in axes:
        for bit in bits_of(lax.axis_size(axis)):
            value = value + swap(value, axis, bit)
    return value


def resident(shape):
    zeros = (0,) * len(shape)
    return pl.BlockSpec(shape, lambda *_: zeros, pipeline_mode=pl.Buffered(1))


def own_block(rows, columns):
    return pl.BlockSpec((rows, columns), lambda i, ids, *_: (ids[0] ^ ids[2 + i], 0))


def step_block(rows, columns):
    return pl.BlockSpec((rows, columns), lambda i, *_: (i, 0))


def half_blocks(groups, rows, columns):
    half = groups // 2
    shape = (pl.Squeezed(), rows, columns)
    return [
        pl.BlockSpec(shape, lambda i, *_: (jnp.minimum(i, half - 1), 0, 0)),
        pl.BlockSpec(shape, lambda i, *_: (jnp.maximum(i - half, 0), 0, 0)),
    ]


def store_half(send, keep, value, step, groups):
    @pl.when(step < groups // 2)
    def _():
        send[...] = value

    @pl.when(step >= groups // 2)
    def _():
        keep[...] = value


class Tokens:
    def __init__(self, pieces, order):
        self.groups, (self.rows, self.model) = len(pieces), pieces[0].shape
        if self.groups <= 4:
            self.arrays = [pieces[j] for j in order]
            self.specs = [resident(x.shape) for x in pieces]
        else:
            self.arrays = [jnp.concatenate([pieces[j] for j in order], axis=0)]
            self.specs = [step_block(self.rows, self.model)]


def pick_piece(pieces, where, step):
    if len(pieces) == 1:
        where[...] = pieces[0][...]
        return
    for at, piece in enumerate(pieces):

        @pl.when(step == at)
        def _(piece=piece):
            where[...] = piece[...]


def store_halves(send, keep, total, number, order, columns=slice(None)):
    half, rows = send.shape[0], send.shape[1]
    for at, j in enumerate(order):
        where = send if at < half else keep
        block = total[pl.ds(pl.multiple_of((number ^ j) * rows, rows), rows), :]
        where[at % half, :, columns] = block.astype(bf16)


def call(kernel, name, grid, prefetch, operands, specs, outs, out_specs, scratch, flops, extra=0):
    size = sum(x.size * x.dtype.itemsize for x in list(operands) + list(outs))
    return pl.pallas_call(
        kernel,
        grid_spec=pltpu.PrefetchScalarGridSpec(
            num_scalar_prefetch=len(prefetch),
            grid=grid,
            in_specs=specs,
            out_specs=out_specs,
            scratch_shapes=scratch,
        ),
        out_shape=outs,
        compiler_params=pltpu.CompilerParams(
            dimension_semantics=("arbitrary",) * len(grid), vmem_limit_bytes=VMEM_MOST
        ),
        cost_estimate=pl.CostEstimate(
            flops=int(flops), bytes_accessed=int(size), transcendentals=int(extra)
        ),
        name=name,
    )(*prefetch, *operands)


def shaped(*shape, dtype=bf16):
    return jax.ShapeDtypeStruct(shape, dtype)


def shift_gain(block, gain, shift):
    return (block.astype(f32) * gain[...] + shift[...]).astype(bf16)


def turn(block, cosine, low_sine, high_sine, sign):
    width = block.shape[1]
    step = min(width, 128)
    done = []
    for start in range(0, width, step):
        part = block[:, start : start + step]
        if step == 128:
            left = pltpu.roll(part, step - ROT // 2, 1)
            right = pltpu.roll(part, ROT // 2, 1)
        else:
            left = jnp.concatenate([part[:, ROT // 2 :], part[:, : ROT // 2]], axis=1)
            right = jnp.concatenate([part[:, -ROT // 2 :], part[:, : -ROT // 2]], axis=1)
        moved = left * low_sine[:, :step] + right * high_sine[:, :step]
        done.append(part * cosine[:, :step] + moved * sign)
    return done[0] if len(done) == 1 else jnp.concatenate(done, axis=1)


def project_qkv(ids, info, sent, gain, shift, pack, bias, tables, width):
    groups, held, pieces = sent.groups, len(sent.arrays), len(pack.arrays)
    rows, model = sent.rows, sent.model

    def kernel(ids, info, *refs):
        sent_refs, refs = refs[:held], refs[held:]
        weight_refs, refs = refs[:pieces], refs[pieces:]
        gain, shift, bias, cos, low, high, q_out, k_out, v_out, whole, block = refs
        step = pl.program_id(0)

        @pl.when(step == 0)
        def _():
            pack.place(weight_refs, whole, ids[1], slice(0, 3 * width))

        pick_piece(sent_refs, block, step)
        qkv = dot_nn(shift_gain(block[...], gain, shift), whole[...]) + bias[...]
        first = (ids[0] ^ ids[2 + step]) * (rows // SEG)
        for at in range(rows // SEG):
            number = first + at
            table = pl.ds(pl.multiple_of(info[number // NB, number % NB, 4] * SEG, SEG), SEG)
            tabs = (cos[table, :], low[table, :], high[table, :])
            own = slice(at * SEG, (at + 1) * SEG)
            q_out[own, :] = (turn(qkv[own, :width], *tabs, 1.0) * HD**-0.5).astype(bf16)
            k_out[own, :] = turn(qkv[own, width : 2 * width], *tabs, 1.0).astype(bf16)
        v_out[...] = qkv[:, 2 * width :].astype(bf16)

    operands = [*sent.arrays, *pack.arrays, gain, shift, bias, *tables]
    out = shaped(groups * rows, width)
    return call(
        kernel,
        "project_qkv",
        (groups,),
        [ids, info],
        operands,
        sent.specs + [resident(x.shape) for x in operands[held:]],
        [out] * 3,
        [own_block(rows, width)] * 3,
        [pltpu.VMEM((model, 3 * width), bf16), pltpu.VMEM((rows, model), bf16)],
        2 * groups * rows * model * 3 * width,
    )


def project_grad(ids, grad, pack, width):
    groups, held, pieces = grad.groups, len(grad.arrays), len(pack.arrays)
    rows, model = grad.rows, grad.model

    def kernel(ids, *refs):
        grad_refs, refs = refs[:held], refs[held:]
        weight_refs, (out, whole, block) = refs[:pieces], refs[pieces:]
        step = pl.program_id(0)

        @pl.when(step == 0)
        def _():
            pack.place(weight_refs, whole, ids[1], slice(3 * width, 4 * width))

        pick_piece(grad_refs, block, step)
        out[...] = dot_nn(block[...], whole[...]).astype(bf16)

    operands = [*grad.arrays, *pack.arrays]
    return call(
        kernel,
        "project_grad",
        (groups,),
        [ids],
        operands,
        grad.specs + [resident(x.shape) for x in operands[held:]],
        [shaped(groups * rows, width)],
        [own_block(rows, width)],
        [pltpu.VMEM((model, width), bf16), pltpu.VMEM((rows, model), bf16)],
        2 * groups * rows * model * width,
    )[0]


def attention_kernel(
    info, q_ref, do_ref, k_ref, v_ref, cos, low, high, ctx_ref, dq_ref, dk_ref, dv_ref, dk_sum, dv_sum
):
    tree, step = pl.program_id(0), pl.program_id(1)
    width = q_ref.shape[1]
    heads = width // HD
    lane_head = lax.broadcasted_iota(jnp.int32, (SEG, width), 1) // HD

    @pl.when(step == 0)
    def _():
        dk_sum[...] = jnp.zeros_like(dk_sum)
        dv_sum[...] = jnp.zeros_like(dv_sum)

    first, second = info[tree, step, 0], info[tree, step, 1]
    first_rows = pl.ds(pl.multiple_of(first * SEG, SEG), SEG)
    second_rows = pl.ds(pl.multiple_of(second * SEG, SEG), SEG)
    queries, grads = q_ref[...], do_ref[...]
    zero = jnp.zeros_like(queries)
    q_rows = jnp.concatenate([jnp.where(lane_head == h, queries, zero) for h in range(heads)], axis=0)
    g_rows = jnp.concatenate([jnp.where(lane_head == h, grads, zero) for h in range(heads)], axis=0)
    q_turned, g_turned = queries.T, grads.T
    ahead = lax.broadcasted_iota(jnp.int32, (SEG, SEG), 1) - lax.broadcasted_iota(
        jnp.int32, (SEG, SEG), 0
    )
    seen = jnp.concatenate([ahead <= info[tree, step, 2], ahead <= info[tree, step, 3]], axis=1)
    seen = jnp.concatenate([seen] * heads, axis=0)
    k_near = jnp.concatenate([k_ref[first_rows, :], k_ref[second_rows, :]], axis=0)
    v_near = jnp.concatenate([v_ref[first_rows, :], v_ref[second_rows, :]], axis=0)

    def work(pairs):
        count = pairs * 2 * SEG
        near = jnp.where(seen, dot_nt(q_rows, k_near), masked_score)
        most = jnp.max(near, axis=1, keepdims=True)
        if count:
            k_far, v_far = k_ref[0:count, :], v_ref[0:count, :]
            far = dot_nt(q_rows, k_far)
            most = jnp.maximum(most, jnp.max(far, axis=1, keepdims=True))
        near = jnp.exp(near - most)
        total = jnp.sum(near, axis=1, keepdims=True)
        if count:
            far = jnp.exp(far - most)
            total = total + jnp.sum(far, axis=1, keepdims=True)
        scale = 1.0 / total
        near = near * scale
        near_low = near.astype(bf16)
        context = dot_nn(near_low, v_near)
        if count:
            far = far * scale
            far_low = far.astype(bf16)
            context = context + dot_nn(far_low, v_far)
        delta = jnp.sum(context * g_rows.astype(f32), axis=1, keepdims=True)
        near = (near * (dot_nt(g_rows, v_near) - delta)).astype(bf16)
        dq = dot_nn(near, k_near)
        if count:
            far = (far * (dot_nt(g_rows, v_far) - delta)).astype(bf16)
            dq = dq + dot_nn(far, k_far)
        ctx_own, dq_own = context[0:SEG], dq[0:SEG]
        for h in range(1, heads):
            ctx_own = jnp.where(lane_head == h, context[h * SEG : (h + 1) * SEG], ctx_own)
            dq_own = jnp.where(lane_head == h, dq[h * SEG : (h + 1) * SEG], dq_own)
        ctx_ref[...] = ctx_own.astype(bf16)
        dq_ref[...] = turn(dq_own * HD**-0.5, cos, low, high, -1.0).astype(bf16)
        for h in range(heads):
            own = slice(h * SEG, (h + 1) * SEG)
            part = slice(h * HD, (h + 1) * HD)
            dk = dot_nn(q_turned[part], near[own])
            dv = dot_nn(g_turned[part], near_low[own])
            dk_sum[first, part, :] += dk[:, :SEG]
            dv_sum[first, part, :] += dv[:, :SEG]
            dk_sum[second, part, :] += dk[:, SEG:]
            dv_sum[second, part, :] += dv[:, SEG:]
            if count:
                dk = dot_nn(q_turned[part], far[own])
                dv = dot_nn(g_turned[part], far_low[own])
                for j in range(2 * pairs):
                    dk_sum[j, part, :] += dk[:, j * SEG : (j + 1) * SEG]
                    dv_sum[j, part, :] += dv[:, j * SEG : (j + 1) * SEG]

    for pairs in range(NT // 2):

        @pl.when(step // 2 == pairs)
        def _(pairs=pairs):
            work(pairs)

    @pl.when(step >= NT)
    def _():
        work(NT // 2)

    @pl.when(step == NB - 1)
    def _():
        def finish(j, carry):
            rows = pl.ds(pl.multiple_of(j * SEG, SEG), SEG)
            dv_ref[rows, :] = dv_sum[j].T.astype(bf16)
            dk_ref[rows, :] = dk_sum[j].T.astype(bf16)
            return carry

        lax.fori_loop(0, NB, finish, 0)


def attention(info, tables, queries, keys, values, grads):
    total, width = queries.shape
    trees = total // TREE
    table_width = tables[0].shape[1]
    block = pl.BlockSpec((SEG, width), lambda t, b, info: (t * NB + b, 0))
    whole = pl.BlockSpec((TREE, width), lambda t, b, info: (t, 0))
    table = pl.BlockSpec((SEG, table_width), lambda t, b, info: (info[t, b, 4], 0))
    scores = trees * (TREE - TRUNK) * (TRUNK + 2 * SEG) * (width // HD)
    return call(
        attention_kernel,
        "attention",
        (trees, NB),
        [info],
        [queries, grads, keys, values, *tables],
        [block, block, whole, whole, table, table, table],
        [shaped(total, width)] * 4,
        [block, block, whole, whole],
        [pltpu.VMEM((NB, width, SEG), f32), pltpu.VMEM((NB, width, SEG), f32)],
        scores * width * 2 * 6 * 1.3,
        scores,
    )


def project_context(ids, context, pack, groups, model):
    pieces = len(pack.arrays)
    rows, width = context.shape[0] // groups, context.shape[1]

    def kernel(ids, ctx, *refs):
        weight_refs, (send, keep, whole) = refs[:pieces], refs[pieces:]
        step = pl.program_id(0)

        @pl.when(step == 0)
        def _():
            pack.place(weight_refs, whole, ids[1], slice(3 * width, 4 * width))

        store_half(send, keep, dot_nt(ctx[...], whole[...]).astype(bf16), step, groups)

    operands = [context, *pack.arrays]
    half = shaped(groups // 2, rows, model)
    return call(
        kernel,
        "project_context",
        (groups,),
        [ids],
        operands,
        [own_block(rows, width)] + [resident(x.shape) for x in operands[1:]],
        [half] * 2,
        half_blocks(groups, rows, model),
        [pltpu.VMEM((model, width), bf16)],
        2 * groups * rows * model * width,
    )


def mlp_forward(ids, sent, grad, gain, shift, fc, bias, out, out_order):
    groups, held, pieces = sent.groups, len(sent.arrays), len(fc.arrays)
    rows, model = sent.rows, sent.model
    units = fc.arrays[0].shape[1]

    def kernel(ids, *refs):
        sent_refs, refs = refs[:held], refs[held:]
        grad_refs, refs = refs[:held], refs[held:]
        fc_refs, refs = refs[:pieces], refs[pieces:]
        out_refs, refs = refs[:pieces], refs[pieces:]
        gain, shift, bias, act_ref, slope_ref, send, keep, out_send, out_keep = refs[:9]
        fc_whole, out_whole, block, grad_block, total = refs[9:]
        step = pl.program_id(0)

        @pl.when(step == 0)
        def _():
            fc.place(fc_refs, fc_whole, ids[1], slice(None))
            out.place(out_refs, out_whole, ids[1], slice(None))
            total[...] = jnp.zeros_like(total)

        pick_piece(sent_refs, block, step)
        pick_piece(grad_refs, grad_block, step)
        hidden = dot_nn(shift_gain(block[...], gain, shift), fc_whole[...]) + bias[...]
        size = jnp.abs(hidden)
        ratio = 1.0 / (1.0 + TAIL_SLOPE * size)
        tail = jnp.full_like(ratio, TAIL_COEFS[-1])
        for coef in TAIL_COEFS[-2::-1]:
            tail = tail * ratio + coef
        bell = jnp.exp(hidden * hidden * -0.5)
        tail = tail * ratio * bell
        chance = jnp.where(hidden < 0, tail, 1.0 - tail)
        active = (hidden * chance).astype(bf16)
        act_ref[...] = active
        slope_ref[...] = chance + hidden * bell * 0.3989422804014327
        store_half(send, keep, dot_nt(active, out_whole[...]).astype(bf16), step, groups)
        total[...] += dot_tn(grad_block[...], active)

        @pl.when(step == groups - 1)
        def _():
            store_halves(out_send, out_keep, total, ids[1], out_order)

    operands = [*sent.arrays, *grad.arrays, *fc.arrays, *out.arrays, gain, shift, bias]
    count = model // fc.rows
    outs = [
        shaped(groups * rows, units),
        shaped(groups * rows, units, dtype=f32),
        shaped(groups // 2, rows, model),
        shaped(groups // 2, rows, model),
        shaped(count // 2, fc.rows, units),
        shaped(count // 2, fc.rows, units),
    ]
    return call(
        kernel,
        "mlp_forward",
        (groups,),
        [ids],
        operands,
        sent.specs + grad.specs + [resident(x.shape) for x in operands[2 * held :]],
        outs,
        [step_block(rows, units)] * 2
        + half_blocks(groups, rows, model)
        + [resident(x.shape) for x in outs[4:]],
        [
            pltpu.VMEM((model, units), bf16),
            pltpu.VMEM((model, units), bf16),
            pltpu.VMEM((rows, model), bf16),
            pltpu.VMEM((rows, model), bf16),
            pltpu.VMEM((model, units), f32),
        ],
        6 * groups * rows * model * units,
    )


def mlp_backward(ids, sent, grad, slope, gain, shift, fc, out, fc_order):
    groups, held, pieces = sent.groups, len(sent.arrays), len(fc.arrays)
    rows, model = sent.rows, sent.model
    units = fc.arrays[0].shape[1]

    def kernel(ids, slope_ref, *refs):
        sent_refs, refs = refs[:held], refs[held:]
        grad_refs, refs = refs[:held], refs[held:]
        fc_refs, refs = refs[:pieces], refs[pieces:]
        out_refs, refs = refs[:pieces], refs[pieces:]
        gain, shift, back_ref, bias_ref, sums_ref, fc_send, fc_keep = refs[:7]
        fc_whole, out_whole, block, grad_block, fc_total = refs[7:]
        step = pl.program_id(0)

        @pl.when(step == 0)
        def _():
            fc.place(fc_refs, fc_whole, ids[1], slice(None))
            out.place(out_refs, out_whole, ids[1], slice(None))
            fc_total[...] = jnp.zeros_like(fc_total)
            bias_ref[...] = jnp.zeros_like(bias_ref)
            sums_ref[...] = jnp.zeros_like(sums_ref)

        pick_piece(sent_refs, block, step)
        pick_piece(grad_refs, grad_block, step)
        hidden = (dot_nn(grad_block[...], out_whole[...]) * slope_ref[...]).astype(bf16)
        bias_ref[0:1, :] += jnp.sum(hidden.astype(f32), axis=0, keepdims=True)
        back = dot_nt(hidden, fc_whole[...])
        back_ref[...] = back
        token = block[...]
        sums_ref[0:1, :] += jnp.sum(back * token.astype(f32), axis=0, keepdims=True)
        sums_ref[1:2, :] += jnp.sum(back, axis=0, keepdims=True)
        fc_total[...] += dot_tn(shift_gain(token, gain, shift), hidden)

        @pl.when(step == groups - 1)
        def _():
            store_halves(fc_send, fc_keep, fc_total, ids[1], fc_order)

    operands = [slope, *sent.arrays, *grad.arrays, *fc.arrays, *out.arrays, gain, shift]
    count = model // fc.rows
    outs = [
        shaped(groups * rows, model, dtype=f32),
        shaped(8, units, dtype=f32),
        shaped(8, model, dtype=f32),
        shaped(count // 2, fc.rows, units),
        shaped(count // 2, fc.rows, units),
    ]
    return call(
        kernel,
        "mlp_backward",
        (groups,),
        [ids],
        operands,
        [step_block(rows, units)]
        + sent.specs
        + grad.specs
        + [resident(x.shape) for x in operands[1 + 2 * held :]],
        outs,
        [step_block(rows, model)] + [resident(x.shape) for x in outs[1:]],
        [
            pltpu.VMEM((model, units), bf16),
            pltpu.VMEM((model, units), bf16),
            pltpu.VMEM((rows, model), bf16),
            pltpu.VMEM((rows, model), bf16),
            pltpu.VMEM((model, units), f32),
        ],
        6 * groups * rows * model * units,
    )


def qkv_backward(
    ids, info, tables, dq, dk, dv, context, sent, grad, back_mlp, gain, shift, gain_mlp, pack, dp_order
):
    groups, held, pieces = sent.groups, len(sent.arrays), len(pack.arrays)
    rows, model = sent.rows, sent.model
    width = dq.shape[1]

    def kernel(ids, info, dq_ref, dk_ref, dv_ref, ctx_ref, mlp_ref, *refs):
        sent_refs, refs = refs[:held], refs[held:]
        grad_refs, refs = refs[:held], refs[held:]
        weight_refs, refs = refs[:pieces], refs[pieces:]
        gain, shift, gain_mlp, cos, low, high = refs[:6]
        part_send, part_keep, bias_ref, sums_ref, send, keep = refs[6:12]
        whole, block, grad_block, total, dense_total, grads = refs[12:]
        step = pl.program_id(0)

        @pl.when(step == 0)
        def _():
            pack.place(weight_refs, whole, ids[1], slice(0, 3 * width))
            total[...] = jnp.zeros_like(total)
            dense_total[...] = jnp.zeros_like(dense_total)
            bias_ref[...] = jnp.zeros_like(bias_ref)
            sums_ref[...] = jnp.zeros_like(sums_ref)

        pick_piece(sent_refs, block, step)
        pick_piece(grad_refs, grad_block, step)
        grads[:, :width] = dq_ref[...]
        first = (ids[0] ^ ids[2 + step]) * (rows // SEG)
        for at in range(rows // SEG):
            number = first + at
            table = pl.ds(pl.multiple_of(info[number // NB, number % NB, 4] * SEG, SEG), SEG)
            own = slice(at * SEG, (at + 1) * SEG)
            turned = turn(dk_ref[own, :], cos[table, :], low[table, :], high[table, :], -1.0)
            grads[own, width : 2 * width] = turned.astype(bf16)
        grads[:, 2 * width :] = dv_ref[...]
        bias_ref[0:1, :] += jnp.sum(grads[...].astype(f32), axis=0, keepdims=True)
        back = dot_nt(grads[...], whole[...])
        token = block[...]
        sums_ref[0:1, :] += jnp.sum(back * token.astype(f32), axis=0, keepdims=True)
        sums_ref[1:2, :] += jnp.sum(back, axis=0, keepdims=True)
        part = (back * gain[...] + mlp_ref[...] * gain_mlp[...]).astype(bf16)
        store_half(part_send, part_keep, part, step, groups)
        total[...] += dot_tn(shift_gain(token, gain, shift), grads[...])
        dense_total[...] += dot_tn(grad_block[...], ctx_ref[...])

        @pl.when(step == groups - 1)
        def _():
            store_halves(send, keep, total, ids[1], dp_order, slice(0, 3 * width))
            store_halves(send, keep, dense_total, ids[1], dp_order, slice(3 * width, 4 * width))

    operands = [
        dq,
        dk,
        dv,
        context,
        back_mlp,
        *sent.arrays,
        *grad.arrays,
        *pack.arrays,
        gain,
        shift,
        gain_mlp,
        *tables,
    ]
    count = model // pack.rows
    outs = [
        shaped(groups // 2, rows, model),
        shaped(groups // 2, rows, model),
        shaped(8, 3 * width, dtype=f32),
        shaped(8, model, dtype=f32),
        shaped(count // 2, pack.rows, 4 * width),
        shaped(count // 2, pack.rows, 4 * width),
    ]
    return call(
        kernel,
        "qkv_backward",
        (groups,),
        [ids, info],
        operands,
        [own_block(rows, width)] * 4
        + [step_block(rows, model)]
        + sent.specs
        + grad.specs
        + [resident(x.shape) for x in operands[5 + 2 * held :]],
        outs,
        half_blocks(groups, rows, model) + [resident(x.shape) for x in outs[2:]],
        [
            pltpu.VMEM((model, 3 * width), bf16),
            pltpu.VMEM((rows, model), bf16),
            pltpu.VMEM((rows, model), bf16),
            pltpu.VMEM((model, 3 * width), f32),
            pltpu.VMEM((model, width), f32),
            pltpu.VMEM((rows, 3 * width), bf16),
        ],
        2 * groups * rows * model * 7 * width,
    )


def tree_table(segment_ids, parent_ids):
    trees = segment_ids.shape[0] // TREE
    segment = segment_ids.reshape(trees, NB, SEG)[:, :, 0]
    parent = parent_ids.reshape(trees, NB, SEG)[:, :, 0]
    block = lax.broadcasted_iota(jnp.int32, (trees, NB), 1)
    trunk = block < NT
    leaf = (parent != segment[:, :1]) & ~trunk
    at = lax.broadcasted_iota(jnp.int32, (trees, NB, NB), 2)
    owner = jnp.sum(jnp.where(segment[:, None, :] == parent[:, :, None], at, 0), axis=2)
    odd = block % 2 == 1
    first = jnp.where(trunk, block // 2 * 2, block)
    second = jnp.where(trunk, block // 2 * 2 + 1, jnp.where(leaf, owner, block))
    first_most = jnp.where(trunk & odd, SEG, 0)
    second_most = jnp.where(trunk, jnp.where(odd, 0, -SEG), jnp.where(leaf, SEG, -SEG))
    table = jnp.where(trunk, block, jnp.where(leaf, NT + 1, NT))
    return jnp.stack([first, second, first_most, second_most, table], axis=2).astype(jnp.int32)


def angle_tables():
    places = TRUNK + 2 * SEG
    place = lax.broadcasted_iota(jnp.int32, (places, 2 * HD), 0).astype(f32)
    lane = lax.broadcasted_iota(jnp.int32, (places, 2 * HD), 1) % HD
    half = ROT // 2
    frequency = 10000.0 ** (-((lane % half).astype(f32) * 2.0 / ROT))
    angle = place * frequency
    cosine = jnp.where(lane < ROT, jnp.cos(angle), 1.0)
    sine = jnp.sin(angle)
    low = jnp.where(lane < half, -sine, 0.0)
    high = jnp.where((lane >= half) & (lane < ROT), sine, 0.0)
    return cosine, low, high


def by_kind(array, heads):
    shape = array.shape[:-1]
    array = array.reshape(*shape, heads, 3, HD)
    return jnp.swapaxes(array, -3, -2).reshape(*shape, 3 * heads * HD)


def by_head(array, heads):
    shape = array.shape[:-1]
    array = array.reshape(*shape, 3, heads, HD)
    return jnp.swapaxes(array, -3, -2).reshape(*shape, 3 * heads * HD)


def local(
    stream_in,
    segment_ids,
    parent_ids,
    norm_gain_attn,
    norm_shift_attn,
    norm_gain_mlp,
    norm_shift_mlp,
    qkv_weight,
    qkv_bias,
    dense_weight,
    dense_bias,
    fc_weight,
    fc_bias,
    out_weight,
    out_bias,
    out_grad,
):
    tensor_rank = lax.axis_index("tensor")
    data_rank = lax.axis_index("dp")
    rows_local = stream_in.shape[0]
    model = stream_in.shape[1]
    qkv_width = qkv_weight.shape[1]
    heads = qkv_width // (3 * HD)
    width = heads * HD
    units = fc_weight.shape[1]
    groups = lax.axis_size("tensor")
    tensor_bits = bits_of(groups)
    far_first = tensor_bits[:0:-1] + tensor_bits[:1]
    order = halving_order(tensor_bits)
    ids = jnp.stack([tensor_rank, data_rank, *order]).astype(jnp.int32)
    data_bits = bits_of(lax.axis_size("dp"))
    rows_first = data_bits[:0:-1] + data_bits[:1]
    columns_first = data_bits[:1] + data_bits[:0:-1]
    out_bits, fc_bits = columns_first[::-1], rows_first[::-1]

    attn_pack = Pack(
        jnp.concatenate(
            [by_kind(qkv_weight.astype(bf16), heads), dense_weight.astype(bf16).T], axis=1
        ),
        "dp",
        rows_first,
    )
    fc_pack = Pack(fc_weight.astype(bf16), "dp", rows_first)
    out_pack = Pack(out_weight.astype(bf16).T, "dp", columns_first)

    row_mean = jnp.mean(stream_in, axis=-1, keepdims=True)
    centred = stream_in - row_mean
    row_var = jnp.mean(centred * centred, axis=-1, keepdims=True)
    inv_std = lax.rsqrt(row_var + eps_norm)
    normalized = centred * inv_std
    sent = gather_far(normalized.astype(bf16), "tensor", tensor_bits)

    attn_pack.double()
    out_pack.double()
    tie_packs(attn_pack, out_pack)
    rounds = len(data_bits)
    for number in range(1, rounds - 1):
        attn_pack.double()
        fc_pack.double()
    sent = tie_packs(attn_pack, fc_pack, out_pack, beside=sent)
    out_grad, sent[0] = tie(out_grad, sent[0])
    grad = gather_far(out_grad, "tensor", tensor_bits)
    sent = gather_near(sent, "tensor")
    attn_pack.double()
    fc_pack.double()
    while len(out_pack.bits) > 1:
        out_pack.double()
    sent = Tokens(tie_packs(attn_pack, fc_pack, out_pack, beside=sent), order)

    info = tree_table(segment_ids, parent_ids)
    tables = angle_tables()
    gain_attn, shift_attn = norm_gain_attn[None, :], norm_shift_attn[None, :]
    gain_mlp, shift_mlp = norm_gain_mlp[None, :], norm_shift_mlp[None, :]
    qkv_bias_own = by_kind(
        lax.dynamic_slice_in_dim(qkv_bias, tensor_rank * qkv_width, qkv_width), heads
    )[None, :]
    fc_bias_own = lax.dynamic_slice_in_dim(fc_bias, tensor_rank * units, units)[None, :]

    queries, keys, values = project_qkv(
        ids, info, sent, gain_attn, shift_attn, attn_pack, qkv_bias_own, tables, width
    )
    queries, keys, values, *grad = tie(queries, keys, values, *grad)
    grad = Tokens(gather_near(grad, "tensor"), order)
    grad_context = project_grad(ids, grad, attn_pack, width)
    fc_pack.double()
    out_pack.double()
    done = attention(info, tables, queries, keys, values, grad_context)
    context, dq, dk, dv = tie_packs(fc_pack, out_pack, beside=done)
    attn_parts = Halving(
        *project_context(ids, context, attn_pack, groups, model), "tensor", tensor_bits
    )
    attn_parts.most()
    sent.arrays[0], attn_parts.send = tie(sent.arrays[0], attn_parts.send)
    attn_parts.swap()
    done = mlp_forward(
        ids,
        sent,
        grad,
        gain_mlp,
        shift_mlp,
        fc_pack,
        fc_bias_own,
        out_pack,
        halving_order(out_bits),
    )
    active, slope, mlp_send, mlp_keep, out_send, out_keep = tie_halves(done, attn_parts)
    attn_parts.add()
    mlp_parts = Halving(mlp_send, mlp_keep, "tensor", tensor_bits)
    mlp_parts.most()
    slope, mlp_parts.send = tie(slope, mlp_parts.send)
    out_parts = Halving(out_send, out_keep, "dp", out_bits)
    mlp_parts.swap()
    out_parts.swap()
    done = mlp_backward(
        ids, sent, grad, slope, gain_mlp, shift_mlp, fc_pack, out_pack, halving_order(fc_bits)
    )
    back_mlp, fc_bias_sums, mlp_sums, fc_send, fc_keep = tie_halves(done, mlp_parts, out_parts)
    mlp_parts.add()
    out_parts.add()
    back_mlp, out_parts.send = tie(back_mlp, out_parts.send)
    fc_parts = Halving(fc_send, fc_keep, "dp", fc_bits)
    out_parts.swap()
    fc_parts.swap()
    done = qkv_backward(
        ids,
        info,
        tables,
        dq,
        dk,
        dv,
        context,
        sent,
        grad,
        back_mlp,
        gain_attn,
        shift_attn,
        gain_mlp,
        attn_pack,
        halving_order(fc_bits),
    )
    done = tie_halves(done, out_parts, fc_parts)
    back_send, back_keep, qkv_bias_sums, attn_sums, qkv_send, qkv_keep = done
    out_parts.add()
    fc_parts.add()
    attn_sum, mlp_sum = attn_parts.total, mlp_parts.total
    qkv_parts = Halving(qkv_send, qkv_keep, "dp", fc_bits)
    grad_sent = Halving(back_send, back_keep, "tensor", tensor_bits).finish()

    fc_weight_grad = fc_parts.finish()
    out_weight_grad = out_parts.finish().T
    attn_total = qkv_parts.finish()
    dense_weight_grad = attn_total[:, 3 * width :].T
    qkv_weight_grad = by_head(attn_total[:, : 3 * width], heads)

    attn_out = attn_sum + dense_bias
    mlp_out = mlp_sum + out_bias
    output = stream_in + attn_out + mlp_out

    mean_grad = jnp.mean(grad_sent, axis=-1, keepdims=True)
    mean_cross = jnp.mean(grad_sent * normalized, axis=-1, keepdims=True)
    stream_grad = out_grad.astype(f32) + inv_std * (
        grad_sent - mean_grad - normalized * mean_cross
    )

    residual_part = jnp.sum(out_grad.astype(f32), axis=0)
    squares = jnp.stack(
        [jnp.sum(output * output), jnp.sum(attn_out * attn_out), jnp.sum(mlp_out * mlp_out)]
    )
    count_all = float(rows_local * lax.axis_size("dp") * groups * model)
    fc_bias_spread = lax.dynamic_update_slice(
        jnp.zeros(fc_bias.shape, f32), fc_bias_sums[0], (tensor_rank * units,)
    )
    qkv_bias_spread = lax.dynamic_update_slice(
        jnp.zeros(qkv_bias.shape, f32), by_head(qkv_bias_sums[0], heads), (tensor_rank * qkv_width,)
    )
    sums = [
        residual_part,
        mlp_sums[0],
        mlp_sums[1],
        attn_sums[0],
        attn_sums[1],
        fc_bias_spread,
        qkv_bias_spread,
        jnp.pad(squares, (0, 125)),
    ]
    packed = sum_everywhere(jnp.concatenate(sums), ("tensor", "dp"))
    split = []
    for part in sums:
        split.append(packed[: part.shape[0]])
        packed = packed[part.shape[0] :]
    residual_grad, gain_mlp_grad, shift_mlp_grad, gain_attn_grad, shift_attn_grad = split[:5]
    fc_bias_grad, qkv_bias_grad, squares = split[5:]
    root_squares = jnp.sqrt(squares[:3] / count_all)
    return (
        output,
        stream_grad,
        gain_attn_grad,
        shift_attn_grad,
        gain_mlp_grad,
        shift_mlp_grad,
        qkv_weight_grad,
        qkv_bias_grad,
        dense_weight_grad,
        residual_grad,
        fc_weight_grad,
        fc_bias_grad,
        out_weight_grad,
        residual_grad,
        root_squares,
    )


def solution(mesh):
    tokens, weights, rows, whole = (
        P(("dp", "tensor"), None),
        P("dp", "tensor"),
        P("tensor", "dp"),
        P(),
    )
    return jax.shard_map(
        local,
        mesh=mesh,
        in_specs=(
            tokens,
            P("dp"),
            P("dp"),
            whole,
            whole,
            whole,
            whole,
            weights,
            whole,
            rows,
            whole,
            weights,
            whole,
            rows,
            whole,
            tokens,
        ),
        out_specs=(
            tokens,
            tokens,
            whole,
            whole,
            whole,
            whole,
            weights,
            whole,
            rows,
            whole,
            weights,
            whole,
            rows,
            whole,
            whole,
        ),
        check_vma=False,
    )
```

```python
import jax
import jax.numpy as jnp
from jax import lax
from jax.experimental import pallas as pl
from jax.experimental.pallas import tpu as pltpu
from jax.sharding import PartitionSpec as P

HD = 64
ROT = 16
TRUNK = 1024
SEG = 128
TREE = 2560
NB = TREE // SEG
NT = TRUNK // SEG

f32 = jnp.float32
bf16 = jnp.bfloat16
eps_norm = 1e-05
masked_score = -1e30
VMEM_MOST = 62 << 20

TAIL_SLOPE = 0.3
TAIL_COEFS = (
    0.11968663334846497,
    0.11957288533449173,
    0.11022695899009705,
    0.07842729985713959,
    0.09605274349451065,
    -0.07923758029937744,
    0.191569522023201,
    -0.22805799543857574,
    0.1123715341091156,
    -0.02061200700700283,
)


def dot_nn(left, right):
    return lax.dot_general(left, right, (((1,), (0,)), ((), ())), preferred_element_type=f32)


def dot_nt(left, right):
    return lax.dot_general(left, right, (((1,), (1,)), ((), ())), preferred_element_type=f32)


def dot_tn(left, right):
    return lax.dot_general(left, right, (((0,), (0,)), ((), ())), preferred_element_type=f32)


def bits_of(size):
    bits = []
    bit = 1
    while bit < size:
        bits.append(bit)
        bit *= 2
    return bits


def swap(block, axis, bit):
    size = lax.axis_size(axis)
    return lax.ppermute(block, axis, [(i, i ^ bit) for i in range(size)])


def tie(*values):
    return lax.optimization_barrier(values)


def gather_far(block, axis, bits):
    pieces = [block]
    for bit in bits[1:]:
        pieces = pieces + [swap(piece, axis, bit) for piece in pieces]
    return pieces


def gather_near(pieces, axis):
    pieces = [x for piece in pieces for x in (piece, swap(piece, axis, 1))]
    return pieces


class Pack:
    def __init__(self, block, axis, bits):
        self.rows, self.axis, self.bits = block.shape[0], axis, list(bits)
        self.arrays, self.owners = [block], [[0]]

    def double(self):
        bit = self.bits.pop(0)
        held = self.arrays[0] if len(self.arrays) == 1 else jnp.concatenate(self.arrays, axis=0)
        self.owners.append([j ^ bit for owners in self.owners for j in owners])
        self.arrays.append(swap(held, self.axis, bit))

    def place(self, refs, where, number, columns):
        for ref, owners in zip(refs, self.owners):
            for at, j in enumerate(owners):
                rows = pl.ds(pl.multiple_of((number ^ j) * self.rows, self.rows), self.rows)
                where[rows, :] = ref[at * self.rows : (at + 1) * self.rows, columns]


def tie_packs(*packs, beside=()):
    flat = tie(*beside, *[x for pack in packs for x in pack.arrays])
    at = len(beside)
    for pack in packs:
        pack.arrays = list(flat[at : at + len(pack.arrays)])
        at += len(pack.arrays)
    return list(flat[: len(beside)])


def halving_order(bits):
    if not bits:
        return [0]
    rest = halving_order(bits[1:])
    return [bits[0] ^ j for j in rest] + rest


class Halving:
    def __init__(self, send, keep, axis, bits):
        self.send, self.terms, self.axis, self.bits = send, [keep], axis, list(bits)

    def swap(self):
        self.got = swap(self.send, self.axis, self.bits.pop(0))

    def add(self):
        terms = self.terms + [self.got]
        if self.got.shape[0] > 1:
            half = self.got.shape[0] // 2
            self.send = sum(x[:half].astype(f32) for x in terms).astype(bf16)
            self.terms = [x[half:] for x in terms]
        else:
            self.terms = [x[0] for x in terms]

    def total(self):
        return sum(x.astype(f32) for x in self.terms)

    def most(self):
        while len(self.bits) > 1:
            self.swap()
            self.add()

    def finish(self):
        while self.bits:
            self.swap()
            self.add()
        return self.total()


def tie_halves(values, *halvings):
    flat = tie(*values, *[x.got for x in halvings])
    for x, got in zip(halvings, flat[len(values) :]):
        x.got = got
    return flat[: len(values)]


def resident(shape):
    zeros = (0,) * len(shape)
    return pl.BlockSpec(shape, lambda *_: zeros, pipeline_mode=pl.Buffered(1))


def own_block(rows, columns):
    return pl.BlockSpec((rows, columns), lambda i, ids, *_: (ids[0] ^ ids[2 + i], 0))


def step_block(rows, columns):
    return pl.BlockSpec((rows, columns), lambda i, *_: (i, 0))


def half_blocks(groups, rows, columns):
    half = groups // 2
    shape = (pl.Squeezed(), rows, columns)
    return [
        pl.BlockSpec(shape, lambda i, *_: (jnp.minimum(i, half - 1), 0, 0)),
        pl.BlockSpec(shape, lambda i, *_: (jnp.maximum(i - half, 0), 0, 0)),
    ]


def store_half(send, keep, value, step, groups):
    @pl.when(step < groups // 2)
    def _():
        send[...] = value

    @pl.when(step >= groups // 2)
    def _():
        keep[...] = value


class Tokens:
    def __init__(self, pieces, order):
        self.groups, (self.rows, self.model) = len(pieces), pieces[0].shape
        if self.groups <= 4:
            self.arrays = [pieces[j] for j in order]
            self.specs = [resident(x.shape) for x in pieces]
        else:
            self.arrays = [jnp.concatenate([pieces[j] for j in order], axis=0)]
            self.specs = [step_block(self.rows, self.model)]


def pick_piece(pieces, where, step):
    if len(pieces) == 1:
        where[...] = pieces[0][...]
        return
    for at, piece in enumerate(pieces):

        @pl.when(step == at)
        def _(piece=piece):
            where[...] = piece[...]


def store_halves(send, keep, total, number, order, columns=slice(None), source=slice(None)):
    half, rows = send.shape[0], send.shape[1]
    for at, j in enumerate(order):
        where = send if at < half else keep
        block = total[pl.ds(pl.multiple_of((number ^ j) * rows, rows), rows), source]
        where[at % half, :, columns] = block.astype(bf16)


def call(kernel, name, grid, prefetch, operands, specs, outs, out_specs, scratch, flops, extra=0):
    size = sum(x.size * x.dtype.itemsize for x in list(operands) + list(outs))
    return pl.pallas_call(
        kernel,
        grid_spec=pltpu.PrefetchScalarGridSpec(
            num_scalar_prefetch=len(prefetch),
            grid=grid,
            in_specs=specs,
            out_specs=out_specs,
            scratch_shapes=scratch,
        ),
        out_shape=outs,
        compiler_params=pltpu.CompilerParams(
            dimension_semantics=("arbitrary",) * len(grid), vmem_limit_bytes=VMEM_MOST
        ),
        cost_estimate=pl.CostEstimate(
            flops=int(flops), bytes_accessed=int(size), transcendentals=int(extra)
        ),
        name=name,
    )(*prefetch, *operands)


def shaped(*shape, dtype=bf16):
    return jax.ShapeDtypeStruct(shape, dtype)


def shift_gain(block, gain, shift):
    return (block.astype(f32) * gain[...] + shift[...]).astype(bf16)


def turn(block, cosine, low_sine, high_sine, sign):
    width = block.shape[1]
    step = min(width, 128)
    done = []
    for start in range(0, width, step):
        part = block[:, start : start + step]
        if step == 128:
            left = pltpu.roll(part, step - ROT // 2, 1)
            right = pltpu.roll(part, ROT // 2, 1)
        else:
            left = jnp.concatenate([part[:, ROT // 2 :], part[:, : ROT // 2]], axis=1)
            right = jnp.concatenate([part[:, -ROT // 2 :], part[:, : -ROT // 2]], axis=1)
        moved = left * low_sine[:, :step] + right * high_sine[:, :step]
        done.append(part * cosine[:, :step] + moved * sign)
    return done[0] if len(done) == 1 else jnp.concatenate(done, axis=1)


def project_qkv(ids, info, sent, gain, shift, pack, bias, tables, width):
    groups, held, pieces = sent.groups, len(sent.arrays), len(pack.arrays)
    rows, model = sent.rows, sent.model

    def kernel(ids, info, *refs):
        sent_refs, refs = refs[:held], refs[held:]
        weight_refs, refs = refs[:pieces], refs[pieces:]
        gain, shift, bias, cos, low, high, q_out, k_out, v_out, whole, block = refs
        step = pl.program_id(0)

        @pl.when(step == 0)
        def _():
            pack.place(weight_refs, whole, ids[1], slice(None))

        pick_piece(sent_refs, block, step)
        qkv = dot_nn(shift_gain(block[...], gain, shift), whole[...]) + bias[...]
        first = (ids[0] ^ ids[2 + step]) * (rows // SEG)
        for at in range(rows // SEG):
            number = first + at
            table = pl.ds(pl.multiple_of(info[number // NB, number % NB, 4] * SEG, SEG), SEG)
            tabs = (cos[table, :], low[table, :], high[table, :])
            own = slice(at * SEG, (at + 1) * SEG)
            q_out[own, :] = (turn(qkv[own, :width], *tabs, 1.0) * HD**-0.5).astype(bf16)
            k_out[own, :] = turn(qkv[own, width : 2 * width], *tabs, 1.0).astype(bf16)
        v_out[...] = qkv[:, 2 * width :].astype(bf16)

    operands = [*sent.arrays, *pack.arrays, gain, shift, bias, *tables]
    out = shaped(groups * rows, width)
    return call(
        kernel,
        "project_qkv",
        (groups,),
        [ids, info],
        operands,
        sent.specs + [resident(x.shape) for x in operands[held:]],
        [out] * 3,
        [own_block(rows, width)] * 3,
        [pltpu.VMEM((model, 3 * width), bf16), pltpu.VMEM((rows, model), bf16)],
        2 * groups * rows * model * 3 * width,
    )


def project_grad(ids, grad, pack, width):
    groups, held, pieces = grad.groups, len(grad.arrays), len(pack.arrays)
    rows, model = grad.rows, grad.model

    def kernel(ids, *refs):
        grad_refs, refs = refs[:held], refs[held:]
        weight_refs, (out, whole, block) = refs[:pieces], refs[pieces:]
        step = pl.program_id(0)

        @pl.when(step == 0)
        def _():
            pack.place(weight_refs, whole, ids[1], slice(None))

        pick_piece(grad_refs, block, step)
        out[...] = dot_nn(block[...], whole[...]).astype(bf16)

    operands = [*grad.arrays, *pack.arrays]
    return call(
        kernel,
        "project_grad",
        (groups,),
        [ids],
        operands,
        grad.specs + [resident(x.shape) for x in operands[held:]],
        [shaped(groups * rows, width)],
        [own_block(rows, width)],
        [pltpu.VMEM((model, width), bf16), pltpu.VMEM((rows, model), bf16)],
        2 * groups * rows * model * width,
    )[0]


def attention_kernel(
    info, q_ref, do_ref, k_ref, v_ref, cos, low, high, ctx_ref, dq_ref, dk_ref, dv_ref, dk_sum, dv_sum
):
    tree, step = pl.program_id(0), pl.program_id(1)
    width = q_ref.shape[1]
    heads = width // HD
    lane_head = lax.broadcasted_iota(jnp.int32, (SEG, width), 1) // HD

    @pl.when(step == 0)
    def _():
        dk_sum[...] = jnp.zeros_like(dk_sum)
        dv_sum[...] = jnp.zeros_like(dv_sum)

    first, second = info[tree, step, 0], info[tree, step, 1]
    first_rows = pl.ds(pl.multiple_of(first * SEG, SEG), SEG)
    second_rows = pl.ds(pl.multiple_of(second * SEG, SEG), SEG)
    queries, grads = q_ref[...], do_ref[...]
    zero = jnp.zeros_like(queries)
    q_rows = jnp.concatenate([jnp.where(lane_head == h, queries, zero) for h in range(heads)], axis=0)
    g_rows = jnp.concatenate([jnp.where(lane_head == h, grads, zero) for h in range(heads)], axis=0)
    q_turned, g_turned = queries.T, grads.T
    ahead = lax.broadcasted_iota(jnp.int32, (SEG, SEG), 1) - lax.broadcasted_iota(
        jnp.int32, (SEG, SEG), 0
    )
    seen = jnp.concatenate([ahead <= info[tree, step, 2], ahead <= info[tree, step, 3]], axis=1)
    seen = jnp.concatenate([seen] * heads, axis=0)
    k_near = jnp.concatenate([k_ref[first_rows, :], k_ref[second_rows, :]], axis=0)
    v_near = jnp.concatenate([v_ref[first_rows, :], v_ref[second_rows, :]], axis=0)

    def work(pairs):
        count = pairs * 2 * SEG
        near = jnp.where(seen, dot_nt(q_rows, k_near), masked_score)
        most = jnp.max(near, axis=1, keepdims=True)
        if count:
            k_far, v_far = k_ref[0:count, :], v_ref[0:count, :]
            far = dot_nt(q_rows, k_far)
            most = jnp.maximum(most, jnp.max(far, axis=1, keepdims=True))
        near = jnp.exp(near - most)
        total = jnp.sum(near, axis=1, keepdims=True)
        if count:
            far = jnp.exp(far - most)
            total = total + jnp.sum(far, axis=1, keepdims=True)
        scale = 1.0 / total
        near = near * scale
        near_low = near.astype(bf16)
        context = dot_nn(near_low, v_near)
        if count:
            far = far * scale
            far_low = far.astype(bf16)
            context = context + dot_nn(far_low, v_far)
        delta = jnp.sum(context * g_rows.astype(f32), axis=1, keepdims=True)
        near = (near * (dot_nt(g_rows, v_near) - delta)).astype(bf16)
        dq = dot_nn(near, k_near)
        if count:
            far = (far * (dot_nt(g_rows, v_far) - delta)).astype(bf16)
            dq = dq + dot_nn(far, k_far)
        ctx_own, dq_own = context[0:SEG], dq[0:SEG]
        for h in range(1, heads):
            ctx_own = jnp.where(lane_head == h, context[h * SEG : (h + 1) * SEG], ctx_own)
            dq_own = jnp.where(lane_head == h, dq[h * SEG : (h + 1) * SEG], dq_own)
        ctx_ref[...] = ctx_own.astype(bf16)
        dq_ref[...] = turn(dq_own * HD**-0.5, cos, low, high, -1.0).astype(bf16)
        for h in range(heads):
            own = slice(h * SEG, (h + 1) * SEG)
            part = slice(h * HD, (h + 1) * HD)
            dk = dot_nn(q_turned[part], near[own])
            dv = dot_nn(g_turned[part], near_low[own])
            dk_sum[first, part, :] += dk[:, :SEG]
            dv_sum[first, part, :] += dv[:, :SEG]
            dk_sum[second, part, :] += dk[:, SEG:]
            dv_sum[second, part, :] += dv[:, SEG:]
            if count:
                dk = dot_nn(q_turned[part], far[own])
                dv = dot_nn(g_turned[part], far_low[own])
                for j in range(2 * pairs):
                    dk_sum[j, part, :] += dk[:, j * SEG : (j + 1) * SEG]
                    dv_sum[j, part, :] += dv[:, j * SEG : (j + 1) * SEG]

    for pairs in range(NT // 2):

        @pl.when(step // 2 == pairs)
        def _(pairs=pairs):
            work(pairs)

    @pl.when(step >= NT)
    def _():
        work(NT // 2)

    @pl.when(step == NB - 1)
    def _():
        def finish(j, carry):
            rows = pl.ds(pl.multiple_of(j * SEG, SEG), SEG)
            dv_ref[rows, :] = dv_sum[j].T.astype(bf16)
            dk_ref[rows, :] = dk_sum[j].T.astype(bf16)
            return carry

        lax.fori_loop(0, NB, finish, 0)


def attention(info, tables, queries, keys, values, grads):
    total, width = queries.shape
    trees = total // TREE
    table_width = tables[0].shape[1]
    block = pl.BlockSpec((SEG, width), lambda t, b, info: (t * NB + b, 0))
    whole = pl.BlockSpec((TREE, width), lambda t, b, info: (t, 0))
    table = pl.BlockSpec((SEG, table_width), lambda t, b, info: (info[t, b, 4], 0))
    scores = trees * (TREE - TRUNK) * (TRUNK + 2 * SEG) * (width // HD)
    return call(
        attention_kernel,
        "attention",
        (trees, NB),
        [info],
        [queries, grads, keys, values, *tables],
        [block, block, whole, whole, table, table, table],
        [shaped(total, width)] * 4,
        [block, block, whole, whole],
        [pltpu.VMEM((NB, width, SEG), f32), pltpu.VMEM((NB, width, SEG), f32)],
        scores * width * 2 * 6 * 1.3,
        scores,
    )


def attention_backward(
    ids, info, tables, context, dq, dk, dv, sent, grad, gain, shift, qkv_pack, dense_pack, bits
):
    groups, held, pieces = sent.groups, len(sent.arrays), len(dense_pack.arrays)
    rows, model = sent.rows, sent.model
    width = dq.shape[1]
    order = halving_order(bits)

    def kernel(ids, info, ctx_ref, dq_ref, dk_ref, dv_ref, *refs):
        sent_refs, refs = refs[:held], refs[held:]
        grad_refs, refs = refs[:held], refs[held:]
        weight_refs, refs = refs[:pieces], refs[pieces:]
        gain, shift, cos, low, high, part_send, part_keep, grads, bias_ref, send, keep = refs[:11]
        whole, block, grad_block, total, dense_total = refs[11:]
        step = pl.program_id(0)

        @pl.when(step == 0)
        def _():
            dense_pack.place(weight_refs, whole, ids[1], slice(None))
            total[...] = jnp.zeros_like(total)
            dense_total[...] = jnp.zeros_like(dense_total)
            bias_ref[...] = jnp.zeros_like(bias_ref)

        pick_piece(sent_refs, block, step)
        pick_piece(grad_refs, grad_block, step)
        store_half(
            part_send, part_keep, dot_nt(ctx_ref[...], whole[...]).astype(bf16), step, groups
        )
        grads[:, :width] = dq_ref[...]
        first = (ids[0] ^ ids[2 + step]) * (rows // SEG)
        for at in range(rows // SEG):
            number = first + at
            table = pl.ds(pl.multiple_of(info[number // NB, number % NB, 4] * SEG, SEG), SEG)
            own = slice(at * SEG, (at + 1) * SEG)
            turned = turn(dk_ref[own, :], cos[table, :], low[table, :], high[table, :], -1.0)
            grads[own, width : 2 * width] = turned.astype(bf16)
        grads[:, 2 * width :] = dv_ref[...]
        bias_ref[0:1, :] += jnp.sum(grads[...].astype(f32), axis=0, keepdims=True)
        total[...] += dot_tn(shift_gain(block[...], gain, shift), grads[...])
        dense_total[...] += dot_tn(grad_block[...], ctx_ref[...])

        @pl.when(step == groups - 1)
        def _():
            store_halves(send, keep, total, ids[1], order, slice(0, 3 * width))
            store_halves(send, keep, dense_total, ids[1], order, slice(3 * width, 4 * width))

    operands = [
        context,
        dq,
        dk,
        dv,
        *sent.arrays,
        *grad.arrays,
        *dense_pack.arrays,
        gain,
        shift,
        *tables,
    ]
    count = model // qkv_pack.rows
    outs = [
        shaped(groups // 2, rows, model),
        shaped(groups // 2, rows, model),
        shaped(groups * rows, 3 * width),
        shaped(8, 3 * width, dtype=f32),
        shaped(count // 2, qkv_pack.rows, 4 * width),
        shaped(count // 2, qkv_pack.rows, 4 * width),
    ]
    return call(
        kernel,
        "attention_backward",
        (groups,),
        [ids, info],
        operands,
        [own_block(rows, width)] * 4
        + sent.specs
        + grad.specs
        + [resident(x.shape) for x in operands[4 + 2 * held :]],
        outs,
        half_blocks(groups, rows, model)
        + [step_block(rows, 3 * width)]
        + [resident(x.shape) for x in outs[3:]],
        [
            pltpu.VMEM((model, width), bf16),
            pltpu.VMEM((rows, model), bf16),
            pltpu.VMEM((rows, model), bf16),
            pltpu.VMEM((model, 3 * width), f32),
            pltpu.VMEM((model, width), f32),
        ],
        2 * groups * rows * model * 5 * width,
    )


def mlp_forward(ids, sent, grad, gain, shift, fc, bias, out, out_order):
    groups, held, pieces = sent.groups, len(sent.arrays), len(fc.arrays)
    rows, model = sent.rows, sent.model
    units = fc.arrays[0].shape[1]

    def kernel(ids, *refs):
        sent_refs, refs = refs[:held], refs[held:]
        grad_refs, refs = refs[:held], refs[held:]
        fc_refs, refs = refs[:pieces], refs[pieces:]
        out_refs, refs = refs[:pieces], refs[pieces:]
        gain, shift, bias, act_ref, slope_ref, send, keep, out_send, out_keep = refs[:9]
        fc_whole, out_whole, block, grad_block, total = refs[9:]
        step = pl.program_id(0)

        @pl.when(step == 0)
        def _():
            fc.place(fc_refs, fc_whole, ids[1], slice(None))
            out.place(out_refs, out_whole, ids[1], slice(None))
            total[...] = jnp.zeros_like(total)

        pick_piece(sent_refs, block, step)
        pick_piece(grad_refs, grad_block, step)
        hidden = dot_nn(shift_gain(block[...], gain, shift), fc_whole[...]) + bias[...]
        size = jnp.abs(hidden)
        ratio = 1.0 / (1.0 + TAIL_SLOPE * size)
        tail = jnp.full_like(ratio, TAIL_COEFS[-1])
        for coef in TAIL_COEFS[-2::-1]:
            tail = tail * ratio + coef
        bell = jnp.exp(hidden * hidden * -0.5)
        tail = tail * ratio * bell
        chance = jnp.where(hidden < 0, tail, 1.0 - tail)
        active = (hidden * chance).astype(bf16)
        act_ref[...] = active
        slope_ref[...] = chance + hidden * bell * 0.3989422804014327
        store_half(send, keep, dot_nt(active, out_whole[...]).astype(bf16), step, groups)
        total[...] += dot_tn(grad_block[...], active)

        @pl.when(step == groups - 1)
        def _():
            store_halves(out_send, out_keep, total, ids[1], out_order)

    operands = [*sent.arrays, *grad.arrays, *fc.arrays, *out.arrays, gain, shift, bias]
    count = model // fc.rows
    outs = [
        shaped(groups * rows, units),
        shaped(groups * rows, units, dtype=f32),
        shaped(groups // 2, rows, model),
        shaped(groups // 2, rows, model),
        shaped(count // 2, fc.rows, units),
        shaped(count // 2, fc.rows, units),
    ]
    return call(
        kernel,
        "mlp_forward",
        (groups,),
        [ids],
        operands,
        sent.specs + grad.specs + [resident(x.shape) for x in operands[2 * held :]],
        outs,
        [step_block(rows, units)] * 2
        + half_blocks(groups, rows, model)
        + [resident(x.shape) for x in outs[4:]],
        [
            pltpu.VMEM((model, units), bf16),
            pltpu.VMEM((model, units), bf16),
            pltpu.VMEM((rows, model), bf16),
            pltpu.VMEM((rows, model), bf16),
            pltpu.VMEM((model, units), f32),
        ],
        6 * groups * rows * model * units,
    )


def hidden_backward(ids, sent, grad, slope, gain, shift, fc, out, orders):
    groups, held, pieces = sent.groups, len(sent.arrays), len(fc.arrays)
    rows, model = sent.rows, sent.model
    units = fc.arrays[0].shape[1]

    def kernel(ids, slope_ref, *refs):
        sent_refs, refs = refs[:held], refs[held:]
        grad_refs, refs = refs[:held], refs[held:]
        out_refs, refs = refs[:pieces], refs[pieces:]
        gain, shift, hidden_ref, bias_ref, *halves = refs[:8]
        out_whole, block, grad_block, fc_total = refs[8:]
        step = pl.program_id(0)

        @pl.when(step == 0)
        def _():
            out.place(out_refs, out_whole, ids[1], slice(None))
            fc_total[...] = jnp.zeros_like(fc_total)
            bias_ref[...] = jnp.zeros_like(bias_ref)

        pick_piece(sent_refs, block, step)
        pick_piece(grad_refs, grad_block, step)
        hidden = (dot_nn(grad_block[...], out_whole[...]) * slope_ref[...]).astype(bf16)
        hidden_ref[...] = hidden
        bias_ref[0:1, :] += jnp.sum(hidden.astype(f32), axis=0, keepdims=True)
        fc_total[...] += dot_tn(shift_gain(block[...], gain, shift), hidden)

        @pl.when(step == groups - 1)
        def _():
            for at, order in enumerate(orders):
                source = slice(at * units // 2, (at + 1) * units // 2)
                send, keep = halves[2 * at : 2 * at + 2]
                store_halves(send, keep, fc_total, ids[1], order, source=source)

    operands = [slope, *sent.arrays, *grad.arrays, *out.arrays, gain, shift]
    count = model // fc.rows
    outs = [shaped(groups * rows, units), shaped(8, units, dtype=f32)]
    outs += [shaped(count // 2, fc.rows, units // 2)] * 4
    return call(
        kernel,
        "hidden_backward",
        (groups,),
        [ids],
        operands,
        [step_block(rows, units)]
        + sent.specs
        + grad.specs
        + [resident(x.shape) for x in operands[1 + 2 * held :]],
        outs,
        [step_block(rows, units)] + [resident(x.shape) for x in outs[1:]],
        [
            pltpu.VMEM((model, units), bf16),
            pltpu.VMEM((rows, model), bf16),
            pltpu.VMEM((rows, model), bf16),
            pltpu.VMEM((model, units), f32),
        ],
        4 * groups * rows * model * units,
    )


def norm_backward(ids, sent, grads, hidden, gain_attn, gain_mlp, qkv_pack, fc):
    groups, held, pieces = sent.groups, len(sent.arrays), len(fc.arrays)
    rows, model = sent.rows, sent.model
    units, columns = hidden.shape[1], grads.shape[1]

    def kernel(ids, grads_ref, hidden_ref, *refs):
        sent_refs, refs = refs[:held], refs[held:]
        qkv_refs, refs = refs[:pieces], refs[pieces:]
        fc_refs, refs = refs[:pieces], refs[pieces:]
        gain_attn, gain_mlp, send, keep, sums_ref, qkv_whole, fc_whole, block = refs
        step = pl.program_id(0)

        @pl.when(step == 0)
        def _():
            qkv_pack.place(qkv_refs, qkv_whole, ids[1], slice(None))
            fc.place(fc_refs, fc_whole, ids[1], slice(None))
            sums_ref[...] = jnp.zeros_like(sums_ref)

        pick_piece(sent_refs, block, step)
        token = block[...].astype(f32)
        back = dot_nt(grads_ref[...], qkv_whole[...])
        sums_ref[0:1, :] += jnp.sum(back * token, axis=0, keepdims=True)
        sums_ref[1:2, :] += jnp.sum(back, axis=0, keepdims=True)
        part = back * gain_attn[...]
        back = dot_nt(hidden_ref[...], fc_whole[...])
        sums_ref[2:3, :] += jnp.sum(back * token, axis=0, keepdims=True)
        sums_ref[3:4, :] += jnp.sum(back, axis=0, keepdims=True)
        part = part + back * gain_mlp[...]
        store_half(send, keep, part.astype(bf16), step, groups)

    operands = [grads, hidden, *sent.arrays, *qkv_pack.arrays, *fc.arrays, gain_attn, gain_mlp]
    outs = [
        shaped(groups // 2, rows, model),
        shaped(groups // 2, rows, model),
        shaped(8, model, dtype=f32),
    ]
    return call(
        kernel,
        "norm_backward",
        (groups,),
        [ids],
        operands,
        [step_block(rows, columns), step_block(rows, units)]
        + sent.specs
        + [resident(x.shape) for x in operands[2 + held :]],
        outs,
        half_blocks(groups, rows, model) + [resident(x.shape) for x in outs[2:]],
        [
            pltpu.VMEM((model, columns), bf16),
            pltpu.VMEM((model, units), bf16),
            pltpu.VMEM((rows, model), bf16),
        ],
        2 * groups * rows * model * (units + columns),
    )


def finish_output(stream, attn_terms, mlp_terms, dense_bias, out_bias):
    rows, model = stream.shape
    block = 128
    first, second = len(attn_terms), len(mlp_terms)

    def kernel(stream_ref, *refs):
        attn_refs, refs = refs[:first], refs[first:]
        mlp_refs, (dense_bias, out_bias, out_ref, sums_ref) = refs[:second], refs[second:]

        @pl.when(pl.program_id(0) == 0)
        def _():
            sums_ref[...] = jnp.zeros_like(sums_ref)

        attn = sum(x[...].astype(f32) for x in attn_refs) + dense_bias[...]
        mlp = sum(x[...].astype(f32) for x in mlp_refs) + out_bias[...]
        output = stream_ref[...] + attn + mlp
        out_ref[...] = output
        for at, value in enumerate((output, attn, mlp)):
            sums_ref[at : at + 1, :] += jnp.sum(value * value, axis=0, keepdims=True)

    operands = [stream, *attn_terms, *mlp_terms, dense_bias, out_bias]
    outs = [shaped(rows, model, dtype=f32), shaped(8, model, dtype=f32)]
    return call(
        kernel,
        "finish_output",
        (rows // block,),
        [],
        operands,
        [step_block(block, model)] * (1 + first + second)
        + [resident(dense_bias.shape), resident(out_bias.shape)],
        outs,
        [step_block(block, model), resident(outs[1].shape)],
        [],
        rows * model * 16,
    )


def finish_grad(grad, normalized, inv_std, terms, chunks):
    rows, model = grad.shape
    count, block = len(chunks), chunks[0].shape[0]
    held = len(terms)

    def kernel(grad_ref, norm_ref, std_ref, *refs):
        term_refs, chunk_refs, (out_ref, last) = refs[:held], refs[held:-2], refs[-2:]
        pick_piece(chunk_refs, last, pl.program_id(0))
        sent = sum(x[...].astype(f32) for x in term_refs) + last[...].astype(f32)
        norm = norm_ref[...]
        mean = jnp.sum(sent, axis=1, keepdims=True) / model
        cross = jnp.sum(sent * norm, axis=1, keepdims=True) / model
        out_ref[...] = grad_ref[...].astype(f32) + std_ref[...] * (sent - mean - norm * cross)

    operands = [grad, normalized, inv_std, *terms, *chunks]
    return call(
        kernel,
        "finish_grad",
        (count,),
        [],
        operands,
        [step_block(block, model), step_block(block, model), step_block(block, 1)]
        + [step_block(block, model)] * held
        + [resident(x.shape) for x in chunks],
        [shaped(rows, model, dtype=f32)],
        [step_block(block, model)],
        [pltpu.VMEM((block, model), bf16)],
        rows * model * 12,
    )[0]


def tree_table(segment_ids, parent_ids):
    trees = segment_ids.shape[0] // TREE
    segment = segment_ids.reshape(trees, NB, SEG)[:, :, 0]
    parent = parent_ids.reshape(trees, NB, SEG)[:, :, 0]
    block = lax.broadcasted_iota(jnp.int32, (trees, NB), 1)
    trunk = block < NT
    leaf = (parent != segment[:, :1]) & ~trunk
    at = lax.broadcasted_iota(jnp.int32, (trees, NB, NB), 2)
    owner = jnp.sum(jnp.where(segment[:, None, :] == parent[:, :, None], at, 0), axis=2)
    odd = block % 2 == 1
    first = jnp.where(trunk, block // 2 * 2, block)
    second = jnp.where(trunk, block // 2 * 2 + 1, jnp.where(leaf, owner, block))
    first_most = jnp.where(trunk & odd, SEG, 0)
    second_most = jnp.where(trunk, jnp.where(odd, 0, -SEG), jnp.where(leaf, SEG, -SEG))
    table = jnp.where(trunk, block, jnp.where(leaf, NT + 1, NT))
    return jnp.stack([first, second, first_most, second_most, table], axis=2).astype(jnp.int32)


def angle_tables():
    places = TRUNK + 2 * SEG
    place = lax.broadcasted_iota(jnp.int32, (places, 2 * HD), 0).astype(f32)
    lane = lax.broadcasted_iota(jnp.int32, (places, 2 * HD), 1) % HD
    half = ROT // 2
    frequency = 10000.0 ** (-((lane % half).astype(f32) * 2.0 / ROT))
    angle = place * frequency
    cosine = jnp.where(lane < ROT, jnp.cos(angle), 1.0)
    sine = jnp.sin(angle)
    low = jnp.where(lane < half, -sine, 0.0)
    high = jnp.where((lane >= half) & (lane < ROT), sine, 0.0)
    return cosine, low, high


def by_kind(array, heads):
    shape = array.shape[:-1]
    array = array.reshape(*shape, heads, 3, HD)
    return jnp.swapaxes(array, -3, -2).reshape(*shape, 3 * heads * HD)


def by_head(array, heads):
    shape = array.shape[:-1]
    array = array.reshape(*shape, 3, heads, HD)
    return jnp.swapaxes(array, -3, -2).reshape(*shape, 3 * heads * HD)


def local(
    stream_in,
    segment_ids,
    parent_ids,
    norm_gain_attn,
    norm_shift_attn,
    norm_gain_mlp,
    norm_shift_mlp,
    qkv_weight,
    qkv_bias,
    dense_weight,
    dense_bias,
    fc_weight,
    fc_bias,
    out_weight,
    out_bias,
    out_grad,
):
    tensor_rank = lax.axis_index("tensor")
    data_rank = lax.axis_index("dp")
    rows_local = stream_in.shape[0]
    model = stream_in.shape[1]
    qkv_width = qkv_weight.shape[1]
    heads = qkv_width // (3 * HD)
    width = heads * HD
    units = fc_weight.shape[1]
    groups = lax.axis_size("tensor")
    tensor_bits = bits_of(groups)
    far_first = tensor_bits[:0:-1] + tensor_bits[:1]
    order = halving_order(tensor_bits)
    ids = jnp.stack([tensor_rank, data_rank, *order]).astype(jnp.int32)
    data_bits = bits_of(lax.axis_size("dp"))
    rows_first = data_bits[:0:-1] + data_bits[:1]
    columns_first = data_bits[:1] + data_bits[:0:-1]
    out_bits, fc_bits = columns_first[::-1], rows_first[::-1]

    qkv_pack = Pack(by_kind(qkv_weight.astype(bf16), heads), "dp", rows_first)
    dense_pack = Pack(dense_weight.astype(bf16).T, "dp", columns_first)
    fc_pack = Pack(fc_weight.astype(bf16), "dp", rows_first)
    out_pack = Pack(out_weight.astype(bf16).T, "dp", columns_first)

    row_mean = jnp.mean(stream_in, axis=-1, keepdims=True)
    centred = stream_in - row_mean
    row_var = jnp.mean(centred * centred, axis=-1, keepdims=True)
    inv_std = lax.rsqrt(row_var + eps_norm)
    normalized = centred * inv_std
    sent = gather_far(normalized.astype(bf16), "tensor", tensor_bits)

    qkv_pack.double()
    dense_pack.double()
    out_pack.double()
    tie_packs(qkv_pack, dense_pack, fc_pack, out_pack)
    while len(qkv_pack.bits) > 1:
        qkv_pack.double()
        dense_pack.double()
    fc_pack.double()
    sent = tie_packs(qkv_pack, dense_pack, fc_pack, out_pack, beside=sent)
    out_grad, sent[0] = tie(out_grad, sent[0])
    grad = gather_far(out_grad, "tensor", tensor_bits)
    sent = gather_near(sent, "tensor")
    qkv_pack.double()
    dense_pack.double()
    while len(out_pack.bits) > 1:
        out_pack.double()
    sent = Tokens(tie_packs(qkv_pack, dense_pack, out_pack, beside=sent), order)

    info = tree_table(segment_ids, parent_ids)
    tables = angle_tables()
    gain_attn, shift_attn = norm_gain_attn[None, :], norm_shift_attn[None, :]
    gain_mlp, shift_mlp = norm_gain_mlp[None, :], norm_shift_mlp[None, :]
    qkv_bias_own = by_kind(
        lax.dynamic_slice_in_dim(qkv_bias, tensor_rank * qkv_width, qkv_width), heads
    )[None, :]
    fc_bias_own = lax.dynamic_slice_in_dim(fc_bias, tensor_rank * units, units)[None, :]

    while len(fc_pack.bits) > 1:
        fc_pack.double()
    done = project_qkv(
        ids, info, sent, gain_attn, shift_attn, qkv_pack, qkv_bias_own, tables, width
    )
    queries, keys, values, *grad = tie_packs(fc_pack, beside=[*done, *grad])
    grad = Tokens(gather_near(grad, "tensor"), order)
    grad_context = project_grad(ids, grad, dense_pack, width)
    fc_pack.double()
    out_pack.double()
    done = attention(info, tables, queries, keys, values, grad_context)
    context, dq, dk, dv = tie_packs(fc_pack, out_pack, beside=done)
    attn_send, attn_keep, grads, qkv_bias_sums, qkv_send, qkv_keep = attention_backward(
        ids,
        info,
        tables,
        context,
        dq,
        dk,
        dv,
        sent,
        grad,
        gain_attn,
        shift_attn,
        qkv_pack,
        dense_pack,
        fc_bits,
    )
    attn_parts = Halving(attn_send, attn_keep, "tensor", tensor_bits)
    qkv_parts = Halving(qkv_send, qkv_keep, "dp", fc_bits)
    attn_parts.most()
    sent.arrays[0], attn_parts.send = tie(sent.arrays[0], attn_parts.send)
    attn_parts.swap()
    qkv_parts.swap()
    done = mlp_forward(
        ids,
        sent,
        grad,
        gain_mlp,
        shift_mlp,
        fc_pack,
        fc_bias_own,
        out_pack,
        halving_order(fc_bits),
    )
    done = tie_halves(done, attn_parts, qkv_parts)
    active, slope, mlp_send, mlp_keep, out_send, out_keep = done
    attn_parts.add()
    qkv_parts.add()
    mlp_parts = Halving(mlp_send, mlp_keep, "tensor", tensor_bits)
    mlp_parts.most()
    slope, mlp_parts.send, qkv_parts.send = tie(slope, mlp_parts.send, qkv_parts.send)
    out_parts = Halving(out_send, out_keep, "dp", fc_bits)
    mlp_parts.swap()
    out_parts.swap()
    qkv_parts.swap()
    done = hidden_backward(
        ids,
        sent,
        grad,
        slope,
        gain_mlp,
        shift_mlp,
        fc_pack,
        out_pack,
        [halving_order(fc_bits), halving_order(out_bits)],
    )
    hidden, fc_bias_sums, *halves = tie_halves(done, qkv_parts)
    qkv_parts.add()
    hidden, qkv_parts.send = tie(hidden, qkv_parts.send)
    low_parts = Halving(*halves[:2], "dp", fc_bits)
    high_parts = Halving(*halves[2:], "dp", out_bits)
    low_parts.swap()
    high_parts.swap()
    qkv_parts.swap()
    done = norm_backward(ids, sent, grads, hidden, gain_attn, gain_mlp, qkv_pack, fc_pack)
    back_send, back_keep, norm_sums = tie_halves(
        done, mlp_parts, out_parts, qkv_parts, low_parts, high_parts
    )
    mlp_parts.add()
    for parts in (out_parts, qkv_parts, low_parts, high_parts):
        parts.add()

    back_parts = Halving(back_send, back_keep, "tensor", tensor_bits)
    while len(back_parts.bits) > 2:
        back_parts.swap()
        back_parts.add()
    back_parts.swap()
    output, squares = tie_halves(
        finish_output(
            stream_in, attn_parts.terms, mlp_parts.terms, dense_bias[None, :], out_bias[None, :]
        ),
        back_parts,
    )
    back_parts.add()
    fc_bias_spread = lax.dynamic_update_slice(
        jnp.zeros(fc_bias.shape, f32), fc_bias_sums[0], (tensor_rank * units,)
    )
    qkv_bias_spread = lax.dynamic_update_slice(
        jnp.zeros(qkv_bias.shape, f32), by_head(qkv_bias_sums[0], heads), (tensor_rank * qkv_width,)
    )
    sums = jnp.concatenate(
        [
            norm_sums[:4].reshape(-1),
            squares[:3].reshape(-1),
            jnp.sum(out_grad.astype(f32), axis=0),
            fc_bias_spread,
            qkv_bias_spread,
        ]
    )
    steps = [(axis, bit) for axis in ("tensor", "dp") for bit in bits_of(lax.axis_size(axis))]
    chunks = jnp.split(back_parts.send, 4, axis=1)
    sums = sums + swap(sums, *steps[0])
    for parts in (out_parts, low_parts, high_parts):
        parts.swap()
    got = []
    for at, step in enumerate(steps[1:]):
        other = swap(sums, *step)
        if at == 1:
            (other,) = tie_halves([other], out_parts, low_parts, high_parts)
        if 1 <= at <= len(chunks):
            other, got[-1] = tie(other, got[-1])
        if at < len(chunks):
            sums, chunk = tie(sums, chunks[at])
            got.append(swap(chunk, "tensor", back_parts.bits[-1]))
        sums = sums + other
    for parts in (out_parts, low_parts, high_parts):
        parts.add()
    stream_grad = finish_grad(
        out_grad, normalized, inv_std, [x[0] for x in back_parts.terms], [x[0] for x in got]
    )

    out_weight_grad = out_parts.finish().T
    attn_total = qkv_parts.finish()
    dense_weight_grad = attn_total[:, 3 * width :].T
    qkv_weight_grad = by_head(attn_total[:, : 3 * width], heads)
    fc_weight_grad = jnp.concatenate([low_parts.finish(), high_parts.finish()], axis=1)

    count_all = float(rows_local * lax.axis_size("dp") * groups * model)
    gain_attn_grad, shift_attn_grad, gain_mlp_grad, shift_mlp_grad = sums[: 4 * model].reshape(
        4, model
    )
    squares = jnp.sum(sums[4 * model : 7 * model].reshape(3, model), axis=1)
    root_squares = jnp.sqrt(squares / count_all)
    residual_grad = sums[7 * model : 8 * model]
    fc_bias_grad = sums[8 * model : 8 * model + fc_bias.shape[0]]
    qkv_bias_grad = sums[8 * model + fc_bias.shape[0] :]
    return (
        output,
        stream_grad,
        gain_attn_grad,
        shift_attn_grad,
        gain_mlp_grad,
        shift_mlp_grad,
        qkv_weight_grad,
        qkv_bias_grad,
        dense_weight_grad,
        residual_grad,
        fc_weight_grad,
        fc_bias_grad,
        out_weight_grad,
        residual_grad,
        root_squares,
    )


def solution(mesh):
    tokens, weights, rows, whole = (
        P(("dp", "tensor"), None),
        P("dp", "tensor"),
        P("tensor", "dp"),
        P(),
    )
    return jax.shard_map(
        local,
        mesh=mesh,
        in_specs=(
            tokens,
            P("dp"),
            P("dp"),
            whole,
            whole,
            whole,
            whole,
            weights,
            whole,
            rows,
            whole,
            weights,
            whole,
            rows,
            whole,
            tokens,
        ),
        out_specs=(
            tokens,
            tokens,
            whole,
            whole,
            whole,
            whole,
            weights,
            whole,
            rows,
            whole,
            weights,
            whole,
            rows,
            whole,
            whole,
        ),
        check_vma=False,
    )
```

```python
import jax
import jax.numpy as jnp
from jax import lax
from jax.experimental import pallas as pl
from jax.experimental.pallas import tpu as pltpu
from jax.sharding import PartitionSpec as P

HD = 64
ROT = 16
TRUNK = 1024
SEG = 128
TREE = 2560
NB = TREE // SEG
NT = TRUNK // SEG

f32 = jnp.float32
bf16 = jnp.bfloat16
eps_norm = 1e-05
masked_score = -1e30
VMEM_MOST = 62 << 20


def dot_nn(left, right):
    return lax.dot_general(left, right, (((1,), (0,)), ((), ())), preferred_element_type=f32)


def dot_nt(left, right):
    return lax.dot_general(left, right, (((1,), (1,)), ((), ())), preferred_element_type=f32)


def dot_tn(left, right):
    return lax.dot_general(left, right, (((0,), (0,)), ((), ())), preferred_element_type=f32)


def bits_of(size):
    bits = []
    bit = 1
    while bit < size:
        bits.append(bit)
        bit *= 2
    return bits


def swap(block, axis, bit):
    size = lax.axis_size(axis)
    return lax.ppermute(block, axis, [(i, i ^ bit) for i in range(size)])


def tie(*values):
    return lax.optimization_barrier(values)


def gather_far(block, axis, bits):
    pieces = [block]
    for bit in bits[1:]:
        pieces = pieces + [swap(piece, axis, bit) for piece in pieces]
    return pieces


def gather_near(pieces, axis):
    pieces = [x for piece in pieces for x in (piece, swap(piece, axis, 1))]
    return pieces


class Pack:
    def __init__(self, block, axis, bits):
        self.rows, self.axis, self.bits = block.shape[0], axis, list(bits)
        self.arrays, self.owners = [block], [[0]]

    def double(self):
        bit = self.bits.pop(0)
        held = self.arrays[0] if len(self.arrays) == 1 else jnp.concatenate(self.arrays, axis=0)
        self.owners.append([j ^ bit for owners in self.owners for j in owners])
        self.arrays.append(swap(held, self.axis, bit))

    def specs(self):
        return [pl.BlockSpec(memory_space=pl.ANY)] * len(self.arrays)

    def pieces(self):
        return sum(len(owners) for owners in self.owners)

    def copies(self, refs, where, number, done):
        started = []
        for ref, owners in zip(refs, self.owners):
            for at, j in enumerate(owners):
                rows = pl.ds(pl.multiple_of((number ^ j) * self.rows, self.rows), self.rows)
                source = ref.at[pl.ds(at * self.rows, self.rows), :]
                copy = pltpu.make_async_copy(source, where.at[rows, :], done.at[len(started)])
                started.append(copy)
        return started


def tie_packs(*packs, beside=()):
    flat = tie(*beside, *[x for pack in packs for x in pack.arrays])
    at = len(beside)
    for pack in packs:
        pack.arrays = list(flat[at : at + len(pack.arrays)])
        at += len(pack.arrays)
    return list(flat[: len(beside)])


def halving_order(bits):
    if not bits:
        return [0]
    rest = halving_order(bits[1:])
    return [bits[0] ^ j for j in rest] + rest


class Halving:
    def __init__(self, send, keep, axis, bits):
        self.send, self.axis, self.bits = send, axis, list(bits)
        self.terms = [(keep, 0)]

    def swap(self):
        self.got = swap(self.send, self.axis, self.bits.pop(0))

    def add(self):
        self.terms.append((self.got, 0))
        half = self.got.shape[0] // 2
        if half:
            sends = [x[at : at + half].astype(f32) for x, at in self.terms]
            self.send = sum(sends).astype(bf16)
            self.terms = [(x, at + half) for x, at in self.terms]

    def most(self):
        while len(self.bits) > 1:
            self.swap()
            self.add()

    def finish(self):
        while self.bits:
            self.swap()
            self.add()
        return sum(x[at].astype(f32) for x, at in self.terms)


def tie_halves(values, *halvings):
    flat = tie(*values, *[x.got for x in halvings])
    for x, got in zip(halvings, flat[len(values) :]):
        x.got = got
    return flat[: len(values)]


def resident(shape):
    zeros = (0,) * len(shape)
    return pl.BlockSpec(shape, lambda *_: zeros, pipeline_mode=pl.Buffered(1))


def own_block(rows, columns):
    return pl.BlockSpec((rows, columns), lambda i, ids, *_: (ids[0] ^ ids[2 + i], 0))


def step_block(rows, columns):
    return pl.BlockSpec((rows, columns), lambda i, *_: (i, 0))


def half_blocks(groups, rows, columns):
    half = groups // 2
    shape = (pl.Squeezed(), rows, columns)
    return [
        pl.BlockSpec(shape, lambda i, *_: (jnp.minimum(i, half - 1), 0, 0)),
        pl.BlockSpec(shape, lambda i, *_: (jnp.maximum(i - half, 0), 0, 0)),
    ]


def store_half(send, keep, value, step, groups):
    @pl.when(step < groups // 2)
    def _():
        send[...] = value

    @pl.when(step >= groups // 2)
    def _():
        keep[...] = value


class Tokens:
    def __init__(self, pieces, order):
        self.groups, (self.rows, self.model) = len(pieces), pieces[0].shape
        self.arrays = [pieces[j] for j in order]
        self.specs = [pl.BlockSpec(memory_space=pl.ANY)] * self.groups

    def scratch(self):
        return [
            pltpu.VMEM((2, self.rows, self.model), bf16),
            pltpu.SemaphoreType.DMA((2,)),
        ]

    def fetch(self, refs, held, done, step):
        def copy(at):
            return pltpu.make_async_copy(refs[at], held.at[at % 2], done.at[at % 2])

        for at in range(self.groups):

            @pl.when(step == at)
            def _(at=at):
                if at == 0:
                    copy(0).start()
                if at + 1 < self.groups:
                    copy(at + 1).start()
                copy(at).wait()


def pick_piece(pieces, where, step):
    for at, piece in enumerate(pieces):

        @pl.when(step == at)
        def _(piece=piece):
            where[...] = piece[...]


def store_halves(send, keep, total, number, order, columns=slice(None), source=slice(None)):
    half, rows = send.shape[0], send.shape[1]
    for at, j in enumerate(order):
        where = send if at < half else keep
        block = total[pl.ds(pl.multiple_of((number ^ j) * rows, rows), rows), source]
        where[at % half, :, columns] = block.astype(bf16)


def call(kernel, name, grid, prefetch, operands, specs, outs, out_specs, scratch, flops, extra=0):
    size = sum(x.size * x.dtype.itemsize for x in list(operands) + list(outs))
    return pl.pallas_call(
        kernel,
        grid_spec=pltpu.PrefetchScalarGridSpec(
            num_scalar_prefetch=len(prefetch),
            grid=grid,
            in_specs=specs,
            out_specs=out_specs,
            scratch_shapes=scratch,
        ),
        out_shape=outs,
        compiler_params=pltpu.CompilerParams(
            dimension_semantics=("arbitrary",) * len(grid), vmem_limit_bytes=VMEM_MOST
        ),
        cost_estimate=pl.CostEstimate(
            flops=int(flops), bytes_accessed=int(size), transcendentals=int(extra)
        ),
        name=name,
    )(*prefetch, *operands)


def shaped(*shape, dtype=bf16):
    return jax.ShapeDtypeStruct(shape, dtype)


def shift_gain(block, gain, shift):
    return (block.astype(f32) * gain[...] + shift[...]).astype(bf16)


def turn(block, cosine, low_sine, high_sine, sign):
    width = block.shape[1]
    step = min(width, 128)
    done = []
    for start in range(0, width, step):
        part = block[:, start : start + step]
        if step == 128:
            left = pltpu.roll(part, step - ROT // 2, 1)
            right = pltpu.roll(part, ROT // 2, 1)
        else:
            left = jnp.concatenate([part[:, ROT // 2 :], part[:, : ROT // 2]], axis=1)
            right = jnp.concatenate([part[:, -ROT // 2 :], part[:, : -ROT // 2]], axis=1)
        moved = left * low_sine[:, :step] + right * high_sine[:, :step]
        done.append(part * cosine[:, :step] + moved * sign)
    return done[0] if len(done) == 1 else jnp.concatenate(done, axis=1)


def weight_scratch(pack):
    model = pack.rows * pack.pieces()
    columns = pack.arrays[0].shape[1]
    return [pltpu.VMEM((model, columns), bf16), pltpu.SemaphoreType.DMA((pack.pieces(),))]


def project_qkv(ids, info, sent, gain, shift, pack, bias, tables, width):
    groups, held, rows, model = sent.groups, len(sent.arrays), sent.rows, sent.model

    def kernel(ids, info, *refs):
        sent_refs, refs = refs[:held], refs[held:]
        weight_refs, refs = refs[: len(pack.arrays)], refs[len(pack.arrays) :]
        gain, shift, bias, cos, low, high, q_out, k_out, v_out = refs[:9]
        block, arrived, whole, placed = refs[9:]
        step = pl.program_id(0)

        @pl.when(step == 0)
        def _():
            for copy in pack.copies(weight_refs, whole, ids[1], placed):
                copy.start()

        sent.fetch(sent_refs, block, arrived, step)

        @pl.when(step == 0)
        def _():
            for copy in pack.copies(weight_refs, whole, ids[1], placed):
                copy.wait()

        token = block[step % 2]
        qkv = dot_nn(shift_gain(token, gain, shift), whole[...]) + bias[...]
        first = (ids[0] ^ ids[2 + step]) * (rows // SEG)
        for at in range(rows // SEG):
            number = first + at
            table = pl.ds(pl.multiple_of(info[number // NB, number % NB, 4] * SEG, SEG), SEG)
            tabs = (cos[table, :], low[table, :], high[table, :])
            own = slice(at * SEG, (at + 1) * SEG)
            q_out[own, :] = (turn(qkv[own, :width], *tabs, 1.0) * HD**-0.5).astype(bf16)
            k_out[own, :] = turn(qkv[own, width : 2 * width], *tabs, 1.0).astype(bf16)
        v_out[...] = qkv[:, 2 * width :].astype(bf16)

    operands = [*sent.arrays, *pack.arrays, gain, shift, bias, *tables]
    out = shaped(groups * rows, width)
    return call(
        kernel,
        "project_qkv",
        (groups,),
        [ids, info],
        operands,
        sent.specs
        + pack.specs()
        + [resident(x.shape) for x in operands[held + len(pack.arrays) :]],
        [out] * 3,
        [own_block(rows, width)] * 3,
        sent.scratch() + weight_scratch(pack),
        2 * groups * rows * model * 3 * width,
    )


def project_grad(ids, grad, pack, width):
    groups, held, rows, model = grad.groups, len(grad.arrays), grad.rows, grad.model

    def kernel(ids, *refs):
        grad_refs, refs = refs[:held], refs[held:]
        weight_refs, (out, block, arrived, whole, placed) = refs[:-5], refs[-5:]
        step = pl.program_id(0)

        @pl.when(step == 0)
        def _():
            for copy in pack.copies(weight_refs, whole, ids[1], placed):
                copy.start()

        grad.fetch(grad_refs, block, arrived, step)

        @pl.when(step == 0)
        def _():
            for copy in pack.copies(weight_refs, whole, ids[1], placed):
                copy.wait()

        out[...] = dot_nn(block[step % 2], whole[...]).astype(bf16)

    operands = [*grad.arrays, *pack.arrays]
    return call(
        kernel,
        "project_grad",
        (groups,),
        [ids],
        operands,
        grad.specs + pack.specs(),
        [shaped(groups * rows, width)],
        [own_block(rows, width)],
        grad.scratch() + weight_scratch(pack),
        2 * groups * rows * model * width,
    )[0]


def attention_kernel(
    info, q_ref, do_ref, k_ref, v_ref, cos, low, high, ctx_ref, dq_ref, dk_ref, dv_ref, dk_sum, dv_sum
):
    tree, step = pl.program_id(0), pl.program_id(1)
    width = q_ref.shape[1]
    heads = width // HD
    lane_head = lax.broadcasted_iota(jnp.int32, (SEG, width), 1) // HD

    @pl.when(step == 0)
    def _():
        dk_sum[...] = jnp.zeros_like(dk_sum)
        dv_sum[...] = jnp.zeros_like(dv_sum)

    first, second = info[tree, step, 0], info[tree, step, 1]
    first_rows = pl.ds(pl.multiple_of(first * SEG, SEG), SEG)
    second_rows = pl.ds(pl.multiple_of(second * SEG, SEG), SEG)
    queries, grads = q_ref[...], do_ref[...]
    zero = jnp.zeros_like(queries)
    q_rows = jnp.concatenate([jnp.where(lane_head == h, queries, zero) for h in range(heads)], axis=0)
    g_rows = jnp.concatenate([jnp.where(lane_head == h, grads, zero) for h in range(heads)], axis=0)
    q_turned, g_turned = queries.T, grads.T
    ahead = lax.broadcasted_iota(jnp.int32, (SEG, SEG), 1) - lax.broadcasted_iota(
        jnp.int32, (SEG, SEG), 0
    )
    seen = jnp.concatenate([ahead <= info[tree, step, 2], ahead <= info[tree, step, 3]], axis=1)
    seen = jnp.concatenate([seen] * heads, axis=0)
    k_near = jnp.concatenate([k_ref[first_rows, :], k_ref[second_rows, :]], axis=0)
    v_near = jnp.concatenate([v_ref[first_rows, :], v_ref[second_rows, :]], axis=0)

    def work(pairs):
        count = pairs * 2 * SEG
        near = jnp.where(seen, dot_nt(q_rows, k_near), masked_score)
        most = jnp.max(near, axis=1, keepdims=True)
        if count:
            k_far, v_far = k_ref[0:count, :], v_ref[0:count, :]
            far = dot_nt(q_rows, k_far)
            most = jnp.maximum(most, jnp.max(far, axis=1, keepdims=True))
        near = jnp.exp(near - most)
        total = jnp.sum(near, axis=1, keepdims=True)
        if count:
            far = jnp.exp(far - most)
            total = total + jnp.sum(far, axis=1, keepdims=True)
        scale = 1.0 / total
        near = near * scale
        near_low = near.astype(bf16)
        context = dot_nn(near_low, v_near)
        if count:
            far = far * scale
            far_low = far.astype(bf16)
            context = context + dot_nn(far_low, v_far)
        delta = jnp.sum(context * g_rows.astype(f32), axis=1, keepdims=True)
        near = (near * (dot_nt(g_rows, v_near) - delta)).astype(bf16)
        dq = dot_nn(near, k_near)
        if count:
            far = (far * (dot_nt(g_rows, v_far) - delta)).astype(bf16)
            dq = dq + dot_nn(far, k_far)
        ctx_own, dq_own = context[0:SEG], dq[0:SEG]
        for h in range(1, heads):
            ctx_own = jnp.where(lane_head == h, context[h * SEG : (h + 1) * SEG], ctx_own)
            dq_own = jnp.where(lane_head == h, dq[h * SEG : (h + 1) * SEG], dq_own)
        ctx_ref[...] = ctx_own.astype(bf16)
        dq_ref[...] = turn(dq_own * HD**-0.5, cos, low, high, -1.0).astype(bf16)
        for h in range(heads):
            own = slice(h * SEG, (h + 1) * SEG)
            part = slice(h * HD, (h + 1) * HD)
            dk = dot_nn(q_turned[part], near[own])
            dv = dot_nn(g_turned[part], near_low[own])
            dk_sum[first, part, :] += dk[:, :SEG]
            dv_sum[first, part, :] += dv[:, :SEG]
            dk_sum[second, part, :] += dk[:, SEG:]
            dv_sum[second, part, :] += dv[:, SEG:]
            if count:
                dk = dot_nn(q_turned[part], far[own])
                dv = dot_nn(g_turned[part], far_low[own])
                for j in range(2 * pairs):
                    dk_sum[j, part, :] += dk[:, j * SEG : (j + 1) * SEG]
                    dv_sum[j, part, :] += dv[:, j * SEG : (j + 1) * SEG]

    for pairs in range(NT // 2):

        @pl.when(step // 2 == pairs)
        def _(pairs=pairs):
            work(pairs)

    @pl.when(step >= NT)
    def _():
        work(NT // 2)

    @pl.when(step == NB - 1)
    def _():
        def finish(j, carry):
            rows = pl.ds(pl.multiple_of(j * SEG, SEG), SEG)
            dv_ref[rows, :] = dv_sum[j].T.astype(bf16)
            dk_ref[rows, :] = dk_sum[j].T.astype(bf16)
            return carry

        lax.fori_loop(0, NB, finish, 0)


def attention(info, tables, queries, keys, values, grads):
    total, width = queries.shape
    trees = total // TREE
    table_width = tables[0].shape[1]
    block = pl.BlockSpec((SEG, width), lambda t, b, info: (t * NB + b, 0))
    whole = pl.BlockSpec((TREE, width), lambda t, b, info: (t, 0))
    table = pl.BlockSpec((SEG, table_width), lambda t, b, info: (info[t, b, 4], 0))
    scores = trees * (TREE - TRUNK) * (TRUNK + 2 * SEG) * (width // HD)
    return call(
        attention_kernel,
        "attention",
        (trees, NB),
        [info],
        [queries, grads, keys, values, *tables],
        [block, block, whole, whole, table, table, table],
        [shaped(total, width)] * 4,
        [block, block, whole, whole],
        [pltpu.VMEM((NB, width, SEG), f32), pltpu.VMEM((NB, width, SEG), f32)],
        scores * width * 2 * 6 * 1.3,
        scores,
    )


def project_context(ids, context, pack, groups, model):
    rows, width = context.shape[0] // groups, context.shape[1]

    def kernel(ids, ctx, *refs):
        weight_refs, (send, keep, whole, placed) = refs[:-4], refs[-4:]
        step = pl.program_id(0)

        @pl.when(step == 0)
        def _():
            copies = pack.copies(weight_refs, whole, ids[1], placed)
            for copy in copies:
                copy.start()
            for copy in copies:
                copy.wait()

        store_half(send, keep, dot_nt(ctx[...], whole[...]).astype(bf16), step, groups)

    operands = [context, *pack.arrays]
    half = shaped(groups // 2, rows, model)
    return call(
        kernel,
        "project_context",
        (groups,),
        [ids],
        operands,
        [own_block(rows, width)] + pack.specs(),
        [half] * 2,
        half_blocks(groups, rows, model),
        weight_scratch(pack),
        2 * groups * rows * model * width,
    )


def mlp(ids, sent, grad, context, gain, shift, fc, bias, out, orders):
    groups, held, rows, model = sent.groups, len(sent.arrays), sent.rows, sent.model
    pieces, units, width = len(fc.arrays), fc.arrays[0].shape[1], context.shape[1]

    def kernel(ids, ctx_ref, *refs):
        sent_refs, refs = refs[:held], refs[held:]
        grad_refs, refs = refs[:held], refs[held:]
        fc_refs, refs = refs[:pieces], refs[pieces:]
        out_refs, refs = refs[:pieces], refs[pieces:]
        gain, shift, bias, part_send, part_keep, hidden_ref, bias_ref = refs[:7]
        stacks, refs = refs[7:11], refs[11:]
        block, arrived, grad_block, grad_arrived, fc_whole, fc_placed, out_whole, out_placed = refs[:8]
        act_ref, fc_total, out_total, dense_total = refs[8:]
        step = pl.program_id(0)

        def weights():
            copies = fc.copies(fc_refs, fc_whole, ids[1], fc_placed)
            return copies + out.copies(out_refs, out_whole, ids[1], out_placed)

        @pl.when(step == 0)
        def _():
            for copy in weights():
                copy.start()
            fc_total[...] = jnp.zeros_like(fc_total)
            out_total[...] = jnp.zeros_like(out_total)
            dense_total[...] = jnp.zeros_like(dense_total)
            bias_ref[...] = jnp.zeros_like(bias_ref)

        sent.fetch(sent_refs, block, arrived, step)
        grad.fetch(grad_refs, grad_block, grad_arrived, step)

        @pl.when(step == 0)
        def _():
            for copy in weights():
                copy.wait()

        token, grads = block[step % 2], grad_block[step % 2]
        normed = shift_gain(token, gain, shift)
        count = 2
        parts = [slice(k * rows // count, (k + 1) * rows // count) for k in range(count)]
        hidden = [dot_nn(normed[x], fc_whole[...]) + bias[...] for x in parts]
        back = [dot_nn(grads[x], out_whole[...]) for x in parts]
        for x, field, slope in zip(parts, hidden, back):
            chance = 0.5 + 0.5 * lax.erf(field * 0.7071067811865476)
            bell = jnp.exp(field * field * -0.5) * 0.3989422804014327
            act_ref[x, :] = (field * chance).astype(bf16)
            low = (slope * (chance + field * bell)).astype(bf16)
            hidden_ref[x, :] = low
            bias_ref[0:1, :] += jnp.sum(low.astype(f32), axis=0, keepdims=True)
        store_half(
            part_send, part_keep, dot_nt(act_ref[...], out_whole[...]).astype(bf16), step, groups
        )
        out_total[...] += dot_tn(grads, act_ref[...])
        fc_total[...] += dot_tn(normed, hidden_ref[...])
        dense_total[...] += dot_tn(grads, ctx_ref[...])

        @pl.when(step == groups - 1)
        def _():
            half = units // 2
            for at, order in enumerate(orders):
                stack = stacks[2 * at : 2 * at + 2]
                source = slice(at * half, (at + 1) * half)
                store_halves(*stack, fc_total, ids[1], order, slice(0, half), source)
                store_halves(*stack, out_total, ids[1], order, slice(half, units), source)
            columns = slice(units, units + width)
            store_halves(*stacks[:2], dense_total, ids[1], orders[0], columns)

    operands = [context, *sent.arrays, *grad.arrays, *fc.arrays, *out.arrays, gain, shift, bias]
    count = model // fc.rows
    outs = [
        shaped(groups // 2, rows, model),
        shaped(groups // 2, rows, model),
        shaped(groups * rows, units),
        shaped(8, units, dtype=f32),
    ]
    outs += [shaped(count // 2, fc.rows, units + width)] * 2
    outs += [shaped(count // 2, fc.rows, units)] * 2
    return call(
        kernel,
        "mlp",
        (groups,),
        [ids],
        operands,
        [own_block(rows, width)]
        + sent.specs
        + grad.specs
        + fc.specs()
        + out.specs()
        + [resident(x.shape) for x in operands[-3:]],
        outs,
        half_blocks(groups, rows, model)
        + [step_block(rows, units)]
        + [resident(x.shape) for x in outs[3:]],
        sent.scratch()
        + grad.scratch()
        + weight_scratch(fc)
        + weight_scratch(out)
        + [
            pltpu.VMEM((rows, units), bf16),
            pltpu.VMEM((model, units), f32),
            pltpu.VMEM((model, units), f32),
            pltpu.VMEM((model, width), f32),
        ],
        10 * groups * rows * model * units,
    )


def norm_backward(
    ids, info, tables, sent, dq, dk, dv, hidden, gain_attn, shift_attn, gain_mlp, qkv_pack, fc, orders
):
    groups, held, rows, model = sent.groups, len(sent.arrays), sent.rows, sent.model
    pieces, units, width = len(fc.arrays), hidden.shape[1], dq.shape[1]

    def kernel(ids, info, dq_ref, dk_ref, dv_ref, hidden_ref, *refs):
        sent_refs, refs = refs[:held], refs[held:]
        qkv_refs, refs = refs[:pieces], refs[pieces:]
        fc_refs, refs = refs[:pieces], refs[pieces:]
        gain_attn, shift_attn, gain_mlp, cos, low, high = refs[:6]
        send, keep, sums_ref, bias_ref, *halves = refs[6:14]
        block, arrived, qkv_whole, qkv_placed, fc_whole, fc_placed, grads, total = refs[14:]
        step = pl.program_id(0)

        def weights():
            copies = qkv_pack.copies(qkv_refs, qkv_whole, ids[1], qkv_placed)
            return copies + fc.copies(fc_refs, fc_whole, ids[1], fc_placed)

        @pl.when(step == 0)
        def _():
            for copy in weights():
                copy.start()
            sums_ref[...] = jnp.zeros_like(sums_ref)
            bias_ref[...] = jnp.zeros_like(bias_ref)
            total[...] = jnp.zeros_like(total)

        sent.fetch(sent_refs, block, arrived, step)
        grads[:, :width] = dq_ref[...]
        first = (ids[0] ^ ids[2 + step]) * (rows // SEG)
        for at in range(rows // SEG):
            number = first + at
            table = pl.ds(pl.multiple_of(info[number // NB, number % NB, 4] * SEG, SEG), SEG)
            own = slice(at * SEG, (at + 1) * SEG)
            turned = turn(dk_ref[own, :], cos[table, :], low[table, :], high[table, :], -1.0)
            grads[own, width : 2 * width] = turned.astype(bf16)
        grads[:, 2 * width :] = dv_ref[...]
        bias_ref[0:1, :] += jnp.sum(grads[...].astype(f32), axis=0, keepdims=True)

        @pl.when(step == 0)
        def _():
            for copy in weights():
                copy.wait()

        token = block[step % 2]
        total[...] += dot_tn(shift_gain(token, gain_attn, shift_attn), grads[...])
        back_attn = dot_nt(grads[...], qkv_whole[...])
        back_mlp = dot_nt(hidden_ref[...], fc_whole[...])
        token = token.astype(f32)
        for at, back in enumerate((back_attn, back_mlp)):
            sums_ref[2 * at : 2 * at + 1, :] += jnp.sum(back * token, axis=0, keepdims=True)
            sums_ref[2 * at + 1 : 2 * at + 2, :] += jnp.sum(back, axis=0, keepdims=True)
        part = back_attn * gain_attn[...] + back_mlp * gain_mlp[...]
        store_half(send, keep, part.astype(bf16), step, groups)

        @pl.when(step == groups - 1)
        def _():
            for at, order in enumerate(orders):
                source = slice(at * 3 * width // 2, (at + 1) * 3 * width // 2)
                store_halves(*halves[2 * at : 2 * at + 2], total, ids[1], order, source=source)

    operands = [
        dq,
        dk,
        dv,
        hidden,
        *sent.arrays,
        *qkv_pack.arrays,
        *fc.arrays,
        gain_attn,
        shift_attn,
        gain_mlp,
        *tables,
    ]
    count = model // fc.rows
    outs = [
        shaped(groups // 2, rows, model),
        shaped(groups // 2, rows, model),
        shaped(8, model, dtype=f32),
        shaped(8, 3 * width, dtype=f32),
    ]
    outs += [shaped(count // 2, fc.rows, 3 * width // 2)] * 4
    return call(
        kernel,
        "norm_backward",
        (groups,),
        [ids, info],
        operands,
        [own_block(rows, width)] * 3
        + [step_block(rows, units)]
        + sent.specs
        + qkv_pack.specs()
        + fc.specs()
        + [resident(x.shape) for x in operands[-6:]],
        outs,
        half_blocks(groups, rows, model) + [resident(x.shape) for x in outs[2:]],
        sent.scratch()
        + weight_scratch(qkv_pack)
        + weight_scratch(fc)
        + [pltpu.VMEM((rows, 3 * width), bf16), pltpu.VMEM((model, 3 * width), f32)],
        2 * groups * rows * model * (units + 6 * width),
    )


def taken(terms, block):
    return [
        pl.BlockSpec((pl.Squeezed(), block, x.shape[2]), lambda i, *_, at=at: (at, i, 0))
        for x, at in terms
    ]


def finish_output(stream, attn_terms, mlp_terms, dense_bias, out_bias):
    rows, model = stream.shape
    block = 128
    first, second = len(attn_terms), len(mlp_terms)

    def kernel(stream_ref, *refs):
        attn_refs, refs = refs[:first], refs[first:]
        mlp_refs, (dense_bias, out_bias, out_ref, sums_ref) = refs[:second], refs[second:]

        @pl.when(pl.program_id(0) == 0)
        def _():
            sums_ref[...] = jnp.zeros_like(sums_ref)

        attn = sum(x[...].astype(f32) for x in attn_refs) + dense_bias[...]
        mlp = sum(x[...].astype(f32) for x in mlp_refs) + out_bias[...]
        output = stream_ref[...] + attn + mlp
        out_ref[...] = output
        for at, value in enumerate((output, attn, mlp)):
            sums_ref[at : at + 1, :] += jnp.sum(value * value, axis=0, keepdims=True)

    terms = [*attn_terms, *mlp_terms]
    operands = [stream, *[x for x, _ in terms], dense_bias, out_bias]
    outs = [shaped(rows, model, dtype=f32), shaped(8, model, dtype=f32)]
    return call(
        kernel,
        "finish_output",
        (rows // block,),
        [],
        operands,
        [step_block(block, model)]
        + taken(terms, block)
        + [resident(dense_bias.shape), resident(out_bias.shape)],
        outs,
        [step_block(block, model), resident(outs[1].shape)],
        [],
        rows * model * 16,
    )


def finish_grad(grad, normalized, inv_std, terms, chunks):
    rows, model = grad.shape
    count, block = len(chunks), chunks[0].shape[0]
    held = len(terms)

    def kernel(grad_ref, norm_ref, std_ref, *refs):
        term_refs, chunk_refs, (out_ref, last) = refs[:held], refs[held:-2], refs[-2:]
        pick_piece(chunk_refs, last, pl.program_id(0))
        sent = sum(x[...].astype(f32) for x in term_refs) + last[...].astype(f32)
        norm = norm_ref[...]
        mean = jnp.sum(sent, axis=1, keepdims=True) / model
        cross = jnp.sum(sent * norm, axis=1, keepdims=True) / model
        out_ref[...] = grad_ref[...].astype(f32) + std_ref[...] * (sent - mean - norm * cross)

    operands = [grad, normalized, inv_std, *[x for x, _ in terms], *chunks]
    return call(
        kernel,
        "finish_grad",
        (count,),
        [],
        operands,
        [step_block(block, model), step_block(block, model), step_block(block, 1)]
        + taken(terms, block)
        + [resident(x.shape) for x in chunks],
        [shaped(rows, model, dtype=f32)],
        [step_block(block, model)],
        [pltpu.VMEM((block, model), bf16)],
        rows * model * 12,
    )[0]


def tree_table(segment_ids, parent_ids):
    trees = segment_ids.shape[0] // TREE
    segment = segment_ids.reshape(trees, NB, SEG)[:, :, 0]
    parent = parent_ids.reshape(trees, NB, SEG)[:, :, 0]
    block = lax.broadcasted_iota(jnp.int32, (trees, NB), 1)
    trunk = block < NT
    leaf = (parent != segment[:, :1]) & ~trunk
    at = lax.broadcasted_iota(jnp.int32, (trees, NB, NB), 2)
    owner = jnp.sum(jnp.where(segment[:, None, :] == parent[:, :, None], at, 0), axis=2)
    odd = block % 2 == 1
    first = jnp.where(trunk, block // 2 * 2, block)
    second = jnp.where(trunk, block // 2 * 2 + 1, jnp.where(leaf, owner, block))
    first_most = jnp.where(trunk & odd, SEG, 0)
    second_most = jnp.where(trunk, jnp.where(odd, 0, -SEG), jnp.where(leaf, SEG, -SEG))
    table = jnp.where(trunk, block, jnp.where(leaf, NT + 1, NT))
    return jnp.stack([first, second, first_most, second_most, table], axis=2).astype(jnp.int32)


def angle_tables():
    places = TRUNK + 2 * SEG
    place = lax.broadcasted_iota(jnp.int32, (places, 2 * HD), 0).astype(f32)
    lane = lax.broadcasted_iota(jnp.int32, (places, 2 * HD), 1) % HD
    half = ROT // 2
    frequency = 10000.0 ** (-((lane % half).astype(f32) * 2.0 / ROT))
    angle = place * frequency
    cosine = jnp.where(lane < ROT, jnp.cos(angle), 1.0)
    sine = jnp.sin(angle)
    low = jnp.where(lane < half, -sine, 0.0)
    high = jnp.where((lane >= half) & (lane < ROT), sine, 0.0)
    return cosine, low, high


def by_kind(array, heads):
    shape = array.shape[:-1]
    array = array.reshape(*shape, heads, 3, HD)
    return jnp.swapaxes(array, -3, -2).reshape(*shape, 3 * heads * HD)


def by_head(array, heads):
    shape = array.shape[:-1]
    array = array.reshape(*shape, 3, heads, HD)
    return jnp.swapaxes(array, -3, -2).reshape(*shape, 3 * heads * HD)


def local(
    stream_in,
    segment_ids,
    parent_ids,
    norm_gain_attn,
    norm_shift_attn,
    norm_gain_mlp,
    norm_shift_mlp,
    qkv_weight,
    qkv_bias,
    dense_weight,
    dense_bias,
    fc_weight,
    fc_bias,
    out_weight,
    out_bias,
    out_grad,
):
    tensor_rank = lax.axis_index("tensor")
    data_rank = lax.axis_index("dp")
    rows_local = stream_in.shape[0]
    model = stream_in.shape[1]
    qkv_width = qkv_weight.shape[1]
    heads = qkv_width // (3 * HD)
    width = heads * HD
    units = fc_weight.shape[1]
    groups = lax.axis_size("tensor")
    tensor_bits = bits_of(groups)
    far_first = tensor_bits[:0:-1] + tensor_bits[:1]
    order = halving_order(tensor_bits)
    ids = jnp.stack([tensor_rank, data_rank, *order]).astype(jnp.int32)
    data_bits = bits_of(lax.axis_size("dp"))
    rows_first = data_bits[:0:-1] + data_bits[:1]
    columns_first = data_bits[:1] + data_bits[:0:-1]
    near_bits = data_bits
    next_bits = data_bits[1:2] + data_bits[:1] + data_bits[2:]

    qkv_pack = Pack(by_kind(qkv_weight.astype(bf16), heads), "dp", rows_first)
    dense_pack = Pack(dense_weight.astype(bf16).T, "dp", columns_first)
    fc_pack = Pack(fc_weight.astype(bf16), "dp", rows_first)
    out_pack = Pack(out_weight.astype(bf16).T, "dp", columns_first)

    row_mean = jnp.mean(stream_in, axis=-1, keepdims=True)
    centred = stream_in - row_mean
    row_var = jnp.mean(centred * centred, axis=-1, keepdims=True)
    inv_std = lax.rsqrt(row_var + eps_norm)
    normalized = centred * inv_std
    sent = gather_far(normalized.astype(bf16), "tensor", tensor_bits)

    qkv_pack.double()
    dense_pack.double()
    out_pack.double()
    tie_packs(qkv_pack, dense_pack, fc_pack, out_pack)
    while len(qkv_pack.bits) > 1:
        qkv_pack.double()
        dense_pack.double()
    fc_pack.double()
    sent = tie_packs(qkv_pack, dense_pack, fc_pack, out_pack, beside=sent)
    out_grad, sent[0] = tie(out_grad, sent[0])
    grad = gather_far(out_grad, "tensor", tensor_bits)
    sent = gather_near(sent, "tensor")
    qkv_pack.double()
    dense_pack.double()
    while len(out_pack.bits) > 1:
        out_pack.double()
    sent = Tokens(tie_packs(qkv_pack, dense_pack, out_pack, beside=sent), order)

    info = tree_table(segment_ids, parent_ids)
    tables = angle_tables()
    gain_attn, shift_attn = norm_gain_attn[None, :], norm_shift_attn[None, :]
    gain_mlp, shift_mlp = norm_gain_mlp[None, :], norm_shift_mlp[None, :]
    qkv_bias_own = by_kind(
        lax.dynamic_slice_in_dim(qkv_bias, tensor_rank * qkv_width, qkv_width), heads
    )[None, :]
    fc_bias_own = lax.dynamic_slice_in_dim(fc_bias, tensor_rank * units, units)[None, :]

    while len(fc_pack.bits) > 1:
        fc_pack.double()
    done = project_qkv(
        ids, info, sent, gain_attn, shift_attn, qkv_pack, qkv_bias_own, tables, width
    )
    queries, keys, values, *grad = tie_packs(fc_pack, beside=[*done, *grad])
    grad = Tokens(gather_near(grad, "tensor"), order)
    grad_context = project_grad(ids, grad, dense_pack, width)
    fc_pack.double()
    out_pack.double()
    done = attention(info, tables, queries, keys, values, grad_context)
    context, dq, dk, dv = tie_packs(fc_pack, out_pack, beside=done)
    attn_parts = Halving(
        *project_context(ids, context, dense_pack, groups, model), "tensor", tensor_bits
    )
    attn_parts.most()
    context, attn_parts.send = tie(context, attn_parts.send)
    attn_parts.swap()
    done = mlp(
        ids,
        sent,
        grad,
        context,
        gain_mlp,
        shift_mlp,
        fc_pack,
        fc_bias_own,
        out_pack,
        [halving_order(near_bits), halving_order(next_bits)],
    )
    done = tie_halves(done, attn_parts)
    mlp_send, mlp_keep, hidden, fc_bias_sums, *stacks = done
    attn_parts.add()
    mlp_parts = Halving(mlp_send, mlp_keep, "tensor", tensor_bits)
    mlp_sums = [
        Halving(*stacks[:2], "dp", near_bits),
        Halving(*stacks[2:], "dp", next_bits),
    ]
    mlp_parts.most()
    hidden, mlp_parts.send = tie(hidden, mlp_parts.send)
    mlp_parts.swap()
    for parts in mlp_sums:
        parts.swap()
    done = norm_backward(
        ids,
        info,
        tables,
        sent,
        dq,
        dk,
        dv,
        hidden,
        gain_attn,
        shift_attn,
        gain_mlp,
        qkv_pack,
        fc_pack,
        [halving_order(near_bits), halving_order(next_bits)],
    )
    done = tie_halves(done, mlp_parts, *mlp_sums)
    back_send, back_keep, norm_sums, qkv_bias_sums, *stacks = done
    qkv_sums = [
        Halving(*stacks[:2], "dp", near_bits),
        Halving(*stacks[2:], "dp", next_bits),
    ]
    mlp_parts.add()
    for parts in mlp_sums:
        parts.add()

    back_parts = Halving(back_send, back_keep, "tensor", tensor_bits)
    while len(back_parts.bits) > 2:
        back_parts.swap()
        back_parts.add()
    back_parts.swap()
    output, squares = tie_halves(
        finish_output(
            stream_in, attn_parts.terms, mlp_parts.terms, dense_bias[None, :], out_bias[None, :]
        ),
        back_parts,
    )
    back_parts.add()
    fc_bias_spread = lax.dynamic_update_slice(
        jnp.zeros(fc_bias.shape, f32), fc_bias_sums[0], (tensor_rank * units,)
    )
    qkv_bias_spread = lax.dynamic_update_slice(
        jnp.zeros(qkv_bias.shape, f32), by_head(qkv_bias_sums[0], heads), (tensor_rank * qkv_width,)
    )
    sums = jnp.concatenate(
        [
            norm_sums[:4].reshape(-1),
            squares[:3].reshape(-1),
            jnp.sum(out_grad.astype(f32), axis=0),
            fc_bias_spread,
            qkv_bias_spread,
        ]
    )
    steps = [(axis, bit) for axis in ("tensor", "dp") for bit in bits_of(lax.axis_size(axis))]
    chunks = jnp.split(back_parts.send, 4, axis=1)
    sums = sums + swap(sums, *steps[0])
    for parts in mlp_sums + qkv_sums:
        parts.swap()
    got = []
    for at, step in enumerate(steps[1:]):
        other = swap(sums, *step)
        if at < len(chunks):
            got.append(swap(chunks[at], "tensor", back_parts.bits[-1]))
            other, got[-1], *chunks[at + 1 :] = tie(other, got[-1], *chunks[at + 1 :])
        if at == 2:
            (other,) = tie_halves([other], *mlp_sums, *qkv_sums)
        sums = sums + other
    for parts in mlp_sums + qkv_sums:
        parts.add()
    stream_grad = finish_grad(
        out_grad, normalized, inv_std, back_parts.terms, [x[0] for x in got]
    )

    first, second = [parts.finish() for parts in mlp_sums]
    half = units // 2
    fc_weight_grad = jnp.concatenate([first[:, :half], second[:, :half]], axis=1)
    out_weight_grad = jnp.concatenate([first[:, half:units], second[:, half:]], axis=1).T
    dense_weight_grad = first[:, units:].T
    total = jnp.concatenate([parts.finish() for parts in qkv_sums], axis=1)
    qkv_weight_grad = by_head(total, heads)

    count_all = float(rows_local * lax.axis_size("dp") * groups * model)
    gain_attn_grad, shift_attn_grad, gain_mlp_grad, shift_mlp_grad = sums[: 4 * model].reshape(
        4, model
    )
    squares = jnp.sum(sums[4 * model : 7 * model].reshape(3, model), axis=1)
    root_squares = jnp.sqrt(squares / count_all)
    residual_grad = sums[7 * model : 8 * model]
    fc_bias_grad = sums[8 * model : 8 * model + fc_bias.shape[0]]
    qkv_bias_grad = sums[8 * model + fc_bias.shape[0] :]
    return (
        output,
        stream_grad,
        gain_attn_grad,
        shift_attn_grad,
        gain_mlp_grad,
        shift_mlp_grad,
        qkv_weight_grad,
        qkv_bias_grad,
        dense_weight_grad,
        residual_grad,
        fc_weight_grad,
        fc_bias_grad,
        out_weight_grad,
        residual_grad,
        root_squares,
    )


def solution(mesh):
    tokens, weights, rows, whole = (
        P(("dp", "tensor"), None),
        P("dp", "tensor"),
        P("tensor", "dp"),
        P(),
    )
    return jax.shard_map(
        local,
        mesh=mesh,
        in_specs=(
            tokens,
            P("dp"),
            P("dp"),
            whole,
            whole,
            whole,
            whole,
            weights,
            whole,
            rows,
            whole,
            weights,
            whole,
            rows,
            whole,
            tokens,
        ),
        out_specs=(
            tokens,
            tokens,
            whole,
            whole,
            whole,
            whole,
            weights,
            whole,
            rows,
            whole,
            weights,
            whole,
            rows,
            whole,
            whole,
        ),
        check_vma=False,
    )
```

```python
import jax
import jax.numpy as jnp
from jax import lax
from jax.experimental import pallas as pl
from jax.experimental.pallas import tpu as pltpu
from jax.sharding import PartitionSpec as P

HD = 64
ROT = 16
TRUNK = 1024
SEG = 128
TREE = 2560
NB = TREE // SEG
NT = TRUNK // SEG

f32 = jnp.float32
bf16 = jnp.bfloat16
eps_norm = 1e-05
masked_score = -1e30
VMEM_MOST = 62 << 20


def dot_nn(left, right):
    return lax.dot_general(left, right, (((1,), (0,)), ((), ())), preferred_element_type=f32)


def dot_nt(left, right):
    return lax.dot_general(left, right, (((1,), (1,)), ((), ())), preferred_element_type=f32)


def dot_tn(left, right):
    return lax.dot_general(left, right, (((0,), (0,)), ((), ())), preferred_element_type=f32)


def bits_of(size):
    bits = []
    bit = 1
    while bit < size:
        bits.append(bit)
        bit *= 2
    return bits


def swap(block, axis, bit):
    size = lax.axis_size(axis)
    return lax.ppermute(block, axis, [(i, i ^ bit) for i in range(size)])


def tie(*values):
    return lax.optimization_barrier(values)


def gather_far(block, axis, bits):
    pieces = [block]
    for bit in bits[1:]:
        pieces = pieces + [swap(piece, axis, bit) for piece in pieces]
    return pieces


def gather_near(pieces, axis):
    pieces = [x for piece in pieces for x in (piece, swap(piece, axis, 1))]
    return pieces


class Pack:
    def __init__(self, block, axis, bits):
        self.rows, self.axis, self.bits = block.shape[0], axis, list(bits)
        self.arrays, self.owners = [block], [[0]]

    def double(self):
        bit = self.bits.pop(0)
        held = self.arrays[0] if len(self.arrays) == 1 else jnp.concatenate(self.arrays, axis=0)
        self.owners.append([j ^ bit for owners in self.owners for j in owners])
        self.arrays.append(swap(held, self.axis, bit))

    def specs(self):
        return [pl.BlockSpec(memory_space=pl.ANY)] * len(self.arrays)

    def pieces(self):
        return sum(len(owners) for owners in self.owners)

    def copies(self, refs, where, number, done):
        started = []
        for ref, owners in zip(refs, self.owners):
            for at, j in enumerate(owners):
                rows = pl.ds(pl.multiple_of((number ^ j) * self.rows, self.rows), self.rows)
                source = ref.at[pl.ds(at * self.rows, self.rows), :]
                copy = pltpu.make_async_copy(source, where.at[rows, :], done.at[len(started)])
                started.append(copy)
        return started


def tie_packs(*packs, beside=()):
    flat = tie(*beside, *[x for pack in packs for x in pack.arrays])
    at = len(beside)
    for pack in packs:
        pack.arrays = list(flat[at : at + len(pack.arrays)])
        at += len(pack.arrays)
    return list(flat[: len(beside)])


def halving_order(bits):
    if not bits:
        return [0]
    rest = halving_order(bits[1:])
    return [bits[0] ^ j for j in rest] + rest


class Halving:
    def __init__(self, send, keep, axis, bits):
        self.send, self.axis, self.bits = send, axis, list(bits)
        self.terms = [(keep, 0)]

    def swap(self):
        self.got = swap(self.send, self.axis, self.bits.pop(0))

    def add(self):
        self.terms.append((self.got, 0))
        half = self.got.shape[0] // 2
        if half:
            self.send = add_terms(self.terms, half)
            self.terms = [(x, at + half) for x, at in self.terms]

    def most(self):
        while len(self.bits) > 1:
            self.swap()
            self.add()

    def finish(self):
        while self.bits:
            self.swap()
            self.add()
        return sum(x[at].astype(f32) for x, at in self.terms)


def tie_halves(values, *halvings):
    flat = tie(*values, *[x.got for x in halvings])
    for x, got in zip(halvings, flat[len(values) :]):
        x.got = got
    return flat[: len(values)]


def resident(shape):
    zeros = (0,) * len(shape)
    return pl.BlockSpec(shape, lambda *_: zeros, pipeline_mode=pl.Buffered(1))


def own_block(rows, columns):
    return pl.BlockSpec((rows, columns), lambda i, ids, *_: (ids[0] ^ ids[2 + i], 0))


def step_block(rows, columns):
    return pl.BlockSpec((rows, columns), lambda i, *_: (i, 0))


def half_blocks(groups, rows, columns):
    half = groups // 2
    shape = (pl.Squeezed(), rows, columns)
    return [
        pl.BlockSpec(shape, lambda i, *_: (jnp.minimum(i, half - 1), 0, 0)),
        pl.BlockSpec(shape, lambda i, *_: (jnp.maximum(i - half, 0), 0, 0)),
    ]


def store_half(send, keep, value, step, groups):
    @pl.when(step < groups // 2)
    def _():
        send[...] = value

    @pl.when(step >= groups // 2)
    def _():
        keep[...] = value


class Tokens:
    def __init__(self, pieces, order):
        self.groups, (self.rows, self.model) = len(pieces), pieces[0].shape
        self.arrays = [pieces[j] for j in order]
        self.specs = [pl.BlockSpec(memory_space=pl.ANY)] * self.groups

    def scratch(self):
        return [
            pltpu.VMEM((2, self.rows, self.model), bf16),
            pltpu.SemaphoreType.DMA((2,)),
        ]

    def fetch(self, refs, held, done, step):
        def copy(at):
            return pltpu.make_async_copy(refs[at], held.at[at % 2], done.at[at % 2])

        for at in range(self.groups):

            @pl.when(step == at)
            def _(at=at):
                if at == 0:
                    copy(0).start()
                if at + 1 < self.groups:
                    copy(at + 1).start()
                copy(at).wait()


def store_halves(send, keep, total, number, order, columns=slice(None), source=slice(None)):
    half, rows = send.shape[0], send.shape[1]
    for at, j in enumerate(order):
        where = send if at < half else keep
        block = total[pl.ds(pl.multiple_of((number ^ j) * rows, rows), rows), source]
        where[at % half, :, columns] = block.astype(bf16)


def call(kernel, name, grid, prefetch, operands, specs, outs, out_specs, scratch, flops, extra=0):
    size = sum(x.size * x.dtype.itemsize for x in list(operands) + list(outs))
    return pl.pallas_call(
        kernel,
        grid_spec=pltpu.PrefetchScalarGridSpec(
            num_scalar_prefetch=len(prefetch),
            grid=grid,
            in_specs=specs,
            out_specs=out_specs,
            scratch_shapes=scratch,
        ),
        out_shape=outs,
        compiler_params=pltpu.CompilerParams(
            dimension_semantics=("arbitrary",) * len(grid), vmem_limit_bytes=VMEM_MOST
        ),
        cost_estimate=pl.CostEstimate(
            flops=int(flops), bytes_accessed=int(size), transcendentals=int(extra)
        ),
        name=name,
    )(*prefetch, *operands)


def shaped(*shape, dtype=bf16):
    return jax.ShapeDtypeStruct(shape, dtype)


def shift_gain(block, gain, shift):
    return (block.astype(f32) * gain[...] + shift[...]).astype(bf16)


def turn(block, cosine, low_sine, high_sine, sign):
    width = block.shape[1]
    step = min(width, 128)
    done = []
    for start in range(0, width, step):
        part = block[:, start : start + step]
        if step == 128:
            left = pltpu.roll(part, step - ROT // 2, 1)
            right = pltpu.roll(part, ROT // 2, 1)
        else:
            left = jnp.concatenate([part[:, ROT // 2 :], part[:, : ROT // 2]], axis=1)
            right = jnp.concatenate([part[:, -ROT // 2 :], part[:, : -ROT // 2]], axis=1)
        moved = left * low_sine[:, :step] + right * high_sine[:, :step]
        done.append(part * cosine[:, :step] + moved * sign)
    return done[0] if len(done) == 1 else jnp.concatenate(done, axis=1)


def weight_scratch(pack):
    model = pack.rows * pack.pieces()
    columns = pack.arrays[0].shape[1]
    return [pltpu.VMEM((model, columns), bf16), pltpu.SemaphoreType.DMA((pack.pieces(),))]


def project_qkv(ids, info, sent, gain, shift, pack, bias, tables, width):
    groups, held, rows, model = sent.groups, len(sent.arrays), sent.rows, sent.model

    def kernel(ids, info, *refs):
        sent_refs, refs = refs[:held], refs[held:]
        weight_refs, refs = refs[: len(pack.arrays)], refs[len(pack.arrays) :]
        gain, shift, bias, cos, low, high, q_out, k_out, v_out = refs[:9]
        block, arrived, whole, placed = refs[9:]
        step = pl.program_id(0)

        @pl.when(step == 0)
        def _():
            for copy in pack.copies(weight_refs, whole, ids[1], placed):
                copy.start()

        sent.fetch(sent_refs, block, arrived, step)

        @pl.when(step == 0)
        def _():
            for copy in pack.copies(weight_refs, whole, ids[1], placed):
                copy.wait()

        token = block[step % 2]
        qkv = dot_nn(shift_gain(token, gain, shift), whole[...]) + bias[...]
        first = (ids[0] ^ ids[2 + step]) * (rows // SEG)
        for at in range(rows // SEG):
            number = first + at
            table = pl.ds(pl.multiple_of(info[number // NB, number % NB, 4] * SEG, SEG), SEG)
            tabs = (cos[table, :], low[table, :], high[table, :])
            own = slice(at * SEG, (at + 1) * SEG)
            q_out[own, :] = (turn(qkv[own, :width], *tabs, 1.0) * HD**-0.5).astype(bf16)
            k_out[own, :] = turn(qkv[own, width : 2 * width], *tabs, 1.0).astype(bf16)
        v_out[...] = qkv[:, 2 * width :].astype(bf16)

    operands = [*sent.arrays, *pack.arrays, gain, shift, bias, *tables]
    out = shaped(groups * rows, width)
    return call(
        kernel,
        "project_qkv",
        (groups,),
        [ids, info],
        operands,
        sent.specs
        + pack.specs()
        + [resident(x.shape) for x in operands[held + len(pack.arrays) :]],
        [out] * 3,
        [own_block(rows, width)] * 3,
        sent.scratch() + weight_scratch(pack),
        2 * groups * rows * model * 3 * width,
    )


def project_grad(ids, grad, pack, width):
    groups, held, rows, model = grad.groups, len(grad.arrays), grad.rows, grad.model

    def kernel(ids, *refs):
        grad_refs, refs = refs[:held], refs[held:]
        weight_refs, (out, block, arrived, whole, placed) = refs[:-5], refs[-5:]
        step = pl.program_id(0)

        @pl.when(step == 0)
        def _():
            for copy in pack.copies(weight_refs, whole, ids[1], placed):
                copy.start()

        grad.fetch(grad_refs, block, arrived, step)

        @pl.when(step == 0)
        def _():
            for copy in pack.copies(weight_refs, whole, ids[1], placed):
                copy.wait()

        out[...] = dot_nn(block[step % 2], whole[...]).astype(bf16)

    operands = [*grad.arrays, *pack.arrays]
    return call(
        kernel,
        "project_grad",
        (groups,),
        [ids],
        operands,
        grad.specs + pack.specs(),
        [shaped(groups * rows, width)],
        [own_block(rows, width)],
        grad.scratch() + weight_scratch(pack),
        2 * groups * rows * model * width,
    )[0]


def attention_kernel(
    info, q_ref, do_ref, k_ref, v_ref, cos, low, high, ctx_ref, dq_ref, dk_ref, dv_ref, dk_sum, dv_sum
):
    tree, step = pl.program_id(0), pl.program_id(1)
    width = q_ref.shape[1]
    heads = width // HD
    lane_head = lax.broadcasted_iota(jnp.int32, (SEG, width), 1) // HD

    @pl.when(step == 0)
    def _():
        dk_sum[...] = jnp.zeros_like(dk_sum)
        dv_sum[...] = jnp.zeros_like(dv_sum)

    first, second = info[tree, step, 0], info[tree, step, 1]
    first_rows = pl.ds(pl.multiple_of(first * SEG, SEG), SEG)
    second_rows = pl.ds(pl.multiple_of(second * SEG, SEG), SEG)
    queries, grads = q_ref[...], do_ref[...]
    zero = jnp.zeros_like(queries)
    q_rows = jnp.concatenate([jnp.where(lane_head == h, queries, zero) for h in range(heads)], axis=0)
    g_rows = jnp.concatenate([jnp.where(lane_head == h, grads, zero) for h in range(heads)], axis=0)
    q_turned, g_turned = queries.T, grads.T
    ahead = lax.broadcasted_iota(jnp.int32, (SEG, SEG), 1) - lax.broadcasted_iota(
        jnp.int32, (SEG, SEG), 0
    )
    seen = jnp.concatenate([ahead <= info[tree, step, 2], ahead <= info[tree, step, 3]], axis=1)
    seen = jnp.concatenate([seen] * heads, axis=0)
    k_near = jnp.concatenate([k_ref[first_rows, :], k_ref[second_rows, :]], axis=0)
    v_near = jnp.concatenate([v_ref[first_rows, :], v_ref[second_rows, :]], axis=0)

    def work(pairs):
        count = pairs * 2 * SEG
        near = jnp.where(seen, dot_nt(q_rows, k_near), masked_score)
        most = jnp.max(near, axis=1, keepdims=True)
        if count:
            k_far, v_far = k_ref[0:count, :], v_ref[0:count, :]
            far = dot_nt(q_rows, k_far)
            most = jnp.maximum(most, jnp.max(far, axis=1, keepdims=True))
        near = jnp.exp(near - most)
        total = jnp.sum(near, axis=1, keepdims=True)
        if count:
            far = jnp.exp(far - most)
            total = total + jnp.sum(far, axis=1, keepdims=True)
        scale = 1.0 / total
        near = near * scale
        near_low = near.astype(bf16)
        context = dot_nn(near_low, v_near)
        if count:
            far = far * scale
            far_low = far.astype(bf16)
            context = context + dot_nn(far_low, v_far)
        delta = jnp.sum(context * g_rows.astype(f32), axis=1, keepdims=True)
        near = (near * (dot_nt(g_rows, v_near) - delta)).astype(bf16)
        dq = dot_nn(near, k_near)
        if count:
            far = (far * (dot_nt(g_rows, v_far) - delta)).astype(bf16)
            dq = dq + dot_nn(far, k_far)
        ctx_own, dq_own = context[0:SEG], dq[0:SEG]
        for h in range(1, heads):
            ctx_own = jnp.where(lane_head == h, context[h * SEG : (h + 1) * SEG], ctx_own)
            dq_own = jnp.where(lane_head == h, dq[h * SEG : (h + 1) * SEG], dq_own)
        ctx_ref[...] = ctx_own.astype(bf16)
        dq_ref[...] = turn(dq_own * HD**-0.5, cos, low, high, -1.0).astype(bf16)
        for h in range(heads):
            own = slice(h * SEG, (h + 1) * SEG)
            part = slice(h * HD, (h + 1) * HD)
            dk = dot_nn(q_turned[part], near[own])
            dv = dot_nn(g_turned[part], near_low[own])
            dk_sum[first, part, :] += dk[:, :SEG]
            dv_sum[first, part, :] += dv[:, :SEG]
            dk_sum[second, part, :] += dk[:, SEG:]
            dv_sum[second, part, :] += dv[:, SEG:]
            if count:
                dk = dot_nn(q_turned[part], far[own])
                dv = dot_nn(g_turned[part], far_low[own])
                for j in range(2 * pairs):
                    dk_sum[j, part, :] += dk[:, j * SEG : (j + 1) * SEG]
                    dv_sum[j, part, :] += dv[:, j * SEG : (j + 1) * SEG]

    for pairs in range(NT // 2):

        @pl.when(step // 2 == pairs)
        def _(pairs=pairs):
            work(pairs)

    @pl.when(step >= NT)
    def _():
        work(NT // 2)

    @pl.when(step == NB - 1)
    def _():
        def finish(j, carry):
            rows = pl.ds(pl.multiple_of(j * SEG, SEG), SEG)
            dv_ref[rows, :] = dv_sum[j].T.astype(bf16)
            dk_ref[rows, :] = dk_sum[j].T.astype(bf16)
            return carry

        lax.fori_loop(0, NB, finish, 0)


def attention(info, tables, queries, keys, values, grads):
    total, width = queries.shape
    trees = total // TREE
    table_width = tables[0].shape[1]
    block = pl.BlockSpec((SEG, width), lambda t, b, info: (t * NB + b, 0))
    whole = pl.BlockSpec((TREE, width), lambda t, b, info: (t, 0))
    table = pl.BlockSpec((SEG, table_width), lambda t, b, info: (info[t, b, 4], 0))
    scores = trees * (TREE - TRUNK) * (TRUNK + 2 * SEG) * (width // HD)
    return call(
        attention_kernel,
        "attention",
        (trees, NB),
        [info],
        [queries, grads, keys, values, *tables],
        [block, block, whole, whole, table, table, table],
        [shaped(total, width)] * 4,
        [block, block, whole, whole],
        [pltpu.VMEM((NB, width, SEG), f32), pltpu.VMEM((NB, width, SEG), f32)],
        scores * width * 2 * 6 * 1.3,
        scores,
    )


def project_context(ids, context, pack, groups, model):
    rows, width = context.shape[0] // groups, context.shape[1]

    def kernel(ids, ctx, *refs):
        weight_refs, (send, keep, whole, placed) = refs[:-4], refs[-4:]
        step = pl.program_id(0)

        @pl.when(step == 0)
        def _():
            copies = pack.copies(weight_refs, whole, ids[1], placed)
            for copy in copies:
                copy.start()
            for copy in copies:
                copy.wait()

        store_half(send, keep, dot_nt(ctx[...], whole[...]).astype(bf16), step, groups)

    operands = [context, *pack.arrays]
    half = shaped(groups // 2, rows, model)
    return call(
        kernel,
        "project_context",
        (groups,),
        [ids],
        operands,
        [own_block(rows, width)] + pack.specs(),
        [half] * 2,
        half_blocks(groups, rows, model),
        weight_scratch(pack),
        2 * groups * rows * model * width,
    )


def attention_weights(ids, info, tables, context, dq, dk, dv, sent, grad, gain, shift, orders):
    groups, held, rows, model = sent.groups, len(sent.arrays), sent.rows, sent.model
    width, count = dq.shape[1], len(orders[0])

    def kernel(ids, info, ctx_ref, dq_ref, dk_ref, dv_ref, *refs):
        sent_refs, refs = refs[:held], refs[held:]
        grad_refs, refs = refs[:held], refs[held:]
        gain, shift, cos, low, high, grads, bias_ref, *stacks = refs[:11]
        block, arrived, grad_block, grad_arrived, total, dense_total = refs[11:]
        step = pl.program_id(0)

        @pl.when(step == 0)
        def _():
            total[...] = jnp.zeros_like(total)
            dense_total[...] = jnp.zeros_like(dense_total)
            bias_ref[...] = jnp.zeros_like(bias_ref)

        sent.fetch(sent_refs, block, arrived, step)
        grad.fetch(grad_refs, grad_block, grad_arrived, step)
        grads[:, :width] = dq_ref[...]
        first = (ids[0] ^ ids[2 + step]) * (rows // SEG)
        for at in range(rows // SEG):
            number = first + at
            table = pl.ds(pl.multiple_of(info[number // NB, number % NB, 4] * SEG, SEG), SEG)
            own = slice(at * SEG, (at + 1) * SEG)
            turned = turn(dk_ref[own, :], cos[table, :], low[table, :], high[table, :], -1.0)
            grads[own, width : 2 * width] = turned.astype(bf16)
        grads[:, 2 * width :] = dv_ref[...]
        bias_ref[0:1, :] += jnp.sum(grads[...].astype(f32), axis=0, keepdims=True)
        total[...] += dot_tn(shift_gain(block[step % 2], gain, shift), grads[...])
        dense_total[...] += dot_tn(grad_block[step % 2], ctx_ref[...])

        @pl.when(step == groups - 1)
        def _():
            store_halves(*stacks[:2], total, ids[1], orders[0], source=slice(0, 2 * width))
            source = slice(2 * width, 3 * width)
            store_halves(*stacks[2:], total, ids[1], orders[1], slice(0, width), source)
            columns = slice(width, 2 * width)
            store_halves(*stacks[2:], dense_total, ids[1], orders[1], columns)

    operands = [context, dq, dk, dv, *sent.arrays, *grad.arrays, gain, shift, *tables]
    outs = [shaped(groups * rows, 3 * width), shaped(8, 3 * width, dtype=f32)]
    outs += [shaped(count // 2, model // count, 2 * width)] * 4
    return call(
        kernel,
        "attention_weights",
        (groups,),
        [ids, info],
        operands,
        [own_block(rows, width)] * 4
        + sent.specs
        + grad.specs
        + [resident(x.shape) for x in operands[-5:]],
        outs,
        [step_block(rows, 3 * width)] + [resident(x.shape) for x in outs[1:]],
        sent.scratch()
        + grad.scratch()
        + [pltpu.VMEM((model, 3 * width), f32), pltpu.VMEM((model, width), f32)],
        2 * groups * rows * model * 4 * width,
    )


def mlp(ids, sent, grad, gain, shift, fc, bias, out, orders):
    groups, held, rows, model = sent.groups, len(sent.arrays), sent.rows, sent.model
    pieces, units = len(fc.arrays), fc.arrays[0].shape[1]

    def kernel(ids, *refs):
        sent_refs, refs = refs[:held], refs[held:]
        grad_refs, refs = refs[:held], refs[held:]
        fc_refs, refs = refs[:pieces], refs[pieces:]
        out_refs, refs = refs[:pieces], refs[pieces:]
        gain, shift, bias, part_send, part_keep, hidden_ref, bias_ref = refs[:7]
        stacks, refs = refs[7:11], refs[11:]
        block, arrived, grad_block, grad_arrived, fc_whole, fc_placed, out_whole, out_placed = refs[:8]
        act_ref, fc_total, out_total = refs[8:]
        step = pl.program_id(0)

        def weights():
            copies = fc.copies(fc_refs, fc_whole, ids[1], fc_placed)
            return copies + out.copies(out_refs, out_whole, ids[1], out_placed)

        @pl.when(step == 0)
        def _():
            for copy in weights():
                copy.start()
            fc_total[...] = jnp.zeros_like(fc_total)
            out_total[...] = jnp.zeros_like(out_total)
            bias_ref[...] = jnp.zeros_like(bias_ref)

        sent.fetch(sent_refs, block, arrived, step)
        grad.fetch(grad_refs, grad_block, grad_arrived, step)

        @pl.when(step == 0)
        def _():
            for copy in weights():
                copy.wait()

        token, grads = block[step % 2], grad_block[step % 2]
        normed = shift_gain(token, gain, shift)
        count = 2
        parts = [slice(k * rows // count, (k + 1) * rows // count) for k in range(count)]
        hidden = [dot_nn(normed[x], fc_whole[...]) + bias[...] for x in parts]
        back = [dot_nn(grads[x], out_whole[...]) for x in parts]
        for x, field, slope in zip(parts, hidden, back):
            chance = 0.5 + 0.5 * lax.erf(field * 0.7071067811865476)
            bell = jnp.exp(field * field * -0.5) * 0.3989422804014327
            act_ref[x, :] = (field * chance).astype(bf16)
            low = (slope * (chance + field * bell)).astype(bf16)
            hidden_ref[x, :] = low
            bias_ref[0:1, :] += jnp.sum(low.astype(f32), axis=0, keepdims=True)
        store_half(
            part_send, part_keep, dot_nt(act_ref[...], out_whole[...]).astype(bf16), step, groups
        )
        out_total[...] += dot_tn(grads, act_ref[...])
        fc_total[...] += dot_tn(normed, hidden_ref[...])

        @pl.when(step == groups - 1)
        def _():
            half = units // 2
            for at, order in enumerate(orders):
                stack = stacks[2 * at : 2 * at + 2]
                source = slice(at * half, (at + 1) * half)
                store_halves(*stack, fc_total, ids[1], order, slice(0, half), source)
                store_halves(*stack, out_total, ids[1], order, slice(half, units), source)

    operands = [*sent.arrays, *grad.arrays, *fc.arrays, *out.arrays, gain, shift, bias]
    count = model // fc.rows
    outs = [
        shaped(groups // 2, rows, model),
        shaped(groups // 2, rows, model),
        shaped(groups * rows, units),
        shaped(8, units, dtype=f32),
    ]
    outs += [shaped(count // 2, fc.rows, units)] * 4
    return call(
        kernel,
        "mlp",
        (groups,),
        [ids],
        operands,
        sent.specs
        + grad.specs
        + fc.specs()
        + out.specs()
        + [resident(x.shape) for x in operands[-3:]],
        outs,
        half_blocks(groups, rows, model)
        + [step_block(rows, units)]
        + [resident(x.shape) for x in outs[3:]],
        sent.scratch()
        + grad.scratch()
        + weight_scratch(fc)
        + weight_scratch(out)
        + [
            pltpu.VMEM((rows, units), bf16),
            pltpu.VMEM((model, units), f32),
            pltpu.VMEM((model, units), f32),
        ],
        10 * groups * rows * model * units,
    )


def norm_backward(ids, sent, grads, hidden, gain_attn, gain_mlp, qkv_pack, fc):
    groups, held, rows, model = sent.groups, len(sent.arrays), sent.rows, sent.model
    pieces, units, columns = len(fc.arrays), hidden.shape[1], grads.shape[1]

    def kernel(ids, grads_ref, hidden_ref, *refs):
        sent_refs, refs = refs[:held], refs[held:]
        qkv_refs, refs = refs[:pieces], refs[pieces:]
        fc_refs, refs = refs[:pieces], refs[pieces:]
        gain_attn, gain_mlp, send, keep, sums_ref = refs[:5]
        block, arrived, qkv_whole, qkv_placed, fc_whole, fc_placed = refs[5:]
        step = pl.program_id(0)

        def weights():
            copies = qkv_pack.copies(qkv_refs, qkv_whole, ids[1], qkv_placed)
            return copies + fc.copies(fc_refs, fc_whole, ids[1], fc_placed)

        @pl.when(step == 0)
        def _():
            for copy in weights():
                copy.start()
            sums_ref[...] = jnp.zeros_like(sums_ref)

        sent.fetch(sent_refs, block, arrived, step)

        @pl.when(step == 0)
        def _():
            for copy in weights():
                copy.wait()

        back_attn = dot_nt(grads_ref[...], qkv_whole[...])
        back_mlp = dot_nt(hidden_ref[...], fc_whole[...])
        token = block[step % 2].astype(f32)
        for at, back in enumerate((back_attn, back_mlp)):
            sums_ref[2 * at : 2 * at + 1, :] += jnp.sum(back * token, axis=0, keepdims=True)
            sums_ref[2 * at + 1 : 2 * at + 2, :] += jnp.sum(back, axis=0, keepdims=True)
        part = back_attn * gain_attn[...] + back_mlp * gain_mlp[...]
        store_half(send, keep, part.astype(bf16), step, groups)

    operands = [grads, hidden, *sent.arrays, *qkv_pack.arrays, *fc.arrays, gain_attn, gain_mlp]
    outs = [
        shaped(groups // 2, rows, model),
        shaped(groups // 2, rows, model),
        shaped(8, model, dtype=f32),
    ]
    return call(
        kernel,
        "norm_backward",
        (groups,),
        [ids],
        operands,
        [step_block(rows, columns), step_block(rows, units)]
        + sent.specs
        + qkv_pack.specs()
        + fc.specs()
        + [resident(x.shape) for x in operands[-2:]],
        outs,
        half_blocks(groups, rows, model) + [resident(x.shape) for x in outs[2:]],
        sent.scratch() + weight_scratch(qkv_pack) + weight_scratch(fc),
        2 * groups * rows * model * (units + columns),
    )


def taken(terms, block):
    return [
        pl.BlockSpec((pl.Squeezed(), block, x.shape[2]), lambda i, *_, at=at: (at, i, 0))
        for x, at in terms
    ]


def add_terms(terms, half, start=0, rows=None):
    columns = terms[0][0].shape[2]
    rows = terms[0][0].shape[1] if rows is None else rows
    block = max(x for x in (320, 160, 128, 64) if rows % x == 0 and start % x == 0)
    skip = start // block

    def kernel(*refs):
        refs[-1][...] = sum(x[...].astype(f32) for x in refs[:-1]).astype(bf16)

    shape = (pl.Squeezed(), block, columns)
    out = shaped(half, rows, columns)
    return call(
        kernel,
        "add_terms",
        (half, rows // block),
        [],
        [x for x, _ in terms],
        [pl.BlockSpec(shape, lambda k, i, *_, at=at: (at + k, i + skip, 0)) for _, at in terms],
        [out],
        [pl.BlockSpec(shape, lambda k, i, *_: (k, i, 0))],
        [],
        half * rows * columns * len(terms),
    )[0]


def finish_output(stream, attn_terms, mlp_terms, dense_bias, out_bias):
    rows, model = stream.shape
    block = 128
    first, second = len(attn_terms), len(mlp_terms)

    def kernel(stream_ref, *refs):
        attn_refs, refs = refs[:first], refs[first:]
        mlp_refs, (dense_bias, out_bias, out_ref, sums_ref) = refs[:second], refs[second:]

        @pl.when(pl.program_id(0) == 0)
        def _():
            sums_ref[...] = jnp.zeros_like(sums_ref)

        attn = sum(x[...].astype(f32) for x in attn_refs) + dense_bias[...]
        mlp = sum(x[...].astype(f32) for x in mlp_refs) + out_bias[...]
        output = stream_ref[...] + attn + mlp
        out_ref[...] = output
        for at, value in enumerate((output, attn, mlp)):
            sums_ref[at : at + 1, :] += jnp.sum(value * value, axis=0, keepdims=True)

    terms = [*attn_terms, *mlp_terms]
    operands = [stream, *[x for x, _ in terms], dense_bias, out_bias]
    outs = [shaped(rows, model, dtype=f32), shaped(8, model, dtype=f32)]
    return call(
        kernel,
        "finish_output",
        (rows // block,),
        [],
        operands,
        [step_block(block, model)]
        + taken(terms, block)
        + [resident(dense_bias.shape), resident(out_bias.shape)],
        outs,
        [step_block(block, model), resident(outs[1].shape)],
        [],
        rows * model * 16,
    )


def finish_grad(grad, normalized, inv_std, terms, first, rest):
    rows, model = grad.shape
    block = first.shape[1]

    def kernel(grad_ref, norm_ref, std_ref, *refs):
        term_refs, (first_ref, rest_ref, out_ref) = refs[:-3], refs[-3:]
        last = jnp.where(pl.program_id(0) == 0, first_ref[...].astype(f32), rest_ref[...].astype(f32))
        sent = sum(x[...].astype(f32) for x in term_refs) + last
        norm = norm_ref[...]
        mean = jnp.sum(sent, axis=1, keepdims=True) / model
        cross = jnp.sum(sent * norm, axis=1, keepdims=True) / model
        out_ref[...] = grad_ref[...].astype(f32) + std_ref[...] * (sent - mean - norm * cross)

    operands = [grad, normalized, inv_std, *[x for x, _ in terms], first, rest]
    piece = (pl.Squeezed(), block, model)
    return call(
        kernel,
        "finish_grad",
        (rows // block,),
        [],
        operands,
        [step_block(block, model), step_block(block, model), step_block(block, 1)]
        + taken(terms, block)
        + [
            pl.BlockSpec(piece, lambda i, *_: (0, 0, 0)),
            pl.BlockSpec(piece, lambda i, *_: (0, jnp.maximum(i - 1, 0), 0)),
        ],
        [shaped(rows, model, dtype=f32)],
        [step_block(block, model)],
        [],
        rows * model * 12,
    )[0]


def tree_table(segment_ids, parent_ids):
    trees = segment_ids.shape[0] // TREE
    segment = segment_ids.reshape(trees, NB, SEG)[:, :, 0]
    parent = parent_ids.reshape(trees, NB, SEG)[:, :, 0]
    block = lax.broadcasted_iota(jnp.int32, (trees, NB), 1)
    trunk = block < NT
    leaf = (parent != segment[:, :1]) & ~trunk
    at = lax.broadcasted_iota(jnp.int32, (trees, NB, NB), 2)
    owner = jnp.sum(jnp.where(segment[:, None, :] == parent[:, :, None], at, 0), axis=2)
    odd = block % 2 == 1
    first = jnp.where(trunk, block // 2 * 2, block)
    second = jnp.where(trunk, block // 2 * 2 + 1, jnp.where(leaf, owner, block))
    first_most = jnp.where(trunk & odd, SEG, 0)
    second_most = jnp.where(trunk, jnp.where(odd, 0, -SEG), jnp.where(leaf, SEG, -SEG))
    table = jnp.where(trunk, block, jnp.where(leaf, NT + 1, NT))
    return jnp.stack([first, second, first_most, second_most, table], axis=2).astype(jnp.int32)


def angle_tables():
    places = TRUNK + 2 * SEG
    place = lax.broadcasted_iota(jnp.int32, (places, 2 * HD), 0).astype(f32)
    lane = lax.broadcasted_iota(jnp.int32, (places, 2 * HD), 1) % HD
    half = ROT // 2
    frequency = 10000.0 ** (-((lane % half).astype(f32) * 2.0 / ROT))
    angle = place * frequency
    cosine = jnp.where(lane < ROT, jnp.cos(angle), 1.0)
    sine = jnp.sin(angle)
    low = jnp.where(lane < half, -sine, 0.0)
    high = jnp.where((lane >= half) & (lane < ROT), sine, 0.0)
    return cosine, low, high


def by_kind(array, heads):
    shape = array.shape[:-1]
    array = array.reshape(*shape, heads, 3, HD)
    return jnp.swapaxes(array, -3, -2).reshape(*shape, 3 * heads * HD)


def by_head(array, heads):
    shape = array.shape[:-1]
    array = array.reshape(*shape, 3, heads, HD)
    return jnp.swapaxes(array, -3, -2).reshape(*shape, 3 * heads * HD)


def local(
    stream_in,
    segment_ids,
    parent_ids,
    norm_gain_attn,
    norm_shift_attn,
    norm_gain_mlp,
    norm_shift_mlp,
    qkv_weight,
    qkv_bias,
    dense_weight,
    dense_bias,
    fc_weight,
    fc_bias,
    out_weight,
    out_bias,
    out_grad,
):
    tensor_rank = lax.axis_index("tensor")
    data_rank = lax.axis_index("dp")
    rows_local = stream_in.shape[0]
    model = stream_in.shape[1]
    qkv_width = qkv_weight.shape[1]
    heads = qkv_width // (3 * HD)
    width = heads * HD
    units = fc_weight.shape[1]
    groups = lax.axis_size("tensor")
    tensor_bits = bits_of(groups)
    far_first = tensor_bits[:0:-1] + tensor_bits[:1]
    order = halving_order(tensor_bits)
    ids = jnp.stack([tensor_rank, data_rank, *order]).astype(jnp.int32)
    data_bits = bits_of(lax.axis_size("dp"))
    rows_first = data_bits[:0:-1] + data_bits[:1]
    columns_first = data_bits[:1] + data_bits[:0:-1]
    between = data_bits[:1:-1] + data_bits[:2]
    near_bits = data_bits
    next_bits = data_bits[1:2] + data_bits[:1] + data_bits[2:]

    qkv_pack = Pack(by_kind(qkv_weight.astype(bf16), heads), "dp", rows_first)
    dense_pack = Pack(dense_weight.astype(bf16).T, "dp", columns_first)
    fc_pack = Pack(fc_weight.astype(bf16), "dp", rows_first)
    out_pack = Pack(out_weight.astype(bf16).T, "dp", between)

    row_mean = jnp.mean(stream_in, axis=-1, keepdims=True)
    centred = stream_in - row_mean
    row_var = jnp.mean(centred * centred, axis=-1, keepdims=True)
    inv_std = lax.rsqrt(row_var + eps_norm)
    normalized = centred * inv_std
    sent = gather_far(normalized.astype(bf16), "tensor", tensor_bits)

    qkv_pack.double()
    dense_pack.double()
    tie_packs(qkv_pack, dense_pack, fc_pack, out_pack)
    fc_pack.double()
    out_pack.double()
    while len(qkv_pack.bits) > 1:
        qkv_pack.double()
        dense_pack.double()
    out_grad, *sent = tie_packs(qkv_pack, dense_pack, beside=[out_grad, *sent])
    grad = gather_far(out_grad, "tensor", tensor_bits)
    sent = gather_near(sent, "tensor")
    qkv_pack.double()
    dense_pack.double()
    sent = tie_packs(qkv_pack, dense_pack, fc_pack, out_pack, beside=sent)
    sent = Tokens(sent, order)

    info = tree_table(segment_ids, parent_ids)
    tables = angle_tables()
    gain_attn, shift_attn = norm_gain_attn[None, :], norm_shift_attn[None, :]
    gain_mlp, shift_mlp = norm_gain_mlp[None, :], norm_shift_mlp[None, :]
    qkv_bias_own = by_kind(
        lax.dynamic_slice_in_dim(qkv_bias, tensor_rank * qkv_width, qkv_width), heads
    )[None, :]
    fc_bias_own = lax.dynamic_slice_in_dim(fc_bias, tensor_rank * units, units)[None, :]

    while len(fc_pack.bits) > 1:
        fc_pack.double()
        out_pack.double()
    done = project_qkv(
        ids, info, sent, gain_attn, shift_attn, qkv_pack, qkv_bias_own, tables, width
    )
    queries, keys, values, *grad = tie_packs(fc_pack, out_pack, beside=[*done, *grad])
    grad = Tokens(gather_near(grad, "tensor"), order)
    grad_context = project_grad(ids, grad, dense_pack, width)
    fc_pack.double()
    out_pack.double()
    done = attention(info, tables, queries, keys, values, grad_context)
    context, dq, dk, dv = tie_packs(fc_pack, out_pack, beside=done)
    dp_orders = [halving_order(near_bits), halving_order(next_bits)]
    attn_parts = Halving(
        *project_context(ids, context, dense_pack, groups, model), "tensor", tensor_bits
    )
    while len(attn_parts.bits) > 2:
        attn_parts.swap()
        attn_parts.add()
    attn_parts.send, context = tie(attn_parts.send, context)
    attn_parts.swap()
    done = attention_weights(
        ids, info, tables, context, dq, dk, dv, sent, grad, gain_attn, shift_attn, dp_orders
    )
    grads, qkv_bias_sums, *stacks = tie_halves(done, attn_parts)
    attn_parts.add()
    qkv_sums = [Halving(*stacks[:2], "dp", near_bits), Halving(*stacks[2:], "dp", next_bits)]
    sent.arrays[0], attn_parts.send = tie(sent.arrays[0], attn_parts.send)
    attn_parts.swap()
    for parts in qkv_sums:
        parts.swap()
    done = mlp(
        ids, sent, grad, gain_mlp, shift_mlp, fc_pack, fc_bias_own, out_pack, dp_orders
    )
    done = tie_halves(done, attn_parts, *qkv_sums)
    mlp_send, mlp_keep, hidden, fc_bias_sums, *stacks = done
    attn_parts.add()
    mlp_parts = Halving(mlp_send, mlp_keep, "tensor", tensor_bits)
    mlp_sums = [Halving(*stacks[:2], "dp", near_bits), Halving(*stacks[2:], "dp", next_bits)]
    while len(mlp_parts.bits) > 2:
        mlp_parts.swap()
        mlp_parts.add()
    mlp_parts.swap()
    for parts in qkv_sums:
        parts.add()
    mlp_parts.got, *sends = tie(mlp_parts.got, *[parts.send for parts in qkv_sums])
    for parts, send in zip(qkv_sums, sends):
        parts.send = send
    mlp_parts.add()
    hidden, mlp_parts.send = tie(hidden, mlp_parts.send)
    mlp_parts.swap()
    for parts in qkv_sums + mlp_sums:
        parts.swap()
    done = norm_backward(ids, sent, grads, hidden, gain_attn, gain_mlp, qkv_pack, fc_pack)
    done = tie_halves(done, mlp_parts, *qkv_sums, *mlp_sums)
    back_send, back_keep, norm_sums = done
    mlp_parts.add()

    back_parts = Halving(back_send, back_keep, "tensor", tensor_bits)
    while len(back_parts.bits) > 2:
        back_parts.swap()
        back_parts.add()
    back_parts.swap()
    for parts in qkv_sums + mlp_sums:
        parts.add()
    back_parts.got, *sends = tie(back_parts.got, *[parts.send for parts in qkv_sums + mlp_sums])
    for parts, send in zip(qkv_sums + mlp_sums, sends):
        parts.send = send
    back_parts.terms.append((back_parts.got, 0))
    quarter, last = rows_local // 4, back_parts.bits[-1]
    first = add_terms(back_parts.terms, 1, 0, quarter)
    rest = add_terms(back_parts.terms, 1, quarter, rows_local - quarter)
    back_parts.terms = [(x, at + 1) for x, at in back_parts.terms]
    stream_in, first, rest = tie(stream_in, first, rest)
    first, rest = swap(first, "tensor", last), swap(rest, "tensor", last)
    for parts in qkv_sums + mlp_sums:
        parts.swap()
    output, squares = finish_output(
        stream_in, attn_parts.terms, mlp_parts.terms, dense_bias[None, :], out_bias[None, :]
    )
    output, squares, first = tie(output, squares, first)
    fc_bias_spread = lax.dynamic_update_slice(
        jnp.zeros(fc_bias.shape, f32), fc_bias_sums[0], (tensor_rank * units,)
    )
    qkv_bias_spread = lax.dynamic_update_slice(
        jnp.zeros(qkv_bias.shape, f32), by_head(qkv_bias_sums[0], heads), (tensor_rank * qkv_width,)
    )
    sums = jnp.concatenate(
        [
            norm_sums[:4].reshape(-1),
            squares[:3].reshape(-1),
            jnp.sum(out_grad.astype(f32), axis=0),
            fc_bias_spread,
            qkv_bias_spread,
        ]
    )
    sums = sums + swap(sums, "tensor", 1)
    (sums,) = tie_halves([sums], *qkv_sums, *mlp_sums)
    for bit in data_bits[1:]:
        sums = sums + swap(sums, "dp", bit)
    for parts in qkv_sums + mlp_sums:
        parts.add()
    sums, *sends = tie(sums, *[parts.send for parts in mlp_sums])
    for parts, send in zip(mlp_sums, sends):
        parts.send = send
    sums = sums + swap(sums, "dp", data_bits[0])
    sums, rest = tie(sums, rest)
    for bit in tensor_bits[1:]:
        sums = sums + swap(sums, "tensor", bit)
    stream_grad = finish_grad(out_grad, normalized, inv_std, back_parts.terms, first, rest)

    first, second = [parts.finish() for parts in mlp_sums]
    half = units // 2
    fc_weight_grad = jnp.concatenate([first[:, :half], second[:, :half]], axis=1)
    out_weight_grad = jnp.concatenate([first[:, half:], second[:, half:]], axis=1).T
    first, second = [parts.finish() for parts in qkv_sums]
    dense_weight_grad = second[:, width:].T
    qkv_weight_grad = by_head(jnp.concatenate([first, second[:, :width]], axis=1), heads)

    count_all = float(rows_local * lax.axis_size("dp") * groups * model)
    gain_attn_grad, shift_attn_grad, gain_mlp_grad, shift_mlp_grad = sums[: 4 * model].reshape(
        4, model
    )
    squares = jnp.sum(sums[4 * model : 7 * model].reshape(3, model), axis=1)
    root_squares = jnp.sqrt(squares / count_all)
    residual_grad = sums[7 * model : 8 * model]
    fc_bias_grad = sums[8 * model : 8 * model + fc_bias.shape[0]]
    qkv_bias_grad = sums[8 * model + fc_bias.shape[0] :]
    return (
        output,
        stream_grad,
        gain_attn_grad,
        shift_attn_grad,
        gain_mlp_grad,
        shift_mlp_grad,
        qkv_weight_grad,
        qkv_bias_grad,
        dense_weight_grad,
        residual_grad,
        fc_weight_grad,
        fc_bias_grad,
        out_weight_grad,
        residual_grad,
        root_squares,
    )


def solution(mesh):
    tokens, weights, rows, whole = (
        P(("dp", "tensor"), None),
        P("dp", "tensor"),
        P("tensor", "dp"),
        P(),
    )
    return jax.shard_map(
        local,
        mesh=mesh,
        in_specs=(
            tokens,
            P("dp"),
            P("dp"),
            whole,
            whole,
            whole,
            whole,
            weights,
            whole,
            rows,
            whole,
            weights,
            whole,
            rows,
            whole,
            tokens,
        ),
        out_specs=(
            tokens,
            tokens,
            whole,
            whole,
            whole,
            whole,
            weights,
            whole,
            rows,
            whole,
            weights,
            whole,
            rows,
            whole,
            whole,
        ),
        check_vma=False,
    )
```

```python
import jax
import jax.numpy as jnp
from jax import lax
from jax.experimental import pallas as pl
from jax.experimental.pallas import tpu as pltpu
from jax.sharding import PartitionSpec as P

HD = 64
ROT = 16
TRUNK = 1024
SEG = 128
TREE = 2560
NB = TREE // SEG
NT = TRUNK // SEG

f32 = jnp.float32
bf16 = jnp.bfloat16
eps_norm = 1e-05
masked_score = -1e30


def dot_nn(left, right):
    return lax.dot_general(left, right, (((1,), (0,)), ((), ())), preferred_element_type=f32)


def dot_nt(left, right):
    return lax.dot_general(left, right, (((1,), (1,)), ((), ())), preferred_element_type=f32)


def dot_tn(left, right):
    return lax.dot_general(left, right, (((0,), (0,)), ((), ())), preferred_element_type=f32)


def bits_of(size):
    bits = []
    bit = 1
    while bit < size:
        bits.append(bit)
        bit *= 2
    return bits


def swap(block, axis, bit):
    size = lax.axis_size(axis)
    return lax.ppermute(block, axis, [(i, i ^ bit) for i in range(size)])


def tie(*values):
    return lax.optimization_barrier(values)


def gather_far(block, axis, bits):
    pieces = [block]
    for bit in bits[1:]:
        pieces = pieces + [swap(piece, axis, bit) for piece in pieces]
    return pieces


class Pack:
    def __init__(self, block, axis, bits):
        self.rows, self.axis, self.bits = block.shape[0], axis, list(bits)
        self.arrays, self.owners = [block], [[0]]

    def double(self):
        bit = self.bits.pop(0)
        held = self.arrays[0] if len(self.arrays) == 1 else jnp.concatenate(self.arrays, axis=0)
        self.owners.append([j ^ bit for owners in self.owners for j in owners])
        self.arrays.append(swap(held, self.axis, bit))

    def specs(self):
        return [pl.BlockSpec(memory_space=pl.ANY)] * len(self.arrays)

    def pieces(self):
        return sum(len(owners) for owners in self.owners)

    def copies(self, refs, where, number, done):
        started = []
        for ref, owners in zip(refs, self.owners):
            for at, j in enumerate(owners):
                rows = pl.ds(pl.multiple_of((number ^ j) * self.rows, self.rows), self.rows)
                source = ref.at[pl.ds(at * self.rows, self.rows), :]
                copy = pltpu.make_async_copy(source, where.at[rows, :], done.at[len(started)])
                started.append(copy)
        return started


def tie_packs(*packs, beside=()):
    flat = tie(*beside, *[x for pack in packs for x in pack.arrays])
    at = len(beside)
    for pack in packs:
        pack.arrays = list(flat[at : at + len(pack.arrays)])
        at += len(pack.arrays)
    return list(flat[: len(beside)])


def halving_order(bits):
    if not bits:
        return [0]
    rest = halving_order(bits[1:])
    return [bits[0] ^ j for j in rest] + rest


class Halving:
    def __init__(self, send, keep, axis, bits):
        self.send, self.axis, self.bits = send, axis, list(bits)
        self.terms = [(keep, 0)]

    def swap(self):
        self.got = swap(self.send, self.axis, self.bits.pop(0))

    def add(self):
        self.terms.append((self.got, 0))
        half = self.got.shape[0] // 2
        if half:
            self.send = add_terms(self.terms, half)
            self.terms = [(x, at + half) for x, at in self.terms]

    def most(self):
        while len(self.bits) > 1:
            self.swap()
            self.add()

    def finish(self):
        while self.bits:
            self.swap()
            self.add()
        return self.terms


def tie_halves(values, *halvings):
    flat = tie(*values, *[x.got for x in halvings])
    for x, got in zip(halvings, flat[len(values) :]):
        x.got = got
    return flat[: len(values)]


def resident(shape):
    zeros = (0,) * len(shape)
    return pl.BlockSpec(shape, lambda *_: zeros, pipeline_mode=pl.Buffered(1))


def own_block(rows, columns):
    return pl.BlockSpec((rows, columns), lambda i, ids, *_: (ids[0] ^ ids[2 + i], 0))


def step_block(rows, columns):
    return pl.BlockSpec((rows, columns), lambda i, *_: (i, 0))


def half_blocks(groups, rows, columns):
    half = groups // 2
    shape = (pl.Squeezed(), rows, columns)
    return [
        pl.BlockSpec(shape, lambda i, *_: (jnp.minimum(i, half - 1), 0, 0)),
        pl.BlockSpec(shape, lambda i, *_: (jnp.maximum(i - half, 0), 0, 0)),
    ]


def store_half(send, keep, value, step, groups):
    @pl.when(step < groups // 2)
    def _():
        send[...] = value

    @pl.when(step >= groups // 2)
    def _():
        keep[...] = value


class Tokens:
    def __init__(self, blocks, order):
        blocks = [blocks[j] for j in order]
        self.groups, self.counts = len(blocks), [len(block) for block in blocks]
        self.rows, self.model = sum(x.shape[0] for x in blocks[0]), blocks[0][0].shape[1]
        self.arrays = [x for block in blocks for x in block]
        self.specs = [pl.BlockSpec(memory_space=pl.ANY)] * len(self.arrays)

    def scratch(self):
        return [
            pltpu.VMEM((2, self.rows, self.model), bf16),
            pltpu.SemaphoreType.DMA((2, max(self.counts))),
        ]

    def fetch(self, refs, held, done, step):
        def copies(at):
            first, start, found = sum(self.counts[:at]), 0, []
            for k, ref in enumerate(refs[first : first + self.counts[at]]):
                where = held.at[at % 2, pl.ds(start, ref.shape[0]), :]
                found.append(pltpu.make_async_copy(ref, where, done.at[at % 2, k]))
                start += ref.shape[0]
            return found

        for at in range(self.groups):

            @pl.when(step == at)
            def _(at=at):
                ahead = copies(at) if at == 0 else []
                if at + 1 < self.groups:
                    ahead = ahead + copies(at + 1)
                for copy in ahead:
                    copy.start()
                for copy in copies(at):
                    copy.wait()


def store_halves(send, keep, total, number, order, columns=slice(None), source=slice(None)):
    half, rows = send.shape[0], send.shape[1]
    for at, j in enumerate(order):
        where = send if at < half else keep
        block = total[pl.ds(pl.multiple_of((number ^ j) * rows, rows), rows), source]
        where[at % half, :, columns] = block.astype(bf16)


def call(
    kernel, name, grid, prefetch, operands, specs, outs, out_specs, scratch, flops, extra=0, room=12
):
    size = sum(x.size * x.dtype.itemsize for x in list(operands) + list(outs))
    return pl.pallas_call(
        kernel,
        grid_spec=pltpu.PrefetchScalarGridSpec(
            num_scalar_prefetch=len(prefetch),
            grid=grid,
            in_specs=specs,
            out_specs=out_specs,
            scratch_shapes=scratch,
        ),
        out_shape=outs,
        compiler_params=pltpu.CompilerParams(
            dimension_semantics=("arbitrary",) * len(grid), vmem_limit_bytes=room << 20
        ),
        cost_estimate=pl.CostEstimate(
            flops=int(flops), bytes_accessed=int(size), transcendentals=int(extra)
        ),
        name=name,
    )(*prefetch, *operands)


def shaped(*shape, dtype=bf16):
    return jax.ShapeDtypeStruct(shape, dtype)


def shift_gain(block, gain, shift):
    return (block.astype(f32) * gain[...] + shift[...]).astype(bf16)


def turn(block, cosine, low_sine, high_sine, sign):
    width = block.shape[1]
    step = min(width, 128)
    done = []
    for start in range(0, width, step):
        part = block[:, start : start + step]
        if step == 128:
            left = pltpu.roll(part, step - ROT // 2, 1)
            right = pltpu.roll(part, ROT // 2, 1)
        else:
            left = jnp.concatenate([part[:, ROT // 2 :], part[:, : ROT // 2]], axis=1)
            right = jnp.concatenate([part[:, -ROT // 2 :], part[:, : -ROT // 2]], axis=1)
        moved = left * low_sine[:, :step] + right * high_sine[:, :step]
        done.append(part * cosine[:, :step] + moved * sign)
    return done[0] if len(done) == 1 else jnp.concatenate(done, axis=1)


def weight_scratch(pack):
    model = pack.rows * pack.pieces()
    columns = pack.arrays[0].shape[1]
    return [pltpu.VMEM((model, columns), bf16), pltpu.SemaphoreType.DMA((pack.pieces(),))]


def project_qkv(ids, info, sent, gain, shift, pack, bias, tables, width):
    groups, held, rows, model = sent.groups, len(sent.arrays), sent.rows, sent.model

    def kernel(ids, info, *refs):
        sent_refs, refs = refs[:held], refs[held:]
        weight_refs, refs = refs[: len(pack.arrays)], refs[len(pack.arrays) :]
        gain, shift, bias, cos, low, high, q_out, k_out, v_out = refs[:9]
        block, arrived, whole, placed = refs[9:]
        step = pl.program_id(0)

        @pl.when(step == 0)
        def _():
            for copy in pack.copies(weight_refs, whole, ids[1], placed):
                copy.start()

        sent.fetch(sent_refs, block, arrived, step)

        @pl.when(step == 0)
        def _():
            for copy in pack.copies(weight_refs, whole, ids[1], placed):
                copy.wait()

        token = block[step % 2]
        qkv = dot_nn(shift_gain(token, gain, shift), whole[...]) + bias[...]
        first = (ids[0] ^ ids[2 + step]) * (rows // SEG)
        for at in range(rows // SEG):
            number = first + at
            table = pl.ds(pl.multiple_of(info[number // NB, number % NB, 4] * SEG, SEG), SEG)
            tabs = (cos[table, :], low[table, :], high[table, :])
            own = slice(at * SEG, (at + 1) * SEG)
            q_out[own, :] = (turn(qkv[own, :width], *tabs, 1.0) * HD**-0.5).astype(bf16)
            k_out[own, :] = turn(qkv[own, width : 2 * width], *tabs, 1.0).astype(bf16)
        v_out[...] = qkv[:, 2 * width :].astype(bf16)

    operands = [*sent.arrays, *pack.arrays, gain, shift, bias, *tables]
    out = shaped(groups * rows, width)
    return call(
        kernel,
        "project_qkv",
        (groups,),
        [ids, info],
        operands,
        sent.specs
        + pack.specs()
        + [resident(x.shape) for x in operands[held + len(pack.arrays) :]],
        [out] * 3,
        [own_block(rows, width)] * 3,
        sent.scratch() + weight_scratch(pack),
        2 * groups * rows * model * 3 * width,
        room=14,
    )


def project_grad(ids, grad, pack, width):
    groups, held, rows, model = grad.groups, len(grad.arrays), grad.rows, grad.model

    def kernel(ids, *refs):
        grad_refs, refs = refs[:held], refs[held:]
        weight_refs, (out, block, arrived, whole, placed) = refs[:-5], refs[-5:]
        step = pl.program_id(0)

        @pl.when(step == 0)
        def _():
            for copy in pack.copies(weight_refs, whole, ids[1], placed):
                copy.start()

        grad.fetch(grad_refs, block, arrived, step)

        @pl.when(step == 0)
        def _():
            for copy in pack.copies(weight_refs, whole, ids[1], placed):
                copy.wait()

        out[...] = dot_nn(block[step % 2], whole[...]).astype(bf16)

    operands = [*grad.arrays, *pack.arrays]
    return call(
        kernel,
        "project_grad",
        (groups,),
        [ids],
        operands,
        grad.specs + pack.specs(),
        [shaped(groups * rows, width)],
        [own_block(rows, width)],
        grad.scratch() + weight_scratch(pack),
        2 * groups * rows * model * width,
    )[0]


def attention_kernel(
    info, q_ref, do_ref, k_ref, v_ref, cos, low, high, ctx_ref, dq_ref, dk_ref, dv_ref, dk_sum, dv_sum
):
    tree, step = pl.program_id(0), pl.program_id(1)
    width = q_ref.shape[1]
    heads = width // HD
    lane_head = lax.broadcasted_iota(jnp.int32, (SEG, width), 1) // HD

    @pl.when(step == 0)
    def _():
        dk_sum[...] = jnp.zeros_like(dk_sum)
        dv_sum[...] = jnp.zeros_like(dv_sum)

    first, second = info[tree, step, 0], info[tree, step, 1]
    first_rows = pl.ds(pl.multiple_of(first * SEG, SEG), SEG)
    second_rows = pl.ds(pl.multiple_of(second * SEG, SEG), SEG)
    queries, grads = q_ref[...], do_ref[...]
    zero = jnp.zeros_like(queries)
    q_rows = jnp.concatenate([jnp.where(lane_head == h, queries, zero) for h in range(heads)], axis=0)
    g_rows = jnp.concatenate([jnp.where(lane_head == h, grads, zero) for h in range(heads)], axis=0)
    q_turned, g_turned = queries.T, grads.T
    ahead = lax.broadcasted_iota(jnp.int32, (SEG, SEG), 1) - lax.broadcasted_iota(
        jnp.int32, (SEG, SEG), 0
    )
    seen = jnp.concatenate([ahead <= info[tree, step, 2], ahead <= info[tree, step, 3]], axis=1)
    seen = jnp.concatenate([seen] * heads, axis=0)
    k_near = jnp.concatenate([k_ref[first_rows, :], k_ref[second_rows, :]], axis=0)
    v_near = jnp.concatenate([v_ref[first_rows, :], v_ref[second_rows, :]], axis=0)

    def work(pairs):
        count = pairs * 2 * SEG
        near = jnp.where(seen, dot_nt(q_rows, k_near), masked_score)
        most = jnp.max(near, axis=1, keepdims=True)
        if count:
            k_far, v_far = k_ref[0:count, :], v_ref[0:count, :]
            far = dot_nt(q_rows, k_far)
            most = jnp.maximum(most, jnp.max(far, axis=1, keepdims=True))
        near = jnp.exp(near - most)
        total = jnp.sum(near, axis=1, keepdims=True)
        if count:
            far = jnp.exp(far - most)
            total = total + jnp.sum(far, axis=1, keepdims=True)
        scale = 1.0 / total
        near = near * scale
        near_low = near.astype(bf16)
        context = dot_nn(near_low, v_near)
        if count:
            far = far * scale
            far_low = far.astype(bf16)
            context = context + dot_nn(far_low, v_far)
        delta = jnp.sum(context * g_rows.astype(f32), axis=1, keepdims=True)
        near = (near * (dot_nt(g_rows, v_near) - delta)).astype(bf16)
        dq = dot_nn(near, k_near)
        if count:
            far = (far * (dot_nt(g_rows, v_far) - delta)).astype(bf16)
            dq = dq + dot_nn(far, k_far)
        ctx_own, dq_own = context[0:SEG], dq[0:SEG]
        for h in range(1, heads):
            ctx_own = jnp.where(lane_head == h, context[h * SEG : (h + 1) * SEG], ctx_own)
            dq_own = jnp.where(lane_head == h, dq[h * SEG : (h + 1) * SEG], dq_own)
        ctx_ref[...] = ctx_own.astype(bf16)
        dq_ref[...] = turn(dq_own * HD**-0.5, cos, low, high, -1.0).astype(bf16)
        for h in range(heads):
            own = slice(h * SEG, (h + 1) * SEG)
            part = slice(h * HD, (h + 1) * HD)
            dk = dot_nn(q_turned[part], near[own])
            dv = dot_nn(g_turned[part], near_low[own])
            dk_sum[first, part, :] += dk[:, :SEG]
            dv_sum[first, part, :] += dv[:, :SEG]
            dk_sum[second, part, :] += dk[:, SEG:]
            dv_sum[second, part, :] += dv[:, SEG:]
            if count:
                dk = dot_nn(q_turned[part], far[own])
                dv = dot_nn(g_turned[part], far_low[own])
                for j in range(2 * pairs):
                    dk_sum[j, part, :] += dk[:, j * SEG : (j + 1) * SEG]
                    dv_sum[j, part, :] += dv[:, j * SEG : (j + 1) * SEG]

    for pairs in range(NT // 2):

        @pl.when(step // 2 == pairs)
        def _(pairs=pairs):
            work(pairs)

    @pl.when(step >= NT)
    def _():
        work(NT // 2)

    @pl.when(step == NB - 1)
    def _():
        def finish(j, carry):
            rows = pl.ds(pl.multiple_of(j * SEG, SEG), SEG)
            dv_ref[rows, :] = dv_sum[j].T.astype(bf16)
            dk_ref[rows, :] = dk_sum[j].T.astype(bf16)
            return carry

        lax.fori_loop(0, NB, finish, 0)


def attention(info, tables, queries, keys, values, grads):
    total, width = queries.shape
    trees = total // TREE
    table_width = tables[0].shape[1]
    block = pl.BlockSpec((SEG, width), lambda t, b, info: (t * NB + b, 0))
    whole = pl.BlockSpec((TREE, width), lambda t, b, info: (t, 0))
    table = pl.BlockSpec((SEG, table_width), lambda t, b, info: (info[t, b, 4], 0))
    scores = trees * (TREE - TRUNK) * (TRUNK + 2 * SEG) * (width // HD)
    return call(
        attention_kernel,
        "attention",
        (trees, NB),
        [info],
        [queries, grads, keys, values, *tables],
        [block, block, whole, whole, table, table, table],
        [shaped(total, width)] * 4,
        [block, block, whole, whole],
        [pltpu.VMEM((NB, width, SEG), f32), pltpu.VMEM((NB, width, SEG), f32)],
        scores * width * 2 * 6 * 1.3,
        scores,
        room=22,
    )


def project_context(ids, context, pack, groups, model):
    rows, width = context.shape[0] // groups, context.shape[1]

    def kernel(ids, ctx, *refs):
        weight_refs, (send, keep, whole, placed) = refs[:-4], refs[-4:]
        step = pl.program_id(0)

        @pl.when(step == 0)
        def _():
            copies = pack.copies(weight_refs, whole, ids[1], placed)
            for copy in copies:
                copy.start()
            for copy in copies:
                copy.wait()

        store_half(send, keep, dot_nt(ctx[...], whole[...]).astype(bf16), step, groups)

    operands = [context, *pack.arrays]
    half = shaped(groups // 2, rows, model)
    return call(
        kernel,
        "project_context",
        (groups,),
        [ids],
        operands,
        [own_block(rows, width)] + pack.specs(),
        [half] * 2,
        half_blocks(groups, rows, model),
        weight_scratch(pack),
        2 * groups * rows * model * width,
    )


def attention_weights(ids, info, tables, context, dq, dk, dv, sent, grad, gain, shift, orders):
    groups, held, rows, model = sent.groups, len(sent.arrays), sent.rows, sent.model
    width, count = dq.shape[1], len(orders[0])

    def kernel(ids, info, ctx_ref, dq_ref, dk_ref, dv_ref, *refs):
        sent_refs, refs = refs[:held], refs[held:]
        grad_refs, refs = refs[: len(grad.arrays)], refs[len(grad.arrays) :]
        gain, shift, cos, low, high, grads, bias_ref, *stacks = refs[:11]
        block, arrived, grad_block, grad_arrived, total, dense_total = refs[11:]
        step = pl.program_id(0)

        @pl.when(step == 0)
        def _():
            total[...] = jnp.zeros_like(total)
            dense_total[...] = jnp.zeros_like(dense_total)
            bias_ref[...] = jnp.zeros_like(bias_ref)

        sent.fetch(sent_refs, block, arrived, step)
        grad.fetch(grad_refs, grad_block, grad_arrived, step)
        grads[:, :width] = dq_ref[...]
        first = (ids[0] ^ ids[2 + step]) * (rows // SEG)
        for at in range(rows // SEG):
            number = first + at
            table = pl.ds(pl.multiple_of(info[number // NB, number % NB, 4] * SEG, SEG), SEG)
            own = slice(at * SEG, (at + 1) * SEG)
            turned = turn(dk_ref[own, :], cos[table, :], low[table, :], high[table, :], -1.0)
            grads[own, width : 2 * width] = turned.astype(bf16)
        grads[:, 2 * width :] = dv_ref[...]
        bias_ref[0:1, :] += jnp.sum(grads[...].astype(f32), axis=0, keepdims=True)
        total[...] += dot_tn(shift_gain(block[step % 2], gain, shift), grads[...])
        dense_total[...] += dot_tn(grad_block[step % 2], ctx_ref[...])

        @pl.when(step == groups - 1)
        def _():
            store_halves(*stacks[:2], total, ids[1], orders[0], source=slice(0, 2 * width))
            source = slice(2 * width, 3 * width)
            store_halves(*stacks[2:], total, ids[1], orders[1], slice(0, width), source)
            columns = slice(width, 2 * width)
            store_halves(*stacks[2:], dense_total, ids[1], orders[1], columns)

    operands = [context, dq, dk, dv, *sent.arrays, *grad.arrays, gain, shift, *tables]
    outs = [shaped(groups * rows, 3 * width), shaped(8, 3 * width, dtype=f32)]
    outs += [shaped(count // 2, model // count, 2 * width)] * 4
    return call(
        kernel,
        "attention_weights",
        (groups,),
        [ids, info],
        operands,
        [own_block(rows, width)] * 4
        + sent.specs
        + grad.specs
        + [resident(x.shape) for x in operands[-5:]],
        outs,
        [step_block(rows, 3 * width)] + [resident(x.shape) for x in outs[1:]],
        sent.scratch()
        + grad.scratch()
        + [pltpu.VMEM((model, 3 * width), f32), pltpu.VMEM((model, width), f32)],
        2 * groups * rows * model * 4 * width,
        room=24,
    )


def mlp(ids, sent, grad, gain, shift, fc, bias, out, orders):
    groups, held, rows, model = sent.groups, len(sent.arrays), sent.rows, sent.model
    pieces, units = len(fc.arrays), fc.arrays[0].shape[1]

    def kernel(ids, *refs):
        sent_refs, refs = refs[:held], refs[held:]
        grad_refs, refs = refs[: len(grad.arrays)], refs[len(grad.arrays) :]
        fc_refs, refs = refs[:pieces], refs[pieces:]
        out_refs, refs = refs[:pieces], refs[pieces:]
        gain, shift, bias, part_send, part_keep, hidden_ref, bias_ref = refs[:7]
        stacks, refs = refs[7:11], refs[11:]
        block, arrived, grad_block, grad_arrived, fc_whole, fc_placed, out_whole, out_placed = refs[:8]
        act_ref, fc_total, out_total = refs[8:]
        step = pl.program_id(0)

        def weights():
            copies = fc.copies(fc_refs, fc_whole, ids[1], fc_placed)
            return copies + out.copies(out_refs, out_whole, ids[1], out_placed)

        @pl.when(step == 0)
        def _():
            for copy in weights():
                copy.start()
            fc_total[...] = jnp.zeros_like(fc_total)
            out_total[...] = jnp.zeros_like(out_total)
            bias_ref[...] = jnp.zeros_like(bias_ref)

        sent.fetch(sent_refs, block, arrived, step)
        grad.fetch(grad_refs, grad_block, grad_arrived, step)

        @pl.when(step == 0)
        def _():
            for copy in weights():
                copy.wait()

        token, grads = block[step % 2], grad_block[step % 2]
        normed = shift_gain(token, gain, shift)
        count = 2
        parts = [slice(k * rows // count, (k + 1) * rows // count) for k in range(count)]
        hidden = [dot_nn(normed[x], fc_whole[...]) + bias[...] for x in parts]
        back = [dot_nn(grads[x], out_whole[...]) for x in parts]
        for x, field, slope in zip(parts, hidden, back):
            chance = 0.5 + 0.5 * lax.erf(field * 0.7071067811865476)
            bell = jnp.exp(field * field * -0.5) * 0.3989422804014327
            act_ref[x, :] = (field * chance).astype(bf16)
            low = (slope * (chance + field * bell)).astype(bf16)
            hidden_ref[x, :] = low
            bias_ref[0:1, :] += jnp.sum(low.astype(f32), axis=0, keepdims=True)
        store_half(
            part_send, part_keep, dot_nt(act_ref[...], out_whole[...]).astype(bf16), step, groups
        )
        out_total[...] += dot_tn(grads, act_ref[...])
        fc_total[...] += dot_tn(normed, hidden_ref[...])

        @pl.when(step == groups - 1)
        def _():
            half = units // 2
            for at, order in enumerate(orders):
                stack = stacks[2 * at : 2 * at + 2]
                source = slice(at * half, (at + 1) * half)
                store_halves(*stack, fc_total, ids[1], order, slice(0, half), source)
                store_halves(*stack, out_total, ids[1], order, slice(half, units), source)

    operands = [*sent.arrays, *grad.arrays, *fc.arrays, *out.arrays, gain, shift, bias]
    count = model // fc.rows
    outs = [
        shaped(groups // 2, rows, model),
        shaped(groups // 2, rows, model),
        shaped(groups * rows, units),
        shaped(8, units, dtype=f32),
    ]
    outs += [shaped(count // 2, fc.rows, units)] * 4
    return call(
        kernel,
        "mlp",
        (groups,),
        [ids],
        operands,
        sent.specs
        + grad.specs
        + fc.specs()
        + out.specs()
        + [resident(x.shape) for x in operands[-3:]],
        outs,
        half_blocks(groups, rows, model)
        + [step_block(rows, units)]
        + [resident(x.shape) for x in outs[3:]],
        sent.scratch()
        + grad.scratch()
        + weight_scratch(fc)
        + weight_scratch(out)
        + [
            pltpu.VMEM((rows, units), bf16),
            pltpu.VMEM((model, units), f32),
            pltpu.VMEM((model, units), f32),
        ],
        10 * groups * rows * model * units,
        room=42,
    )


def norm_backward(ids, sent, grads, hidden, gain_attn, gain_mlp, qkv_pack, fc):
    groups, held, rows, model = sent.groups, len(sent.arrays), sent.rows, sent.model
    pieces, units, columns = len(fc.arrays), hidden.shape[1], grads.shape[1]

    def kernel(ids, grads_ref, hidden_ref, *refs):
        sent_refs, refs = refs[:held], refs[held:]
        qkv_refs, refs = refs[:pieces], refs[pieces:]
        fc_refs, refs = refs[:pieces], refs[pieces:]
        gain_attn, gain_mlp, send, keep, sums_ref = refs[:5]
        block, arrived, qkv_whole, qkv_placed, fc_whole, fc_placed = refs[5:]
        step = pl.program_id(0)

        def weights():
            copies = qkv_pack.copies(qkv_refs, qkv_whole, ids[1], qkv_placed)
            return copies + fc.copies(fc_refs, fc_whole, ids[1], fc_placed)

        @pl.when(step == 0)
        def _():
            for copy in weights():
                copy.start()
            sums_ref[...] = jnp.zeros_like(sums_ref)

        sent.fetch(sent_refs, block, arrived, step)

        @pl.when(step == 0)
        def _():
            for copy in weights():
                copy.wait()

        back_attn = dot_nt(grads_ref[...], qkv_whole[...])
        back_mlp = dot_nt(hidden_ref[...], fc_whole[...])
        token = block[step % 2].astype(f32)
        for at, back in enumerate((back_attn, back_mlp)):
            sums_ref[2 * at : 2 * at + 1, :] += jnp.sum(back * token, axis=0, keepdims=True)
            sums_ref[2 * at + 1 : 2 * at + 2, :] += jnp.sum(back, axis=0, keepdims=True)
        part = back_attn * gain_attn[...] + back_mlp * gain_mlp[...]
        store_half(send, keep, part.astype(bf16), step, groups)

    operands = [grads, hidden, *sent.arrays, *qkv_pack.arrays, *fc.arrays, gain_attn, gain_mlp]
    outs = [
        shaped(groups // 2, rows, model),
        shaped(groups // 2, rows, model),
        shaped(8, model, dtype=f32),
    ]
    return call(
        kernel,
        "norm_backward",
        (groups,),
        [ids],
        operands,
        [step_block(rows, columns), step_block(rows, units)]
        + sent.specs
        + qkv_pack.specs()
        + fc.specs()
        + [resident(x.shape) for x in operands[-2:]],
        outs,
        half_blocks(groups, rows, model) + [resident(x.shape) for x in outs[2:]],
        sent.scratch() + weight_scratch(qkv_pack) + weight_scratch(fc),
        2 * groups * rows * model * (units + columns),
        room=26,
    )


def taken(terms, block):
    return [
        pl.BlockSpec((pl.Squeezed(), block, x.shape[2]), lambda i, *_, at=at: (at, i, 0))
        for x, at in terms
    ]


def add_terms(terms, half):
    _, rows, columns = terms[0][0].shape
    block = max(x for x in (320, 128, 64) if rows % x == 0)

    def kernel(*refs):
        refs[-1][...] = sum(x[...].astype(f32) for x in refs[:-1]).astype(bf16)

    shape = (pl.Squeezed(), block, columns)
    out = shaped(half, rows, columns)
    return call(
        kernel,
        "add_terms",
        (half, rows // block),
        [],
        [x for x, _ in terms],
        [pl.BlockSpec(shape, lambda k, i, *_, at=at: (at + k, i, 0)) for _, at in terms],
        [out],
        [pl.BlockSpec(shape, lambda k, i, *_: (k, i, 0))],
        [],
        half * rows * columns * len(terms),
    )[0]


def add_split(terms, count):
    _, rows, columns = terms[0][0].shape
    block = rows // count

    def kernel(*refs):
        total = sum(x[...].astype(f32) for x in refs[:-2]).astype(bf16)

        @pl.when(pl.program_id(0) == 0)
        def _():
            refs[-2][...] = total

        @pl.when(pl.program_id(0) > 0)
        def _():
            refs[-1][...] = total

    shape = (pl.Squeezed(), block, columns)
    return call(
        kernel,
        "add_split",
        (count,),
        [],
        [x for x, _ in terms],
        [pl.BlockSpec(shape, lambda i, *_, at=at: (at, i, 0)) for _, at in terms],
        [shaped(1, block, columns), shaped(1, rows - block, columns)],
        [
            pl.BlockSpec(shape, lambda i, *_: (0, 0, 0)),
            pl.BlockSpec(shape, lambda i, *_: (0, jnp.maximum(i - 1, 0), 0)),
        ],
        [],
        rows * columns * len(terms),
    )


def whole_terms(terms, count):
    return [
        pl.BlockSpec((count, *x.shape[1:]), lambda *_, at=at: (at // count, 0, 0)) for x, at in terms
    ]


def add_stacks(stacks):
    counts = []
    for parts in stacks:
        parts.terms.append((parts.got, 0))
        counts.append(parts.got.shape[0] // 2)
    held = [len(parts.terms) for parts in stacks]
    operands = [x for parts in stacks for x, _ in parts.terms]

    def kernel(*refs):
        for at, half in enumerate(counts):
            first = sum(held[:at])
            total = sum(x[...].astype(f32) for x in refs[first : first + held[at]])
            refs[len(operands) + at][...] = total.astype(bf16)

    outs = [shaped(n, *parts.got.shape[1:]) for n, parts in zip(counts, stacks)]
    sends = call(
        kernel,
        "add_stacks",
        (1,),
        [],
        operands,
        [x for n, parts in zip(counts, stacks) for x in whole_terms(parts.terms, n)],
        outs,
        [resident(x.shape) for x in outs],
        [],
        sum(x.size for x in operands) // 2,
        room=16,
    )
    for n, parts, send in zip(counts, stacks, sends):
        parts.send = send
        parts.terms = [(x, at + n) for x, at in parts.terms]


def finish_mlp_weights(first, second):
    held, (_, rows, units) = len(first), first[0][0].shape
    half = units // 2

    def kernel(*refs):
        low = sum(x[0].astype(f32) for x in refs[:held])
        high = sum(x[0].astype(f32) for x in refs[held:-2])
        refs[-2][:, :half] = low[:, :half]
        refs[-2][:, half:] = high[:, :half]
        refs[-1][:half, :] = low[:, half:].T
        refs[-1][half:, :] = high[:, half:].T

    operands = [x for x, _ in [*first, *second]]
    outs = [shaped(rows, units, dtype=f32), shaped(units, rows, dtype=f32)]
    return call(
        kernel,
        "finish_mlp_weights",
        (1,),
        [],
        operands,
        whole_terms([*first, *second], 1),
        outs,
        [resident(x.shape) for x in outs],
        [],
        len(operands) * rows * units,
    )


def finish_attention_weights(first, second):
    held, (_, rows, columns) = len(first), first[0][0].shape
    width = columns // 2

    def kernel(*refs):
        low = sum(x[0].astype(f32) for x in refs[:held])
        high = sum(x[0].astype(f32) for x in refs[held:-2])
        for head in range(width // HD):
            for kind, (source, start) in enumerate(((low, 0), (low, width), (high, 0))):
                at = (3 * head + kind) * HD
                own = start + head * HD
                refs[-2][:, at : at + HD] = source[:, own : own + HD]
        refs[-1][...] = high[:, width:].T

    operands = [x for x, _ in [*first, *second]]
    outs = [shaped(rows, 3 * width, dtype=f32), shaped(width, rows, dtype=f32)]
    return call(
        kernel,
        "finish_attention_weights",
        (1,),
        [],
        operands,
        whole_terms([*first, *second], 1),
        outs,
        [resident(x.shape) for x in outs],
        [],
        len(operands) * rows * columns,
    )


def sum_rows(groups):
    return (12 + groups + 7) // 8 * 8


def finish_output(ids, stream, grad, attn_terms, mlp_terms, dense_bias, out_bias, norm_sums, fc_sums, qkv_sums, groups):
    rows, model = stream.shape
    block = 160
    first, second = len(attn_terms), len(mlp_terms)
    units, columns = fc_sums.shape[1], qkv_sums.shape[1]
    across = model // units

    def kernel(ids, stream_ref, grad_ref, *refs):
        attn_refs, refs = refs[:first], refs[first:]
        mlp_refs, refs = refs[:second], refs[second:]
        dense_bias, out_bias, norm_ref, fc_ref, qkv_ref, out_ref, sums_ref = refs

        @pl.when(pl.program_id(0) == 0)
        def _():
            sums_ref[...] = jnp.zeros_like(sums_ref)
            sums_ref[0:4, :] = norm_ref[0:4, :]
            own = jnp.concatenate([fc_ref[0:1, :]] * across, axis=1) if across > 1 else fc_ref[0:1, :]
            lane = lax.broadcasted_iota(jnp.int32, (1, model), 1) // units
            sums_ref[pl.ds(8 + ids[0] // across, 1), :] = jnp.where(lane == ids[0] % across, own, 0.0)
            sums_ref[pl.ds(12 + ids[0], 1), :columns] = qkv_ref[0:1, :]

        attn = sum(x[...].astype(f32) for x in attn_refs) + dense_bias[...]
        mlp = sum(x[...].astype(f32) for x in mlp_refs) + out_bias[...]
        output = stream_ref[...] + attn + mlp
        out_ref[...] = output
        for at, value in enumerate((output, attn, mlp)):
            sums_ref[4 + at : 5 + at, :] += jnp.sum(value * value, axis=0, keepdims=True)
        sums_ref[7:8, :] += jnp.sum(grad_ref[...].astype(f32), axis=0, keepdims=True)

    terms = [*attn_terms, *mlp_terms]
    operands = [stream, grad, *[x for x, _ in terms], dense_bias, out_bias, norm_sums, fc_sums, qkv_sums]
    outs = [shaped(rows, model, dtype=f32), shaped(sum_rows(groups), model, dtype=f32)]
    return call(
        kernel,
        "finish_output",
        (rows // block,),
        [ids],
        operands,
        [step_block(block, model), step_block(block, model)]
        + taken(terms, block)
        + [resident(x.shape) for x in operands[-5:]],
        outs,
        [step_block(block, model), resident(outs[1].shape)],
        [],
        rows * model * 16,
        room=16,
    )


def finish_grad(grad, normalized, inv_std, terms, first, rest):
    rows, model = grad.shape
    block = first.shape[1]

    def kernel(grad_ref, norm_ref, std_ref, *refs):
        term_refs, (first_ref, rest_ref, out_ref) = refs[:-3], refs[-3:]
        last = jnp.where(pl.program_id(0) == 0, first_ref[...].astype(f32), rest_ref[...].astype(f32))
        sent = sum(x[...].astype(f32) for x in term_refs) + last
        norm = norm_ref[...]
        mean = jnp.sum(sent, axis=1, keepdims=True) / model
        cross = jnp.sum(sent * norm, axis=1, keepdims=True) / model
        out_ref[...] = grad_ref[...].astype(f32) + std_ref[...] * (sent - mean - norm * cross)

    operands = [grad, normalized, inv_std, *[x for x, _ in terms], first, rest]
    piece = (pl.Squeezed(), block, model)
    return call(
        kernel,
        "finish_grad",
        (rows // block,),
        [],
        operands,
        [step_block(block, model), step_block(block, model), step_block(block, 1)]
        + taken(terms, block)
        + [
            pl.BlockSpec(piece, lambda i, *_: (0, 0, 0)),
            pl.BlockSpec(piece, lambda i, *_: (0, jnp.maximum(i - 1, 0), 0)),
        ],
        [shaped(rows, model, dtype=f32)],
        [step_block(block, model)],
        [],
        rows * model * 12,
    )[0]


def tree_table(segment_ids, parent_ids):
    trees = segment_ids.shape[0] // TREE
    segment = segment_ids.reshape(trees, NB, SEG)[:, :, 0]
    parent = parent_ids.reshape(trees, NB, SEG)[:, :, 0]
    block = lax.broadcasted_iota(jnp.int32, (trees, NB), 1)
    trunk = block < NT
    leaf = (parent != segment[:, :1]) & ~trunk
    at = lax.broadcasted_iota(jnp.int32, (trees, NB, NB), 2)
    owner = jnp.sum(jnp.where(segment[:, None, :] == parent[:, :, None], at, 0), axis=2)
    odd = block % 2 == 1
    first = jnp.where(trunk, block // 2 * 2, block)
    second = jnp.where(trunk, block // 2 * 2 + 1, jnp.where(leaf, owner, block))
    first_most = jnp.where(trunk & odd, SEG, 0)
    second_most = jnp.where(trunk, jnp.where(odd, 0, -SEG), jnp.where(leaf, SEG, -SEG))
    table = jnp.where(trunk, block, jnp.where(leaf, NT + 1, NT))
    return jnp.stack([first, second, first_most, second_most, table], axis=2).astype(jnp.int32)


def angle_tables():
    places = TRUNK + 2 * SEG
    place = lax.broadcasted_iota(jnp.int32, (places, 2 * HD), 0).astype(f32)
    lane = lax.broadcasted_iota(jnp.int32, (places, 2 * HD), 1) % HD
    half = ROT // 2
    frequency = 10000.0 ** (-((lane % half).astype(f32) * 2.0 / ROT))
    angle = place * frequency
    cosine = jnp.where(lane < ROT, jnp.cos(angle), 1.0)
    sine = jnp.sin(angle)
    low = jnp.where(lane < half, -sine, 0.0)
    high = jnp.where((lane >= half) & (lane < ROT), sine, 0.0)
    return cosine, low, high


def by_kind(array, heads):
    shape = array.shape[:-1]
    array = array.reshape(*shape, heads, 3, HD)
    return jnp.swapaxes(array, -3, -2).reshape(*shape, 3 * heads * HD)


def by_head(array, heads):
    shape = array.shape[:-1]
    array = array.reshape(*shape, 3, heads, HD)
    return jnp.swapaxes(array, -3, -2).reshape(*shape, 3 * heads * HD)


def local(
    stream_in,
    segment_ids,
    parent_ids,
    norm_gain_attn,
    norm_shift_attn,
    norm_gain_mlp,
    norm_shift_mlp,
    qkv_weight,
    qkv_bias,
    dense_weight,
    dense_bias,
    fc_weight,
    fc_bias,
    out_weight,
    out_bias,
    out_grad,
):
    tensor_rank = lax.axis_index("tensor")
    data_rank = lax.axis_index("dp")
    rows_local = stream_in.shape[0]
    model = stream_in.shape[1]
    qkv_width = qkv_weight.shape[1]
    heads = qkv_width // (3 * HD)
    width = heads * HD
    units = fc_weight.shape[1]
    groups = lax.axis_size("tensor")
    tensor_bits = bits_of(groups)
    far_first = tensor_bits[:0:-1] + tensor_bits[:1]
    order = halving_order(tensor_bits)
    ids = jnp.stack([tensor_rank, data_rank, *order]).astype(jnp.int32)
    data_bits = bits_of(lax.axis_size("dp"))
    rows_first = data_bits[:0:-1] + data_bits[:1]
    columns_first = data_bits[:1] + data_bits[:0:-1]
    near_bits = data_bits
    next_bits = data_bits[1:2] + data_bits[:1] + data_bits[2:]

    qkv_pack = Pack(by_kind(qkv_weight.astype(bf16), heads), "dp", rows_first)
    dense_pack = Pack(dense_weight.astype(bf16).T, "dp", columns_first)
    fc_pack = Pack(fc_weight.astype(bf16), "dp", rows_first)
    out_pack = Pack(out_weight.astype(bf16).T, "dp", rows_first)

    row_mean = jnp.mean(stream_in, axis=-1, keepdims=True)
    centred = stream_in - row_mean
    row_var = jnp.mean(centred * centred, axis=-1, keepdims=True)
    inv_std = lax.rsqrt(row_var + eps_norm)
    normalized = centred * inv_std
    sent = gather_far(normalized.astype(bf16), "tensor", tensor_bits)

    sent_near, near = swap(sent[0], "tensor", 1), swap(out_grad, "tensor", 1)
    qkv_pack.double()
    dense_pack.double()
    (near,) = tie_packs(qkv_pack, dense_pack, fc_pack, beside=[near])
    while len(qkv_pack.bits) > 1:
        qkv_pack.double()
        dense_pack.double()
    fc_pack.double()
    cut = rows_local * 3 // 5
    early, late = out_grad[:cut], out_grad[cut:]
    early, late, sent_near, *sent = tie_packs(
        qkv_pack, dense_pack, fc_pack, out_pack, beside=[early, late, sent_near, *sent]
    )
    early_far = gather_far(early, "tensor", tensor_bits)[1:]
    sent_near = [sent_near] + [swap(x, "tensor", 1) for x in sent[1:]]
    sent = [x for pair in zip(sent, sent_near) for x in pair]
    qkv_pack.double()
    dense_pack.double()
    while len(fc_pack.bits) > 1:
        fc_pack.double()
    out_pack.double()
    late, *done = tie_packs(
        qkv_pack, dense_pack, fc_pack, out_pack, beside=[late, *sent, *early_far]
    )
    sent, early_far = Tokens([(x,) for x in done[:groups]], order), done[groups:]
    late_far = gather_far(late, "tensor", tensor_bits)[1:]
    early_near = [swap(x, "tensor", 1) for x in early_far]
    while len(out_pack.bits) > 1:
        out_pack.double()

    info = tree_table(segment_ids, parent_ids)
    tables = angle_tables()
    gain_attn, shift_attn = norm_gain_attn[None, :], norm_shift_attn[None, :]
    gain_mlp, shift_mlp = norm_gain_mlp[None, :], norm_shift_mlp[None, :]
    qkv_bias_own = by_kind(
        lax.dynamic_slice_in_dim(qkv_bias, tensor_rank * qkv_width, qkv_width), heads
    )[None, :]
    fc_bias_own = lax.dynamic_slice_in_dim(fc_bias, tensor_rank * units, units)[None, :]

    done = project_qkv(
        ids, info, sent, gain_attn, shift_attn, qkv_pack, qkv_bias_own, tables, width
    )
    done = tie_packs(out_pack, beside=[*done, *early_near, *late_far])
    (queries, keys, values), done = done[:3], done[3:]
    early_near, late_far = done[: groups // 2 - 1], done[groups // 2 - 1 :]
    late_near = [swap(x, "tensor", 1) for x in late_far]
    far = zip(zip(early_far, late_far), zip(early_near, late_near))
    grad = Tokens([(out_grad,), (near,), *[x for pair in far for x in pair]], order)
    grad_context = project_grad(ids, grad, dense_pack, width)
    fc_pack.double()
    out_pack.double()
    done = attention(info, tables, queries, keys, values, grad_context)
    context, dq, dk, dv = tie_packs(fc_pack, out_pack, beside=done)
    dp_orders = [halving_order(near_bits), halving_order(next_bits)]
    attn_parts = Halving(
        *project_context(ids, context, dense_pack, groups, model), "tensor", tensor_bits
    )
    while len(attn_parts.bits) > 2:
        attn_parts.swap()
        attn_parts.add()
    attn_parts.send, context = tie(attn_parts.send, context)
    attn_parts.swap()
    done = attention_weights(
        ids, info, tables, context, dq, dk, dv, sent, grad, gain_attn, shift_attn, dp_orders
    )
    grads, qkv_bias_sums, *stacks = tie_halves(done, attn_parts)
    attn_parts.add()
    qkv_sums = [Halving(*stacks[:2], "dp", near_bits), Halving(*stacks[2:], "dp", next_bits)]
    sent.arrays[0], attn_parts.send = tie(sent.arrays[0], attn_parts.send)
    attn_parts.swap()
    for parts in qkv_sums:
        parts.swap()
    done = mlp(
        ids, sent, grad, gain_mlp, shift_mlp, fc_pack, fc_bias_own, out_pack, dp_orders
    )
    done = tie_halves(done, attn_parts, *qkv_sums)
    mlp_send, mlp_keep, hidden, fc_bias_sums, *stacks = done
    attn_parts.add()
    mlp_parts = Halving(mlp_send, mlp_keep, "tensor", tensor_bits)
    mlp_sums = [Halving(*stacks[:2], "dp", near_bits), Halving(*stacks[2:], "dp", next_bits)]
    while len(mlp_parts.bits) > 2:
        mlp_parts.swap()
        mlp_parts.add()
    mlp_parts.swap()
    add_stacks(qkv_sums)
    mlp_parts.add()
    hidden, mlp_parts.send = tie(hidden, mlp_parts.send)
    mlp_parts.swap()
    for parts in qkv_sums + mlp_sums:
        parts.swap()
    done = norm_backward(ids, sent, grads, hidden, gain_attn, gain_mlp, qkv_pack, fc_pack)
    done = tie_halves(done, mlp_parts, *qkv_sums, *mlp_sums)
    back_send, back_keep, norm_sums = done
    mlp_parts.add()

    back_parts = Halving(back_send, back_keep, "tensor", tensor_bits)
    while len(back_parts.bits) > 2:
        back_parts.swap()
        back_parts.add()
    back_parts.swap()
    add_stacks(qkv_sums + mlp_sums)

    back_parts.terms.append((back_parts.got, 0))
    last = back_parts.bits[-1]
    first, rest = add_split(back_parts.terms, 4)
    back_parts.terms = [(x, at + 1) for x, at in back_parts.terms]
    stream_in, first, rest = tie(stream_in, first, rest)
    first, rest = swap(first, "tensor", last), swap(rest, "tensor", last)
    for parts in qkv_sums + mlp_sums:
        parts.swap()
    output, sums = finish_output(
        ids,
        stream_in,
        out_grad,
        attn_parts.terms,
        mlp_parts.terms,
        dense_bias[None, :],
        out_bias[None, :],
        norm_sums,
        fc_bias_sums,
        qkv_bias_sums,
        groups,
    )
    output, sums, first = tie(output, sums, first)

    sums = sums + swap(sums, "tensor", 1)
    (sums,) = tie_halves([sums], *qkv_sums, *mlp_sums)
    for bit in data_bits[1:]:
        sums = sums + swap(sums, "dp", bit)
    for parts in qkv_sums:
        parts.add()
    add_stacks(mlp_sums)
    sums, *sends = tie(sums, *[parts.send for parts in mlp_sums])
    for parts, send in zip(mlp_sums, sends):
        parts.send = send
    sums = sums + swap(sums, "dp", data_bits[0])
    sums, rest = tie(sums, rest)
    for bit in tensor_bits[1:]:
        sums = sums + swap(sums, "tensor", bit)
    stream_grad = finish_grad(out_grad, normalized, inv_std, back_parts.terms, first, rest)

    fc_weight_grad, out_weight_grad = finish_mlp_weights(*[x.finish() for x in mlp_sums])
    qkv_weight_grad, dense_weight_grad = finish_attention_weights(*[x.finish() for x in qkv_sums])

    count_all = float(rows_local * lax.axis_size("dp") * groups * model)
    gain_attn_grad, shift_attn_grad, gain_mlp_grad, shift_mlp_grad = (sums[x] for x in range(4))
    root_squares = jnp.sqrt(jnp.sum(sums[4:7], axis=1) / count_all)
    residual_grad = sums[7]
    fc_bias_grad = sums[8:12].reshape(-1)
    qkv_bias_grad = by_head(sums[12 : 12 + groups, :qkv_width], heads).reshape(-1)
    return (
        output,
        stream_grad,
        gain_attn_grad,
        shift_attn_grad,
        gain_mlp_grad,
        shift_mlp_grad,
        qkv_weight_grad,
        qkv_bias_grad,
        dense_weight_grad,
        residual_grad,
        fc_weight_grad,
        fc_bias_grad,
        out_weight_grad,
        residual_grad,
        root_squares,
    )


def solution(mesh):
    tokens, weights, rows, whole = (
        P(("dp", "tensor"), None),
        P("dp", "tensor"),
        P("tensor", "dp"),
        P(),
    )
    return jax.shard_map(
        local,
        mesh=mesh,
        in_specs=(
            tokens,
            P("dp"),
            P("dp"),
            whole,
            whole,
            whole,
            whole,
            weights,
            whole,
            rows,
            whole,
            weights,
            whole,
            rows,
            whole,
            tokens,
        ),
        out_specs=(
            tokens,
            tokens,
            whole,
            whole,
            whole,
            whole,
            weights,
            whole,
            rows,
            whole,
            weights,
            whole,
            rows,
            whole,
            whole,
        ),
        check_vma=False,
    )
```

```python
import jax
import jax.numpy as jnp
from jax import lax
from jax.experimental import pallas as pl
from jax.experimental.pallas import tpu as pltpu
from jax.sharding import PartitionSpec as P

HD = 64
ROT = 16
TRUNK = 1024
SEG = 128
TREE = 2560
NB = TREE // SEG
NT = TRUNK // SEG

f32 = jnp.float32
bf16 = jnp.bfloat16
eps_norm = 1e-05
masked_score = -1e30


def dot_nn(left, right):
    return lax.dot_general(left, right, (((1,), (0,)), ((), ())), preferred_element_type=f32)


def dot_nt(left, right):
    return lax.dot_general(left, right, (((1,), (1,)), ((), ())), preferred_element_type=f32)


def dot_tn(left, right):
    return lax.dot_general(left, right, (((0,), (0,)), ((), ())), preferred_element_type=f32)


def bits_of(size):
    bits = []
    bit = 1
    while bit < size:
        bits.append(bit)
        bit *= 2
    return bits


def swap(block, axis, bit):
    size = lax.axis_size(axis)
    return lax.ppermute(block, axis, [(i, i ^ bit) for i in range(size)])


def tie(*values):
    return lax.optimization_barrier(values)


def gather_far(block, axis, bits):
    pieces = [block]
    for bit in bits[1:]:
        pieces = pieces + [swap(piece, axis, bit) for piece in pieces]
    return pieces


class Pack:
    def __init__(self, block, axis, bits):
        self.rows, self.axis, self.bits = block.shape[0], axis, list(bits)
        self.arrays, self.owners = [block], [[0]]

    def double(self):
        bit = self.bits.pop(0)
        held = self.arrays[0] if len(self.arrays) == 1 else jnp.concatenate(self.arrays, axis=0)
        self.owners.append([j ^ bit for owners in self.owners for j in owners])
        self.arrays.append(swap(held, self.axis, bit))

    def specs(self):
        return [pl.BlockSpec(memory_space=pltpu.HBM)] * len(self.arrays)

    def pieces(self):
        return sum(len(owners) for owners in self.owners)

    def copies(self, refs, where, number, done):
        started = []
        for ref, owners in zip(refs, self.owners):
            for at, j in enumerate(owners):
                rows = pl.ds(pl.multiple_of((number ^ j) * self.rows, self.rows), self.rows)
                source = ref.at[pl.ds(at * self.rows, self.rows), :]
                copy = pltpu.make_async_copy(source, where.at[rows, :], done.at[len(started)])
                started.append(copy)
        return started


def tie_packs(*packs, beside=()):
    flat = tie(*beside, *[x for pack in packs for x in pack.arrays])
    at = len(beside)
    for pack in packs:
        pack.arrays = list(flat[at : at + len(pack.arrays)])
        at += len(pack.arrays)
    return list(flat[: len(beside)])


def halving_order(bits):
    if not bits:
        return [0]
    rest = halving_order(bits[1:])
    return [bits[0] ^ j for j in rest] + rest


class Halving:
    def __init__(self, send, keep, axis, bits):
        self.send, self.axis, self.bits = send, axis, list(bits)
        self.terms = [(keep, 0)]

    def swap(self):
        self.got = swap(self.send, self.axis, self.bits.pop(0))

    def add(self):
        self.terms.append((self.got, 0))
        half = self.got.shape[0] // 2
        if half:
            self.send = add_terms(self.terms, half)
            self.terms = [(x, at + half) for x, at in self.terms]

    def most(self):
        while len(self.bits) > 1:
            self.swap()
            self.add()

    def finish(self):
        while self.bits:
            self.swap()
            self.add()
        return self.terms


def tie_halves(values, *halvings):
    flat = tie(*values, *[x.got for x in halvings])
    for x, got in zip(halvings, flat[len(values) :]):
        x.got = got
    return flat[: len(values)]


def resident(shape):
    zeros = (0,) * len(shape)
    return pl.BlockSpec(shape, lambda *_: zeros, pipeline_mode=pl.Buffered(1))


def own_block(rows, columns):
    return pl.BlockSpec((rows, columns), lambda i, ids, *_: (ids[0] ^ ids[2 + i], 0))


def step_block(rows, columns):
    return pl.BlockSpec((rows, columns), lambda i, *_: (i, 0))


def half_blocks(groups, rows, columns):
    half = groups // 2
    shape = (pl.Squeezed(), rows, columns)
    return [
        pl.BlockSpec(shape, lambda i, *_: (jnp.minimum(i, half - 1), 0, 0)),
        pl.BlockSpec(shape, lambda i, *_: (jnp.maximum(i - half, 0), 0, 0)),
    ]


def store_half(send, keep, value, step, groups):
    @pl.when(step < groups // 2)
    def _():
        send[...] = value

    @pl.when(step >= groups // 2)
    def _():
        keep[...] = value


class Tokens:
    def __init__(self, blocks, order):
        blocks = [blocks[j] for j in order]
        self.groups, self.counts = len(blocks), [len(block) for block in blocks]
        self.rows, self.model = sum(x.shape[0] for x in blocks[0]), blocks[0][0].shape[1]
        self.arrays = [x for block in blocks for x in block]
        self.specs = [pl.BlockSpec(memory_space=pltpu.HBM)] * len(self.arrays)

    def scratch(self):
        return [
            pltpu.VMEM((2, self.rows, self.model), bf16),
            pltpu.SemaphoreType.DMA((2, max(self.counts))),
        ]

    def fetch(self, refs, held, done, step):
        def copies(at):
            first, start, found = sum(self.counts[:at]), 0, []
            for k, ref in enumerate(refs[first : first + self.counts[at]]):
                where = held.at[at % 2, pl.ds(start, ref.shape[0]), :]
                found.append(pltpu.make_async_copy(ref, where, done.at[at % 2, k]))
                start += ref.shape[0]
            return found

        for at in range(self.groups):

            @pl.when(step == at)
            def _(at=at):
                ahead = copies(at) if at == 0 else []
                if at + 1 < self.groups:
                    ahead = ahead + copies(at + 1)
                for copy in ahead:
                    copy.start()
                for copy in copies(at):
                    copy.wait()


def store_halves(send, keep, total, number, order, columns=slice(None), source=slice(None)):
    half, rows = send.shape[0], send.shape[1]
    for at, j in enumerate(order):
        where = send if at < half else keep
        block = total[pl.ds(pl.multiple_of((number ^ j) * rows, rows), rows), source]
        where[at % half, :, columns] = block.astype(bf16)


def call(
    kernel, name, grid, prefetch, operands, specs, outs, out_specs, scratch, flops, extra=0, room=12
):
    size = sum(x.size * x.dtype.itemsize for x in list(operands) + list(outs))
    return pl.pallas_call(
        kernel,
        grid_spec=pltpu.PrefetchScalarGridSpec(
            num_scalar_prefetch=len(prefetch),
            grid=grid,
            in_specs=specs,
            out_specs=out_specs,
            scratch_shapes=scratch,
        ),
        out_shape=outs,
        compiler_params=pltpu.CompilerParams(
            dimension_semantics=("arbitrary",) * len(grid), vmem_limit_bytes=room << 20
        ),
        cost_estimate=pl.CostEstimate(
            flops=int(flops), bytes_accessed=int(size), transcendentals=int(extra)
        ),
        name=name,
    )(*prefetch, *operands)


def shaped(*shape, dtype=bf16):
    return jax.ShapeDtypeStruct(shape, dtype)


def shift_gain(block, gain, shift):
    return (block.astype(f32) * gain[...] + shift[...]).astype(bf16)


def turn(block, cosine, low_sine, high_sine, sign):
    width = block.shape[1]
    step = min(width, 128)
    done = []
    for start in range(0, width, step):
        part = block[:, start : start + step]
        if step == 128:
            left = pltpu.roll(part, step - ROT // 2, 1)
            right = pltpu.roll(part, ROT // 2, 1)
        else:
            left = jnp.concatenate([part[:, ROT // 2 :], part[:, : ROT // 2]], axis=1)
            right = jnp.concatenate([part[:, -ROT // 2 :], part[:, : -ROT // 2]], axis=1)
        moved = left * low_sine[:, :step] + right * high_sine[:, :step]
        done.append(part * cosine[:, :step] + moved * sign)
    return done[0] if len(done) == 1 else jnp.concatenate(done, axis=1)


def weight_scratch(pack):
    model = pack.rows * pack.pieces()
    columns = pack.arrays[0].shape[1]
    return [pltpu.VMEM((model, columns), bf16), pltpu.SemaphoreType.DMA((pack.pieces(),))]


def project_qkv(ids, info, sent, gain, shift, pack, bias, tables, width):
    groups, held, rows, model = sent.groups, len(sent.arrays), sent.rows, sent.model

    def kernel(ids, info, *refs):
        sent_refs, refs = refs[:held], refs[held:]
        weight_refs, refs = refs[: len(pack.arrays)], refs[len(pack.arrays) :]
        gain, shift, bias, cos, low, high, q_out, k_out, v_out = refs[:9]
        block, arrived, whole, placed = refs[9:]
        step = pl.program_id(0)

        @pl.when(step == 0)
        def _():
            for copy in pack.copies(weight_refs, whole, ids[1], placed):
                copy.start()

        sent.fetch(sent_refs, block, arrived, step)

        @pl.when(step == 0)
        def _():
            for copy in pack.copies(weight_refs, whole, ids[1], placed):
                copy.wait()

        token = block[step % 2]
        qkv = dot_nn(shift_gain(token, gain, shift), whole[...]) + bias[...]
        first = (ids[0] ^ ids[2 + step]) * (rows // SEG)
        for at in range(rows // SEG):
            number = first + at
            table = pl.ds(pl.multiple_of(info[number // NB, number % NB, 4] * SEG, SEG), SEG)
            tabs = (cos[table, :], low[table, :], high[table, :])
            own = slice(at * SEG, (at + 1) * SEG)
            q_out[own, :] = (turn(qkv[own, :width], *tabs, 1.0) * HD**-0.5).astype(bf16)
            k_out[own, :] = turn(qkv[own, width : 2 * width], *tabs, 1.0).astype(bf16)
        v_out[...] = qkv[:, 2 * width :].astype(bf16)

    operands = [*sent.arrays, *pack.arrays, gain, shift, bias, *tables]
    out = shaped(groups * rows, width)
    return call(
        kernel,
        "project_qkv",
        (groups,),
        [ids, info],
        operands,
        sent.specs
        + pack.specs()
        + [resident(x.shape) for x in operands[held + len(pack.arrays) :]],
        [out] * 3,
        [own_block(rows, width)] * 3,
        sent.scratch() + weight_scratch(pack),
        2 * groups * rows * model * 3 * width,
        room=14,
    )


def project_grad(ids, grad, pack, width):
    groups, held, rows, model = grad.groups, len(grad.arrays), grad.rows, grad.model

    def kernel(ids, *refs):
        grad_refs, refs = refs[:held], refs[held:]
        weight_refs, (out, block, arrived, whole, placed) = refs[:-5], refs[-5:]
        step = pl.program_id(0)

        @pl.when(step == 0)
        def _():
            for copy in pack.copies(weight_refs, whole, ids[1], placed):
                copy.start()

        grad.fetch(grad_refs, block, arrived, step)

        @pl.when(step == 0)
        def _():
            for copy in pack.copies(weight_refs, whole, ids[1], placed):
                copy.wait()

        out[...] = dot_nn(block[step % 2], whole[...]).astype(bf16)

    operands = [*grad.arrays, *pack.arrays]
    return call(
        kernel,
        "project_grad",
        (groups,),
        [ids],
        operands,
        grad.specs + pack.specs(),
        [shaped(groups * rows, width)],
        [own_block(rows, width)],
        grad.scratch() + weight_scratch(pack),
        2 * groups * rows * model * width,
    )[0]


def attention_kernel(
    info, q_ref, do_ref, k_ref, v_ref, cos, low, high, ctx_ref, dq_ref, dk_ref, dv_ref, dk_sum, dv_sum
):
    tree, step = pl.program_id(0), pl.program_id(1)
    width = q_ref.shape[1]
    heads = width // HD
    lane_head = lax.broadcasted_iota(jnp.int32, (SEG, width), 1) // HD

    @pl.when(step == 0)
    def _():
        dk_sum[...] = jnp.zeros_like(dk_sum)
        dv_sum[...] = jnp.zeros_like(dv_sum)

    first, second = info[tree, step, 0], info[tree, step, 1]
    first_rows = pl.ds(pl.multiple_of(first * SEG, SEG), SEG)
    second_rows = pl.ds(pl.multiple_of(second * SEG, SEG), SEG)
    queries, grads = q_ref[...], do_ref[...]
    zero = jnp.zeros_like(queries)
    q_rows = jnp.concatenate([jnp.where(lane_head == h, queries, zero) for h in range(heads)], axis=0)
    g_rows = jnp.concatenate([jnp.where(lane_head == h, grads, zero) for h in range(heads)], axis=0)
    q_turned, g_turned = queries.T, grads.T
    ahead = lax.broadcasted_iota(jnp.int32, (SEG, SEG), 1) - lax.broadcasted_iota(
        jnp.int32, (SEG, SEG), 0
    )
    seen = jnp.concatenate([ahead <= info[tree, step, 2], ahead <= info[tree, step, 3]], axis=1)
    seen = jnp.concatenate([seen] * heads, axis=0)
    k_near = jnp.concatenate([k_ref[first_rows, :], k_ref[second_rows, :]], axis=0)
    v_near = jnp.concatenate([v_ref[first_rows, :], v_ref[second_rows, :]], axis=0)

    def work(pairs):
        count = pairs * 2 * SEG
        near = jnp.where(seen, dot_nt(q_rows, k_near), masked_score)
        most = jnp.max(near, axis=1, keepdims=True)
        if count:
            k_far, v_far = k_ref[0:count, :], v_ref[0:count, :]
            far = dot_nt(q_rows, k_far)
            most = jnp.maximum(most, jnp.max(far, axis=1, keepdims=True))
        near = jnp.exp(near - most)
        total = jnp.sum(near, axis=1, keepdims=True)
        if count:
            far = jnp.exp(far - most)
            total = total + jnp.sum(far, axis=1, keepdims=True)
        scale = 1.0 / total
        near = near * scale
        near_low = near.astype(bf16)
        context = dot_nn(near_low, v_near)
        if count:
            far = far * scale
            far_low = far.astype(bf16)
            context = context + dot_nn(far_low, v_far)
        delta = jnp.sum(context * g_rows.astype(f32), axis=1, keepdims=True)
        near = (near * (dot_nt(g_rows, v_near) - delta)).astype(bf16)
        dq = dot_nn(near, k_near)
        if count:
            far = (far * (dot_nt(g_rows, v_far) - delta)).astype(bf16)
            dq = dq + dot_nn(far, k_far)
        ctx_own, dq_own = context[0:SEG], dq[0:SEG]
        for h in range(1, heads):
            ctx_own = jnp.where(lane_head == h, context[h * SEG : (h + 1) * SEG], ctx_own)
            dq_own = jnp.where(lane_head == h, dq[h * SEG : (h + 1) * SEG], dq_own)
        ctx_ref[...] = ctx_own.astype(bf16)
        dq_ref[...] = turn(dq_own * HD**-0.5, cos, low, high, -1.0).astype(bf16)
        for h in range(heads):
            own = slice(h * SEG, (h + 1) * SEG)
            part = slice(h * HD, (h + 1) * HD)
            dk = dot_nn(q_turned[part], near[own])
            dv = dot_nn(g_turned[part], near_low[own])
            dk_sum[first, part, :] += dk[:, :SEG]
            dv_sum[first, part, :] += dv[:, :SEG]
            dk_sum[second, part, :] += dk[:, SEG:]
            dv_sum[second, part, :] += dv[:, SEG:]
            if count:
                dk = dot_nn(q_turned[part], far[own])
                dv = dot_nn(g_turned[part], far_low[own])
                for j in range(2 * pairs):
                    dk_sum[j, part, :] += dk[:, j * SEG : (j + 1) * SEG]
                    dv_sum[j, part, :] += dv[:, j * SEG : (j + 1) * SEG]

    for pairs in range(NT // 2):

        @pl.when(step // 2 == pairs)
        def _(pairs=pairs):
            work(pairs)

    @pl.when(step >= NT)
    def _():
        work(NT // 2)

    @pl.when(step == NB - 1)
    def _():
        def finish(j, carry):
            rows = pl.ds(pl.multiple_of(j * SEG, SEG), SEG)
            dv_ref[rows, :] = dv_sum[j].T.astype(bf16)
            dk_ref[rows, :] = dk_sum[j].T.astype(bf16)
            return carry

        lax.fori_loop(0, NB, finish, 0)


def attention(info, tables, queries, keys, values, grads):
    total, width = queries.shape
    trees = total // TREE
    table_width = tables[0].shape[1]
    block = pl.BlockSpec((SEG, width), lambda t, b, info: (t * NB + b, 0))
    whole = pl.BlockSpec((TREE, width), lambda t, b, info: (t, 0))
    table = pl.BlockSpec((SEG, table_width), lambda t, b, info: (info[t, b, 4], 0))
    scores = trees * (TREE - TRUNK) * (TRUNK + 2 * SEG) * (width // HD)
    return call(
        attention_kernel,
        "attention",
        (trees, NB),
        [info],
        [queries, grads, keys, values, *tables],
        [block, block, whole, whole, table, table, table],
        [shaped(total, width)] * 4,
        [block, block, whole, whole],
        [pltpu.VMEM((NB, width, SEG), f32), pltpu.VMEM((NB, width, SEG), f32)],
        scores * width * 2 * 6 * 1.3,
        scores,
        room=22,
    )


def project_context(ids, context, pack, groups, model):
    rows, width = context.shape[0] // groups, context.shape[1]

    def kernel(ids, ctx, *refs):
        weight_refs, (send, keep, whole, placed) = refs[:-4], refs[-4:]
        step = pl.program_id(0)

        @pl.when(step == 0)
        def _():
            copies = pack.copies(weight_refs, whole, ids[1], placed)
            for copy in copies:
                copy.start()
            for copy in copies:
                copy.wait()

        store_half(send, keep, dot_nt(ctx[...], whole[...]).astype(bf16), step, groups)

    operands = [context, *pack.arrays]
    half = shaped(groups // 2, rows, model)
    return call(
        kernel,
        "project_context",
        (groups,),
        [ids],
        operands,
        [own_block(rows, width)] + pack.specs(),
        [half] * 2,
        half_blocks(groups, rows, model),
        weight_scratch(pack),
        2 * groups * rows * model * width,
        room=14,
    )


def attention_weights(ids, info, tables, context, dq, dk, dv, sent, grad, gain, shift, orders):
    groups, held, rows, model = sent.groups, len(sent.arrays), sent.rows, sent.model
    width, count = dq.shape[1], len(orders[0])

    def kernel(ids, info, ctx_ref, dq_ref, dk_ref, dv_ref, *refs):
        sent_refs, refs = refs[:held], refs[held:]
        grad_refs, refs = refs[: len(grad.arrays)], refs[len(grad.arrays) :]
        gain, shift, cos, low, high, grads, bias_ref, *stacks = refs[:11]
        block, arrived, grad_block, grad_arrived, total, dense_total = refs[11:]
        step = pl.program_id(0)

        @pl.when(step == 0)
        def _():
            total[...] = jnp.zeros_like(total)
            dense_total[...] = jnp.zeros_like(dense_total)
            bias_ref[...] = jnp.zeros_like(bias_ref)

        sent.fetch(sent_refs, block, arrived, step)
        grad.fetch(grad_refs, grad_block, grad_arrived, step)
        grads[:, :width] = dq_ref[...]
        first = (ids[0] ^ ids[2 + step]) * (rows // SEG)
        for at in range(rows // SEG):
            number = first + at
            table = pl.ds(pl.multiple_of(info[number // NB, number % NB, 4] * SEG, SEG), SEG)
            own = slice(at * SEG, (at + 1) * SEG)
            turned = turn(dk_ref[own, :], cos[table, :], low[table, :], high[table, :], -1.0)
            grads[own, width : 2 * width] = turned.astype(bf16)
        grads[:, 2 * width :] = dv_ref[...]
        bias_ref[0:1, :] += jnp.sum(grads[...].astype(f32), axis=0, keepdims=True)
        total[...] += dot_tn(shift_gain(block[step % 2], gain, shift), grads[...])
        dense_total[...] += dot_tn(grad_block[step % 2], ctx_ref[...])

        @pl.when(step == groups - 1)
        def _():
            store_halves(*stacks[:2], total, ids[1], orders[0], source=slice(0, 2 * width))
            source = slice(2 * width, 3 * width)
            store_halves(*stacks[2:], total, ids[1], orders[1], slice(0, width), source)
            columns = slice(width, 2 * width)
            store_halves(*stacks[2:], dense_total, ids[1], orders[1], columns)

    operands = [context, dq, dk, dv, *sent.arrays, *grad.arrays, gain, shift, *tables]
    outs = [shaped(groups * rows, 3 * width), shaped(8, 3 * width, dtype=f32)]
    outs += [shaped(count // 2, model // count, 2 * width)] * 4
    return call(
        kernel,
        "attention_weights",
        (groups,),
        [ids, info],
        operands,
        [own_block(rows, width)] * 4
        + sent.specs
        + grad.specs
        + [resident(x.shape) for x in operands[-5:]],
        outs,
        [step_block(rows, 3 * width)] + [resident(x.shape) for x in outs[1:]],
        sent.scratch()
        + grad.scratch()
        + [pltpu.VMEM((model, 3 * width), f32), pltpu.VMEM((model, width), f32)],
        2 * groups * rows * model * 4 * width,
        room=24,
    )


def mlp(ids, sent, grad, gain, shift, fc, bias, out, orders):
    groups, held, rows, model = sent.groups, len(sent.arrays), sent.rows, sent.model
    pieces, units = len(fc.arrays), fc.arrays[0].shape[1]

    def kernel(ids, *refs):
        sent_refs, refs = refs[:held], refs[held:]
        grad_refs, refs = refs[: len(grad.arrays)], refs[len(grad.arrays) :]
        fc_refs, refs = refs[:pieces], refs[pieces:]
        out_refs, refs = refs[:pieces], refs[pieces:]
        gain, shift, bias, part_send, part_keep, hidden_ref, bias_ref = refs[:7]
        stacks, refs = refs[7:11], refs[11:]
        block, arrived, grad_block, grad_arrived, fc_whole, fc_placed, out_whole, out_placed = refs[:8]
        act_ref, fc_total, out_total = refs[8:]
        step = pl.program_id(0)

        def weights():
            copies = fc.copies(fc_refs, fc_whole, ids[1], fc_placed)
            return copies + out.copies(out_refs, out_whole, ids[1], out_placed)

        @pl.when(step == 0)
        def _():
            for copy in weights():
                copy.start()
            fc_total[...] = jnp.zeros_like(fc_total)
            out_total[...] = jnp.zeros_like(out_total)
            bias_ref[...] = jnp.zeros_like(bias_ref)

        sent.fetch(sent_refs, block, arrived, step)
        grad.fetch(grad_refs, grad_block, grad_arrived, step)

        @pl.when(step == 0)
        def _():
            for copy in weights():
                copy.wait()

        token, grads = block[step % 2], grad_block[step % 2]
        normed = shift_gain(token, gain, shift)
        count = 2
        parts = [slice(k * rows // count, (k + 1) * rows // count) for k in range(count)]
        hidden = [dot_nn(normed[x], fc_whole[...]) + bias[...] for x in parts]
        back = [dot_nn(grads[x], out_whole[...]) for x in parts]
        for x, field, slope in zip(parts, hidden, back):
            chance = 0.5 + 0.5 * lax.erf(field * 0.7071067811865476)
            bell = jnp.exp(field * field * -0.5) * 0.3989422804014327
            act_ref[x, :] = (field * chance).astype(bf16)
            low = (slope * (chance + field * bell)).astype(bf16)
            hidden_ref[x, :] = low
            bias_ref[0:1, :] += jnp.sum(low.astype(f32), axis=0, keepdims=True)
        store_half(
            part_send, part_keep, dot_nt(act_ref[...], out_whole[...]).astype(bf16), step, groups
        )
        out_total[...] += dot_tn(grads, act_ref[...])
        fc_total[...] += dot_tn(normed, hidden_ref[...])

        @pl.when(step == groups - 1)
        def _():
            half = units // 2
            for at, order in enumerate(orders):
                stack = stacks[2 * at : 2 * at + 2]
                source = slice(at * half, (at + 1) * half)
                store_halves(*stack, fc_total, ids[1], order, slice(0, half), source)
                store_halves(*stack, out_total, ids[1], order, slice(half, units), source)

    operands = [*sent.arrays, *grad.arrays, *fc.arrays, *out.arrays, gain, shift, bias]
    count = model // fc.rows
    outs = [
        shaped(groups // 2, rows, model),
        shaped(groups // 2, rows, model),
        shaped(groups * rows, units),
        shaped(8, units, dtype=f32),
    ]
    outs += [shaped(count // 2, fc.rows, units)] * 4
    return call(
        kernel,
        "mlp",
        (groups,),
        [ids],
        operands,
        sent.specs
        + grad.specs
        + fc.specs()
        + out.specs()
        + [resident(x.shape) for x in operands[-3:]],
        outs,
        half_blocks(groups, rows, model)
        + [step_block(rows, units)]
        + [resident(x.shape) for x in outs[3:]],
        sent.scratch()
        + grad.scratch()
        + weight_scratch(fc)
        + weight_scratch(out)
        + [
            pltpu.VMEM((rows, units), bf16),
            pltpu.VMEM((model, units), f32),
            pltpu.VMEM((model, units), f32),
        ],
        10 * groups * rows * model * units,
        room=42,
    )


def norm_backward(ids, sent, grads, hidden, gain_attn, gain_mlp, qkv_pack, fc):
    groups, held, rows, model = sent.groups, len(sent.arrays), sent.rows, sent.model
    pieces, units, columns = len(fc.arrays), hidden.shape[1], grads.shape[1]

    def kernel(ids, grads_ref, hidden_ref, *refs):
        sent_refs, refs = refs[:held], refs[held:]
        qkv_refs, refs = refs[:pieces], refs[pieces:]
        fc_refs, refs = refs[:pieces], refs[pieces:]
        gain_attn, gain_mlp, send, keep, sums_ref = refs[:5]
        block, arrived, qkv_whole, qkv_placed, fc_whole, fc_placed = refs[5:]
        step = pl.program_id(0)

        def weights():
            copies = qkv_pack.copies(qkv_refs, qkv_whole, ids[1], qkv_placed)
            return copies + fc.copies(fc_refs, fc_whole, ids[1], fc_placed)

        @pl.when(step == 0)
        def _():
            for copy in weights():
                copy.start()
            sums_ref[...] = jnp.zeros_like(sums_ref)

        sent.fetch(sent_refs, block, arrived, step)

        @pl.when(step == 0)
        def _():
            for copy in weights():
                copy.wait()

        back_attn = dot_nt(grads_ref[...], qkv_whole[...])
        back_mlp = dot_nt(hidden_ref[...], fc_whole[...])
        token = block[step % 2].astype(f32)
        for at, back in enumerate((back_attn, back_mlp)):
            sums_ref[2 * at : 2 * at + 1, :] += jnp.sum(back * token, axis=0, keepdims=True)
            sums_ref[2 * at + 1 : 2 * at + 2, :] += jnp.sum(back, axis=0, keepdims=True)
        part = back_attn * gain_attn[...] + back_mlp * gain_mlp[...]
        store_half(send, keep, part.astype(bf16), step, groups)

    operands = [grads, hidden, *sent.arrays, *qkv_pack.arrays, *fc.arrays, gain_attn, gain_mlp]
    outs = [
        shaped(groups // 2, rows, model),
        shaped(groups // 2, rows, model),
        shaped(8, model, dtype=f32),
    ]
    return call(
        kernel,
        "norm_backward",
        (groups,),
        [ids],
        operands,
        [step_block(rows, columns), step_block(rows, units)]
        + sent.specs
        + qkv_pack.specs()
        + fc.specs()
        + [resident(x.shape) for x in operands[-2:]],
        outs,
        half_blocks(groups, rows, model) + [resident(x.shape) for x in outs[2:]],
        sent.scratch() + weight_scratch(qkv_pack) + weight_scratch(fc),
        2 * groups * rows * model * (units + columns),
        room=26,
    )


def taken(terms, block):
    return [
        pl.BlockSpec((pl.Squeezed(), block, x.shape[2]), lambda i, *_, at=at: (at, i, 0))
        for x, at in terms
    ]


def add_terms(terms, half):
    _, rows, columns = terms[0][0].shape
    block = max(x for x in (320, 128, 64) if rows % x == 0)

    def kernel(*refs):
        refs[-1][...] = sum(x[...].astype(f32) for x in refs[:-1]).astype(bf16)

    shape = (pl.Squeezed(), block, columns)
    out = shaped(half, rows, columns)
    return call(
        kernel,
        "add_terms",
        (half, rows // block),
        [],
        [x for x, _ in terms],
        [pl.BlockSpec(shape, lambda k, i, *_, at=at: (at + k, i, 0)) for _, at in terms],
        [out],
        [pl.BlockSpec(shape, lambda k, i, *_: (k, i, 0))],
        [],
        half * rows * columns * len(terms),
    )[0]


def whole_terms(terms, count):
    return [
        pl.BlockSpec((count, *x.shape[1:]), lambda *_, at=at: (at // count, 0, 0)) for x, at in terms
    ]


def add_stacks(stacks):
    counts = []
    for parts in stacks:
        parts.terms.append((parts.got, 0))
        counts.append(parts.got.shape[0] // 2)
    held = [len(parts.terms) for parts in stacks]
    operands = [x for parts in stacks for x, _ in parts.terms]

    def kernel(*refs):
        for at, half in enumerate(counts):
            first = sum(held[:at])
            total = sum(x[...].astype(f32) for x in refs[first : first + held[at]])
            refs[len(operands) + at][...] = total.astype(bf16)

    outs = [shaped(n, *parts.got.shape[1:]) for n, parts in zip(counts, stacks)]
    sends = call(
        kernel,
        "add_stacks",
        (1,),
        [],
        operands,
        [x for n, parts in zip(counts, stacks) for x in whole_terms(parts.terms, n)],
        outs,
        [resident(x.shape) for x in outs],
        [],
        sum(x.size for x in operands) // 2,
        room=16,
    )
    for n, parts, send in zip(counts, stacks, sends):
        parts.send = send
        parts.terms = [(x, at + n) for x, at in parts.terms]


def finish_mlp_weights(first, second):
    held, (_, rows, units) = len(first), first[0][0].shape
    half = units // 2

    def kernel(*refs):
        low = sum(x[0].astype(f32) for x in refs[:held])
        high = sum(x[0].astype(f32) for x in refs[held:-2])
        refs[-2][:, :half] = low[:, :half]
        refs[-2][:, half:] = high[:, :half]
        refs[-1][:half, :] = low[:, half:].T
        refs[-1][half:, :] = high[:, half:].T

    operands = [x for x, _ in [*first, *second]]
    outs = [shaped(rows, units, dtype=f32), shaped(units, rows, dtype=f32)]
    return call(
        kernel,
        "finish_mlp_weights",
        (1,),
        [],
        operands,
        whole_terms([*first, *second], 1),
        outs,
        [resident(x.shape) for x in outs],
        [],
        len(operands) * rows * units,
    )


def finish_attention_weights(first, second):
    held, (_, rows, columns) = len(first), first[0][0].shape
    width = columns // 2

    def kernel(*refs):
        low = sum(x[0].astype(f32) for x in refs[:held])
        high = sum(x[0].astype(f32) for x in refs[held:-2])
        for head in range(width // HD):
            for kind, (source, start) in enumerate(((low, 0), (low, width), (high, 0))):
                at = (3 * head + kind) * HD
                own = start + head * HD
                refs[-2][:, at : at + HD] = source[:, own : own + HD]
        refs[-1][...] = high[:, width:].T

    operands = [x for x, _ in [*first, *second]]
    outs = [shaped(rows, 3 * width, dtype=f32), shaped(width, rows, dtype=f32)]
    return call(
        kernel,
        "finish_attention_weights",
        (1,),
        [],
        operands,
        whole_terms([*first, *second], 1),
        outs,
        [resident(x.shape) for x in outs],
        [],
        len(operands) * rows * columns,
    )


def sum_rows(groups):
    return (12 + groups + 7) // 8 * 8


def finish_output(ids, stream, grad, attn_terms, mlp_terms, dense_bias, out_bias, norm_sums, fc_sums, qkv_sums, groups):
    rows, model = stream.shape
    block = 160
    first, second = len(attn_terms), len(mlp_terms)
    units, columns = fc_sums.shape[1], qkv_sums.shape[1]
    across = model // units

    def kernel(ids, stream_ref, grad_ref, *refs):
        attn_refs, refs = refs[:first], refs[first:]
        mlp_refs, refs = refs[:second], refs[second:]
        dense_bias, out_bias, norm_ref, fc_ref, qkv_ref, out_ref, sums_ref = refs

        @pl.when(pl.program_id(0) == 0)
        def _():
            sums_ref[...] = jnp.zeros_like(sums_ref)
            sums_ref[0:4, :] = norm_ref[0:4, :]
            own = jnp.concatenate([fc_ref[0:1, :]] * across, axis=1) if across > 1 else fc_ref[0:1, :]
            lane = lax.broadcasted_iota(jnp.int32, (1, model), 1) // units
            sums_ref[pl.ds(8 + ids[0] // across, 1), :] = jnp.where(lane == ids[0] % across, own, 0.0)
            sums_ref[pl.ds(12 + ids[0], 1), :columns] = qkv_ref[0:1, :]

        attn = sum(x[...].astype(f32) for x in attn_refs) + dense_bias[...]
        mlp = sum(x[...].astype(f32) for x in mlp_refs) + out_bias[...]
        output = stream_ref[...] + attn + mlp
        out_ref[...] = output
        for at, value in enumerate((output, attn, mlp)):
            sums_ref[4 + at : 5 + at, :] += jnp.sum(value * value, axis=0, keepdims=True)
        sums_ref[7:8, :] += jnp.sum(grad_ref[...].astype(f32), axis=0, keepdims=True)

    terms = [*attn_terms, *mlp_terms]
    operands = [stream, grad, *[x for x, _ in terms], dense_bias, out_bias, norm_sums, fc_sums, qkv_sums]
    outs = [shaped(rows, model, dtype=f32), shaped(sum_rows(groups), model, dtype=f32)]
    return call(
        kernel,
        "finish_output",
        (rows // block,),
        [ids],
        operands,
        [step_block(block, model), step_block(block, model)]
        + taken(terms, block)
        + [resident(x.shape) for x in operands[-5:]],
        outs,
        [step_block(block, model), resident(outs[1].shape)],
        [],
        rows * model * 16,
        room=16,
    )


def finish_grad(grad, normalized, inv_std, terms):
    rows, model = grad.shape
    block = 160

    def kernel(grad_ref, norm_ref, std_ref, *refs):
        term_refs, out_ref = refs[:-1], refs[-1]
        sent = sum(x[...].astype(f32) for x in term_refs)
        norm = norm_ref[...]
        mean = jnp.sum(sent, axis=1, keepdims=True) / model
        cross = jnp.sum(sent * norm, axis=1, keepdims=True) / model
        out_ref[...] = grad_ref[...].astype(f32) + std_ref[...] * (sent - mean - norm * cross)

    operands = [grad, normalized, inv_std, *[x for x, _ in terms]]
    return call(
        kernel,
        "finish_grad",
        (rows // block,),
        [],
        operands,
        [step_block(block, model), step_block(block, model), step_block(block, 1)]
        + taken(terms, block),
        [shaped(rows, model, dtype=f32)],
        [step_block(block, model)],
        [],
        rows * model * 12,
    )[0]


def tree_table(segment_ids, parent_ids):
    trees = segment_ids.shape[0] // TREE
    segment = segment_ids.reshape(trees, NB, SEG)[:, :, 0]
    parent = parent_ids.reshape(trees, NB, SEG)[:, :, 0]
    block = lax.broadcasted_iota(jnp.int32, (trees, NB), 1)
    trunk = block < NT
    leaf = (parent != segment[:, :1]) & ~trunk
    at = lax.broadcasted_iota(jnp.int32, (trees, NB, NB), 2)
    owner = jnp.sum(jnp.where(segment[:, None, :] == parent[:, :, None], at, 0), axis=2)
    odd = block % 2 == 1
    first = jnp.where(trunk, block // 2 * 2, block)
    second = jnp.where(trunk, block // 2 * 2 + 1, jnp.where(leaf, owner, block))
    first_most = jnp.where(trunk & odd, SEG, 0)
    second_most = jnp.where(trunk, jnp.where(odd, 0, -SEG), jnp.where(leaf, SEG, -SEG))
    table = jnp.where(trunk, block, jnp.where(leaf, NT + 1, NT))
    return jnp.stack([first, second, first_most, second_most, table], axis=2).astype(jnp.int32)


def angle_tables():
    places = TRUNK + 2 * SEG
    place = lax.broadcasted_iota(jnp.int32, (places, 2 * HD), 0).astype(f32)
    lane = lax.broadcasted_iota(jnp.int32, (places, 2 * HD), 1) % HD
    half = ROT // 2
    frequency = 10000.0 ** (-((lane % half).astype(f32) * 2.0 / ROT))
    angle = place * frequency
    cosine = jnp.where(lane < ROT, jnp.cos(angle), 1.0)
    sine = jnp.sin(angle)
    low = jnp.where(lane < half, -sine, 0.0)
    high = jnp.where((lane >= half) & (lane < ROT), sine, 0.0)
    return cosine, low, high


def by_kind(array, heads):
    shape = array.shape[:-1]
    array = array.reshape(*shape, heads, 3, HD)
    return jnp.swapaxes(array, -3, -2).reshape(*shape, 3 * heads * HD)


def by_head(array, heads):
    shape = array.shape[:-1]
    array = array.reshape(*shape, 3, heads, HD)
    return jnp.swapaxes(array, -3, -2).reshape(*shape, 3 * heads * HD)


def local(
    stream_in,
    segment_ids,
    parent_ids,
    norm_gain_attn,
    norm_shift_attn,
    norm_gain_mlp,
    norm_shift_mlp,
    qkv_weight,
    qkv_bias,
    dense_weight,
    dense_bias,
    fc_weight,
    fc_bias,
    out_weight,
    out_bias,
    out_grad,
):
    tensor_rank = lax.axis_index("tensor")
    data_rank = lax.axis_index("dp")
    rows_local = stream_in.shape[0]
    model = stream_in.shape[1]
    qkv_width = qkv_weight.shape[1]
    heads = qkv_width // (3 * HD)
    width = heads * HD
    units = fc_weight.shape[1]
    groups = lax.axis_size("tensor")
    tensor_bits = bits_of(groups)
    far_first = tensor_bits[:0:-1] + tensor_bits[:1]
    order = halving_order(tensor_bits)
    ids = jnp.stack([tensor_rank, data_rank, *order]).astype(jnp.int32)
    data_bits = bits_of(lax.axis_size("dp"))
    rows_first = data_bits[:0:-1] + data_bits[:1]
    columns_first = data_bits[:1] + data_bits[:0:-1]
    near_bits = data_bits
    next_bits = data_bits[1:2] + data_bits[:1] + data_bits[2:]

    qkv_pack = Pack(by_kind(qkv_weight.astype(bf16), heads), "dp", rows_first)
    dense_pack = Pack(dense_weight.astype(bf16).T, "dp", columns_first)
    fc_pack = Pack(fc_weight.astype(bf16), "dp", rows_first)
    out_pack = Pack(out_weight.astype(bf16).T, "dp", rows_first)

    row_mean = jnp.mean(stream_in, axis=-1, keepdims=True)
    centred = stream_in - row_mean
    row_var = jnp.mean(centred * centred, axis=-1, keepdims=True)
    inv_std = lax.rsqrt(row_var + eps_norm)
    normalized = centred * inv_std
    sent = gather_far(normalized.astype(bf16), "tensor", tensor_bits)

    info = tree_table(segment_ids, parent_ids)
    tables = angle_tables()
    gain_attn, shift_attn = norm_gain_attn[None, :], norm_shift_attn[None, :]
    gain_mlp, shift_mlp = norm_gain_mlp[None, :], norm_shift_mlp[None, :]
    qkv_bias_own = by_kind(
        lax.dynamic_slice_in_dim(qkv_bias, tensor_rank * qkv_width, qkv_width), heads
    )[None, :]
    fc_bias_own = lax.dynamic_slice_in_dim(fc_bias, tensor_rank * units, units)[None, :]

    sent_near, near = swap(sent[0], "tensor", 1), swap(out_grad, "tensor", 1)
    cut = rows_local * 3 // 5
    early, late = out_grad[:cut], out_grad[cut:]
    qkv_pack.double()
    dense_pack.double()
    near, early, late = tie_packs(qkv_pack, dense_pack, fc_pack, beside=[near, early, late])
    while len(qkv_pack.bits) > 1:
        qkv_pack.double()
        dense_pack.double()
    fc_pack.double()
    done = tie_packs(
        qkv_pack,
        dense_pack,
        out_pack,
        beside=[early, late, info, *tables, qkv_bias_own, fc_bias_own, sent_near, *sent],
    )
    early, late, info, *done = done
    tables, (qkv_bias_own, fc_bias_own, sent_near), sent = done[:3], done[3:6], done[6:]
    early_far = gather_far(early, "tensor", tensor_bits)[1:]
    sent_near = [sent_near] + [swap(x, "tensor", 1) for x in sent[1:]]
    sent = [x for pair in zip(sent, sent_near) for x in pair]
    qkv_pack.double()
    dense_pack.double()
    late, *done = tie_packs(
        qkv_pack, dense_pack, fc_pack, out_pack, beside=[late, *sent, *early_far]
    )
    sent, early_far = Tokens([(x,) for x in done[:groups]], order), done[groups:]
    late_far = gather_far(late, "tensor", tensor_bits)[1:]
    early_near = [swap(x, "tensor", 1) for x in early_far]
    out_pack.double()
    while len(fc_pack.bits) > 1:
        fc_pack.double()

    done = project_qkv(
        ids, info, sent, gain_attn, shift_attn, qkv_pack, qkv_bias_own, tables, width
    )
    done = tie_packs(fc_pack, out_pack, beside=[*done, *early_near, *late_far])
    (queries, keys, values), done = done[:3], done[3:]
    early_near, late_far = done[: groups // 2 - 1], done[groups // 2 - 1 :]
    late_near = [swap(x, "tensor", 1) for x in late_far]
    far = zip(zip(early_far, late_far), zip(early_near, late_near))
    grad = Tokens([(out_grad,), (near,), *[x for pair in far for x in pair]], order)
    grad_context = project_grad(ids, grad, dense_pack, width)
    fc_pack.double()
    while len(out_pack.bits) > 1:
        out_pack.double()
    done = attention(info, tables, queries, keys, values, grad_context)
    context, dq, dk, dv = tie_packs(fc_pack, out_pack, beside=done)
    dp_orders = [halving_order(near_bits), halving_order(next_bits)]
    attn_parts = Halving(
        *project_context(ids, context, dense_pack, groups, model), "tensor", tensor_bits
    )
    while len(attn_parts.bits) > 2:
        attn_parts.swap()
        attn_parts.add()
    attn_parts.send, context = tie(attn_parts.send, context)
    attn_parts.swap()
    out_pack.double()
    done = attention_weights(
        ids, info, tables, context, dq, dk, dv, sent, grad, gain_attn, shift_attn, dp_orders
    )
    grads, qkv_bias_sums, *stacks = tie_halves(tie_packs(out_pack, beside=done), attn_parts)
    attn_parts.add()
    qkv_sums = [Halving(*stacks[:2], "dp", near_bits), Halving(*stacks[2:], "dp", next_bits)]
    sent.arrays[0], attn_parts.send = tie(sent.arrays[0], attn_parts.send)
    attn_parts.swap()
    for parts in qkv_sums:
        parts.swap()
    done = mlp(
        ids, sent, grad, gain_mlp, shift_mlp, fc_pack, fc_bias_own, out_pack, dp_orders
    )
    done = tie_halves(done, attn_parts, *qkv_sums)
    mlp_send, mlp_keep, hidden, fc_bias_sums, *stacks = done
    attn_parts.add()
    mlp_parts = Halving(mlp_send, mlp_keep, "tensor", tensor_bits)
    mlp_sums = [Halving(*stacks[:2], "dp", near_bits), Halving(*stacks[2:], "dp", next_bits)]
    while len(mlp_parts.bits) > 2:
        mlp_parts.swap()
        mlp_parts.add()
    mlp_parts.swap()
    add_stacks(qkv_sums)
    mlp_parts.add()
    hidden, mlp_parts.send = tie(hidden, mlp_parts.send)
    mlp_parts.swap()
    for parts in qkv_sums + mlp_sums:
        parts.swap()
    done = norm_backward(ids, sent, grads, hidden, gain_attn, gain_mlp, qkv_pack, fc_pack)
    done = tie_halves(done, mlp_parts, *qkv_sums, *mlp_sums)
    back_send, back_keep, norm_sums = done
    mlp_parts.add()

    back_parts = Halving(back_send, back_keep, "tensor", tensor_bits)
    while len(back_parts.bits) > 2:
        back_parts.swap()
        back_parts.add()
    back_parts.swap()
    add_stacks(qkv_sums + mlp_sums)

    back_parts.add()
    stream_in, back_parts.send = tie(stream_in, back_parts.send)
    back_parts.swap()
    for parts in qkv_sums + mlp_sums:
        parts.swap()
    output, sums = finish_output(
        ids,
        stream_in,
        out_grad,
        attn_parts.terms,
        mlp_parts.terms,
        dense_bias[None, :],
        out_bias[None, :],
        norm_sums,
        fc_bias_sums,
        qkv_bias_sums,
        groups,
    )

    sums = sums + swap(sums, "tensor", 1)
    (sums,) = tie_halves([sums], *qkv_sums, *mlp_sums)
    for bit in data_bits[1:]:
        sums = sums + swap(sums, "dp", bit)
    for parts in qkv_sums:
        parts.add()
    add_stacks(mlp_sums)
    sums, *sends = tie(sums, *[parts.send for parts in mlp_sums])
    for parts, send in zip(mlp_sums, sends):
        parts.send = send
    sums = sums + swap(sums, "dp", data_bits[0])
    sums, back_parts.got = tie(sums, back_parts.got)
    back_parts.add()
    for bit in tensor_bits[1:]:
        sums = sums + swap(sums, "tensor", bit)
    stream_grad = finish_grad(out_grad, normalized, inv_std, back_parts.terms)

    fc_weight_grad, out_weight_grad = finish_mlp_weights(*[x.finish() for x in mlp_sums])
    qkv_weight_grad, dense_weight_grad = finish_attention_weights(*[x.finish() for x in qkv_sums])

    count_all = float(rows_local * lax.axis_size("dp") * groups * model)
    gain_attn_grad, shift_attn_grad, gain_mlp_grad, shift_mlp_grad = (sums[x] for x in range(4))
    root_squares = jnp.sqrt(jnp.sum(sums[4:7], axis=1) / count_all)
    residual_grad = sums[7]
    fc_bias_grad = sums[8:12].reshape(-1)
    qkv_bias_grad = by_head(sums[12 : 12 + groups, :qkv_width], heads).reshape(-1)
    return (
        output,
        stream_grad,
        gain_attn_grad,
        shift_attn_grad,
        gain_mlp_grad,
        shift_mlp_grad,
        qkv_weight_grad,
        qkv_bias_grad,
        dense_weight_grad,
        residual_grad,
        fc_weight_grad,
        fc_bias_grad,
        out_weight_grad,
        residual_grad,
        root_squares,
    )


def solution(mesh):
    tokens, weights, rows, whole = (
        P(("dp", "tensor"), None),
        P("dp", "tensor"),
        P("tensor", "dp"),
        P(),
    )
    return jax.shard_map(
        local,
        mesh=mesh,
        in_specs=(
            tokens,
            P("dp"),
            P("dp"),
            whole,
            whole,
            whole,
            whole,
            weights,
            whole,
            rows,
            whole,
            weights,
            whole,
            rows,
            whole,
            tokens,
        ),
        out_specs=(
            tokens,
            tokens,
            whole,
            whole,
            whole,
            whole,
            weights,
            whole,
            rows,
            whole,
            weights,
            whole,
            rows,
            whole,
            whole,
        ),
        check_vma=False,
    )
```

```python
import jax
import jax.numpy as jnp
from jax import lax
from jax.experimental import pallas as pl
from jax.experimental.pallas import tpu as pltpu
from jax.sharding import PartitionSpec as P

HD = 64
ROT = 16
TRUNK = 1024
SEG = 128
TREE = 2560
NB = TREE // SEG
NT = TRUNK // SEG

f32 = jnp.float32
bf16 = jnp.bfloat16
eps_norm = 1e-05
masked_score = -1e30


def dot_nn(left, right):
    return lax.dot_general(left, right, (((1,), (0,)), ((), ())), preferred_element_type=f32)


def dot_nt(left, right):
    return lax.dot_general(left, right, (((1,), (1,)), ((), ())), preferred_element_type=f32)


def dot_tn(left, right):
    return lax.dot_general(left, right, (((0,), (0,)), ((), ())), preferred_element_type=f32)


def bits_of(size):
    bits = []
    bit = 1
    while bit < size:
        bits.append(bit)
        bit *= 2
    return bits


def swap(block, axis, bit):
    size = lax.axis_size(axis)
    return lax.ppermute(block, axis, [(i, i ^ bit) for i in range(size)])


def tie(*values):
    return lax.optimization_barrier(values)


def gather_far(block, axis, bits):
    pieces = [block]
    for bit in bits[1:]:
        pieces = pieces + [swap(piece, axis, bit) for piece in pieces]
    return pieces


class Pack:
    def __init__(self, block, axis, bits):
        self.rows, self.axis, self.bits = block.shape[0], axis, list(bits)
        self.arrays, self.owners = [block], [[0]]

    def double(self):
        bit = self.bits.pop(0)
        held = self.arrays[0] if len(self.arrays) == 1 else jnp.concatenate(self.arrays, axis=0)
        self.owners.append([j ^ bit for owners in self.owners for j in owners])
        self.arrays.append(swap(held, self.axis, bit))

    def specs(self):
        return [pl.BlockSpec(memory_space=pltpu.HBM)] * len(self.arrays)

    def pieces(self):
        return sum(len(owners) for owners in self.owners)

    def copies(self, refs, where, number, done):
        started = []
        for ref, owners in zip(refs, self.owners):
            for at, j in enumerate(owners):
                rows = pl.ds(pl.multiple_of((number ^ j) * self.rows, self.rows), self.rows)
                source = ref.at[pl.ds(at * self.rows, self.rows), :]
                copy = pltpu.make_async_copy(source, where.at[rows, :], done.at[len(started)])
                started.append(copy)
        return started


def tie_packs(*packs, beside=()):
    flat = tie(*beside, *[x for pack in packs for x in pack.arrays])
    at = len(beside)
    for pack in packs:
        pack.arrays = list(flat[at : at + len(pack.arrays)])
        at += len(pack.arrays)
    return list(flat[: len(beside)])


def halving_order(bits):
    if not bits:
        return [0]
    rest = halving_order(bits[1:])
    return [bits[0] ^ j for j in rest] + rest


class Halving:
    def __init__(self, send, keep, axis, bits):
        self.send, self.axis, self.bits = send, axis, list(bits)
        self.terms = [(keep, 0)]

    def swap(self):
        self.got = swap(self.send, self.axis, self.bits.pop(0))

    def add(self):
        self.terms.append((self.got, 0))
        half = self.got.shape[0] // 2
        if half:
            self.send = add_terms(self.terms, half)
            self.terms = [(x, at + half) for x, at in self.terms]

    def most(self):
        while len(self.bits) > 1:
            self.swap()
            self.add()

    def finish(self):
        while self.bits:
            self.swap()
            self.add()
        return self.terms


def tie_halves(values, *halvings):
    flat = tie(*values, *[x.got for x in halvings])
    for x, got in zip(halvings, flat[len(values) :]):
        x.got = got
    return flat[: len(values)]


def resident(shape):
    zeros = (0,) * len(shape)
    return pl.BlockSpec(shape, lambda *_: zeros, pipeline_mode=pl.Buffered(1))


def own_block(rows, columns):
    return pl.BlockSpec((rows, columns), lambda i, ids, *_: (ids[0] ^ ids[2 + i], 0))


def step_block(rows, columns):
    return pl.BlockSpec((rows, columns), lambda i, *_: (i, 0))


def half_blocks(groups, rows, columns):
    half = groups // 2
    shape = (pl.Squeezed(), rows, columns)
    return [
        pl.BlockSpec(shape, lambda i, *_: (jnp.minimum(i, half - 1), 0, 0)),
        pl.BlockSpec(shape, lambda i, *_: (jnp.maximum(i - half, 0), 0, 0)),
    ]


def store_half(send, keep, value, step, groups):
    @pl.when(step < groups // 2)
    def _():
        send[...] = value

    @pl.when(step >= groups // 2)
    def _():
        keep[...] = value


class Tokens:
    def __init__(self, blocks, order):
        blocks = [blocks[j] for j in order]
        self.groups, self.counts = len(blocks), [len(block) for block in blocks]
        self.rows, self.model = sum(x.shape[0] for x in blocks[0]), blocks[0][0].shape[1]
        self.arrays = [x for block in blocks for x in block]
        self.specs = [pl.BlockSpec(memory_space=pltpu.HBM)] * len(self.arrays)

    def scratch(self):
        return [
            pltpu.VMEM((2, self.rows, self.model), bf16),
            pltpu.SemaphoreType.DMA((2, max(self.counts))),
        ]

    def fetch(self, refs, held, done, step):
        def copies(at):
            first, start, found = sum(self.counts[:at]), 0, []
            for k, ref in enumerate(refs[first : first + self.counts[at]]):
                where = held.at[at % 2, pl.ds(start, ref.shape[0]), :]
                found.append(pltpu.make_async_copy(ref, where, done.at[at % 2, k]))
                start += ref.shape[0]
            return found

        for at in range(self.groups):

            @pl.when(step == at)
            def _(at=at):
                ahead = copies(at) if at == 0 else []
                if at + 1 < self.groups:
                    ahead = ahead + copies(at + 1)
                for copy in ahead:
                    copy.start()
                for copy in copies(at):
                    copy.wait()


def store_halves(send, keep, total, number, order, columns=slice(None), source=slice(None)):
    half, rows = send.shape[0], send.shape[1]
    for at, j in enumerate(order):
        where = send if at < half else keep
        block = total[pl.ds(pl.multiple_of((number ^ j) * rows, rows), rows), source]
        where[at % half, :, columns] = block.astype(bf16)


def call(
    kernel, name, grid, prefetch, operands, specs, outs, out_specs, scratch, flops, extra=0, room=12
):
    size = sum(x.size * x.dtype.itemsize for x in list(operands) + list(outs))
    return pl.pallas_call(
        kernel,
        grid_spec=pltpu.PrefetchScalarGridSpec(
            num_scalar_prefetch=len(prefetch),
            grid=grid,
            in_specs=specs,
            out_specs=out_specs,
            scratch_shapes=scratch,
        ),
        out_shape=outs,
        compiler_params=pltpu.CompilerParams(
            dimension_semantics=("arbitrary",) * len(grid), vmem_limit_bytes=room << 20
        ),
        cost_estimate=pl.CostEstimate(
            flops=int(flops), bytes_accessed=int(size), transcendentals=int(extra)
        ),
        name=name,
    )(*prefetch, *operands)


def shaped(*shape, dtype=bf16):
    return jax.ShapeDtypeStruct(shape, dtype)


def shift_gain(block, gain, shift):
    return (block.astype(f32) * gain[...] + shift[...]).astype(bf16)


def turn(block, cosine, sine, sign):
    width = block.shape[1]
    step = min(width, 128)
    lane = lax.broadcasted_iota(jnp.int32, (block.shape[0], step), 1) % HD
    done = []
    for start in range(0, width, step):
        part = block[:, start : start + step]
        if step == 128:
            left = pltpu.roll(part, step - ROT // 2, 1)
            right = pltpu.roll(part, ROT // 2, 1)
        else:
            left = jnp.concatenate([part[:, ROT // 2 :], part[:, : ROT // 2]], axis=1)
            right = jnp.concatenate([part[:, -ROT // 2 :], part[:, : -ROT // 2]], axis=1)
        moved = jnp.where(lane < ROT // 2, -left, right) * sine[:, :step]
        done.append(part * cosine[:, :step] + moved * sign)
    return done[0] if len(done) == 1 else jnp.concatenate(done, axis=1)


def weight_scratch(pack):
    model = pack.rows * pack.pieces()
    columns = pack.arrays[0].shape[1]
    return [pltpu.VMEM((model, columns), bf16), pltpu.SemaphoreType.DMA((pack.pieces(),))]


def prepare_weights(qkv, dense, fc, out):
    rows, columns = qkv.shape
    width = columns // 3

    def kernel(qkv_ref, dense_ref, fc_ref, out_ref, qkv_to, dense_to, fc_to, out_to):
        for head in range(width // HD):
            for kind in range(3):
                at, own = (3 * head + kind) * HD, kind * width + head * HD
                qkv_to[:, own : own + HD] = qkv_ref[:, at : at + HD].astype(bf16)
        dense_to[...] = dense_ref[...].T.astype(bf16)
        fc_to[...] = fc_ref[...].astype(bf16)
        out_to[...] = out_ref[...].T.astype(bf16)

    operands = [qkv, dense, fc, out]
    outs = [shaped(*qkv.shape), shaped(*dense.shape[::-1]), shaped(*fc.shape), shaped(*out.shape[::-1])]
    return call(
        kernel,
        "prepare_weights",
        (1,),
        [],
        operands,
        [resident(x.shape) for x in operands],
        outs,
        [resident(x.shape) for x in outs],
        [],
        rows * columns,
    )


def normalize(stream):
    rows, model = stream.shape
    block = 160

    def kernel(stream_ref, sent_ref, norm_ref, std_ref):
        field = stream_ref[...]
        centred = field - jnp.sum(field, axis=1, keepdims=True) / model
        variance = jnp.sum(centred * centred, axis=1, keepdims=True) / model
        scale = lax.rsqrt(variance + eps_norm)
        norm = centred * scale
        norm_ref[...] = norm
        sent_ref[...] = norm.astype(bf16)
        std_ref[...] = scale

    return call(
        kernel,
        "normalize",
        (rows // block,),
        [],
        [stream],
        [step_block(block, model)],
        [shaped(rows, model), shaped(rows, model, dtype=f32), shaped(rows, 1, dtype=f32)],
        [step_block(block, model), step_block(block, model), step_block(block, 1)],
        [],
        rows * model * 8,
    )


def project_qkv(ids, info, sent, gain, shift, pack, bias, tables, width):
    groups, held, rows, model = sent.groups, len(sent.arrays), sent.rows, sent.model

    def kernel(ids, info, *refs):
        sent_refs, refs = refs[:held], refs[held:]
        weight_refs, refs = refs[: len(pack.arrays)], refs[len(pack.arrays) :]
        gain, shift, bias, cos, sine, q_out, k_out, v_out = refs[:8]
        block, arrived, whole, placed = refs[8:]
        step = pl.program_id(0)

        @pl.when(step == 0)
        def _():
            for copy in pack.copies(weight_refs, whole, ids[1], placed):
                copy.start()

        sent.fetch(sent_refs, block, arrived, step)

        @pl.when(step == 0)
        def _():
            for copy in pack.copies(weight_refs, whole, ids[1], placed):
                copy.wait()

        token = block[step % 2]
        qkv = dot_nn(shift_gain(token, gain, shift), whole[...]) + bias[...]
        first = (ids[0] ^ ids[2 + step]) * (rows // SEG)
        for at in range(rows // SEG):
            number = first + at
            table = pl.ds(pl.multiple_of(info[number // NB, number % NB, 4] * SEG, SEG), SEG)
            tabs = (cos[table, :], sine[table, :])
            own = slice(at * SEG, (at + 1) * SEG)
            q_out[own, :] = (turn(qkv[own, :width], *tabs, 1.0) * HD**-0.5).astype(bf16)
            k_out[own, :] = turn(qkv[own, width : 2 * width], *tabs, 1.0).astype(bf16)
        v_out[...] = qkv[:, 2 * width :].astype(bf16)

    operands = [*sent.arrays, *pack.arrays, gain, shift, bias, *tables]
    out = shaped(groups * rows, width)
    return call(
        kernel,
        "project_qkv",
        (groups,),
        [ids, info],
        operands,
        sent.specs
        + pack.specs()
        + [resident(x.shape) for x in operands[held + len(pack.arrays) :]],
        [out] * 3,
        [own_block(rows, width)] * 3,
        sent.scratch() + weight_scratch(pack),
        2 * groups * rows * model * 3 * width,
        room=14,
    )


def project_grad(ids, grad, pack, width):
    groups, held, rows, model = grad.groups, len(grad.arrays), grad.rows, grad.model

    def kernel(ids, *refs):
        grad_refs, refs = refs[:held], refs[held:]
        weight_refs, (out, block, arrived, whole, placed) = refs[:-5], refs[-5:]
        step = pl.program_id(0)

        @pl.when(step == 0)
        def _():
            for copy in pack.copies(weight_refs, whole, ids[1], placed):
                copy.start()

        grad.fetch(grad_refs, block, arrived, step)

        @pl.when(step == 0)
        def _():
            for copy in pack.copies(weight_refs, whole, ids[1], placed):
                copy.wait()

        out[...] = dot_nn(block[step % 2], whole[...]).astype(bf16)

    operands = [*grad.arrays, *pack.arrays]
    return call(
        kernel,
        "project_grad",
        (groups,),
        [ids],
        operands,
        grad.specs + pack.specs(),
        [shaped(groups * rows, width)],
        [own_block(rows, width)],
        grad.scratch() + weight_scratch(pack),
        2 * groups * rows * model * width,
    )[0]


def attention_kernel(
    info, q_ref, do_ref, k_ref, v_ref, cos, sine, ctx_ref, dq_ref, dk_ref, dv_ref, dk_sum, dv_sum
):
    tree, step = pl.program_id(0), pl.program_id(1)
    width = q_ref.shape[1]
    heads = width // HD
    lane_head = lax.broadcasted_iota(jnp.int32, (SEG, width), 1) // HD

    @pl.when(step == 0)
    def _():
        dk_sum[...] = jnp.zeros_like(dk_sum)
        dv_sum[...] = jnp.zeros_like(dv_sum)

    first, second = info[tree, step, 0], info[tree, step, 1]
    first_rows = pl.ds(pl.multiple_of(first * SEG, SEG), SEG)
    second_rows = pl.ds(pl.multiple_of(second * SEG, SEG), SEG)
    queries, grads = q_ref[...], do_ref[...]
    zero = jnp.zeros_like(queries)
    q_rows = jnp.concatenate([jnp.where(lane_head == h, queries, zero) for h in range(heads)], axis=0)
    g_rows = jnp.concatenate([jnp.where(lane_head == h, grads, zero) for h in range(heads)], axis=0)
    q_turned, g_turned = queries.T, grads.T
    ahead = lax.broadcasted_iota(jnp.int32, (SEG, SEG), 1) - lax.broadcasted_iota(
        jnp.int32, (SEG, SEG), 0
    )
    seen = jnp.concatenate([ahead <= info[tree, step, 2], ahead <= info[tree, step, 3]], axis=1)
    seen = jnp.concatenate([seen] * heads, axis=0)
    k_near = jnp.concatenate([k_ref[first_rows, :], k_ref[second_rows, :]], axis=0)
    v_near = jnp.concatenate([v_ref[first_rows, :], v_ref[second_rows, :]], axis=0)

    def work(pairs):
        count = pairs * 2 * SEG
        near = jnp.where(seen, dot_nt(q_rows, k_near), masked_score)
        most = jnp.max(near, axis=1, keepdims=True)
        if count:
            k_far, v_far = k_ref[0:count, :], v_ref[0:count, :]
            far = dot_nt(q_rows, k_far)
            most = jnp.maximum(most, jnp.max(far, axis=1, keepdims=True))
        near = jnp.exp(near - most)
        total = jnp.sum(near, axis=1, keepdims=True)
        if count:
            far = jnp.exp(far - most)
            total = total + jnp.sum(far, axis=1, keepdims=True)
        scale = 1.0 / total
        near = near * scale
        near_low = near.astype(bf16)
        context = dot_nn(near_low, v_near)
        if count:
            far = far * scale
            far_low = far.astype(bf16)
            context = context + dot_nn(far_low, v_far)
        delta = jnp.sum(context * g_rows.astype(f32), axis=1, keepdims=True)
        near = (near * (dot_nt(g_rows, v_near) - delta)).astype(bf16)
        dq = dot_nn(near, k_near)
        if count:
            far = (far * (dot_nt(g_rows, v_far) - delta)).astype(bf16)
            dq = dq + dot_nn(far, k_far)
        ctx_own, dq_own = context[0:SEG], dq[0:SEG]
        for h in range(1, heads):
            ctx_own = jnp.where(lane_head == h, context[h * SEG : (h + 1) * SEG], ctx_own)
            dq_own = jnp.where(lane_head == h, dq[h * SEG : (h + 1) * SEG], dq_own)
        ctx_ref[...] = ctx_own.astype(bf16)
        dq_ref[...] = turn(dq_own * HD**-0.5, cos, sine, -1.0).astype(bf16)
        for h in range(heads):
            own = slice(h * SEG, (h + 1) * SEG)
            part = slice(h * HD, (h + 1) * HD)
            dk = dot_nn(q_turned[part], near[own])
            dv = dot_nn(g_turned[part], near_low[own])
            dk_sum[first, part, :] += dk[:, :SEG]
            dv_sum[first, part, :] += dv[:, :SEG]
            dk_sum[second, part, :] += dk[:, SEG:]
            dv_sum[second, part, :] += dv[:, SEG:]
            if count:
                dk = dot_nn(q_turned[part], far[own])
                dv = dot_nn(g_turned[part], far_low[own])
                for j in range(2 * pairs):
                    dk_sum[j, part, :] += dk[:, j * SEG : (j + 1) * SEG]
                    dv_sum[j, part, :] += dv[:, j * SEG : (j + 1) * SEG]

    for pairs in range(NT // 2):

        @pl.when(step // 2 == pairs)
        def _(pairs=pairs):
            work(pairs)

    @pl.when(step >= NT)
    def _():
        work(NT // 2)

    @pl.when(step == NB - 1)
    def _():
        def finish(j, carry):
            rows = pl.ds(pl.multiple_of(j * SEG, SEG), SEG)
            dv_ref[rows, :] = dv_sum[j].T.astype(bf16)
            dk_ref[rows, :] = dk_sum[j].T.astype(bf16)
            return carry

        lax.fori_loop(0, NB, finish, 0)


def attention(info, tables, queries, keys, values, grads):
    total, width = queries.shape
    trees = total // TREE
    table_width = tables[0].shape[1]
    block = pl.BlockSpec((SEG, width), lambda t, b, info: (t * NB + b, 0))
    whole = pl.BlockSpec((TREE, width), lambda t, b, info: (t, 0))
    table = pl.BlockSpec((SEG, table_width), lambda t, b, info: (info[t, b, 4], 0))
    scores = trees * (TREE - TRUNK) * (TRUNK + 2 * SEG) * (width // HD)
    return call(
        attention_kernel,
        "attention",
        (trees, NB),
        [info],
        [queries, grads, keys, values, *tables],
        [block, block, whole, whole, table, table],
        [shaped(total, width)] * 4,
        [block, block, whole, whole],
        [pltpu.VMEM((NB, width, SEG), f32), pltpu.VMEM((NB, width, SEG), f32)],
        scores * width * 2 * 6 * 1.3,
        scores,
        room=22,
    )


def project_context(ids, context, pack, groups, model):
    rows, width = context.shape[0] // groups, context.shape[1]

    def kernel(ids, ctx, *refs):
        weight_refs, (send, keep, whole, placed) = refs[:-4], refs[-4:]
        step = pl.program_id(0)

        @pl.when(step == 0)
        def _():
            copies = pack.copies(weight_refs, whole, ids[1], placed)
            for copy in copies:
                copy.start()
            for copy in copies:
                copy.wait()

        store_half(send, keep, dot_nt(ctx[...], whole[...]).astype(bf16), step, groups)

    operands = [context, *pack.arrays]
    half = shaped(groups // 2, rows, model)
    return call(
        kernel,
        "project_context",
        (groups,),
        [ids],
        operands,
        [own_block(rows, width)] + pack.specs(),
        [half] * 2,
        half_blocks(groups, rows, model),
        weight_scratch(pack),
        2 * groups * rows * model * width,
        room=14,
    )


def attention_weights(ids, info, tables, context, dq, dk, dv, sent, grad, gain, shift, orders):
    groups, held, rows, model = sent.groups, len(sent.arrays), sent.rows, sent.model
    width, count = dq.shape[1], len(orders[0])

    def kernel(ids, info, ctx_ref, dq_ref, dk_ref, dv_ref, *refs):
        sent_refs, refs = refs[:held], refs[held:]
        grad_refs, refs = refs[: len(grad.arrays)], refs[len(grad.arrays) :]
        gain, shift, cos, sine, grads, bias_ref, *stacks = refs[:10]
        block, arrived, grad_block, grad_arrived, total, dense_total = refs[10:]
        step = pl.program_id(0)

        @pl.when(step == 0)
        def _():
            total[...] = jnp.zeros_like(total)
            dense_total[...] = jnp.zeros_like(dense_total)
            bias_ref[...] = jnp.zeros_like(bias_ref)

        sent.fetch(sent_refs, block, arrived, step)
        grad.fetch(grad_refs, grad_block, grad_arrived, step)
        grads[:, :width] = dq_ref[...]
        first = (ids[0] ^ ids[2 + step]) * (rows // SEG)
        for at in range(rows // SEG):
            number = first + at
            table = pl.ds(pl.multiple_of(info[number // NB, number % NB, 4] * SEG, SEG), SEG)
            own = slice(at * SEG, (at + 1) * SEG)
            turned = turn(dk_ref[own, :], cos[table, :], sine[table, :], -1.0)
            grads[own, width : 2 * width] = turned.astype(bf16)
        grads[:, 2 * width :] = dv_ref[...]
        bias_ref[0:1, :] += jnp.sum(grads[...].astype(f32), axis=0, keepdims=True)
        total[...] += dot_tn(shift_gain(block[step % 2], gain, shift), grads[...])
        dense_total[...] += dot_tn(grad_block[step % 2], ctx_ref[...])

        @pl.when(step == groups - 1)
        def _():
            store_halves(*stacks[:2], total, ids[1], orders[0], source=slice(0, 2 * width))
            source = slice(2 * width, 3 * width)
            store_halves(*stacks[2:], total, ids[1], orders[1], slice(0, width), source)
            columns = slice(width, 2 * width)
            store_halves(*stacks[2:], dense_total, ids[1], orders[1], columns)

    operands = [context, dq, dk, dv, *sent.arrays, *grad.arrays, gain, shift, *tables]
    outs = [shaped(groups * rows, 3 * width), shaped(8, 3 * width, dtype=f32)]
    outs += [shaped(count // 2, model // count, 2 * width)] * 4
    return call(
        kernel,
        "attention_weights",
        (groups,),
        [ids, info],
        operands,
        [own_block(rows, width)] * 4
        + sent.specs
        + grad.specs
        + [resident(x.shape) for x in operands[-4:]],
        outs,
        [step_block(rows, 3 * width)] + [resident(x.shape) for x in outs[1:]],
        sent.scratch()
        + grad.scratch()
        + [pltpu.VMEM((model, 3 * width), f32), pltpu.VMEM((model, width), f32)],
        2 * groups * rows * model * 4 * width,
        room=24,
    )


def mlp(ids, sent, grad, gain, shift, fc, bias, out, orders):
    groups, held, rows, model = sent.groups, len(sent.arrays), sent.rows, sent.model
    pieces, units = len(fc.arrays), fc.arrays[0].shape[1]

    def kernel(ids, *refs):
        sent_refs, refs = refs[:held], refs[held:]
        grad_refs, refs = refs[: len(grad.arrays)], refs[len(grad.arrays) :]
        fc_refs, refs = refs[:pieces], refs[pieces:]
        out_refs, refs = refs[:pieces], refs[pieces:]
        gain, shift, bias, part_send, part_keep, hidden_ref, bias_ref = refs[:7]
        stacks, refs = refs[7:11], refs[11:]
        block, arrived, grad_block, grad_arrived, fc_whole, fc_placed, out_whole, out_placed = refs[:8]
        act_ref, fc_total, out_total = refs[8:]
        step = pl.program_id(0)

        def weights():
            copies = fc.copies(fc_refs, fc_whole, ids[1], fc_placed)
            return copies + out.copies(out_refs, out_whole, ids[1], out_placed)

        @pl.when(step == 0)
        def _():
            for copy in weights():
                copy.start()
            fc_total[...] = jnp.zeros_like(fc_total)
            out_total[...] = jnp.zeros_like(out_total)
            bias_ref[...] = jnp.zeros_like(bias_ref)

        sent.fetch(sent_refs, block, arrived, step)
        grad.fetch(grad_refs, grad_block, grad_arrived, step)

        @pl.when(step == 0)
        def _():
            for copy in weights():
                copy.wait()

        token, grads = block[step % 2], grad_block[step % 2]
        normed = shift_gain(token, gain, shift)
        count = 2
        parts = [slice(k * rows // count, (k + 1) * rows // count) for k in range(count)]
        hidden = [dot_nn(normed[x], fc_whole[...]) + bias[...] for x in parts]
        back = [dot_nn(grads[x], out_whole[...]) for x in parts]
        for x, field, slope in zip(parts, hidden, back):
            chance = 0.5 + 0.5 * lax.erf(field * 0.7071067811865476)
            bell = jnp.exp(field * field * -0.5) * 0.3989422804014327
            act_ref[x, :] = (field * chance).astype(bf16)
            low = (slope * (chance + field * bell)).astype(bf16)
            hidden_ref[x, :] = low
            bias_ref[0:1, :] += jnp.sum(low.astype(f32), axis=0, keepdims=True)
        store_half(
            part_send, part_keep, dot_nt(act_ref[...], out_whole[...]).astype(bf16), step, groups
        )
        out_total[...] += dot_tn(grads, act_ref[...])
        fc_total[...] += dot_tn(normed, hidden_ref[...])

        @pl.when(step == groups - 1)
        def _():
            half = units // 2
            for at, order in enumerate(orders):
                stack = stacks[2 * at : 2 * at + 2]
                source = slice(at * half, (at + 1) * half)
                store_halves(*stack, fc_total, ids[1], order, slice(0, half), source)
                store_halves(*stack, out_total, ids[1], order, slice(half, units), source)

    operands = [*sent.arrays, *grad.arrays, *fc.arrays, *out.arrays, gain, shift, bias]
    count = model // fc.rows
    outs = [
        shaped(groups // 2, rows, model),
        shaped(groups // 2, rows, model),
        shaped(groups * rows, units),
        shaped(8, units, dtype=f32),
    ]
    outs += [shaped(count // 2, fc.rows, units)] * 4
    return call(
        kernel,
        "mlp",
        (groups,),
        [ids],
        operands,
        sent.specs
        + grad.specs
        + fc.specs()
        + out.specs()
        + [resident(x.shape) for x in operands[-3:]],
        outs,
        half_blocks(groups, rows, model)
        + [step_block(rows, units)]
        + [resident(x.shape) for x in outs[3:]],
        sent.scratch()
        + grad.scratch()
        + weight_scratch(fc)
        + weight_scratch(out)
        + [
            pltpu.VMEM((rows, units), bf16),
            pltpu.VMEM((model, units), f32),
            pltpu.VMEM((model, units), f32),
        ],
        10 * groups * rows * model * units,
        room=42,
    )


def norm_backward(ids, sent, grads, hidden, gain_attn, gain_mlp, qkv_pack, fc):
    groups, held, rows, model = sent.groups, len(sent.arrays), sent.rows, sent.model
    pieces, units, columns = len(fc.arrays), hidden.shape[1], grads.shape[1]

    def kernel(ids, grads_ref, hidden_ref, *refs):
        sent_refs, refs = refs[:held], refs[held:]
        qkv_refs, refs = refs[:pieces], refs[pieces:]
        fc_refs, refs = refs[:pieces], refs[pieces:]
        gain_attn, gain_mlp, send, keep, sums_ref = refs[:5]
        block, arrived, qkv_whole, qkv_placed, fc_whole, fc_placed = refs[5:]
        step = pl.program_id(0)

        def weights():
            copies = qkv_pack.copies(qkv_refs, qkv_whole, ids[1], qkv_placed)
            return copies + fc.copies(fc_refs, fc_whole, ids[1], fc_placed)

        @pl.when(step == 0)
        def _():
            for copy in weights():
                copy.start()
            sums_ref[...] = jnp.zeros_like(sums_ref)

        sent.fetch(sent_refs, block, arrived, step)

        @pl.when(step == 0)
        def _():
            for copy in weights():
                copy.wait()

        back_attn = dot_nt(grads_ref[...], qkv_whole[...])
        back_mlp = dot_nt(hidden_ref[...], fc_whole[...])
        token = block[step % 2].astype(f32)
        for at, back in enumerate((back_attn, back_mlp)):
            sums_ref[2 * at : 2 * at + 1, :] += jnp.sum(back * token, axis=0, keepdims=True)
            sums_ref[2 * at + 1 : 2 * at + 2, :] += jnp.sum(back, axis=0, keepdims=True)
        part = back_attn * gain_attn[...] + back_mlp * gain_mlp[...]
        store_half(send, keep, part.astype(bf16), step, groups)

    operands = [grads, hidden, *sent.arrays, *qkv_pack.arrays, *fc.arrays, gain_attn, gain_mlp]
    outs = [
        shaped(groups // 2, rows, model),
        shaped(groups // 2, rows, model),
        shaped(8, model, dtype=f32),
    ]
    return call(
        kernel,
        "norm_backward",
        (groups,),
        [ids],
        operands,
        [step_block(rows, columns), step_block(rows, units)]
        + sent.specs
        + qkv_pack.specs()
        + fc.specs()
        + [resident(x.shape) for x in operands[-2:]],
        outs,
        half_blocks(groups, rows, model) + [resident(x.shape) for x in outs[2:]],
        sent.scratch() + weight_scratch(qkv_pack) + weight_scratch(fc),
        2 * groups * rows * model * (units + columns),
        room=26,
    )


def taken(terms, block):
    return [
        pl.BlockSpec((pl.Squeezed(), block, x.shape[2]), lambda i, *_, at=at: (at, i, 0))
        for x, at in terms
    ]


def add_terms(terms, half):
    _, rows, columns = terms[0][0].shape
    block = max(x for x in (320, 128, 64) if rows % x == 0)

    def kernel(*refs):
        refs[-1][...] = sum(x[...].astype(f32) for x in refs[:-1]).astype(bf16)

    shape = (pl.Squeezed(), block, columns)
    out = shaped(half, rows, columns)
    return call(
        kernel,
        "add_terms",
        (half, rows // block),
        [],
        [x for x, _ in terms],
        [pl.BlockSpec(shape, lambda k, i, *_, at=at: (at + k, i, 0)) for _, at in terms],
        [out],
        [pl.BlockSpec(shape, lambda k, i, *_: (k, i, 0))],
        [],
        half * rows * columns * len(terms),
    )[0]


def whole_terms(terms, count):
    return [
        pl.BlockSpec((count, *x.shape[1:]), lambda *_, at=at: (at // count, 0, 0)) for x, at in terms
    ]


def add_stacks(stacks):
    counts = []
    for parts in stacks:
        parts.terms.append((parts.got, 0))
        counts.append(parts.got.shape[0] // 2)
    held = [len(parts.terms) for parts in stacks]
    operands = [x for parts in stacks for x, _ in parts.terms]

    def kernel(*refs):
        for at, half in enumerate(counts):
            first = sum(held[:at])
            total = sum(x[...].astype(f32) for x in refs[first : first + held[at]])
            refs[len(operands) + at][...] = total.astype(bf16)

    outs = [shaped(n, *parts.got.shape[1:]) for n, parts in zip(counts, stacks)]
    sends = call(
        kernel,
        "add_stacks",
        (1,),
        [],
        operands,
        [x for n, parts in zip(counts, stacks) for x in whole_terms(parts.terms, n)],
        outs,
        [resident(x.shape) for x in outs],
        [],
        sum(x.size for x in operands) // 2,
        room=16,
    )
    for n, parts, send in zip(counts, stacks, sends):
        parts.send = send
        parts.terms = [(x, at + n) for x, at in parts.terms]


def finish_mlp_weights(first, second):
    held, (_, rows, units) = len(first), first[0][0].shape
    half = units // 2

    def kernel(*refs):
        low = sum(x[0].astype(f32) for x in refs[:held])
        high = sum(x[0].astype(f32) for x in refs[held:-2])
        refs[-2][:, :half] = low[:, :half]
        refs[-2][:, half:] = high[:, :half]
        refs[-1][:half, :] = low[:, half:].T
        refs[-1][half:, :] = high[:, half:].T

    operands = [x for x, _ in [*first, *second]]
    outs = [shaped(rows, units, dtype=f32), shaped(units, rows, dtype=f32)]
    return call(
        kernel,
        "finish_mlp_weights",
        (1,),
        [],
        operands,
        whole_terms([*first, *second], 1),
        outs,
        [resident(x.shape) for x in outs],
        [],
        len(operands) * rows * units,
    )


def finish_attention_weights(first, second):
    held, (_, rows, columns) = len(first), first[0][0].shape
    width = columns // 2

    def kernel(*refs):
        low = sum(x[0].astype(f32) for x in refs[:held])
        high = sum(x[0].astype(f32) for x in refs[held:-2])
        for head in range(width // HD):
            for kind, (source, start) in enumerate(((low, 0), (low, width), (high, 0))):
                at = (3 * head + kind) * HD
                own = start + head * HD
                refs[-2][:, at : at + HD] = source[:, own : own + HD]
        refs[-1][...] = high[:, width:].T

    operands = [x for x, _ in [*first, *second]]
    outs = [shaped(rows, 3 * width, dtype=f32), shaped(width, rows, dtype=f32)]
    return call(
        kernel,
        "finish_attention_weights",
        (1,),
        [],
        operands,
        whole_terms([*first, *second], 1),
        outs,
        [resident(x.shape) for x in outs],
        [],
        len(operands) * rows * columns,
    )


def sum_rows(groups):
    return (12 + groups + 7) // 8 * 8


def finish_output(ids, stream, grad, attn_terms, mlp_terms, dense_bias, out_bias, norm_sums, fc_sums, qkv_sums, groups):
    rows, model = stream.shape
    block = 160
    first, second = len(attn_terms), len(mlp_terms)
    units, columns = fc_sums.shape[1], qkv_sums.shape[1]
    across = model // units

    def kernel(ids, stream_ref, grad_ref, *refs):
        attn_refs, refs = refs[:first], refs[first:]
        mlp_refs, refs = refs[:second], refs[second:]
        dense_bias, out_bias, norm_ref, fc_ref, qkv_ref, out_ref, sums_ref = refs

        @pl.when(pl.program_id(0) == 0)
        def _():
            sums_ref[...] = jnp.zeros_like(sums_ref)
            sums_ref[0:4, :] = norm_ref[0:4, :]
            own = jnp.concatenate([fc_ref[0:1, :]] * across, axis=1) if across > 1 else fc_ref[0:1, :]
            lane = lax.broadcasted_iota(jnp.int32, (1, model), 1) // units
            sums_ref[pl.ds(8 + ids[0] // across, 1), :] = jnp.where(lane == ids[0] % across, own, 0.0)
            sums_ref[pl.ds(12 + ids[0], 1), :columns] = qkv_ref[0:1, :]

        attn = sum(x[...].astype(f32) for x in attn_refs) + dense_bias[...]
        mlp = sum(x[...].astype(f32) for x in mlp_refs) + out_bias[...]
        output = stream_ref[...] + attn + mlp
        out_ref[...] = output
        for at, value in enumerate((output, attn, mlp)):
            sums_ref[4 + at : 5 + at, :] += jnp.sum(value * value, axis=0, keepdims=True)
        sums_ref[7:8, :] += jnp.sum(grad_ref[...].astype(f32), axis=0, keepdims=True)

    terms = [*attn_terms, *mlp_terms]
    operands = [stream, grad, *[x for x, _ in terms], dense_bias, out_bias, norm_sums, fc_sums, qkv_sums]
    outs = [shaped(rows, model, dtype=f32), shaped(sum_rows(groups), model, dtype=f32)]
    return call(
        kernel,
        "finish_output",
        (rows // block,),
        [ids],
        operands,
        [step_block(block, model), step_block(block, model)]
        + taken(terms, block)
        + [resident(x.shape) for x in operands[-5:]],
        outs,
        [step_block(block, model), resident(outs[1].shape)],
        [],
        rows * model * 16,
        room=16,
    )


def finish_grad(grad, normalized, inv_std, terms):
    rows, model = grad.shape
    block = 160

    def kernel(grad_ref, norm_ref, std_ref, *refs):
        term_refs, out_ref = refs[:-1], refs[-1]
        sent = sum(x[...].astype(f32) for x in term_refs)
        norm = norm_ref[...]
        mean = jnp.sum(sent, axis=1, keepdims=True) / model
        cross = jnp.sum(sent * norm, axis=1, keepdims=True) / model
        out_ref[...] = grad_ref[...].astype(f32) + std_ref[...] * (sent - mean - norm * cross)

    operands = [grad, normalized, inv_std, *[x for x, _ in terms]]
    return call(
        kernel,
        "finish_grad",
        (rows // block,),
        [],
        operands,
        [step_block(block, model), step_block(block, model), step_block(block, 1)]
        + taken(terms, block),
        [shaped(rows, model, dtype=f32)],
        [step_block(block, model)],
        [],
        rows * model * 12,
    )[0]


def tree_table(segment_ids, parent_ids):
    trees = segment_ids.shape[0] // TREE
    segment = segment_ids.reshape(trees, NB, SEG)[:, :, 0]
    parent = parent_ids.reshape(trees, NB, SEG)[:, :, 0]
    block = lax.broadcasted_iota(jnp.int32, (trees, NB), 1)
    trunk = block < NT
    leaf = (parent != segment[:, :1]) & ~trunk
    at = lax.broadcasted_iota(jnp.int32, (trees, NB, NB), 2)
    owner = jnp.sum(jnp.where(segment[:, None, :] == parent[:, :, None], at, 0), axis=2)
    odd = block % 2 == 1
    first = jnp.where(trunk, block // 2 * 2, block)
    second = jnp.where(trunk, block // 2 * 2 + 1, jnp.where(leaf, owner, block))
    first_most = jnp.where(trunk & odd, SEG, 0)
    second_most = jnp.where(trunk, jnp.where(odd, 0, -SEG), jnp.where(leaf, SEG, -SEG))
    table = jnp.where(trunk, block, jnp.where(leaf, NT + 1, NT))
    return jnp.stack([first, second, first_most, second_most, table], axis=2).astype(jnp.int32)


def angle_tables():
    places = TRUNK + 2 * SEG
    place = lax.broadcasted_iota(jnp.int32, (places, 2 * HD), 0).astype(f32)
    lane = lax.broadcasted_iota(jnp.int32, (places, 2 * HD), 1) % HD
    half = ROT // 2
    frequency = 10000.0 ** (-((lane % half).astype(f32) * 2.0 / ROT))
    angle = place * frequency
    cosine = jnp.where(lane < ROT, jnp.cos(angle), 1.0)
    sine = jnp.where(lane < ROT, jnp.sin(angle), 0.0)
    return cosine, sine


def by_kind(array, heads):
    shape = array.shape[:-1]
    array = array.reshape(*shape, heads, 3, HD)
    return jnp.swapaxes(array, -3, -2).reshape(*shape, 3 * heads * HD)


def by_head(array, heads):
    shape = array.shape[:-1]
    array = array.reshape(*shape, 3, heads, HD)
    return jnp.swapaxes(array, -3, -2).reshape(*shape, 3 * heads * HD)


def local(
    stream_in,
    segment_ids,
    parent_ids,
    norm_gain_attn,
    norm_shift_attn,
    norm_gain_mlp,
    norm_shift_mlp,
    qkv_weight,
    qkv_bias,
    dense_weight,
    dense_bias,
    fc_weight,
    fc_bias,
    out_weight,
    out_bias,
    out_grad,
):
    tensor_rank = lax.axis_index("tensor")
    data_rank = lax.axis_index("dp")
    rows_local = stream_in.shape[0]
    model = stream_in.shape[1]
    qkv_width = qkv_weight.shape[1]
    heads = qkv_width // (3 * HD)
    width = heads * HD
    units = fc_weight.shape[1]
    groups = lax.axis_size("tensor")
    tensor_bits = bits_of(groups)
    far_first = tensor_bits[:0:-1] + tensor_bits[:1]
    order = halving_order(tensor_bits)
    ids = jnp.stack([tensor_rank, data_rank, *order]).astype(jnp.int32)
    data_bits = bits_of(lax.axis_size("dp"))
    rows_first = data_bits[:0:-1] + data_bits[:1]
    columns_first = data_bits[:1] + data_bits[:0:-1]
    near_bits = data_bits
    next_bits = data_bits[1:2] + data_bits[:1] + data_bits[2:]

    blocks = prepare_weights(qkv_weight, dense_weight, fc_weight, out_weight)
    qkv_pack = Pack(blocks[0], "dp", rows_first)
    dense_pack = Pack(blocks[1], "dp", columns_first)
    fc_pack = Pack(blocks[2], "dp", rows_first)
    out_pack = Pack(blocks[3], "dp", rows_first)

    sent_norm, normalized, inv_std = normalize(stream_in)
    sent = gather_far(sent_norm, "tensor", tensor_bits)

    info = tree_table(segment_ids, parent_ids)
    tables = angle_tables()
    gain_attn, shift_attn = norm_gain_attn[None, :], norm_shift_attn[None, :]
    gain_mlp, shift_mlp = norm_gain_mlp[None, :], norm_shift_mlp[None, :]
    qkv_bias_own = by_kind(
        lax.dynamic_slice_in_dim(qkv_bias, tensor_rank * qkv_width, qkv_width), heads
    )[None, :]
    fc_bias_own = lax.dynamic_slice_in_dim(fc_bias, tensor_rank * units, units)[None, :]

    sent_near, near = swap(sent[0], "tensor", 1), swap(out_grad, "tensor", 1)
    cut = rows_local * 3 // 5
    early, late = out_grad[:cut], out_grad[cut:]
    qkv_pack.double()
    dense_pack.double()
    near, early, late = tie_packs(qkv_pack, dense_pack, fc_pack, beside=[near, early, late])
    while len(qkv_pack.bits) > 1:
        qkv_pack.double()
        dense_pack.double()
    fc_pack.double()
    done = tie_packs(
        qkv_pack,
        dense_pack,
        out_pack,
        beside=[early, late, info, *tables, qkv_bias_own, fc_bias_own, sent_near, *sent],
    )
    early, late, info, *done = done
    tables, (qkv_bias_own, fc_bias_own, sent_near), sent = done[:2], done[2:5], done[5:]
    early_far = gather_far(early, "tensor", tensor_bits)[1:]
    sent_near = [sent_near] + [swap(x, "tensor", 1) for x in sent[1:]]
    sent = [x for pair in zip(sent, sent_near) for x in pair]
    qkv_pack.double()
    dense_pack.double()
    late, *done = tie_packs(
        qkv_pack, dense_pack, fc_pack, out_pack, beside=[late, *sent, *early_far]
    )
    sent, early_far = Tokens([(x,) for x in done[:groups]], order), done[groups:]
    late_far = gather_far(late, "tensor", tensor_bits)[1:]
    early_near = [swap(x, "tensor", 1) for x in early_far]
    out_pack.double()
    while len(fc_pack.bits) > 1:
        fc_pack.double()

    done = project_qkv(
        ids, info, sent, gain_attn, shift_attn, qkv_pack, qkv_bias_own, tables, width
    )
    done = tie_packs(fc_pack, out_pack, beside=[*done, *early_near, *late_far])
    (queries, keys, values), done = done[:3], done[3:]
    early_near, late_far = done[: groups // 2 - 1], done[groups // 2 - 1 :]
    late_near = [swap(x, "tensor", 1) for x in late_far]
    far = zip(zip(early_far, late_far), zip(early_near, late_near))
    grad = Tokens([(out_grad,), (near,), *[x for pair in far for x in pair]], order)
    while len(out_pack.bits) > 1:
        out_pack.double()
    (grad_context,) = tie_packs(out_pack, beside=[project_grad(ids, grad, dense_pack, width)])
    fc_pack.double()
    out_pack.double()
    done = attention(info, tables, queries, keys, values, grad_context)
    context, dq, dk, dv = tie_packs(fc_pack, out_pack, beside=done)
    dp_orders = [halving_order(near_bits), halving_order(next_bits)]
    attn_parts = Halving(
        *project_context(ids, context, dense_pack, groups, model), "tensor", tensor_bits
    )
    while len(attn_parts.bits) > 2:
        attn_parts.swap()
        attn_parts.add()
    attn_parts.send, context = tie(attn_parts.send, context)
    attn_parts.swap()
    done = attention_weights(
        ids, info, tables, context, dq, dk, dv, sent, grad, gain_attn, shift_attn, dp_orders
    )
    grads, qkv_bias_sums, *stacks = tie_halves(done, attn_parts)
    attn_parts.add()
    qkv_sums = [Halving(*stacks[:2], "dp", near_bits), Halving(*stacks[2:], "dp", next_bits)]
    sent.arrays[0], attn_parts.send = tie(sent.arrays[0], attn_parts.send)
    attn_parts.swap()
    for parts in qkv_sums:
        parts.swap()
    done = mlp(
        ids, sent, grad, gain_mlp, shift_mlp, fc_pack, fc_bias_own, out_pack, dp_orders
    )
    done = tie_halves(done, attn_parts, *qkv_sums)
    mlp_send, mlp_keep, hidden, fc_bias_sums, *stacks = done
    attn_parts.add()
    mlp_parts = Halving(mlp_send, mlp_keep, "tensor", tensor_bits)
    mlp_sums = [Halving(*stacks[:2], "dp", near_bits), Halving(*stacks[2:], "dp", next_bits)]
    while len(mlp_parts.bits) > 2:
        mlp_parts.swap()
        mlp_parts.add()
    mlp_parts.swap()
    add_stacks(qkv_sums)
    mlp_parts.add()
    hidden, mlp_parts.send = tie(hidden, mlp_parts.send)
    mlp_parts.swap()
    for parts in qkv_sums + mlp_sums:
        parts.swap()
    done = norm_backward(ids, sent, grads, hidden, gain_attn, gain_mlp, qkv_pack, fc_pack)
    done = tie_halves(done, mlp_parts, *qkv_sums, *mlp_sums)
    back_send, back_keep, norm_sums = done
    mlp_parts.add()

    back_parts = Halving(back_send, back_keep, "tensor", tensor_bits)
    while len(back_parts.bits) > 2:
        back_parts.swap()
        back_parts.add()
    back_parts.swap()
    add_stacks(qkv_sums + mlp_sums)

    back_parts.add()
    stream_in, back_parts.send = tie(stream_in, back_parts.send)
    back_parts.swap()
    for parts in qkv_sums + mlp_sums:
        parts.swap()
    output, sums = finish_output(
        ids,
        stream_in,
        out_grad,
        attn_parts.terms,
        mlp_parts.terms,
        dense_bias[None, :],
        out_bias[None, :],
        norm_sums,
        fc_bias_sums,
        qkv_bias_sums,
        groups,
    )

    output, sums = tie_halves([output, sums], *qkv_sums)
    for parts in qkv_sums:
        parts.add()

    sums = sums + swap(sums, "tensor", 1)
    (sums,) = tie_halves([sums], *mlp_sums)
    add_stacks(mlp_sums)
    sums, *sends = tie(sums, *[parts.send for parts in mlp_sums])
    for parts, send in zip(mlp_sums, sends):
        parts.send = send
    for bit in data_bits[::-1]:
        sums = sums + swap(sums, "dp", bit)
    sums, back_parts.got = tie(sums, back_parts.got)
    back_parts.add()
    for bit in tensor_bits[1:]:
        sums = sums + swap(sums, "tensor", bit)
    stream_grad = finish_grad(out_grad, normalized, inv_std, back_parts.terms)

    fc_weight_grad, out_weight_grad = finish_mlp_weights(*[x.finish() for x in mlp_sums])
    qkv_weight_grad, dense_weight_grad = finish_attention_weights(*[x.finish() for x in qkv_sums])

    count_all = float(rows_local * lax.axis_size("dp") * groups * model)
    gain_attn_grad, shift_attn_grad, gain_mlp_grad, shift_mlp_grad = (sums[x] for x in range(4))
    root_squares = jnp.sqrt(jnp.sum(sums[4:7], axis=1) / count_all)
    residual_grad = sums[7]
    fc_bias_grad = sums[8:12].reshape(-1)
    qkv_bias_grad = by_head(sums[12 : 12 + groups, :qkv_width], heads).reshape(-1)
    return (
        output,
        stream_grad,
        gain_attn_grad,
        shift_attn_grad,
        gain_mlp_grad,
        shift_mlp_grad,
        qkv_weight_grad,
        qkv_bias_grad,
        dense_weight_grad,
        residual_grad,
        fc_weight_grad,
        fc_bias_grad,
        out_weight_grad,
        residual_grad,
        root_squares,
    )


def solution(mesh):
    tokens, weights, rows, whole = (
        P(("dp", "tensor"), None),
        P("dp", "tensor"),
        P("tensor", "dp"),
        P(),
    )
    return jax.shard_map(
        local,
        mesh=mesh,
        in_specs=(
            tokens,
            P("dp"),
            P("dp"),
            whole,
            whole,
            whole,
            whole,
            weights,
            whole,
            rows,
            whole,
            weights,
            whole,
            rows,
            whole,
            tokens,
        ),
        out_specs=(
            tokens,
            tokens,
            whole,
            whole,
            whole,
            whole,
            weights,
            whole,
            rows,
            whole,
            weights,
            whole,
            rows,
            whole,
            whole,
        ),
        check_vma=False,
    )
```

```python
import jax
import jax.numpy as jnp
from jax import lax
from jax.experimental import pallas as pl
from jax.experimental.pallas import tpu as pltpu
from jax.sharding import PartitionSpec as P

HD = 64
ROT = 16
TRUNK = 1024
SEG = 128
TREE = 2560
NB = TREE // SEG
NT = TRUNK // SEG

f32 = jnp.float32
bf16 = jnp.bfloat16
eps_norm = 1e-05
masked_score = -1e30


def dot_nn(left, right):
    return lax.dot_general(left, right, (((1,), (0,)), ((), ())), preferred_element_type=f32)


def dot_nt(left, right):
    return lax.dot_general(left, right, (((1,), (1,)), ((), ())), preferred_element_type=f32)


def dot_tn(left, right):
    return lax.dot_general(left, right, (((0,), (0,)), ((), ())), preferred_element_type=f32)


def bits_of(size):
    bits = []
    bit = 1
    while bit < size:
        bits.append(bit)
        bit *= 2
    return bits


def swap(block, axis, bit):
    size = lax.axis_size(axis)
    return lax.ppermute(block, axis, [(i, i ^ bit) for i in range(size)])


def tie(*values):
    return lax.optimization_barrier(values)


def gather_far(block, axis, bits):
    pieces = [block]
    for bit in bits[1:]:
        pieces = pieces + [swap(piece, axis, bit) for piece in pieces]
    return pieces


class Pack:
    def __init__(self, block, axis, bits):
        self.rows, self.axis, self.bits = block.shape[0], axis, list(bits)
        self.arrays, self.owners = [block], [[0]]

    def double(self):
        bit = self.bits.pop(0)
        held = self.arrays[0] if len(self.arrays) == 1 else jnp.concatenate(self.arrays, axis=0)
        self.owners.append([j ^ bit for owners in self.owners for j in owners])
        self.arrays.append(swap(held, self.axis, bit))

    def specs(self):
        return [pl.BlockSpec(memory_space=pltpu.HBM)] * len(self.arrays)

    def pieces(self):
        return sum(len(owners) for owners in self.owners)

    def copies(self, refs, where, number, done):
        started = []
        for ref, owners in zip(refs, self.owners):
            for at, j in enumerate(owners):
                rows = pl.ds(pl.multiple_of((number ^ j) * self.rows, self.rows), self.rows)
                source = ref.at[pl.ds(at * self.rows, self.rows), :]
                copy = pltpu.make_async_copy(source, where.at[rows, :], done.at[len(started)])
                started.append(copy)
        return started


def tie_packs(*packs, beside=()):
    flat = tie(*beside, *[x for pack in packs for x in pack.arrays])
    at = len(beside)
    for pack in packs:
        pack.arrays = list(flat[at : at + len(pack.arrays)])
        at += len(pack.arrays)
    return list(flat[: len(beside)])


def halving_order(bits):
    if not bits:
        return [0]
    rest = halving_order(bits[1:])
    return [bits[0] ^ j for j in rest] + rest


class Halving:
    def __init__(self, send, keep, axis, bits):
        self.send, self.axis, self.bits = send, axis, list(bits)
        self.terms = [(keep, 0)]

    def swap(self):
        self.got = swap(self.send, self.axis, self.bits.pop(0))

    def add(self):
        self.terms.append((self.got, 0))
        half = self.got.shape[0] // 2
        if half:
            self.send = add_terms(self.terms, half)
            self.terms = [(x, at + half) for x, at in self.terms]

    def most(self):
        while len(self.bits) > 1:
            self.swap()
            self.add()

    def finish(self):
        while self.bits:
            self.swap()
            self.add()
        return self.terms


def tie_halves(values, *halvings):
    flat = tie(*values, *[x.got for x in halvings])
    for x, got in zip(halvings, flat[len(values) :]):
        x.got = got
    return flat[: len(values)]


def resident(shape):
    zeros = (0,) * len(shape)
    return pl.BlockSpec(shape, lambda *_: zeros, pipeline_mode=pl.Buffered(1))


def own_block(rows, columns):
    return pl.BlockSpec((rows, columns), lambda i, ids, *_: (ids[0] ^ ids[2 + i], 0))


def step_block(rows, columns):
    return pl.BlockSpec((rows, columns), lambda i, *_: (i, 0))


def half_blocks(groups, rows, columns):
    half = groups // 2
    shape = (pl.Squeezed(), rows, columns)
    return [
        pl.BlockSpec(shape, lambda i, *_: (jnp.minimum(i, half - 1), 0, 0)),
        pl.BlockSpec(shape, lambda i, *_: (jnp.maximum(i - half, 0), 0, 0)),
    ]


def store_half(send, keep, value, step, groups):
    @pl.when(step < groups // 2)
    def _():
        send[...] = value

    @pl.when(step >= groups // 2)
    def _():
        keep[...] = value


class Tokens:
    def __init__(self, blocks, order):
        blocks = [blocks[j] for j in order]
        self.groups, self.counts = len(blocks), [len(block) for block in blocks]
        self.rows, self.model = sum(x.shape[0] for x in blocks[0]), blocks[0][0].shape[1]
        self.arrays = [x for block in blocks for x in block]
        self.specs = [pl.BlockSpec(memory_space=pltpu.HBM)] * len(self.arrays)

    def scratch(self):
        return [
            pltpu.VMEM((2, self.rows, self.model), bf16),
            pltpu.SemaphoreType.DMA((2, max(self.counts))),
        ]

    def fetch(self, refs, held, done, step):
        def copies(at):
            first, start, found = sum(self.counts[:at]), 0, []
            for k, ref in enumerate(refs[first : first + self.counts[at]]):
                where = held.at[at % 2, pl.ds(start, ref.shape[0]), :]
                found.append(pltpu.make_async_copy(ref, where, done.at[at % 2, k]))
                start += ref.shape[0]
            return found

        for at in range(self.groups):

            @pl.when(step == at)
            def _(at=at):
                ahead = copies(at) if at == 0 else []
                if at + 1 < self.groups:
                    ahead = ahead + copies(at + 1)
                for copy in ahead:
                    copy.start()
                for copy in copies(at):
                    copy.wait()


def store_halves(send, keep, total, number, order, columns=slice(None), source=slice(None)):
    half, rows = send.shape[0], send.shape[1]
    for at, j in enumerate(order):
        where = send if at < half else keep
        block = total[pl.ds(pl.multiple_of((number ^ j) * rows, rows), rows), source]
        where[at % half, :, columns] = block.astype(bf16)


def call(
    kernel, name, grid, prefetch, operands, specs, outs, out_specs, scratch, flops, extra=0, room=12
):
    size = sum(x.size * x.dtype.itemsize for x in list(operands) + list(outs))
    return pl.pallas_call(
        kernel,
        grid_spec=pltpu.PrefetchScalarGridSpec(
            num_scalar_prefetch=len(prefetch),
            grid=grid,
            in_specs=specs,
            out_specs=out_specs,
            scratch_shapes=scratch,
        ),
        out_shape=outs,
        compiler_params=pltpu.CompilerParams(
            dimension_semantics=("arbitrary",) * len(grid), vmem_limit_bytes=room << 20
        ),
        cost_estimate=pl.CostEstimate(
            flops=int(flops), bytes_accessed=int(size), transcendentals=int(extra)
        ),
        name=name,
    )(*prefetch, *operands)


def shaped(*shape, dtype=bf16):
    return jax.ShapeDtypeStruct(shape, dtype)


def shift_gain(block, gain, shift):
    return (block.astype(f32) * gain[...] + shift[...]).astype(bf16)


def turn(block, cosine, sine, sign):
    width = block.shape[1]
    step = min(width, 128)
    lane = lax.broadcasted_iota(jnp.int32, (block.shape[0], step), 1) % HD
    done = []
    for start in range(0, width, step):
        part = block[:, start : start + step]
        if step == 128:
            left = pltpu.roll(part, step - ROT // 2, 1)
            right = pltpu.roll(part, ROT // 2, 1)
        else:
            left = jnp.concatenate([part[:, ROT // 2 :], part[:, : ROT // 2]], axis=1)
            right = jnp.concatenate([part[:, -ROT // 2 :], part[:, : -ROT // 2]], axis=1)
        moved = jnp.where(lane < ROT // 2, -left, right) * sine[:, :step]
        done.append(part * cosine[:, :step] + moved * sign)
    return done[0] if len(done) == 1 else jnp.concatenate(done, axis=1)


def weight_scratch(pack):
    model = pack.rows * pack.pieces()
    columns = pack.arrays[0].shape[1]
    return [pltpu.VMEM((model, columns), bf16), pltpu.SemaphoreType.DMA((pack.pieces(),))]


def prepare_weights(qkv, dense, fc, out):
    rows, columns = qkv.shape
    width = columns // 3

    def kernel(qkv_ref, dense_ref, fc_ref, out_ref, qkv_to, dense_to, fc_to, out_to):
        for head in range(width // HD):
            for kind in range(3):
                at, own = (3 * head + kind) * HD, kind * width + head * HD
                qkv_to[:, own : own + HD] = qkv_ref[:, at : at + HD].astype(bf16)
        dense_to[...] = dense_ref[...].T.astype(bf16)
        fc_to[...] = fc_ref[...].astype(bf16)
        out_to[...] = out_ref[...].T.astype(bf16)

    operands = [qkv, dense, fc, out]
    outs = [shaped(*qkv.shape), shaped(*dense.shape[::-1]), shaped(*fc.shape), shaped(*out.shape[::-1])]
    return call(
        kernel,
        "prepare_weights",
        (1,),
        [],
        operands,
        [resident(x.shape) for x in operands],
        outs,
        [resident(x.shape) for x in outs],
        [],
        rows * columns,
    )


def normalize(stream):
    rows, model = stream.shape
    block = 160

    def kernel(stream_ref, sent_ref, norm_ref, std_ref):
        field = stream_ref[...]
        centred = field - jnp.sum(field, axis=1, keepdims=True) / model
        variance = jnp.sum(centred * centred, axis=1, keepdims=True) / model
        scale = lax.rsqrt(variance + eps_norm)
        norm = centred * scale
        norm_ref[...] = norm
        sent_ref[...] = norm.astype(bf16)
        std_ref[...] = scale

    return call(
        kernel,
        "normalize",
        (rows // block,),
        [],
        [stream],
        [step_block(block, model)],
        [shaped(rows, model), shaped(rows, model, dtype=f32), shaped(rows, 1, dtype=f32)],
        [step_block(block, model), step_block(block, model), step_block(block, 1)],
        [],
        rows * model * 8,
    )


def project_qkv(ids, info, sent, gain, shift, pack, bias, tables, width):
    groups, held, rows, model = sent.groups, len(sent.arrays), sent.rows, sent.model

    def kernel(ids, info, *refs):
        sent_refs, refs = refs[:held], refs[held:]
        weight_refs, refs = refs[: len(pack.arrays)], refs[len(pack.arrays) :]
        gain, shift, bias, cos, sine, q_out, k_out, v_out = refs[:8]
        block, arrived, whole, placed, added = refs[8:]
        step = pl.program_id(0)

        @pl.when(step == 0)
        def _():
            for copy in pack.copies(weight_refs, whole, ids[1], placed):
                copy.start()

        sent.fetch(sent_refs, block, arrived, step)

        @pl.when(step == 0)
        def _():
            for copy in pack.copies(weight_refs, whole, ids[1], placed):
                copy.wait()
            own = bias[pl.ds(ids[0], 1), :]
            for head in range(width // HD):
                for kind in range(3):
                    at, to = (3 * head + kind) * HD, kind * width + head * HD
                    added[:, to : to + HD] = own[:, at : at + HD]

        token = block[step % 2]
        qkv = dot_nn(shift_gain(token, gain, shift), whole[...]) + added[...]
        first = (ids[0] ^ ids[2 + step]) * (rows // SEG)
        for at in range(rows // SEG):
            number = first + at
            table = pl.ds(pl.multiple_of(info[number // NB, number % NB, 4] * SEG, SEG), SEG)
            tabs = (cos[table, :], sine[table, :])
            own = slice(at * SEG, (at + 1) * SEG)
            q_out[own, :] = (turn(qkv[own, :width], *tabs, 1.0) * HD**-0.5).astype(bf16)
            k_out[own, :] = turn(qkv[own, width : 2 * width], *tabs, 1.0).astype(bf16)
        v_out[...] = qkv[:, 2 * width :].astype(bf16)

    operands = [*sent.arrays, *pack.arrays, gain, shift, bias, *tables]
    out = shaped(groups * rows, width)
    return call(
        kernel,
        "project_qkv",
        (groups,),
        [ids, info],
        operands,
        sent.specs
        + pack.specs()
        + [resident(x.shape) for x in operands[held + len(pack.arrays) :]],
        [out] * 3,
        [own_block(rows, width)] * 3,
        sent.scratch() + weight_scratch(pack) + [pltpu.VMEM((1, 3 * width), f32)],
        2 * groups * rows * model * 3 * width,
        room=62,
    )


def project_grad(ids, grad, pack, width):
    groups, held, rows, model = grad.groups, len(grad.arrays), grad.rows, grad.model

    def kernel(ids, *refs):
        grad_refs, refs = refs[:held], refs[held:]
        weight_refs, (out, block, arrived, whole, placed) = refs[:-5], refs[-5:]
        step = pl.program_id(0)

        @pl.when(step == 0)
        def _():
            for copy in pack.copies(weight_refs, whole, ids[1], placed):
                copy.start()

        grad.fetch(grad_refs, block, arrived, step)

        @pl.when(step == 0)
        def _():
            for copy in pack.copies(weight_refs, whole, ids[1], placed):
                copy.wait()

        out[...] = dot_nn(block[step % 2], whole[...]).astype(bf16)

    operands = [*grad.arrays, *pack.arrays]
    return call(
        kernel,
        "project_grad",
        (groups,),
        [ids],
        operands,
        grad.specs + pack.specs(),
        [shaped(groups * rows, width)],
        [own_block(rows, width)],
        grad.scratch() + weight_scratch(pack),
        2 * groups * rows * model * width,
    )[0]


def attention_kernel(
    info, q_ref, do_ref, k_ref, v_ref, cos, sine, ctx_ref, dq_ref, dk_ref, dv_ref, dk_sum, dv_sum
):
    tree, step = pl.program_id(0), pl.program_id(1)
    width = q_ref.shape[1]
    heads = width // HD
    lane_head = lax.broadcasted_iota(jnp.int32, (SEG, width), 1) // HD

    @pl.when(step == 0)
    def _():
        dk_sum[...] = jnp.zeros_like(dk_sum)
        dv_sum[...] = jnp.zeros_like(dv_sum)

    first, second = info[tree, step, 0], info[tree, step, 1]
    first_rows = pl.ds(pl.multiple_of(first * SEG, SEG), SEG)
    second_rows = pl.ds(pl.multiple_of(second * SEG, SEG), SEG)
    queries, grads = q_ref[...], do_ref[...]
    zero = jnp.zeros_like(queries)
    q_rows = jnp.concatenate([jnp.where(lane_head == h, queries, zero) for h in range(heads)], axis=0)
    g_rows = jnp.concatenate([jnp.where(lane_head == h, grads, zero) for h in range(heads)], axis=0)
    q_turned, g_turned = queries.T, grads.T
    ahead = lax.broadcasted_iota(jnp.int32, (SEG, SEG), 1) - lax.broadcasted_iota(
        jnp.int32, (SEG, SEG), 0
    )
    seen = jnp.concatenate([ahead <= info[tree, step, 2], ahead <= info[tree, step, 3]], axis=1)
    seen = jnp.concatenate([seen] * heads, axis=0)
    k_near = jnp.concatenate([k_ref[first_rows, :], k_ref[second_rows, :]], axis=0)
    v_near = jnp.concatenate([v_ref[first_rows, :], v_ref[second_rows, :]], axis=0)

    def work(pairs):
        count = pairs * 2 * SEG
        near = jnp.where(seen, dot_nt(q_rows, k_near), masked_score)
        most = jnp.max(near, axis=1, keepdims=True)
        if count:
            k_far, v_far = k_ref[0:count, :], v_ref[0:count, :]
            far = dot_nt(q_rows, k_far)
            most = jnp.maximum(most, jnp.max(far, axis=1, keepdims=True))
        near = jnp.exp(near - most)
        total = jnp.sum(near, axis=1, keepdims=True)
        if count:
            far = jnp.exp(far - most)
            total = total + jnp.sum(far, axis=1, keepdims=True)
        scale = 1.0 / total
        near = near * scale
        near_low = near.astype(bf16)
        context = dot_nn(near_low, v_near)
        if count:
            far = far * scale
            far_low = far.astype(bf16)
            context = context + dot_nn(far_low, v_far)
        delta = jnp.sum(context * g_rows.astype(f32), axis=1, keepdims=True)
        near = (near * (dot_nt(g_rows, v_near) - delta)).astype(bf16)
        dq = dot_nn(near, k_near)
        if count:
            far = (far * (dot_nt(g_rows, v_far) - delta)).astype(bf16)
            dq = dq + dot_nn(far, k_far)
        ctx_own, dq_own = context[0:SEG], dq[0:SEG]
        for h in range(1, heads):
            ctx_own = jnp.where(lane_head == h, context[h * SEG : (h + 1) * SEG], ctx_own)
            dq_own = jnp.where(lane_head == h, dq[h * SEG : (h + 1) * SEG], dq_own)
        ctx_ref[...] = ctx_own.astype(bf16)
        dq_ref[...] = turn(dq_own * HD**-0.5, cos, sine, -1.0).astype(bf16)
        for h in range(heads):
            own = slice(h * SEG, (h + 1) * SEG)
            part = slice(h * HD, (h + 1) * HD)
            dk = dot_nn(q_turned[part], near[own])
            dv = dot_nn(g_turned[part], near_low[own])
            dk_sum[first, part, :] += dk[:, :SEG]
            dv_sum[first, part, :] += dv[:, :SEG]
            dk_sum[second, part, :] += dk[:, SEG:]
            dv_sum[second, part, :] += dv[:, SEG:]
            if count:
                dk = dot_nn(q_turned[part], far[own])
                dv = dot_nn(g_turned[part], far_low[own])
                for j in range(2 * pairs):
                    dk_sum[j, part, :] += dk[:, j * SEG : (j + 1) * SEG]
                    dv_sum[j, part, :] += dv[:, j * SEG : (j + 1) * SEG]

    for pairs in range(NT // 2):

        @pl.when(step // 2 == pairs)
        def _(pairs=pairs):
            work(pairs)

    @pl.when(step >= NT)
    def _():
        work(NT // 2)

    @pl.when(step == NB - 1)
    def _():
        def finish(j, carry):
            rows = pl.ds(pl.multiple_of(j * SEG, SEG), SEG)
            dv_ref[rows, :] = dv_sum[j].T.astype(bf16)
            dk_ref[rows, :] = dk_sum[j].T.astype(bf16)
            return carry

        lax.fori_loop(0, NB, finish, 0)


def attention(info, tables, queries, keys, values, grads):
    total, width = queries.shape
    trees = total // TREE
    table_width = tables[0].shape[1]
    block = pl.BlockSpec((SEG, width), lambda t, b, info: (t * NB + b, 0))
    whole = pl.BlockSpec((TREE, width), lambda t, b, info: (t, 0))
    table = pl.BlockSpec((SEG, table_width), lambda t, b, info: (info[t, b, 4], 0))
    scores = trees * (TREE - TRUNK) * (TRUNK + 2 * SEG) * (width // HD)
    return call(
        attention_kernel,
        "attention",
        (trees, NB),
        [info],
        [queries, grads, keys, values, *tables],
        [block, block, whole, whole, table, table],
        [shaped(total, width)] * 4,
        [block, block, whole, whole],
        [pltpu.VMEM((NB, width, SEG), f32), pltpu.VMEM((NB, width, SEG), f32)],
        scores * width * 2 * 6 * 1.3,
        scores,
        room=22,
    )


def project_context(ids, context, pack, groups, model):
    rows, width = context.shape[0] // groups, context.shape[1]

    def kernel(ids, ctx, *refs):
        weight_refs, (send, keep, whole, placed) = refs[:-4], refs[-4:]
        step = pl.program_id(0)

        @pl.when(step == 0)
        def _():
            copies = pack.copies(weight_refs, whole, ids[1], placed)
            for copy in copies:
                copy.start()
            for copy in copies:
                copy.wait()

        store_half(send, keep, dot_nt(ctx[...], whole[...]).astype(bf16), step, groups)

    operands = [context, *pack.arrays]
    half = shaped(groups // 2, rows, model)
    return call(
        kernel,
        "project_context",
        (groups,),
        [ids],
        operands,
        [own_block(rows, width)] + pack.specs(),
        [half] * 2,
        half_blocks(groups, rows, model),
        weight_scratch(pack),
        2 * groups * rows * model * width,
        room=14,
    )


def attention_weights(ids, info, tables, context, dq, dk, dv, sent, grad, gain, shift, orders):
    groups, held, rows, model = sent.groups, len(sent.arrays), sent.rows, sent.model
    width, count = dq.shape[1], len(orders[0])

    def kernel(ids, info, ctx_ref, dq_ref, dk_ref, dv_ref, *refs):
        sent_refs, refs = refs[:held], refs[held:]
        grad_refs, refs = refs[: len(grad.arrays)], refs[len(grad.arrays) :]
        gain, shift, cos, sine, grads, bias_ref, *stacks = refs[:10]
        block, arrived, grad_block, grad_arrived, total, dense_total = refs[10:]
        step = pl.program_id(0)

        @pl.when(step == 0)
        def _():
            total[...] = jnp.zeros_like(total)
            dense_total[...] = jnp.zeros_like(dense_total)
            bias_ref[...] = jnp.zeros_like(bias_ref)

        sent.fetch(sent_refs, block, arrived, step)
        grad.fetch(grad_refs, grad_block, grad_arrived, step)
        grads[:, :width] = dq_ref[...]
        first = (ids[0] ^ ids[2 + step]) * (rows // SEG)
        for at in range(rows // SEG):
            number = first + at
            table = pl.ds(pl.multiple_of(info[number // NB, number % NB, 4] * SEG, SEG), SEG)
            own = slice(at * SEG, (at + 1) * SEG)
            turned = turn(dk_ref[own, :], cos[table, :], sine[table, :], -1.0)
            grads[own, width : 2 * width] = turned.astype(bf16)
        grads[:, 2 * width :] = dv_ref[...]
        bias_ref[0:1, :] += jnp.sum(grads[...].astype(f32), axis=0, keepdims=True)
        total[...] += dot_tn(shift_gain(block[step % 2], gain, shift), grads[...])
        dense_total[...] += dot_tn(grad_block[step % 2], ctx_ref[...])

        @pl.when(step == groups - 1)
        def _():
            store_halves(*stacks[:2], total, ids[1], orders[0], source=slice(0, 2 * width))
            source = slice(2 * width, 3 * width)
            store_halves(*stacks[2:], total, ids[1], orders[1], slice(0, width), source)
            columns = slice(width, 2 * width)
            store_halves(*stacks[2:], dense_total, ids[1], orders[1], columns)

    operands = [context, dq, dk, dv, *sent.arrays, *grad.arrays, gain, shift, *tables]
    outs = [shaped(groups * rows, 3 * width), shaped(8, 3 * width, dtype=f32)]
    outs += [shaped(count // 2, model // count, 2 * width)] * 4
    return call(
        kernel,
        "attention_weights",
        (groups,),
        [ids, info],
        operands,
        [own_block(rows, width)] * 4
        + sent.specs
        + grad.specs
        + [resident(x.shape) for x in operands[-4:]],
        outs,
        [step_block(rows, 3 * width)] + [resident(x.shape) for x in outs[1:]],
        sent.scratch()
        + grad.scratch()
        + [pltpu.VMEM((model, 3 * width), f32), pltpu.VMEM((model, width), f32)],
        2 * groups * rows * model * 4 * width,
        room=24,
    )


def mlp(ids, sent, grad, gain, shift, fc, bias, out, orders):
    groups, held, rows, model = sent.groups, len(sent.arrays), sent.rows, sent.model
    pieces, units = len(fc.arrays), fc.arrays[0].shape[1]

    def kernel(ids, *refs):
        sent_refs, refs = refs[:held], refs[held:]
        grad_refs, refs = refs[: len(grad.arrays)], refs[len(grad.arrays) :]
        fc_refs, refs = refs[:pieces], refs[pieces:]
        out_refs, refs = refs[:pieces], refs[pieces:]
        gain, shift, bias, part_send, part_keep, hidden_ref, bias_ref = refs[:7]
        stacks, refs = refs[7:11], refs[11:]
        block, arrived, grad_block, grad_arrived, fc_whole, fc_placed, out_whole, out_placed = refs[:8]
        act_ref, fc_total, out_total = refs[8:]
        step = pl.program_id(0)

        def weights():
            copies = fc.copies(fc_refs, fc_whole, ids[1], fc_placed)
            return copies + out.copies(out_refs, out_whole, ids[1], out_placed)

        @pl.when(step == 0)
        def _():
            for copy in weights():
                copy.start()
            fc_total[...] = jnp.zeros_like(fc_total)
            out_total[...] = jnp.zeros_like(out_total)
            bias_ref[...] = jnp.zeros_like(bias_ref)

        sent.fetch(sent_refs, block, arrived, step)
        grad.fetch(grad_refs, grad_block, grad_arrived, step)

        @pl.when(step == 0)
        def _():
            for copy in weights():
                copy.wait()

        token, grads = block[step % 2], grad_block[step % 2]
        normed = shift_gain(token, gain, shift)
        count = 2
        parts = [slice(k * rows // count, (k + 1) * rows // count) for k in range(count)]
        added = bias[pl.ds(ids[0], 1), :]
        hidden = [dot_nn(normed[x], fc_whole[...]) + added for x in parts]
        back = [dot_nn(grads[x], out_whole[...]) for x in parts]
        for x, field, slope in zip(parts, hidden, back):
            chance = 0.5 + 0.5 * lax.erf(field * 0.7071067811865476)
            bell = jnp.exp(field * field * -0.5) * 0.3989422804014327
            act_ref[x, :] = (field * chance).astype(bf16)
            low = (slope * (chance + field * bell)).astype(bf16)
            hidden_ref[x, :] = low
            bias_ref[0:1, :] += jnp.sum(low.astype(f32), axis=0, keepdims=True)
        store_half(
            part_send, part_keep, dot_nt(act_ref[...], out_whole[...]).astype(bf16), step, groups
        )
        out_total[...] += dot_tn(grads, act_ref[...])
        fc_total[...] += dot_tn(normed, hidden_ref[...])

        @pl.when(step == groups - 1)
        def _():
            half = units // 2
            for at, order in enumerate(orders):
                stack = stacks[2 * at : 2 * at + 2]
                source = slice(at * half, (at + 1) * half)
                store_halves(*stack, fc_total, ids[1], order, slice(0, half), source)
                store_halves(*stack, out_total, ids[1], order, slice(half, units), source)

    operands = [*sent.arrays, *grad.arrays, *fc.arrays, *out.arrays, gain, shift, bias]
    count = model // fc.rows
    outs = [
        shaped(groups // 2, rows, model),
        shaped(groups // 2, rows, model),
        shaped(groups * rows, units),
        shaped(8, units, dtype=f32),
    ]
    outs += [shaped(count // 2, fc.rows, units)] * 4
    return call(
        kernel,
        "mlp",
        (groups,),
        [ids],
        operands,
        sent.specs
        + grad.specs
        + fc.specs()
        + out.specs()
        + [resident(x.shape) for x in operands[-3:]],
        outs,
        half_blocks(groups, rows, model)
        + [step_block(rows, units)]
        + [resident(x.shape) for x in outs[3:]],
        sent.scratch()
        + grad.scratch()
        + weight_scratch(fc)
        + weight_scratch(out)
        + [
            pltpu.VMEM((rows, units), bf16),
            pltpu.VMEM((model, units), f32),
            pltpu.VMEM((model, units), f32),
        ],
        10 * groups * rows * model * units,
        room=42,
    )


def norm_backward(ids, sent, grads, hidden, gain_attn, gain_mlp, qkv_pack, fc):
    groups, held, rows, model = sent.groups, len(sent.arrays), sent.rows, sent.model
    pieces, units, columns = len(fc.arrays), hidden.shape[1], grads.shape[1]

    def kernel(ids, grads_ref, hidden_ref, *refs):
        sent_refs, refs = refs[:held], refs[held:]
        qkv_refs, refs = refs[:pieces], refs[pieces:]
        fc_refs, refs = refs[:pieces], refs[pieces:]
        gain_attn, gain_mlp, send, keep, sums_ref = refs[:5]
        block, arrived, qkv_whole, qkv_placed, fc_whole, fc_placed = refs[5:]
        step = pl.program_id(0)

        def weights():
            copies = qkv_pack.copies(qkv_refs, qkv_whole, ids[1], qkv_placed)
            return copies + fc.copies(fc_refs, fc_whole, ids[1], fc_placed)

        @pl.when(step == 0)
        def _():
            for copy in weights():
                copy.start()
            sums_ref[...] = jnp.zeros_like(sums_ref)

        sent.fetch(sent_refs, block, arrived, step)

        @pl.when(step == 0)
        def _():
            for copy in weights():
                copy.wait()

        back_attn = dot_nt(grads_ref[...], qkv_whole[...])
        back_mlp = dot_nt(hidden_ref[...], fc_whole[...])
        token = block[step % 2].astype(f32)
        for at, back in enumerate((back_attn, back_mlp)):
            sums_ref[2 * at : 2 * at + 1, :] += jnp.sum(back * token, axis=0, keepdims=True)
            sums_ref[2 * at + 1 : 2 * at + 2, :] += jnp.sum(back, axis=0, keepdims=True)
        part = back_attn * gain_attn[...] + back_mlp * gain_mlp[...]
        store_half(send, keep, part.astype(bf16), step, groups)

    operands = [grads, hidden, *sent.arrays, *qkv_pack.arrays, *fc.arrays, gain_attn, gain_mlp]
    outs = [
        shaped(groups // 2, rows, model),
        shaped(groups // 2, rows, model),
        shaped(8, model, dtype=f32),
    ]
    return call(
        kernel,
        "norm_backward",
        (groups,),
        [ids],
        operands,
        [step_block(rows, columns), step_block(rows, units)]
        + sent.specs
        + qkv_pack.specs()
        + fc.specs()
        + [resident(x.shape) for x in operands[-2:]],
        outs,
        half_blocks(groups, rows, model) + [resident(x.shape) for x in outs[2:]],
        sent.scratch() + weight_scratch(qkv_pack) + weight_scratch(fc),
        2 * groups * rows * model * (units + columns),
        room=26,
    )


def taken(terms, block):
    return [
        pl.BlockSpec((pl.Squeezed(), block, x.shape[2]), lambda i, *_, at=at: (at, i, 0))
        for x, at in terms
    ]


def add_terms(terms, half):
    _, rows, columns = terms[0][0].shape
    block = max(x for x in (320, 128, 64) if rows % x == 0)

    def kernel(*refs):
        refs[-1][...] = sum(x[...].astype(f32) for x in refs[:-1]).astype(bf16)

    shape = (pl.Squeezed(), block, columns)
    out = shaped(half, rows, columns)
    return call(
        kernel,
        "add_terms",
        (half, rows // block),
        [],
        [x for x, _ in terms],
        [pl.BlockSpec(shape, lambda k, i, *_, at=at: (at + k, i, 0)) for _, at in terms],
        [out],
        [pl.BlockSpec(shape, lambda k, i, *_: (k, i, 0))],
        [],
        half * rows * columns * len(terms),
    )[0]


def whole_terms(terms, count):
    return [
        pl.BlockSpec((count, *x.shape[1:]), lambda *_, at=at: (at // count, 0, 0)) for x, at in terms
    ]


def add_stacks(stacks):
    counts = []
    for parts in stacks:
        parts.terms.append((parts.got, 0))
        counts.append(parts.got.shape[0] // 2)
    held = [len(parts.terms) for parts in stacks]
    operands = [x for parts in stacks for x, _ in parts.terms]

    def kernel(*refs):
        for at, half in enumerate(counts):
            first = sum(held[:at])
            total = sum(x[...].astype(f32) for x in refs[first : first + held[at]])
            refs[len(operands) + at][...] = total.astype(bf16)

    outs = [shaped(n, *parts.got.shape[1:]) for n, parts in zip(counts, stacks)]
    sends = call(
        kernel,
        "add_stacks",
        (1,),
        [],
        operands,
        [x for n, parts in zip(counts, stacks) for x in whole_terms(parts.terms, n)],
        outs,
        [resident(x.shape) for x in outs],
        [],
        sum(x.size for x in operands) // 2,
        room=16,
    )
    for n, parts, send in zip(counts, stacks, sends):
        parts.send = send
        parts.terms = [(x, at + n) for x, at in parts.terms]


def finish_mlp_weights(first, second):
    held, (_, rows, units) = len(first), first[0][0].shape
    half = units // 2

    def kernel(*refs):
        low = sum(x[0].astype(f32) for x in refs[:held])
        high = sum(x[0].astype(f32) for x in refs[held:-2])
        refs[-2][:, :half] = low[:, :half]
        refs[-2][:, half:] = high[:, :half]
        refs[-1][:half, :] = low[:, half:].T
        refs[-1][half:, :] = high[:, half:].T

    operands = [x for x, _ in [*first, *second]]
    outs = [shaped(rows, units, dtype=f32), shaped(units, rows, dtype=f32)]
    return call(
        kernel,
        "finish_mlp_weights",
        (1,),
        [],
        operands,
        whole_terms([*first, *second], 1),
        outs,
        [resident(x.shape) for x in outs],
        [],
        len(operands) * rows * units,
    )


def finish_attention_weights(first, second):
    held, (_, rows, columns) = len(first), first[0][0].shape
    width = columns // 2

    def kernel(*refs):
        low = sum(x[0].astype(f32) for x in refs[:held])
        high = sum(x[0].astype(f32) for x in refs[held:-2])
        for head in range(width // HD):
            for kind, (source, start) in enumerate(((low, 0), (low, width), (high, 0))):
                at = (3 * head + kind) * HD
                own = start + head * HD
                refs[-2][:, at : at + HD] = source[:, own : own + HD]
        refs[-1][...] = high[:, width:].T

    operands = [x for x, _ in [*first, *second]]
    outs = [shaped(rows, 3 * width, dtype=f32), shaped(width, rows, dtype=f32)]
    return call(
        kernel,
        "finish_attention_weights",
        (1,),
        [],
        operands,
        whole_terms([*first, *second], 1),
        outs,
        [resident(x.shape) for x in outs],
        [],
        len(operands) * rows * columns,
    )


def sum_rows(groups):
    return (12 + groups + 7) // 8 * 8


def finish_output(ids, stream, grad, attn_terms, mlp_terms, dense_bias, out_bias, norm_sums, fc_sums, qkv_sums, groups):
    rows, model = stream.shape
    block = 160
    first, second = len(attn_terms), len(mlp_terms)
    units, columns = fc_sums.shape[1], qkv_sums.shape[1]
    across = model // units

    def kernel(ids, stream_ref, grad_ref, *refs):
        attn_refs, refs = refs[:first], refs[first:]
        mlp_refs, refs = refs[:second], refs[second:]
        dense_bias, out_bias, norm_ref, fc_ref, qkv_ref, out_ref, sums_ref = refs

        @pl.when(pl.program_id(0) == 0)
        def _():
            sums_ref[...] = jnp.zeros_like(sums_ref)
            sums_ref[0:4, :] = norm_ref[0:4, :]
            own = jnp.concatenate([fc_ref[0:1, :]] * across, axis=1) if across > 1 else fc_ref[0:1, :]
            lane = lax.broadcasted_iota(jnp.int32, (1, model), 1) // units
            sums_ref[pl.ds(8 + ids[0] // across, 1), :] = jnp.where(lane == ids[0] % across, own, 0.0)
            sums_ref[pl.ds(12 + ids[0], 1), :columns] = qkv_ref[0:1, :]

        attn = sum(x[...].astype(f32) for x in attn_refs) + dense_bias[...]
        mlp = sum(x[...].astype(f32) for x in mlp_refs) + out_bias[...]
        output = stream_ref[...] + attn + mlp
        out_ref[...] = output
        for at, value in enumerate((output, attn, mlp)):
            sums_ref[4 + at : 5 + at, :] += jnp.sum(value * value, axis=0, keepdims=True)
        sums_ref[7:8, :] += jnp.sum(grad_ref[...].astype(f32), axis=0, keepdims=True)

    terms = [*attn_terms, *mlp_terms]
    operands = [stream, grad, *[x for x, _ in terms], dense_bias, out_bias, norm_sums, fc_sums, qkv_sums]
    outs = [shaped(rows, model, dtype=f32), shaped(sum_rows(groups), model, dtype=f32)]
    return call(
        kernel,
        "finish_output",
        (rows // block,),
        [ids],
        operands,
        [step_block(block, model), step_block(block, model)]
        + taken(terms, block)
        + [resident(x.shape) for x in operands[-5:]],
        outs,
        [step_block(block, model), resident(outs[1].shape)],
        [],
        rows * model * 16,
        room=16,
    )


def finish_grad(grad, normalized, inv_std, terms):
    rows, model = grad.shape
    block = 160

    def kernel(grad_ref, norm_ref, std_ref, *refs):
        term_refs, out_ref = refs[:-1], refs[-1]
        sent = sum(x[...].astype(f32) for x in term_refs)
        norm = norm_ref[...]
        mean = jnp.sum(sent, axis=1, keepdims=True) / model
        cross = jnp.sum(sent * norm, axis=1, keepdims=True) / model
        out_ref[...] = grad_ref[...].astype(f32) + std_ref[...] * (sent - mean - norm * cross)

    operands = [grad, normalized, inv_std, *[x for x, _ in terms]]
    return call(
        kernel,
        "finish_grad",
        (rows // block,),
        [],
        operands,
        [step_block(block, model), step_block(block, model), step_block(block, 1)]
        + taken(terms, block),
        [shaped(rows, model, dtype=f32)],
        [step_block(block, model)],
        [],
        rows * model * 12,
    )[0]


def tree_table(segment_ids, parent_ids):
    trees = segment_ids.shape[0] // TREE

    def kernel(segment, parent, table):
        for tree in range(trees):
            for block in range(NT):
                odd = block % 2
                row = (block - odd, block - odd + 1, SEG * odd, -SEG * (1 - odd), block)
                for at, value in enumerate(row):
                    table[tree, block, at] = value

            def place(block, carry):
                first = tree * TREE
                owner = parent[first + block * SEG]
                leaf = (owner != segment[first]).astype(jnp.int32)
                at = block
                for other in range(NT, NB):
                    at = jnp.where(segment[first + other * SEG] == owner, other, at)
                table[tree, block, 0] = block
                table[tree, block, 1] = at
                table[tree, block, 2] = 0
                table[tree, block, 3] = SEG * (2 * leaf - 1)
                table[tree, block, 4] = NT + leaf
                return carry

            lax.fori_loop(NT, NB, place, 0)

    smem = pl.BlockSpec(memory_space=pltpu.SMEM)
    return pl.pallas_call(
        kernel,
        in_specs=[smem, smem],
        out_specs=smem,
        out_shape=jax.ShapeDtypeStruct((trees, NB, 5), jnp.int32),
        name="tree_table",
    )(segment_ids, parent_ids)


def angle_tables(zero):
    places = TRUNK + 2 * SEG
    place = lax.broadcasted_iota(jnp.int32, (places, 2 * HD), 0).astype(f32)
    lane = lax.broadcasted_iota(jnp.int32, (places, 2 * HD), 1) % HD
    half = ROT // 2
    frequency = 10000.0 ** (-((lane % half).astype(f32) * 2.0 / ROT))
    angle = (place + zero) * frequency
    cosine = jnp.where(lane < ROT, jnp.cos(angle), 1.0)
    sine = jnp.where(lane < ROT, jnp.sin(angle), 0.0)
    return cosine, sine


def by_kind(array, heads):
    shape = array.shape[:-1]
    array = array.reshape(*shape, heads, 3, HD)
    return jnp.swapaxes(array, -3, -2).reshape(*shape, 3 * heads * HD)


def by_head(array, heads):
    shape = array.shape[:-1]
    array = array.reshape(*shape, 3, heads, HD)
    return jnp.swapaxes(array, -3, -2).reshape(*shape, 3 * heads * HD)


def local(
    stream_in,
    segment_ids,
    parent_ids,
    norm_gain_attn,
    norm_shift_attn,
    norm_gain_mlp,
    norm_shift_mlp,
    qkv_weight,
    qkv_bias,
    dense_weight,
    dense_bias,
    fc_weight,
    fc_bias,
    out_weight,
    out_bias,
    out_grad,
):
    tensor_rank = lax.axis_index("tensor")
    data_rank = lax.axis_index("dp")
    rows_local = stream_in.shape[0]
    model = stream_in.shape[1]
    qkv_width = qkv_weight.shape[1]
    heads = qkv_width // (3 * HD)
    width = heads * HD
    units = fc_weight.shape[1]
    groups = lax.axis_size("tensor")
    tensor_bits = bits_of(groups)
    far_first = tensor_bits[:0:-1] + tensor_bits[:1]
    order = halving_order(tensor_bits)
    ids = jnp.stack([tensor_rank, data_rank, *order]).astype(jnp.int32)
    data_bits = bits_of(lax.axis_size("dp"))
    rows_first = data_bits[:0:-1] + data_bits[:1]
    columns_first = data_bits[:1] + data_bits[:0:-1]
    near_bits = data_bits
    next_bits = data_bits[1:2] + data_bits[:1] + data_bits[2:]
    qkv_bits = [data_bits[:1] + data_bits[:0:-1], data_bits[1:2] + data_bits[2:] + data_bits[:1]]

    blocks = prepare_weights(qkv_weight, dense_weight, fc_weight, out_weight)
    qkv_pack = Pack(blocks[0], "dp", rows_first)
    dense_pack = Pack(blocks[1], "dp", columns_first)
    fc_pack = Pack(blocks[2], "dp", rows_first)
    out_pack = Pack(blocks[3], "dp", rows_first)

    sent_norm, normalized, inv_std = normalize(stream_in)
    sent = gather_far(sent_norm, "tensor", tensor_bits)

    info = tree_table(segment_ids, parent_ids)
    gain_attn, shift_attn = norm_gain_attn[None, :], norm_shift_attn[None, :]
    gain_mlp, shift_mlp = norm_gain_mlp[None, :], norm_shift_mlp[None, :]
    sent_near, near = swap(sent[0], "tensor", 1), swap(out_grad, "tensor", 1)
    cut = rows_local * 3 // 5
    early, late = out_grad[:cut], out_grad[cut:]
    qkv_pack.double()
    dense_pack.double()
    zero = jnp.zeros((), f32)
    near, early, late, zero, qkv_bias, fc_bias, info = tie_packs(
        qkv_pack, dense_pack, fc_pack, beside=[near, early, late, zero, qkv_bias, fc_bias, info]
    )
    tables = angle_tables(zero)
    qkv_rows, fc_rows = qkv_bias.reshape(groups, qkv_width), fc_bias.reshape(groups, units)
    while len(qkv_pack.bits) > 1:
        qkv_pack.double()
        dense_pack.double()
    fc_pack.double()
    done = tie_packs(
        qkv_pack,
        dense_pack,
        out_pack,
        beside=[early, late, *tables, qkv_rows, fc_rows, sent_near, *sent],
    )
    early, late, *done = done
    tables, (qkv_rows, fc_rows, sent_near), sent = done[:2], done[2:5], done[5:]
    early_far = gather_far(early, "tensor", tensor_bits)[1:]
    sent_near = [sent_near] + [swap(x, "tensor", 1) for x in sent[1:]]
    sent = [x for pair in zip(sent, sent_near) for x in pair]
    qkv_pack.double()
    dense_pack.double()
    late, *done = tie_packs(
        qkv_pack, dense_pack, fc_pack, out_pack, beside=[late, *sent, *early_far]
    )
    sent, early_far = Tokens([(x,) for x in done[:groups]], order), done[groups:]
    late_far = gather_far(late, "tensor", tensor_bits)[1:]
    early_near = [swap(x, "tensor", 1) for x in early_far]
    out_pack.double()
    while len(fc_pack.bits) > 1:
        fc_pack.double()

    done = project_qkv(
        ids, info, sent, gain_attn, shift_attn, qkv_pack, qkv_rows, tables, width
    )
    done = tie_packs(fc_pack, out_pack, beside=[*done, *early_near, *late_far])
    (queries, keys, values), done = done[:3], done[3:]
    early_near, late_far = done[: groups // 2 - 1], done[groups // 2 - 1 :]
    late_near = [swap(x, "tensor", 1) for x in late_far]
    far = zip(zip(early_far, late_far), zip(early_near, late_near))
    grad = Tokens([(out_grad,), (near,), *[x for pair in far for x in pair]], order)
    while len(out_pack.bits) > 1:
        out_pack.double()
    (grad_context,) = tie_packs(out_pack, beside=[project_grad(ids, grad, dense_pack, width)])
    fc_pack.double()
    out_pack.double()
    done = attention(info, tables, queries, keys, values, grad_context)
    context, dq, dk, dv = tie_packs(fc_pack, out_pack, beside=done)
    dp_orders = [halving_order(near_bits), halving_order(next_bits)]
    qkv_orders = [halving_order(bits) for bits in qkv_bits]
    attn_parts = Halving(
        *project_context(ids, context, dense_pack, groups, model), "tensor", tensor_bits
    )
    while len(attn_parts.bits) > 2:
        attn_parts.swap()
        attn_parts.add()
    attn_parts.send, context = tie(attn_parts.send, context)
    attn_parts.swap()
    done = attention_weights(
        ids, info, tables, context, dq, dk, dv, sent, grad, gain_attn, shift_attn, qkv_orders
    )
    grads, qkv_bias_sums, *stacks = tie_halves(done, attn_parts)
    attn_parts.add()
    qkv_sums = [Halving(*stacks[:2], "dp", qkv_bits[0]), Halving(*stacks[2:], "dp", qkv_bits[1])]
    sent.arrays[0], attn_parts.send = tie(sent.arrays[0], attn_parts.send)
    attn_parts.swap()
    for parts in qkv_sums:
        parts.swap()
    done = mlp(
        ids, sent, grad, gain_mlp, shift_mlp, fc_pack, fc_rows, out_pack, dp_orders
    )
    done = tie_halves(done, attn_parts, *qkv_sums)
    mlp_send, mlp_keep, hidden, fc_bias_sums, *stacks = done
    attn_parts.add()
    mlp_parts = Halving(mlp_send, mlp_keep, "tensor", tensor_bits)
    mlp_sums = [Halving(*stacks[:2], "dp", near_bits), Halving(*stacks[2:], "dp", next_bits)]
    while len(mlp_parts.bits) > 2:
        mlp_parts.swap()
        mlp_parts.add()
    mlp_parts.swap()
    add_stacks(qkv_sums)
    mlp_parts.add()
    hidden, mlp_parts.send = tie(hidden, mlp_parts.send)
    mlp_parts.swap()
    for parts in qkv_sums + mlp_sums:
        parts.swap()
    done = norm_backward(ids, sent, grads, hidden, gain_attn, gain_mlp, qkv_pack, fc_pack)
    done = tie_halves(done, mlp_parts, *qkv_sums, *mlp_sums)
    back_send, back_keep, norm_sums = done
    mlp_parts.add()

    back_parts = Halving(back_send, back_keep, "tensor", tensor_bits)
    while len(back_parts.bits) > 2:
        back_parts.swap()
        back_parts.add()
    back_parts.swap()
    add_stacks(qkv_sums + mlp_sums)

    back_parts.add()
    stream_in, back_parts.send = tie(stream_in, back_parts.send)
    back_parts.swap()
    for parts in qkv_sums + mlp_sums:
        parts.swap()
    output, sums = finish_output(
        ids,
        stream_in,
        out_grad,
        attn_parts.terms,
        mlp_parts.terms,
        dense_bias[None, :],
        out_bias[None, :],
        norm_sums,
        fc_bias_sums,
        qkv_bias_sums,
        groups,
    )

    output, sums = tie_halves([output, sums], *qkv_sums)
    for parts in qkv_sums:
        parts.add()

    sums = sums + swap(sums, "tensor", 1)
    (sums,) = tie_halves([sums], *mlp_sums)
    add_stacks(mlp_sums)
    for bit in data_bits[2:]:
        sums = sums + swap(sums, "dp", bit)
    sums, *sends = tie(sums, *[parts.send for parts in mlp_sums])
    for parts, send in zip(mlp_sums, sends):
        parts.send = send
    for bit in data_bits[:2]:
        sums = sums + swap(sums, "dp", bit)
    sums, back_parts.got = tie(sums, back_parts.got)
    back_parts.add()
    for bit in tensor_bits[1:]:
        sums = sums + swap(sums, "tensor", bit)
    stream_grad = finish_grad(out_grad, normalized, inv_std, back_parts.terms)

    fc_weight_grad, out_weight_grad = finish_mlp_weights(*[x.finish() for x in mlp_sums])
    qkv_weight_grad, dense_weight_grad = finish_attention_weights(*[x.finish() for x in qkv_sums])

    count_all = float(rows_local * lax.axis_size("dp") * groups * model)
    gain_attn_grad, shift_attn_grad, gain_mlp_grad, shift_mlp_grad = (sums[x] for x in range(4))
    root_squares = jnp.sqrt(jnp.sum(sums[4:7], axis=1) / count_all)
    residual_grad = sums[7]
    fc_bias_grad = sums[8:12].reshape(-1)
    qkv_bias_grad = by_head(sums[12 : 12 + groups, :qkv_width], heads).reshape(-1)
    return (
        output,
        stream_grad,
        gain_attn_grad,
        shift_attn_grad,
        gain_mlp_grad,
        shift_mlp_grad,
        qkv_weight_grad,
        qkv_bias_grad,
        dense_weight_grad,
        residual_grad,
        fc_weight_grad,
        fc_bias_grad,
        out_weight_grad,
        residual_grad,
        root_squares,
    )


def solution(mesh):
    tokens, weights, rows, whole = (
        P(("dp", "tensor"), None),
        P("dp", "tensor"),
        P("tensor", "dp"),
        P(),
    )
    return jax.shard_map(
        local,
        mesh=mesh,
        in_specs=(
            tokens,
            P("dp"),
            P("dp"),
            whole,
            whole,
            whole,
            whole,
            weights,
            whole,
            rows,
            whole,
            weights,
            whole,
            rows,
            whole,
            tokens,
        ),
        out_specs=(
            tokens,
            tokens,
            whole,
            whole,
            whole,
            whole,
            weights,
            whole,
            rows,
            whole,
            weights,
            whole,
            rows,
            whole,
            whole,
        ),
        check_vma=False,
    )
```

```python
import jax
import jax.numpy as jnp
from jax import lax
from jax.experimental import pallas as pl
from jax.experimental.pallas import tpu as pltpu
from jax.sharding import PartitionSpec as P

HD = 64
ROT = 16
TRUNK = 1024
SEG = 128
TREE = 2560
NB = TREE // SEG
NT = TRUNK // SEG

f32 = jnp.float32
bf16 = jnp.bfloat16
eps_norm = 1e-05
masked_score = -1e30


def dot_nn(left, right):
    return lax.dot_general(left, right, (((1,), (0,)), ((), ())), preferred_element_type=f32)


def dot_nt(left, right):
    return lax.dot_general(left, right, (((1,), (1,)), ((), ())), preferred_element_type=f32)


def dot_tn(left, right):
    return lax.dot_general(left, right, (((0,), (0,)), ((), ())), preferred_element_type=f32)


def bits_of(size):
    bits = []
    bit = 1
    while bit < size:
        bits.append(bit)
        bit *= 2
    return bits


def swap(block, axis, bit):
    size = lax.axis_size(axis)
    return lax.ppermute(block, axis, [(i, i ^ bit) for i in range(size)])


def tie(*values):
    return lax.optimization_barrier(values)


def gather_far(block, axis, bits):
    pieces = [block]
    for bit in bits[1:]:
        pieces = pieces + [swap(piece, axis, bit) for piece in pieces]
    return pieces


class Pack:
    def __init__(self, block, axis, bits):
        self.rows, self.axis, self.bits = block.shape[0], axis, list(bits)
        self.arrays, self.owners = [block], [[0]]

    def double(self):
        bit = self.bits.pop(0)
        held = self.arrays[0] if len(self.arrays) == 1 else jnp.concatenate(self.arrays, axis=0)
        self.owners.append([j ^ bit for owners in self.owners for j in owners])
        self.arrays.append(swap(held, self.axis, bit))

    def specs(self):
        return [pl.BlockSpec(memory_space=pltpu.HBM)] * len(self.arrays)

    def pieces(self):
        return sum(len(owners) for owners in self.owners)

    def copies(self, refs, where, number, done):
        started = []
        for ref, owners in zip(refs, self.owners):
            for at, j in enumerate(owners):
                rows = pl.ds(pl.multiple_of((number ^ j) * self.rows, self.rows), self.rows)
                source = ref.at[pl.ds(at * self.rows, self.rows), :]
                copy = pltpu.make_async_copy(source, where.at[rows, :], done.at[len(started)])
                started.append(copy)
        return started


def tie_packs(*packs, beside=()):
    flat = tie(*beside, *[x for pack in packs for x in pack.arrays])
    at = len(beside)
    for pack in packs:
        pack.arrays = list(flat[at : at + len(pack.arrays)])
        at += len(pack.arrays)
    return list(flat[: len(beside)])


def halving_order(bits):
    if not bits:
        return [0]
    rest = halving_order(bits[1:])
    return [bits[0] ^ j for j in rest] + rest


class Halving:
    def __init__(self, send, keep, axis, bits):
        self.send, self.axis, self.bits = send, axis, list(bits)
        self.terms = [(keep, 0)]

    def swap(self):
        self.got = swap(self.send, self.axis, self.bits.pop(0))

    def add(self):
        self.terms.append((self.got, 0))
        half = self.got.shape[0] // 2
        if half:
            self.send = add_terms(self.terms, half)
            self.terms = [(x, at + half) for x, at in self.terms]

    def most(self):
        while len(self.bits) > 1:
            self.swap()
            self.add()

    def finish(self):
        while self.bits:
            self.swap()
            self.add()
        return self.terms


def tie_halves(values, *halvings):
    flat = tie(*values, *[x.got for x in halvings])
    for x, got in zip(halvings, flat[len(values) :]):
        x.got = got
    return flat[: len(values)]


def resident(shape):
    zeros = (0,) * len(shape)
    return pl.BlockSpec(shape, lambda *_: zeros, pipeline_mode=pl.Buffered(1))


def own_block(rows, columns):
    return pl.BlockSpec((rows, columns), lambda i, ids, *_: (ids[0] ^ ids[2 + i], 0))


def step_block(rows, columns):
    return pl.BlockSpec((rows, columns), lambda i, *_: (i, 0))


def half_blocks(groups, rows, columns):
    half = groups // 2
    shape = (pl.Squeezed(), rows, columns)
    return [
        pl.BlockSpec(shape, lambda i, *_: (jnp.minimum(i, half - 1), 0, 0)),
        pl.BlockSpec(shape, lambda i, *_: (jnp.maximum(i - half, 0), 0, 0)),
    ]


def store_half(send, keep, value, step, groups):
    @pl.when(step < groups // 2)
    def _():
        send[...] = value

    @pl.when(step >= groups // 2)
    def _():
        keep[...] = value


class Tokens:
    def __init__(self, blocks, order):
        blocks = [blocks[j] for j in order]
        self.groups, self.counts = len(blocks), [len(block) for block in blocks]
        self.rows, self.model = sum(x.shape[0] for x in blocks[0]), blocks[0][0].shape[1]
        self.arrays = [x for block in blocks for x in block]
        self.specs = [pl.BlockSpec(memory_space=pltpu.HBM)] * len(self.arrays)

    def scratch(self):
        return [
            pltpu.VMEM((2, self.rows, self.model), bf16),
            pltpu.SemaphoreType.DMA((2, max(self.counts))),
        ]

    def fetch(self, refs, held, done, step):
        def copies(at):
            first, start, found = sum(self.counts[:at]), 0, []
            for k, ref in enumerate(refs[first : first + self.counts[at]]):
                where = held.at[at % 2, pl.ds(start, ref.shape[0]), :]
                found.append(pltpu.make_async_copy(ref, where, done.at[at % 2, k]))
                start += ref.shape[0]
            return found

        for at in range(self.groups):

            @pl.when(step == at)
            def _(at=at):
                ahead = copies(at) if at == 0 else []
                if at + 1 < self.groups:
                    ahead = ahead + copies(at + 1)
                for copy in ahead:
                    copy.start()
                for copy in copies(at):
                    copy.wait()


def store_halves(send, keep, total, number, order, columns=slice(None), source=slice(None)):
    half, rows = send.shape[0], send.shape[1]
    for at, j in enumerate(order):
        where = send if at < half else keep
        block = total[pl.ds(pl.multiple_of((number ^ j) * rows, rows), rows), source]
        where[at % half, :, columns] = block.astype(bf16)


def call(
    kernel, name, grid, prefetch, operands, specs, outs, out_specs, scratch, flops, extra=0, room=12
):
    size = sum(x.size * x.dtype.itemsize for x in list(operands) + list(outs))
    return pl.pallas_call(
        kernel,
        grid_spec=pltpu.PrefetchScalarGridSpec(
            num_scalar_prefetch=len(prefetch),
            grid=grid,
            in_specs=specs,
            out_specs=out_specs,
            scratch_shapes=scratch,
        ),
        out_shape=outs,
        compiler_params=pltpu.CompilerParams(
            dimension_semantics=("arbitrary",) * len(grid), vmem_limit_bytes=room << 20
        ),
        cost_estimate=pl.CostEstimate(
            flops=int(flops), bytes_accessed=int(size), transcendentals=int(extra)
        ),
        name=name,
    )(*prefetch, *operands)


def shaped(*shape, dtype=bf16):
    return jax.ShapeDtypeStruct(shape, dtype)


def shift_gain(block, gain, shift):
    return (block.astype(f32) * gain[...] + shift[...]).astype(bf16)


def turn(block, cosine, sine, sign):
    width = block.shape[1]
    step = min(width, 128)
    lane = lax.broadcasted_iota(jnp.int32, (block.shape[0], step), 1) % HD
    done = []
    for start in range(0, width, step):
        part = block[:, start : start + step]
        if step == 128:
            left = pltpu.roll(part, step - ROT // 2, 1)
            right = pltpu.roll(part, ROT // 2, 1)
        else:
            left = jnp.concatenate([part[:, ROT // 2 :], part[:, : ROT // 2]], axis=1)
            right = jnp.concatenate([part[:, -ROT // 2 :], part[:, : -ROT // 2]], axis=1)
        moved = jnp.where(lane < ROT // 2, -left, right) * sine[:, :step]
        done.append(part * cosine[:, :step] + moved * sign)
    return done[0] if len(done) == 1 else jnp.concatenate(done, axis=1)


def weight_scratch(pack):
    model = pack.rows * pack.pieces()
    columns = pack.arrays[0].shape[1]
    return [pltpu.VMEM((model, columns), bf16), pltpu.SemaphoreType.DMA((pack.pieces(),))]


def prepare_weights(qkv, dense, fc, out):
    rows, columns = qkv.shape
    width = columns // 3

    def kernel(qkv_ref, dense_ref, fc_ref, out_ref, qkv_to, dense_to, fc_to, out_to):
        for head in range(width // HD):
            for kind in range(3):
                at, own = (3 * head + kind) * HD, kind * width + head * HD
                qkv_to[:, own : own + HD] = qkv_ref[:, at : at + HD].astype(bf16)
        dense_to[...] = dense_ref[...].T.astype(bf16)
        fc_to[...] = fc_ref[...].astype(bf16)
        out_to[...] = out_ref[...].T.astype(bf16)

    operands = [qkv, dense, fc, out]
    outs = [shaped(*qkv.shape), shaped(*dense.shape[::-1]), shaped(*fc.shape), shaped(*out.shape[::-1])]
    return call(
        kernel,
        "prepare_weights",
        (1,),
        [],
        operands,
        [resident(x.shape) for x in operands],
        outs,
        [resident(x.shape) for x in outs],
        [],
        rows * columns,
    )


def normalize(stream):
    rows, model = stream.shape
    block = 160

    def kernel(stream_ref, sent_ref, norm_ref, std_ref):
        field = stream_ref[...]
        centred = field - jnp.sum(field, axis=1, keepdims=True) / model
        variance = jnp.sum(centred * centred, axis=1, keepdims=True) / model
        scale = lax.rsqrt(variance + eps_norm)
        norm = centred * scale
        norm_ref[...] = norm
        sent_ref[...] = norm.astype(bf16)
        std_ref[...] = scale

    return call(
        kernel,
        "normalize",
        (rows // block,),
        [],
        [stream],
        [step_block(block, model)],
        [shaped(rows, model), shaped(rows, model, dtype=f32), shaped(rows, 1, dtype=f32)],
        [step_block(block, model), step_block(block, model), step_block(block, 1)],
        [],
        rows * model * 8,
    )


def project_qkv(ids, info, sent, gain, shift, pack, bias, tables, width):
    groups, held, rows, model = sent.groups, len(sent.arrays), sent.rows, sent.model

    def kernel(ids, info, *refs):
        sent_refs, refs = refs[:held], refs[held:]
        weight_refs, refs = refs[: len(pack.arrays)], refs[len(pack.arrays) :]
        gain, shift, bias, cos, sine, q_out, k_out, v_out = refs[:8]
        block, arrived, whole, placed, added = refs[8:]
        step = pl.program_id(0)

        @pl.when(step == 0)
        def _():
            for copy in pack.copies(weight_refs, whole, ids[1], placed):
                copy.start()

        sent.fetch(sent_refs, block, arrived, step)

        @pl.when(step == 0)
        def _():
            for copy in pack.copies(weight_refs, whole, ids[1], placed):
                copy.wait()
            own = bias[pl.ds(ids[0], 1), :]
            for head in range(width // HD):
                for kind in range(3):
                    at, to = (3 * head + kind) * HD, kind * width + head * HD
                    added[:, to : to + HD] = own[:, at : at + HD]

        token = block[step % 2]
        qkv = dot_nn(shift_gain(token, gain, shift), whole[...]) + added[...]
        first = (ids[0] ^ ids[2 + step]) * (rows // SEG)
        for at in range(rows // SEG):
            number = first + at
            table = pl.ds(pl.multiple_of(info[number // NB, number % NB, 4] * SEG, SEG), SEG)
            tabs = (cos[table, :], sine[table, :])
            own = slice(at * SEG, (at + 1) * SEG)
            q_out[own, :] = (turn(qkv[own, :width], *tabs, 1.0) * HD**-0.5).astype(bf16)
            k_out[own, :] = turn(qkv[own, width : 2 * width], *tabs, 1.0).astype(bf16)
        v_out[...] = qkv[:, 2 * width :].astype(bf16)

    operands = [*sent.arrays, *pack.arrays, gain, shift, bias, *tables]
    out = shaped(groups * rows, width)
    return call(
        kernel,
        "project_qkv",
        (groups,),
        [ids, info],
        operands,
        sent.specs
        + pack.specs()
        + [resident(x.shape) for x in operands[held + len(pack.arrays) :]],
        [out] * 3,
        [own_block(rows, width)] * 3,
        sent.scratch() + weight_scratch(pack) + [pltpu.VMEM((1, 3 * width), f32)],
        2 * groups * rows * model * 3 * width,
        room=62,
    )


def project_grad(ids, grad, pack, width):
    groups, held, rows, model = grad.groups, len(grad.arrays), grad.rows, grad.model

    def kernel(ids, *refs):
        grad_refs, refs = refs[:held], refs[held:]
        weight_refs, (out, block, arrived, whole, placed) = refs[:-5], refs[-5:]
        step = pl.program_id(0)

        @pl.when(step == 0)
        def _():
            for copy in pack.copies(weight_refs, whole, ids[1], placed):
                copy.start()

        grad.fetch(grad_refs, block, arrived, step)

        @pl.when(step == 0)
        def _():
            for copy in pack.copies(weight_refs, whole, ids[1], placed):
                copy.wait()

        out[...] = dot_nn(block[step % 2], whole[...]).astype(bf16)

    operands = [*grad.arrays, *pack.arrays]
    return call(
        kernel,
        "project_grad",
        (groups,),
        [ids],
        operands,
        grad.specs + pack.specs(),
        [shaped(groups * rows, width)],
        [own_block(rows, width)],
        grad.scratch() + weight_scratch(pack),
        2 * groups * rows * model * width,
    )[0]


def attention_kernel(
    info, q_ref, do_ref, k_ref, v_ref, cos, sine, ctx_ref, dq_ref, dk_ref, dv_ref, dk_sum, dv_sum
):
    tree, step = pl.program_id(0), pl.program_id(1)
    width = q_ref.shape[1]
    heads = width // HD
    lane_head = lax.broadcasted_iota(jnp.int32, (SEG, width), 1) // HD

    @pl.when(step == 0)
    def _():
        dk_sum[...] = jnp.zeros_like(dk_sum)
        dv_sum[...] = jnp.zeros_like(dv_sum)

    first, second = info[tree, step, 0], info[tree, step, 1]
    first_rows = pl.ds(pl.multiple_of(first * SEG, SEG), SEG)
    second_rows = pl.ds(pl.multiple_of(second * SEG, SEG), SEG)
    queries, grads = q_ref[...], do_ref[...]
    zero = jnp.zeros_like(queries)
    q_rows = jnp.concatenate([jnp.where(lane_head == h, queries, zero) for h in range(heads)], axis=0)
    g_rows = jnp.concatenate([jnp.where(lane_head == h, grads, zero) for h in range(heads)], axis=0)
    q_turned, g_turned = queries.T, grads.T
    ahead = lax.broadcasted_iota(jnp.int32, (SEG, SEG), 1) - lax.broadcasted_iota(
        jnp.int32, (SEG, SEG), 0
    )
    seen = jnp.concatenate([ahead <= info[tree, step, 2], ahead <= info[tree, step, 3]], axis=1)
    seen = jnp.concatenate([seen] * heads, axis=0)
    k_near = jnp.concatenate([k_ref[first_rows, :], k_ref[second_rows, :]], axis=0)
    v_near = jnp.concatenate([v_ref[first_rows, :], v_ref[second_rows, :]], axis=0)

    def work(pairs):
        count = pairs * 2 * SEG
        near = jnp.where(seen, dot_nt(q_rows, k_near), masked_score)
        most = jnp.max(near, axis=1, keepdims=True)
        if count:
            k_far, v_far = k_ref[0:count, :], v_ref[0:count, :]
            far = dot_nt(q_rows, k_far)
            most = jnp.maximum(most, jnp.max(far, axis=1, keepdims=True))
        near = jnp.exp(near - most)
        total = jnp.sum(near, axis=1, keepdims=True)
        if count:
            far = jnp.exp(far - most)
            total = total + jnp.sum(far, axis=1, keepdims=True)
        scale = 1.0 / total
        near = near * scale
        near_low = near.astype(bf16)
        context = dot_nn(near_low, v_near)
        if count:
            far = far * scale
            far_low = far.astype(bf16)
            context = context + dot_nn(far_low, v_far)
        delta = jnp.sum(context * g_rows.astype(f32), axis=1, keepdims=True)
        near = (near * (dot_nt(g_rows, v_near) - delta)).astype(bf16)
        dq = dot_nn(near, k_near)
        if count:
            far = (far * (dot_nt(g_rows, v_far) - delta)).astype(bf16)
            dq = dq + dot_nn(far, k_far)
        ctx_own, dq_own = context[0:SEG], dq[0:SEG]
        for h in range(1, heads):
            ctx_own = jnp.where(lane_head == h, context[h * SEG : (h + 1) * SEG], ctx_own)
            dq_own = jnp.where(lane_head == h, dq[h * SEG : (h + 1) * SEG], dq_own)
        ctx_ref[...] = ctx_own.astype(bf16)
        dq_ref[...] = turn(dq_own * HD**-0.5, cos, sine, -1.0).astype(bf16)
        for h in range(heads):
            own = slice(h * SEG, (h + 1) * SEG)
            part = slice(h * HD, (h + 1) * HD)
            dk = dot_nn(q_turned[part], near[own])
            dv = dot_nn(g_turned[part], near_low[own])
            dk_sum[first, part, :] += dk[:, :SEG]
            dv_sum[first, part, :] += dv[:, :SEG]
            dk_sum[second, part, :] += dk[:, SEG:]
            dv_sum[second, part, :] += dv[:, SEG:]
            if count:
                dk = dot_nn(q_turned[part], far[own])
                dv = dot_nn(g_turned[part], far_low[own])
                for j in range(2 * pairs):
                    dk_sum[j, part, :] += dk[:, j * SEG : (j + 1) * SEG]
                    dv_sum[j, part, :] += dv[:, j * SEG : (j + 1) * SEG]

    for pairs in range(NT // 2):

        @pl.when(step // 2 == pairs)
        def _(pairs=pairs):
            work(pairs)

    @pl.when(step >= NT)
    def _():
        work(NT // 2)

    @pl.when(step == NB - 1)
    def _():
        def finish(j, carry):
            rows = pl.ds(pl.multiple_of(j * SEG, SEG), SEG)
            dv_ref[rows, :] = dv_sum[j].T.astype(bf16)
            dk_ref[rows, :] = dk_sum[j].T.astype(bf16)
            return carry

        lax.fori_loop(0, NB, finish, 0)


def attention(info, tables, queries, keys, values, grads):
    total, width = queries.shape
    trees = total // TREE
    table_width = tables[0].shape[1]
    block = pl.BlockSpec((SEG, width), lambda t, b, info: (t * NB + b, 0))
    whole = pl.BlockSpec((TREE, width), lambda t, b, info: (t, 0))
    table = pl.BlockSpec((SEG, table_width), lambda t, b, info: (info[t, b, 4], 0))
    scores = trees * (TREE - TRUNK) * (TRUNK + 2 * SEG) * (width // HD)
    return call(
        attention_kernel,
        "attention",
        (trees, NB),
        [info],
        [queries, grads, keys, values, *tables],
        [block, block, whole, whole, table, table],
        [shaped(total, width)] * 4,
        [block, block, whole, whole],
        [pltpu.VMEM((NB, width, SEG), f32), pltpu.VMEM((NB, width, SEG), f32)],
        scores * width * 2 * 6 * 1.3,
        scores,
        room=22,
    )


def project_context(ids, context, pack, groups, model):
    rows, width = context.shape[0] // groups, context.shape[1]

    def kernel(ids, ctx, *refs):
        weight_refs, (send, keep, whole, placed) = refs[:-4], refs[-4:]
        step = pl.program_id(0)

        @pl.when(step == 0)
        def _():
            copies = pack.copies(weight_refs, whole, ids[1], placed)
            for copy in copies:
                copy.start()
            for copy in copies:
                copy.wait()

        store_half(send, keep, dot_nt(ctx[...], whole[...]).astype(bf16), step, groups)

    operands = [context, *pack.arrays]
    half = shaped(groups // 2, rows, model)
    return call(
        kernel,
        "project_context",
        (groups,),
        [ids],
        operands,
        [own_block(rows, width)] + pack.specs(),
        [half] * 2,
        half_blocks(groups, rows, model),
        weight_scratch(pack),
        2 * groups * rows * model * width,
        room=14,
    )


def attention_weights(ids, info, tables, context, dq, dk, dv, sent, grad, gain, shift, orders):
    groups, held, rows, model = sent.groups, len(sent.arrays), sent.rows, sent.model
    width, count = dq.shape[1], len(orders[0])

    def kernel(ids, info, ctx_ref, dq_ref, dk_ref, dv_ref, *refs):
        sent_refs, refs = refs[:held], refs[held:]
        grad_refs, refs = refs[: len(grad.arrays)], refs[len(grad.arrays) :]
        gain, shift, cos, sine, grads, bias_ref, *stacks = refs[:10]
        block, arrived, grad_block, grad_arrived, total, dense_total = refs[10:]
        step = pl.program_id(0)

        @pl.when(step == 0)
        def _():
            total[...] = jnp.zeros_like(total)
            dense_total[...] = jnp.zeros_like(dense_total)
            bias_ref[...] = jnp.zeros_like(bias_ref)

        sent.fetch(sent_refs, block, arrived, step)
        grad.fetch(grad_refs, grad_block, grad_arrived, step)
        grads[:, :width] = dq_ref[...]
        first = (ids[0] ^ ids[2 + step]) * (rows // SEG)
        for at in range(rows // SEG):
            number = first + at
            table = pl.ds(pl.multiple_of(info[number // NB, number % NB, 4] * SEG, SEG), SEG)
            own = slice(at * SEG, (at + 1) * SEG)
            turned = turn(dk_ref[own, :], cos[table, :], sine[table, :], -1.0)
            grads[own, width : 2 * width] = turned.astype(bf16)
        grads[:, 2 * width :] = dv_ref[...]
        bias_ref[0:1, :] += jnp.sum(grads[...].astype(f32), axis=0, keepdims=True)
        total[...] += dot_tn(shift_gain(block[step % 2], gain, shift), grads[...])
        dense_total[...] += dot_tn(grad_block[step % 2], ctx_ref[...])

        @pl.when(step == groups - 1)
        def _():
            store_halves(*stacks[:2], total, ids[1], orders[0], source=slice(0, 2 * width))
            source = slice(2 * width, 3 * width)
            store_halves(*stacks[2:], total, ids[1], orders[1], slice(0, width), source)
            columns = slice(width, 2 * width)
            store_halves(*stacks[2:], dense_total, ids[1], orders[1], columns)

    operands = [context, dq, dk, dv, *sent.arrays, *grad.arrays, gain, shift, *tables]
    outs = [shaped(groups * rows, 3 * width), shaped(8, 3 * width, dtype=f32)]
    outs += [shaped(count // 2, model // count, 2 * width)] * 4
    return call(
        kernel,
        "attention_weights",
        (groups,),
        [ids, info],
        operands,
        [own_block(rows, width)] * 4
        + sent.specs
        + grad.specs
        + [resident(x.shape) for x in operands[-4:]],
        outs,
        [step_block(rows, 3 * width)] + [resident(x.shape) for x in outs[1:]],
        sent.scratch()
        + grad.scratch()
        + [pltpu.VMEM((model, 3 * width), f32), pltpu.VMEM((model, width), f32)],
        2 * groups * rows * model * 4 * width,
        room=24,
    )


def mlp(ids, sent, grad, gain, shift, fc, bias, out, orders):
    groups, held, rows, model = sent.groups, len(sent.arrays), sent.rows, sent.model
    pieces, units = len(fc.arrays), fc.arrays[0].shape[1]

    def kernel(ids, *refs):
        sent_refs, refs = refs[:held], refs[held:]
        grad_refs, refs = refs[: len(grad.arrays)], refs[len(grad.arrays) :]
        fc_refs, refs = refs[:pieces], refs[pieces:]
        out_refs, refs = refs[:pieces], refs[pieces:]
        gain, shift, bias, part_send, part_keep, hidden_ref, bias_ref = refs[:7]
        stacks, refs = refs[7:11], refs[11:]
        block, arrived, grad_block, grad_arrived, fc_whole, fc_placed, out_whole, out_placed = refs[:8]
        act_ref, fc_total, out_total = refs[8:]
        step = pl.program_id(0)

        def weights():
            copies = fc.copies(fc_refs, fc_whole, ids[1], fc_placed)
            return copies + out.copies(out_refs, out_whole, ids[1], out_placed)

        @pl.when(step == 0)
        def _():
            for copy in weights():
                copy.start()
            fc_total[...] = jnp.zeros_like(fc_total)
            out_total[...] = jnp.zeros_like(out_total)
            bias_ref[...] = jnp.zeros_like(bias_ref)

        sent.fetch(sent_refs, block, arrived, step)
        grad.fetch(grad_refs, grad_block, grad_arrived, step)

        @pl.when(step == 0)
        def _():
            for copy in weights():
                copy.wait()

        token, grads = block[step % 2], grad_block[step % 2]
        normed = shift_gain(token, gain, shift)
        count = 2
        parts = [slice(k * rows // count, (k + 1) * rows // count) for k in range(count)]
        added = bias[pl.ds(ids[0], 1), :]
        hidden = [dot_nn(normed[x], fc_whole[...]) + added for x in parts]
        back = [dot_nn(grads[x], out_whole[...]) for x in parts]
        for x, field, slope in zip(parts, hidden, back):
            chance = 0.5 + 0.5 * lax.erf(field * 0.7071067811865476)
            bell = jnp.exp(field * field * -0.5) * 0.3989422804014327
            act_ref[x, :] = (field * chance).astype(bf16)
            low = (slope * (chance + field * bell)).astype(bf16)
            hidden_ref[x, :] = low
            bias_ref[0:1, :] += jnp.sum(low.astype(f32), axis=0, keepdims=True)
        store_half(
            part_send, part_keep, dot_nt(act_ref[...], out_whole[...]).astype(bf16), step, groups
        )
        out_total[...] += dot_tn(grads, act_ref[...])
        fc_total[...] += dot_tn(normed, hidden_ref[...])

        @pl.when(step == groups - 1)
        def _():
            half = units // 2
            for at, order in enumerate(orders):
                stack = stacks[2 * at : 2 * at + 2]
                source = slice(at * half, (at + 1) * half)
                store_halves(*stack, fc_total, ids[1], order, slice(0, half), source)
                store_halves(*stack, out_total, ids[1], order, slice(half, units), source)

    operands = [*sent.arrays, *grad.arrays, *fc.arrays, *out.arrays, gain, shift, bias]
    count = model // fc.rows
    outs = [
        shaped(groups // 2, rows, model),
        shaped(groups // 2, rows, model),
        shaped(groups * rows, units),
        shaped(8, units, dtype=f32),
    ]
    outs += [shaped(count // 2, fc.rows, units)] * 4
    return call(
        kernel,
        "mlp",
        (groups,),
        [ids],
        operands,
        sent.specs
        + grad.specs
        + fc.specs()
        + out.specs()
        + [resident(x.shape) for x in operands[-3:]],
        outs,
        half_blocks(groups, rows, model)
        + [step_block(rows, units)]
        + [resident(x.shape) for x in outs[3:]],
        sent.scratch()
        + grad.scratch()
        + weight_scratch(fc)
        + weight_scratch(out)
        + [
            pltpu.VMEM((rows, units), bf16),
            pltpu.VMEM((model, units), f32),
            pltpu.VMEM((model, units), f32),
        ],
        10 * groups * rows * model * units,
        room=42,
    )


def norm_backward(ids, sent, grads, hidden, gain_attn, gain_mlp, qkv_pack, fc):
    groups, held, rows, model = sent.groups, len(sent.arrays), sent.rows, sent.model
    pieces, units, columns = len(fc.arrays), hidden.shape[1], grads.shape[1]

    def kernel(ids, grads_ref, hidden_ref, *refs):
        sent_refs, refs = refs[:held], refs[held:]
        qkv_refs, refs = refs[:pieces], refs[pieces:]
        fc_refs, refs = refs[:pieces], refs[pieces:]
        gain_attn, gain_mlp, send, keep, sums_ref = refs[:5]
        block, arrived, qkv_whole, qkv_placed, fc_whole, fc_placed = refs[5:]
        step = pl.program_id(0)

        def weights():
            copies = qkv_pack.copies(qkv_refs, qkv_whole, ids[1], qkv_placed)
            return copies + fc.copies(fc_refs, fc_whole, ids[1], fc_placed)

        @pl.when(step == 0)
        def _():
            for copy in weights():
                copy.start()
            sums_ref[...] = jnp.zeros_like(sums_ref)

        sent.fetch(sent_refs, block, arrived, step)

        @pl.when(step == 0)
        def _():
            for copy in weights():
                copy.wait()

        back_attn = dot_nt(grads_ref[...], qkv_whole[...])
        back_mlp = dot_nt(hidden_ref[...], fc_whole[...])
        token = block[step % 2].astype(f32)
        for at, back in enumerate((back_attn, back_mlp)):
            sums_ref[2 * at : 2 * at + 1, :] += jnp.sum(back * token, axis=0, keepdims=True)
            sums_ref[2 * at + 1 : 2 * at + 2, :] += jnp.sum(back, axis=0, keepdims=True)
        part = back_attn * gain_attn[...] + back_mlp * gain_mlp[...]
        store_half(send, keep, part.astype(bf16), step, groups)

    operands = [grads, hidden, *sent.arrays, *qkv_pack.arrays, *fc.arrays, gain_attn, gain_mlp]
    outs = [
        shaped(groups // 2, rows, model),
        shaped(groups // 2, rows, model),
        shaped(8, model, dtype=f32),
    ]
    return call(
        kernel,
        "norm_backward",
        (groups,),
        [ids],
        operands,
        [step_block(rows, columns), step_block(rows, units)]
        + sent.specs
        + qkv_pack.specs()
        + fc.specs()
        + [resident(x.shape) for x in operands[-2:]],
        outs,
        half_blocks(groups, rows, model) + [resident(x.shape) for x in outs[2:]],
        sent.scratch() + weight_scratch(qkv_pack) + weight_scratch(fc),
        2 * groups * rows * model * (units + columns),
        room=26,
    )


def taken(terms, block):
    return [
        pl.BlockSpec((pl.Squeezed(), block, x.shape[2]), lambda i, *_, at=at: (at, i, 0))
        for x, at in terms
    ]


def add_terms(terms, half):
    _, rows, columns = terms[0][0].shape
    block = max(x for x in (320, 128, 64) if rows % x == 0)

    def kernel(*refs):
        refs[-1][...] = sum(x[...].astype(f32) for x in refs[:-1]).astype(bf16)

    shape = (pl.Squeezed(), block, columns)
    out = shaped(half, rows, columns)
    return call(
        kernel,
        "add_terms",
        (half, rows // block),
        [],
        [x for x, _ in terms],
        [pl.BlockSpec(shape, lambda k, i, *_, at=at: (at + k, i, 0)) for _, at in terms],
        [out],
        [pl.BlockSpec(shape, lambda k, i, *_: (k, i, 0))],
        [],
        half * rows * columns * len(terms),
    )[0]


def whole_terms(terms, count):
    return [
        pl.BlockSpec((count, *x.shape[1:]), lambda *_, at=at: (at // count, 0, 0)) for x, at in terms
    ]


def add_stacks(stacks):
    counts = []
    for parts in stacks:
        parts.terms.append((parts.got, 0))
        counts.append(parts.got.shape[0] // 2)
    held = [len(parts.terms) for parts in stacks]
    operands = [x for parts in stacks for x, _ in parts.terms]

    def kernel(*refs):
        for at, half in enumerate(counts):
            first = sum(held[:at])
            total = sum(x[...].astype(f32) for x in refs[first : first + held[at]])
            refs[len(operands) + at][...] = total.astype(bf16)

    outs = [shaped(n, *parts.got.shape[1:]) for n, parts in zip(counts, stacks)]
    sends = call(
        kernel,
        "add_stacks",
        (1,),
        [],
        operands,
        [x for n, parts in zip(counts, stacks) for x in whole_terms(parts.terms, n)],
        outs,
        [resident(x.shape) for x in outs],
        [],
        sum(x.size for x in operands) // 2,
        room=16,
    )
    for n, parts, send in zip(counts, stacks, sends):
        parts.send = send
        parts.terms = [(x, at + n) for x, at in parts.terms]


def finish_mlp_weights(first, second):
    held, (_, rows, units) = len(first), first[0][0].shape
    half = units // 2

    def kernel(*refs):
        low = sum(x[0].astype(f32) for x in refs[:held])
        high = sum(x[0].astype(f32) for x in refs[held:-2])
        refs[-2][:, :half] = low[:, :half]
        refs[-2][:, half:] = high[:, :half]
        refs[-1][:half, :] = low[:, half:].T
        refs[-1][half:, :] = high[:, half:].T

    operands = [x for x, _ in [*first, *second]]
    outs = [shaped(rows, units, dtype=f32), shaped(units, rows, dtype=f32)]
    return call(
        kernel,
        "finish_mlp_weights",
        (1,),
        [],
        operands,
        whole_terms([*first, *second], 1),
        outs,
        [resident(x.shape) for x in outs],
        [],
        len(operands) * rows * units,
    )


def finish_attention_weights(first, second):
    held, (_, rows, columns) = len(first), first[0][0].shape
    width = columns // 2

    def kernel(*refs):
        low = sum(x[0].astype(f32) for x in refs[:held])
        high = sum(x[0].astype(f32) for x in refs[held:-2])
        for head in range(width // HD):
            for kind, (source, start) in enumerate(((low, 0), (low, width), (high, 0))):
                at = (3 * head + kind) * HD
                own = start + head * HD
                refs[-2][:, at : at + HD] = source[:, own : own + HD]
        refs[-1][...] = high[:, width:].T

    operands = [x for x, _ in [*first, *second]]
    outs = [shaped(rows, 3 * width, dtype=f32), shaped(width, rows, dtype=f32)]
    return call(
        kernel,
        "finish_attention_weights",
        (1,),
        [],
        operands,
        whole_terms([*first, *second], 1),
        outs,
        [resident(x.shape) for x in outs],
        [],
        len(operands) * rows * columns,
    )


def sum_rows(groups):
    return (12 + groups + 7) // 8 * 8


def finish_output(ids, stream, grad, attn_terms, mlp_terms, dense_bias, out_bias, norm_sums, fc_sums, qkv_sums, groups):
    rows, model = stream.shape
    block = 160
    first, second = len(attn_terms), len(mlp_terms)
    units, columns = fc_sums.shape[1], qkv_sums.shape[1]
    across = model // units

    def kernel(ids, stream_ref, grad_ref, *refs):
        attn_refs, refs = refs[:first], refs[first:]
        mlp_refs, refs = refs[:second], refs[second:]
        dense_bias, out_bias, norm_ref, fc_ref, qkv_ref, out_ref, sums_ref = refs

        @pl.when(pl.program_id(0) == 0)
        def _():
            sums_ref[...] = jnp.zeros_like(sums_ref)
            sums_ref[0:4, :] = norm_ref[0:4, :]
            own = jnp.concatenate([fc_ref[0:1, :]] * across, axis=1) if across > 1 else fc_ref[0:1, :]
            lane = lax.broadcasted_iota(jnp.int32, (1, model), 1) // units
            sums_ref[pl.ds(8 + ids[0] // across, 1), :] = jnp.where(lane == ids[0] % across, own, 0.0)
            sums_ref[pl.ds(12 + ids[0], 1), :columns] = qkv_ref[0:1, :]

        attn = sum(x[...].astype(f32) for x in attn_refs) + dense_bias[...]
        mlp = sum(x[...].astype(f32) for x in mlp_refs) + out_bias[...]
        output = stream_ref[...] + attn + mlp
        out_ref[...] = output
        for at, value in enumerate((output, attn, mlp)):
            sums_ref[4 + at : 5 + at, :] += jnp.sum(value * value, axis=0, keepdims=True)
        sums_ref[7:8, :] += jnp.sum(grad_ref[...].astype(f32), axis=0, keepdims=True)

    terms = [*attn_terms, *mlp_terms]
    operands = [stream, grad, *[x for x, _ in terms], dense_bias, out_bias, norm_sums, fc_sums, qkv_sums]
    outs = [shaped(rows, model, dtype=f32), shaped(sum_rows(groups), model, dtype=f32)]
    return call(
        kernel,
        "finish_output",
        (rows // block,),
        [ids],
        operands,
        [step_block(block, model), step_block(block, model)]
        + taken(terms, block)
        + [resident(x.shape) for x in operands[-5:]],
        outs,
        [step_block(block, model), resident(outs[1].shape)],
        [],
        rows * model * 16,
        room=16,
    )


def finish_grad(grad, normalized, inv_std, terms):
    rows, model = grad.shape
    block = 160

    def kernel(grad_ref, norm_ref, std_ref, *refs):
        term_refs, out_ref = refs[:-1], refs[-1]
        sent = sum(x[...].astype(f32) for x in term_refs)
        norm = norm_ref[...]
        mean = jnp.sum(sent, axis=1, keepdims=True) / model
        cross = jnp.sum(sent * norm, axis=1, keepdims=True) / model
        out_ref[...] = grad_ref[...].astype(f32) + std_ref[...] * (sent - mean - norm * cross)

    operands = [grad, normalized, inv_std, *[x for x, _ in terms]]
    return call(
        kernel,
        "finish_grad",
        (rows // block,),
        [],
        operands,
        [step_block(block, model), step_block(block, model), step_block(block, 1)]
        + taken(terms, block),
        [shaped(rows, model, dtype=f32)],
        [step_block(block, model)],
        [],
        rows * model * 12,
    )[0]


def tree_table(segment_ids, parent_ids):
    trees = segment_ids.shape[0] // TREE

    def kernel(segment, parent, table):
        for tree in range(trees):
            for block in range(NT):
                odd = block % 2
                row = (block - odd, block - odd + 1, SEG * odd, -SEG * (1 - odd), block)
                for at, value in enumerate(row):
                    table[tree, block, at] = value

            def place(block, carry):
                first = tree * TREE
                owner = parent[first + block * SEG]
                leaf = (owner != segment[first]).astype(jnp.int32)
                at = block
                for other in range(NT, NB):
                    at = jnp.where(segment[first + other * SEG] == owner, other, at)
                table[tree, block, 0] = block
                table[tree, block, 1] = at
                table[tree, block, 2] = 0
                table[tree, block, 3] = SEG * (2 * leaf - 1)
                table[tree, block, 4] = NT + leaf
                return carry

            lax.fori_loop(NT, NB, place, 0)

    smem = pl.BlockSpec(memory_space=pltpu.SMEM)
    return pl.pallas_call(
        kernel,
        in_specs=[smem, smem],
        out_specs=smem,
        out_shape=jax.ShapeDtypeStruct((trees, NB, 5), jnp.int32),
        name="tree_table",
    )(segment_ids, parent_ids)


def angle_tables(zero):
    places = TRUNK + 2 * SEG
    place = lax.broadcasted_iota(jnp.int32, (places, 2 * HD), 0).astype(f32)
    lane = lax.broadcasted_iota(jnp.int32, (places, 2 * HD), 1) % HD
    half = ROT // 2
    frequency = 10000.0 ** (-((lane % half).astype(f32) * 2.0 / ROT))
    angle = (place + zero) * frequency
    cosine = jnp.where(lane < ROT, jnp.cos(angle), 1.0)
    sine = jnp.where(lane < ROT, jnp.sin(angle), 0.0)
    return cosine, sine


def by_kind(array, heads):
    shape = array.shape[:-1]
    array = array.reshape(*shape, heads, 3, HD)
    return jnp.swapaxes(array, -3, -2).reshape(*shape, 3 * heads * HD)


def by_head(array, heads):
    shape = array.shape[:-1]
    array = array.reshape(*shape, 3, heads, HD)
    return jnp.swapaxes(array, -3, -2).reshape(*shape, 3 * heads * HD)


def local(
    stream_in,
    segment_ids,
    parent_ids,
    norm_gain_attn,
    norm_shift_attn,
    norm_gain_mlp,
    norm_shift_mlp,
    qkv_weight,
    qkv_bias,
    dense_weight,
    dense_bias,
    fc_weight,
    fc_bias,
    out_weight,
    out_bias,
    out_grad,
):
    tensor_rank = lax.axis_index("tensor")
    data_rank = lax.axis_index("dp")
    rows_local = stream_in.shape[0]
    model = stream_in.shape[1]
    qkv_width = qkv_weight.shape[1]
    heads = qkv_width // (3 * HD)
    width = heads * HD
    units = fc_weight.shape[1]
    groups = lax.axis_size("tensor")
    tensor_bits = bits_of(groups)
    far_first = tensor_bits[:0:-1] + tensor_bits[:1]
    order = halving_order(tensor_bits)
    ids = jnp.stack([tensor_rank, data_rank, *order]).astype(jnp.int32)
    data_bits = bits_of(lax.axis_size("dp"))
    rows_first = data_bits[:0:-1] + data_bits[:1]
    columns_first = data_bits[:1] + data_bits[:0:-1]
    near_bits = data_bits
    next_bits = data_bits[1:2] + data_bits[:1] + data_bits[2:]
    qkv_bits = [data_bits[:1] + data_bits[:0:-1], data_bits[1:2] + data_bits[2:] + data_bits[:1]]

    blocks = prepare_weights(qkv_weight, dense_weight, fc_weight, out_weight)
    qkv_pack = Pack(blocks[0], "dp", rows_first)
    dense_pack = Pack(blocks[1], "dp", columns_first)
    fc_pack = Pack(blocks[2], "dp", rows_first)
    out_pack = Pack(blocks[3], "dp", rows_first)

    sent_norm, normalized, inv_std = normalize(stream_in)
    sent = gather_far(sent_norm, "tensor", tensor_bits)

    info = tree_table(segment_ids, parent_ids)
    gain_attn, shift_attn = norm_gain_attn[None, :], norm_shift_attn[None, :]
    gain_mlp, shift_mlp = norm_gain_mlp[None, :], norm_shift_mlp[None, :]
    sent_near, near = swap(sent[0], "tensor", 1), swap(out_grad, "tensor", 1)
    cut = rows_local * 3 // 5
    early, late = out_grad[:cut], out_grad[cut:]
    qkv_pack.double()
    dense_pack.double()
    zero = jnp.zeros((), f32)
    near, early, late, zero, qkv_bias, fc_bias, info = tie_packs(
        qkv_pack, dense_pack, fc_pack, beside=[near, early, late, zero, qkv_bias, fc_bias, info]
    )
    tables = angle_tables(zero)
    qkv_rows, fc_rows = qkv_bias.reshape(groups, qkv_width), fc_bias.reshape(groups, units)
    while len(qkv_pack.bits) > 1:
        qkv_pack.double()
        dense_pack.double()
    fc_pack.double()
    done = tie_packs(
        qkv_pack,
        dense_pack,
        out_pack,
        beside=[early, late, *tables, qkv_rows, fc_rows, sent_near, *sent],
    )
    early, late, *done = done
    tables, (qkv_rows, fc_rows, sent_near), sent = done[:2], done[2:5], done[5:]
    early_far = gather_far(early, "tensor", tensor_bits)[1:]
    sent_near = [sent_near] + [swap(x, "tensor", 1) for x in sent[1:]]
    sent = [x for pair in zip(sent, sent_near) for x in pair]
    qkv_pack.double()
    dense_pack.double()
    late, *done = tie_packs(
        qkv_pack, dense_pack, fc_pack, out_pack, beside=[late, *sent, *early_far]
    )
    sent, early_far = Tokens([(x,) for x in done[:groups]], order), done[groups:]
    late_far = gather_far(late, "tensor", tensor_bits)[1:]
    early_near = [swap(x, "tensor", 1) for x in early_far]
    out_pack.double()
    while len(fc_pack.bits) > 1:
        fc_pack.double()

    done = project_qkv(
        ids, info, sent, gain_attn, shift_attn, qkv_pack, qkv_rows, tables, width
    )
    done = tie_packs(fc_pack, out_pack, beside=[*done, *early_near, *late_far])
    (queries, keys, values), done = done[:3], done[3:]
    early_near, late_far = done[: groups // 2 - 1], done[groups // 2 - 1 :]
    late_near = [swap(x, "tensor", 1) for x in late_far]
    far = zip(zip(early_far, late_far), zip(early_near, late_near))
    grad = Tokens([(out_grad,), (near,), *[x for pair in far for x in pair]], order)
    while len(out_pack.bits) > 1:
        out_pack.double()
    (grad_context,) = tie_packs(out_pack, beside=[project_grad(ids, grad, dense_pack, width)])
    fc_pack.double()
    out_pack.double()
    done = attention(info, tables, queries, keys, values, grad_context)
    context, dq, dk, dv = tie_packs(fc_pack, out_pack, beside=done)
    dp_orders = [halving_order(near_bits), halving_order(next_bits)]
    qkv_orders = [halving_order(bits) for bits in qkv_bits]
    attn_parts = Halving(
        *project_context(ids, context, dense_pack, groups, model), "tensor", tensor_bits
    )
    while len(attn_parts.bits) > 2:
        attn_parts.swap()
        attn_parts.add()
    attn_parts.send, context = tie(attn_parts.send, context)
    attn_parts.swap()
    done = attention_weights(
        ids, info, tables, context, dq, dk, dv, sent, grad, gain_attn, shift_attn, qkv_orders
    )
    grads, qkv_bias_sums, *stacks = tie_halves(done, attn_parts)
    attn_parts.add()
    qkv_sums = [Halving(*stacks[:2], "dp", qkv_bits[0]), Halving(*stacks[2:], "dp", qkv_bits[1])]
    sent.arrays[0], attn_parts.send = tie(sent.arrays[0], attn_parts.send)
    attn_parts.swap()
    for parts in qkv_sums:
        parts.swap()
    done = mlp(
        ids, sent, grad, gain_mlp, shift_mlp, fc_pack, fc_rows, out_pack, dp_orders
    )
    done = tie_halves(done, attn_parts, *qkv_sums)
    mlp_send, mlp_keep, hidden, fc_bias_sums, *stacks = done
    attn_parts.add()
    mlp_parts = Halving(mlp_send, mlp_keep, "tensor", tensor_bits)
    mlp_sums = [Halving(*stacks[:2], "dp", near_bits), Halving(*stacks[2:], "dp", next_bits)]
    while len(mlp_parts.bits) > 2:
        mlp_parts.swap()
        mlp_parts.add()
    mlp_parts.swap()
    add_stacks(qkv_sums)
    mlp_parts.add()
    hidden, mlp_parts.send = tie(hidden, mlp_parts.send)
    mlp_parts.swap()
    for parts in qkv_sums + mlp_sums:
        parts.swap()
    done = norm_backward(ids, sent, grads, hidden, gain_attn, gain_mlp, qkv_pack, fc_pack)
    done = tie_halves(done, mlp_parts, *qkv_sums, *mlp_sums)
    back_send, back_keep, norm_sums = done
    mlp_parts.add()

    back_parts = Halving(back_send, back_keep, "tensor", tensor_bits)
    while len(back_parts.bits) > 2:
        back_parts.swap()
        back_parts.add()
    back_parts.swap()
    add_stacks(qkv_sums + mlp_sums)

    back_parts.add()
    stream_in, back_parts.send = tie(stream_in, back_parts.send)
    back_parts.swap()
    for parts in qkv_sums + mlp_sums:
        parts.swap()
    output, sums = finish_output(
        ids,
        stream_in,
        out_grad,
        attn_parts.terms,
        mlp_parts.terms,
        dense_bias[None, :],
        out_bias[None, :],
        norm_sums,
        fc_bias_sums,
        qkv_bias_sums,
        groups,
    )


    sums = sums + swap(sums, "tensor", 1)
    for bit in data_bits[3:]:
        sums = sums + swap(sums, "dp", bit)
    other, *_ = tie_halves([swap(sums, "dp", data_bits[2])], *mlp_sums)
    sums = sums + other
    add_stacks(mlp_sums)
    sums, *sends = tie(sums, *[parts.send for parts in mlp_sums])
    for parts, send in zip(mlp_sums, sends):
        parts.send = send
    for bit in data_bits[:2]:
        sums = sums + swap(sums, "dp", bit)
    sums, back_parts.got = tie(sums, back_parts.got)
    back_parts.add()
    for bit in tensor_bits[1:]:
        sums = sums + swap(sums, "tensor", bit)
    stream_grad = finish_grad(out_grad, normalized, inv_std, back_parts.terms)

    fc_weight_grad, out_weight_grad = finish_mlp_weights(*[x.finish() for x in mlp_sums])
    for parts in qkv_sums:
        parts.add()
    qkv_weight_grad, dense_weight_grad = finish_attention_weights(*[x.finish() for x in qkv_sums])

    count_all = float(rows_local * lax.axis_size("dp") * groups * model)
    gain_attn_grad, shift_attn_grad, gain_mlp_grad, shift_mlp_grad = (sums[x] for x in range(4))
    root_squares = jnp.sqrt(jnp.sum(sums[4:7], axis=1) / count_all)
    residual_grad = sums[7]
    fc_bias_grad = sums[8:12].reshape(-1)
    qkv_bias_grad = by_head(sums[12 : 12 + groups, :qkv_width], heads).reshape(-1)
    return (
        output,
        stream_grad,
        gain_attn_grad,
        shift_attn_grad,
        gain_mlp_grad,
        shift_mlp_grad,
        qkv_weight_grad,
        qkv_bias_grad,
        dense_weight_grad,
        residual_grad,
        fc_weight_grad,
        fc_bias_grad,
        out_weight_grad,
        residual_grad,
        root_squares,
    )


def solution(mesh):
    tokens, weights, rows, whole = (
        P(("dp", "tensor"), None),
        P("dp", "tensor"),
        P("tensor", "dp"),
        P(),
    )
    return jax.shard_map(
        local,
        mesh=mesh,
        in_specs=(
            tokens,
            P("dp"),
            P("dp"),
            whole,
            whole,
            whole,
            whole,
            weights,
            whole,
            rows,
            whole,
            weights,
            whole,
            rows,
            whole,
            tokens,
        ),
        out_specs=(
            tokens,
            tokens,
            whole,
            whole,
            whole,
            whole,
            weights,
            whole,
            rows,
            whole,
            weights,
            whole,
            rows,
            whole,
            whole,
        ),
        check_vma=False,
    )
```

```python
import jax
import jax.numpy as jnp
from jax import lax
from jax.experimental import pallas as pl
from jax.experimental.pallas import tpu as pltpu
from jax.sharding import PartitionSpec as P

HD = 64
ROT = 16
TRUNK = 1024
SEG = 128
TREE = 2560
NB = TREE // SEG
NT = TRUNK // SEG

f32 = jnp.float32
bf16 = jnp.bfloat16
eps_norm = 1e-05
masked_score = -1e30


def dot_nn(left, right):
    return lax.dot_general(left, right, (((1,), (0,)), ((), ())), preferred_element_type=f32)


def dot_nt(left, right):
    return lax.dot_general(left, right, (((1,), (1,)), ((), ())), preferred_element_type=f32)


def dot_tn(left, right):
    return lax.dot_general(left, right, (((0,), (0,)), ((), ())), preferred_element_type=f32)


def bits_of(size):
    bits = []
    bit = 1
    while bit < size:
        bits.append(bit)
        bit *= 2
    return bits


def swap(block, axis, bit):
    size = lax.axis_size(axis)
    return lax.ppermute(block, axis, [(i, i ^ bit) for i in range(size)])


def tie(*values):
    return lax.optimization_barrier(values)


def gather_far(block, axis, bits):
    pieces = [block]
    for bit in bits[1:]:
        pieces = pieces + [swap(piece, axis, bit) for piece in pieces]
    return pieces


class Pack:
    def __init__(self, block, axis, bits):
        self.rows, self.axis, self.bits = block.shape[0], axis, list(bits)
        self.arrays, self.owners = [block], [[0]]

    def double(self):
        bit = self.bits.pop(0)
        held = self.arrays[0] if len(self.arrays) == 1 else jnp.concatenate(self.arrays, axis=0)
        self.owners.append([j ^ bit for owners in self.owners for j in owners])
        self.arrays.append(swap(held, self.axis, bit))

    def specs(self):
        return [pl.BlockSpec(memory_space=pltpu.HBM)] * len(self.arrays)

    def pieces(self):
        return sum(len(owners) for owners in self.owners)

    def copies(self, refs, where, number, done):
        started = []
        for ref, owners in zip(refs, self.owners):
            for at, j in enumerate(owners):
                rows = pl.ds(pl.multiple_of((number ^ j) * self.rows, self.rows), self.rows)
                source = ref.at[pl.ds(at * self.rows, self.rows), :]
                copy = pltpu.make_async_copy(source, where.at[rows, :], done.at[len(started)])
                started.append(copy)
        return started


def tie_packs(*packs, beside=()):
    flat = tie(*beside, *[x for pack in packs for x in pack.arrays])
    at = len(beside)
    for pack in packs:
        pack.arrays = list(flat[at : at + len(pack.arrays)])
        at += len(pack.arrays)
    return list(flat[: len(beside)])


def halving_order(bits):
    if not bits:
        return [0]
    rest = halving_order(bits[1:])
    return [bits[0] ^ j for j in rest] + rest


class Halving:
    def __init__(self, send, keep, axis, bits):
        self.send, self.axis, self.bits = send, axis, list(bits)
        self.terms = [(keep, 0)]

    def swap(self):
        self.got = swap(self.send, self.axis, self.bits.pop(0))

    def add(self):
        self.terms.append((self.got, 0))
        half = self.got.shape[0] // 2
        if half:
            self.send = add_terms(self.terms, half)
            self.terms = [(x, at + half) for x, at in self.terms]

    def most(self):
        while len(self.bits) > 1:
            self.swap()
            self.add()

    def finish(self):
        while self.bits:
            self.swap()
            self.add()
        return self.terms


def tie_halves(values, *halvings):
    flat = tie(*values, *[x.got for x in halvings])
    for x, got in zip(halvings, flat[len(values) :]):
        x.got = got
    return flat[: len(values)]


def resident(shape):
    zeros = (0,) * len(shape)
    return pl.BlockSpec(shape, lambda *_: zeros, pipeline_mode=pl.Buffered(1))


def own_block(rows, columns):
    return pl.BlockSpec((rows, columns), lambda i, ids, *_: (ids[0] ^ ids[2 + i], 0))


def step_block(rows, columns):
    return pl.BlockSpec((rows, columns), lambda i, *_: (i, 0))


def half_blocks(groups, rows, columns):
    half = groups // 2
    shape = (pl.Squeezed(), rows, columns)
    return [
        pl.BlockSpec(shape, lambda i, *_: (jnp.minimum(i, half - 1), 0, 0)),
        pl.BlockSpec(shape, lambda i, *_: (jnp.maximum(i - half, 0), 0, 0)),
    ]


def store_half(send, keep, value, step, groups):
    @pl.when(step < groups // 2)
    def _():
        send[...] = value

    @pl.when(step >= groups // 2)
    def _():
        keep[...] = value


class Tokens:
    def __init__(self, blocks, order):
        blocks = [blocks[j] for j in order]
        self.groups, self.counts = len(blocks), [len(block) for block in blocks]
        self.rows, self.model = sum(x.shape[0] for x in blocks[0]), blocks[0][0].shape[1]
        self.arrays = [x for block in blocks for x in block]
        self.specs = [pl.BlockSpec(memory_space=pltpu.HBM)] * len(self.arrays)

    def scratch(self):
        return [
            pltpu.VMEM((2, self.rows, self.model), bf16),
            pltpu.SemaphoreType.DMA((2, max(self.counts))),
        ]

    def fetch(self, refs, held, done, step):
        def copies(at):
            first, start, found = sum(self.counts[:at]), 0, []
            for k, ref in enumerate(refs[first : first + self.counts[at]]):
                where = held.at[at % 2, pl.ds(start, ref.shape[0]), :]
                found.append(pltpu.make_async_copy(ref, where, done.at[at % 2, k]))
                start += ref.shape[0]
            return found

        for at in range(self.groups):

            @pl.when(step == at)
            def _(at=at):
                ahead = copies(at) if at == 0 else []
                if at + 1 < self.groups:
                    ahead = ahead + copies(at + 1)
                for copy in ahead:
                    copy.start()
                for copy in copies(at):
                    copy.wait()


def store_halves(send, keep, total, number, order, columns=slice(None), source=slice(None)):
    half, rows = send.shape[0], send.shape[1]
    for at, j in enumerate(order):
        where = send if at < half else keep
        block = total[pl.ds(pl.multiple_of((number ^ j) * rows, rows), rows), source]
        where[at % half, :, columns] = block.astype(bf16)


def call(
    kernel, name, grid, prefetch, operands, specs, outs, out_specs, scratch, flops, extra=0, room=12
):
    size = sum(x.size * x.dtype.itemsize for x in list(operands) + list(outs))
    return pl.pallas_call(
        kernel,
        grid_spec=pltpu.PrefetchScalarGridSpec(
            num_scalar_prefetch=len(prefetch),
            grid=grid,
            in_specs=specs,
            out_specs=out_specs,
            scratch_shapes=scratch,
        ),
        out_shape=outs,
        compiler_params=pltpu.CompilerParams(
            dimension_semantics=("arbitrary",) * len(grid), vmem_limit_bytes=room << 20
        ),
        cost_estimate=pl.CostEstimate(
            flops=int(flops), bytes_accessed=int(size), transcendentals=int(extra)
        ),
        name=name,
    )(*prefetch, *operands)


def shaped(*shape, dtype=bf16):
    return jax.ShapeDtypeStruct(shape, dtype)


def shift_gain(block, gain, shift):
    return (block.astype(f32) * gain[...] + shift[...]).astype(bf16)


def turn(block, cosine, sine, sign):
    width = block.shape[1]
    step = min(width, 128)
    lane = lax.broadcasted_iota(jnp.int32, (block.shape[0], step), 1) % HD
    done = []
    for start in range(0, width, step):
        part = block[:, start : start + step]
        if step == 128:
            left = pltpu.roll(part, step - ROT // 2, 1)
            right = pltpu.roll(part, ROT // 2, 1)
        else:
            left = jnp.concatenate([part[:, ROT // 2 :], part[:, : ROT // 2]], axis=1)
            right = jnp.concatenate([part[:, -ROT // 2 :], part[:, : -ROT // 2]], axis=1)
        moved = jnp.where(lane < ROT // 2, -left, right) * sine[:, :step]
        done.append(part * cosine[:, :step] + moved * sign)
    return done[0] if len(done) == 1 else jnp.concatenate(done, axis=1)


def weight_scratch(pack):
    model = pack.rows * pack.pieces()
    columns = pack.arrays[0].shape[1]
    return [pltpu.VMEM((model, columns), bf16), pltpu.SemaphoreType.DMA((pack.pieces(),))]


def prepare_weights(qkv, dense, fc, out):
    rows, columns = qkv.shape
    width = columns // 3

    def kernel(qkv_ref, dense_ref, fc_ref, out_ref, qkv_to, dense_to, fc_to, out_to):
        for head in range(width // HD):
            for kind in range(3):
                at, own = (3 * head + kind) * HD, kind * width + head * HD
                qkv_to[:, own : own + HD] = qkv_ref[:, at : at + HD].astype(bf16)
        dense_to[...] = dense_ref[...].T.astype(bf16)
        fc_to[...] = fc_ref[...].astype(bf16)
        out_to[...] = out_ref[...].T.astype(bf16)

    operands = [qkv, dense, fc, out]
    outs = [shaped(*qkv.shape), shaped(*dense.shape[::-1]), shaped(*fc.shape), shaped(*out.shape[::-1])]
    return call(
        kernel,
        "prepare_weights",
        (1,),
        [],
        operands,
        [resident(x.shape) for x in operands],
        outs,
        [resident(x.shape) for x in outs],
        [],
        rows * columns,
    )


def normalize(stream):
    rows, model = stream.shape
    block = 160

    def kernel(stream_ref, sent_ref, norm_ref, std_ref):
        field = stream_ref[...]
        centred = field - jnp.sum(field, axis=1, keepdims=True) / model
        variance = jnp.sum(centred * centred, axis=1, keepdims=True) / model
        scale = lax.rsqrt(variance + eps_norm)
        norm = centred * scale
        norm_ref[...] = norm
        sent_ref[...] = norm.astype(bf16)
        std_ref[...] = scale

    return call(
        kernel,
        "normalize",
        (rows // block,),
        [],
        [stream],
        [step_block(block, model)],
        [shaped(rows, model), shaped(rows, model, dtype=f32), shaped(rows, 1, dtype=f32)],
        [step_block(block, model), step_block(block, model), step_block(block, 1)],
        [],
        rows * model * 8,
    )


def project_qkv(ids, info, sent, gain, shift, pack, bias, tables, width):
    groups, held, rows, model = sent.groups, len(sent.arrays), sent.rows, sent.model

    def kernel(ids, info, *refs):
        sent_refs, refs = refs[:held], refs[held:]
        weight_refs, refs = refs[: len(pack.arrays)], refs[len(pack.arrays) :]
        gain, shift, bias, cos, sine, q_out, k_out, v_out = refs[:8]
        block, arrived, whole, placed, added = refs[8:]
        step = pl.program_id(0)

        @pl.when(step == 0)
        def _():
            for copy in pack.copies(weight_refs, whole, ids[1], placed):
                copy.start()

        sent.fetch(sent_refs, block, arrived, step)

        @pl.when(step == 0)
        def _():
            for copy in pack.copies(weight_refs, whole, ids[1], placed):
                copy.wait()
            own = bias[pl.ds(ids[0], 1), :]
            for head in range(width // HD):
                for kind in range(3):
                    at, to = (3 * head + kind) * HD, kind * width + head * HD
                    added[:, to : to + HD] = own[:, at : at + HD]

        token = block[step % 2]
        qkv = dot_nn(shift_gain(token, gain, shift), whole[...]) + added[...]
        first = (ids[0] ^ ids[2 + step]) * (rows // SEG)
        for at in range(rows // SEG):
            number = first + at
            table = pl.ds(pl.multiple_of(info[number // NB, number % NB, 4] * SEG, SEG), SEG)
            tabs = (cos[table, :], sine[table, :])
            own = slice(at * SEG, (at + 1) * SEG)
            q_out[own, :] = (turn(qkv[own, :width], *tabs, 1.0) * HD**-0.5).astype(bf16)
            k_out[own, :] = turn(qkv[own, width : 2 * width], *tabs, 1.0).astype(bf16)
        v_out[...] = qkv[:, 2 * width :].astype(bf16)

    operands = [*sent.arrays, *pack.arrays, gain, shift, bias, *tables]
    out = shaped(groups * rows, width)
    return call(
        kernel,
        "project_qkv",
        (groups,),
        [ids, info],
        operands,
        sent.specs
        + pack.specs()
        + [resident(x.shape) for x in operands[held + len(pack.arrays) :]],
        [out] * 3,
        [own_block(rows, width)] * 3,
        sent.scratch() + weight_scratch(pack) + [pltpu.VMEM((1, 3 * width), f32)],
        2 * groups * rows * model * 3 * width,
        room=62,
    )


def project_grad(ids, grad, pack, width):
    groups, held, rows, model = grad.groups, len(grad.arrays), grad.rows, grad.model

    def kernel(ids, *refs):
        grad_refs, refs = refs[:held], refs[held:]
        weight_refs, (out, block, arrived, whole, placed) = refs[:-5], refs[-5:]
        step = pl.program_id(0)

        @pl.when(step == 0)
        def _():
            for copy in pack.copies(weight_refs, whole, ids[1], placed):
                copy.start()

        grad.fetch(grad_refs, block, arrived, step)

        @pl.when(step == 0)
        def _():
            for copy in pack.copies(weight_refs, whole, ids[1], placed):
                copy.wait()

        out[...] = dot_nn(block[step % 2], whole[...]).astype(bf16)

    operands = [*grad.arrays, *pack.arrays]
    return call(
        kernel,
        "project_grad",
        (groups,),
        [ids],
        operands,
        grad.specs + pack.specs(),
        [shaped(groups * rows, width)],
        [own_block(rows, width)],
        grad.scratch() + weight_scratch(pack),
        2 * groups * rows * model * width,
    )[0]


def attention_kernel(
    info, q_ref, do_ref, k_ref, v_ref, cos, sine, ctx_ref, dq_ref, dk_ref, dv_ref, dk_sum, dv_sum
):
    tree, step = pl.program_id(0), pl.program_id(1)
    width = q_ref.shape[1]
    heads = width // HD
    lane_head = lax.broadcasted_iota(jnp.int32, (SEG, width), 1) // HD

    @pl.when(step == 0)
    def _():
        dk_sum[...] = jnp.zeros_like(dk_sum)
        dv_sum[...] = jnp.zeros_like(dv_sum)

    first, second = info[tree, step, 0], info[tree, step, 1]
    first_rows = pl.ds(pl.multiple_of(first * SEG, SEG), SEG)
    second_rows = pl.ds(pl.multiple_of(second * SEG, SEG), SEG)
    queries, grads = q_ref[...], do_ref[...]
    zero = jnp.zeros_like(queries)
    q_rows = jnp.concatenate([jnp.where(lane_head == h, queries, zero) for h in range(heads)], axis=0)
    g_rows = jnp.concatenate([jnp.where(lane_head == h, grads, zero) for h in range(heads)], axis=0)
    q_turned, g_turned = queries.T, grads.T
    ahead = lax.broadcasted_iota(jnp.int32, (SEG, SEG), 1) - lax.broadcasted_iota(
        jnp.int32, (SEG, SEG), 0
    )
    seen = jnp.concatenate([ahead <= info[tree, step, 2], ahead <= info[tree, step, 3]], axis=1)
    seen = jnp.concatenate([seen] * heads, axis=0)
    k_near = jnp.concatenate([k_ref[first_rows, :], k_ref[second_rows, :]], axis=0)
    v_near = jnp.concatenate([v_ref[first_rows, :], v_ref[second_rows, :]], axis=0)

    def work(pairs):
        count = pairs * 2 * SEG
        near = jnp.where(seen, dot_nt(q_rows, k_near), masked_score)
        most = jnp.max(near, axis=1, keepdims=True)
        if count:
            k_far, v_far = k_ref[0:count, :], v_ref[0:count, :]
            far = dot_nt(q_rows, k_far)
            most = jnp.maximum(most, jnp.max(far, axis=1, keepdims=True))
        near = jnp.exp(near - most)
        total = jnp.sum(near, axis=1, keepdims=True)
        if count:
            far = jnp.exp(far - most)
            total = total + jnp.sum(far, axis=1, keepdims=True)
        scale = 1.0 / total
        near = near * scale
        near_low = near.astype(bf16)
        context = dot_nn(near_low, v_near)
        if count:
            far = far * scale
            far_low = far.astype(bf16)
            context = context + dot_nn(far_low, v_far)
        delta = jnp.sum(context * g_rows.astype(f32), axis=1, keepdims=True)
        near = (near * (dot_nt(g_rows, v_near) - delta)).astype(bf16)
        dq = dot_nn(near, k_near)
        if count:
            far = (far * (dot_nt(g_rows, v_far) - delta)).astype(bf16)
            dq = dq + dot_nn(far, k_far)
        ctx_own, dq_own = context[0:SEG], dq[0:SEG]
        for h in range(1, heads):
            ctx_own = jnp.where(lane_head == h, context[h * SEG : (h + 1) * SEG], ctx_own)
            dq_own = jnp.where(lane_head == h, dq[h * SEG : (h + 1) * SEG], dq_own)
        ctx_ref[...] = ctx_own.astype(bf16)
        dq_ref[...] = turn(dq_own * HD**-0.5, cos, sine, -1.0).astype(bf16)
        for h in range(heads):
            own = slice(h * SEG, (h + 1) * SEG)
            part = slice(h * HD, (h + 1) * HD)
            dk = dot_nn(q_turned[part], near[own])
            dv = dot_nn(g_turned[part], near_low[own])
            dk_sum[first, part, :] += dk[:, :SEG]
            dv_sum[first, part, :] += dv[:, :SEG]
            dk_sum[second, part, :] += dk[:, SEG:]
            dv_sum[second, part, :] += dv[:, SEG:]
            if count:
                dk = dot_nn(q_turned[part], far[own])
                dv = dot_nn(g_turned[part], far_low[own])
                for j in range(2 * pairs):
                    dk_sum[j, part, :] += dk[:, j * SEG : (j + 1) * SEG]
                    dv_sum[j, part, :] += dv[:, j * SEG : (j + 1) * SEG]

    for pairs in range(NT // 2):

        @pl.when(step // 2 == pairs)
        def _(pairs=pairs):
            work(pairs)

    @pl.when(step >= NT)
    def _():
        work(NT // 2)

    @pl.when(step == NB - 1)
    def _():
        def finish(j, carry):
            rows = pl.ds(pl.multiple_of(j * SEG, SEG), SEG)
            dv_ref[rows, :] = dv_sum[j].T.astype(bf16)
            dk_ref[rows, :] = dk_sum[j].T.astype(bf16)
            return carry

        lax.fori_loop(0, NB, finish, 0)


def attention(info, tables, queries, keys, values, grads):
    total, width = queries.shape
    trees = total // TREE
    table_width = tables[0].shape[1]
    block = pl.BlockSpec((SEG, width), lambda t, b, info: (t * NB + b, 0))
    whole = pl.BlockSpec((TREE, width), lambda t, b, info: (t, 0))
    table = pl.BlockSpec((SEG, table_width), lambda t, b, info: (info[t, b, 4], 0))
    scores = trees * (TREE - TRUNK) * (TRUNK + 2 * SEG) * (width // HD)
    return call(
        attention_kernel,
        "attention",
        (trees, NB),
        [info],
        [queries, grads, keys, values, *tables],
        [block, block, whole, whole, table, table],
        [shaped(total, width)] * 4,
        [block, block, whole, whole],
        [pltpu.VMEM((NB, width, SEG), f32), pltpu.VMEM((NB, width, SEG), f32)],
        scores * width * 2 * 6 * 1.3,
        scores,
        room=22,
    )


def project_context(ids, context, pack, groups, model):
    rows, width = context.shape[0] // groups, context.shape[1]

    def kernel(ids, ctx, *refs):
        weight_refs, (send, keep, whole, placed) = refs[:-4], refs[-4:]
        step = pl.program_id(0)

        @pl.when(step == 0)
        def _():
            copies = pack.copies(weight_refs, whole, ids[1], placed)
            for copy in copies:
                copy.start()
            for copy in copies:
                copy.wait()

        store_half(send, keep, dot_nt(ctx[...], whole[...]).astype(bf16), step, groups)

    operands = [context, *pack.arrays]
    half = shaped(groups // 2, rows, model)
    return call(
        kernel,
        "project_context",
        (groups,),
        [ids],
        operands,
        [own_block(rows, width)] + pack.specs(),
        [half] * 2,
        half_blocks(groups, rows, model),
        weight_scratch(pack),
        2 * groups * rows * model * width,
        room=14,
    )


def attention_weights(ids, info, tables, context, dq, dk, dv, sent, grad, gain, shift, orders):
    groups, held, rows, model = sent.groups, len(sent.arrays), sent.rows, sent.model
    width, count = dq.shape[1], len(orders[0])

    def kernel(ids, info, ctx_ref, dq_ref, dk_ref, dv_ref, *refs):
        sent_refs, refs = refs[:held], refs[held:]
        grad_refs, refs = refs[: len(grad.arrays)], refs[len(grad.arrays) :]
        gain, shift, cos, sine, grads, bias_ref, *stacks = refs[:10]
        block, arrived, grad_block, grad_arrived, total, dense_total = refs[10:]
        step = pl.program_id(0)

        @pl.when(step == 0)
        def _():
            total[...] = jnp.zeros_like(total)
            dense_total[...] = jnp.zeros_like(dense_total)
            bias_ref[...] = jnp.zeros_like(bias_ref)

        sent.fetch(sent_refs, block, arrived, step)
        grad.fetch(grad_refs, grad_block, grad_arrived, step)
        grads[:, :width] = dq_ref[...]
        first = (ids[0] ^ ids[2 + step]) * (rows // SEG)
        for at in range(rows // SEG):
            number = first + at
            table = pl.ds(pl.multiple_of(info[number // NB, number % NB, 4] * SEG, SEG), SEG)
            own = slice(at * SEG, (at + 1) * SEG)
            turned = turn(dk_ref[own, :], cos[table, :], sine[table, :], -1.0)
            grads[own, width : 2 * width] = turned.astype(bf16)
        grads[:, 2 * width :] = dv_ref[...]
        bias_ref[0:1, :] += jnp.sum(grads[...].astype(f32), axis=0, keepdims=True)
        total[...] += dot_tn(shift_gain(block[step % 2], gain, shift), grads[...])
        dense_total[...] += dot_tn(grad_block[step % 2], ctx_ref[...])

        @pl.when(step == groups - 1)
        def _():
            store_halves(*stacks[:2], total, ids[1], orders[0], source=slice(0, 2 * width))
            source = slice(2 * width, 3 * width)
            store_halves(*stacks[2:], total, ids[1], orders[1], slice(0, width), source)
            columns = slice(width, 2 * width)
            store_halves(*stacks[2:], dense_total, ids[1], orders[1], columns)

    operands = [context, dq, dk, dv, *sent.arrays, *grad.arrays, gain, shift, *tables]
    outs = [shaped(groups * rows, 3 * width), shaped(8, 3 * width, dtype=f32)]
    outs += [shaped(count // 2, model // count, 2 * width)] * 4
    return call(
        kernel,
        "attention_weights",
        (groups,),
        [ids, info],
        operands,
        [own_block(rows, width)] * 4
        + sent.specs
        + grad.specs
        + [resident(x.shape) for x in operands[-4:]],
        outs,
        [step_block(rows, 3 * width)] + [resident(x.shape) for x in outs[1:]],
        sent.scratch()
        + grad.scratch()
        + [pltpu.VMEM((model, 3 * width), f32), pltpu.VMEM((model, width), f32)],
        2 * groups * rows * model * 4 * width,
        room=24,
    )


def mlp(ids, sent, grad, gain, shift, fc, bias, out, orders):
    groups, held, rows, model = sent.groups, len(sent.arrays), sent.rows, sent.model
    pieces, units = len(fc.arrays), fc.arrays[0].shape[1]

    def kernel(ids, *refs):
        sent_refs, refs = refs[:held], refs[held:]
        grad_refs, refs = refs[: len(grad.arrays)], refs[len(grad.arrays) :]
        fc_refs, refs = refs[:pieces], refs[pieces:]
        out_refs, refs = refs[:pieces], refs[pieces:]
        gain, shift, bias, part_send, part_keep, hidden_ref, bias_ref = refs[:7]
        stacks, refs = refs[7:11], refs[11:]
        block, arrived, grad_block, grad_arrived, fc_whole, fc_placed, out_whole, out_placed = refs[:8]
        act_ref, fc_total, out_total = refs[8:]
        step = pl.program_id(0)

        def weights():
            copies = fc.copies(fc_refs, fc_whole, ids[1], fc_placed)
            return copies + out.copies(out_refs, out_whole, ids[1], out_placed)

        @pl.when(step == 0)
        def _():
            for copy in weights():
                copy.start()
            fc_total[...] = jnp.zeros_like(fc_total)
            out_total[...] = jnp.zeros_like(out_total)
            bias_ref[...] = jnp.zeros_like(bias_ref)

        sent.fetch(sent_refs, block, arrived, step)
        grad.fetch(grad_refs, grad_block, grad_arrived, step)

        @pl.when(step == 0)
        def _():
            for copy in weights():
                copy.wait()

        token, grads = block[step % 2], grad_block[step % 2]
        normed = shift_gain(token, gain, shift)
        count = 2
        parts = [slice(k * rows // count, (k + 1) * rows // count) for k in range(count)]
        added = bias[pl.ds(ids[0], 1), :]
        hidden = [dot_nn(normed[x], fc_whole[...]) + added for x in parts]
        back = [dot_nn(grads[x], out_whole[...]) for x in parts]
        for x, field, slope in zip(parts, hidden, back):
            chance = 0.5 + 0.5 * lax.erf(field * 0.7071067811865476)
            bell = jnp.exp(field * field * -0.5) * 0.3989422804014327
            act_ref[x, :] = (field * chance).astype(bf16)
            low = (slope * (chance + field * bell)).astype(bf16)
            hidden_ref[x, :] = low
            bias_ref[0:1, :] += jnp.sum(low.astype(f32), axis=0, keepdims=True)
        store_half(
            part_send, part_keep, dot_nt(act_ref[...], out_whole[...]).astype(bf16), step, groups
        )
        out_total[...] += dot_tn(grads, act_ref[...])
        fc_total[...] += dot_tn(normed, hidden_ref[...])

        @pl.when(step == groups - 1)
        def _():
            half = units // 2
            for at, order in enumerate(orders):
                stack = stacks[2 * at : 2 * at + 2]
                source = slice(at * half, (at + 1) * half)
                store_halves(*stack, fc_total, ids[1], order, slice(0, half), source)
                store_halves(*stack, out_total, ids[1], order, slice(half, units), source)

    operands = [*sent.arrays, *grad.arrays, *fc.arrays, *out.arrays, gain, shift, bias]
    count = model // fc.rows
    outs = [
        shaped(groups // 2, rows, model),
        shaped(groups // 2, rows, model),
        shaped(groups * rows, units),
        shaped(8, units, dtype=f32),
    ]
    outs += [shaped(count // 2, fc.rows, units)] * 4
    return call(
        kernel,
        "mlp",
        (groups,),
        [ids],
        operands,
        sent.specs
        + grad.specs
        + fc.specs()
        + out.specs()
        + [resident(x.shape) for x in operands[-3:]],
        outs,
        half_blocks(groups, rows, model)
        + [step_block(rows, units)]
        + [resident(x.shape) for x in outs[3:]],
        sent.scratch()
        + grad.scratch()
        + weight_scratch(fc)
        + weight_scratch(out)
        + [
            pltpu.VMEM((rows, units), bf16),
            pltpu.VMEM((model, units), f32),
            pltpu.VMEM((model, units), f32),
        ],
        10 * groups * rows * model * units,
        room=42,
    )


def norm_backward(ids, sent, grads, hidden, gain_attn, gain_mlp, qkv_pack, fc):
    groups, held, rows, model = sent.groups, len(sent.arrays), sent.rows, sent.model
    pieces, units, columns = len(fc.arrays), hidden.shape[1], grads.shape[1]

    def kernel(ids, grads_ref, hidden_ref, *refs):
        sent_refs, refs = refs[:held], refs[held:]
        qkv_refs, refs = refs[:pieces], refs[pieces:]
        fc_refs, refs = refs[:pieces], refs[pieces:]
        gain_attn, gain_mlp, send, keep, sums_ref = refs[:5]
        block, arrived, qkv_whole, qkv_placed, fc_whole, fc_placed = refs[5:]
        step = pl.program_id(0)

        def weights():
            copies = qkv_pack.copies(qkv_refs, qkv_whole, ids[1], qkv_placed)
            return copies + fc.copies(fc_refs, fc_whole, ids[1], fc_placed)

        @pl.when(step == 0)
        def _():
            for copy in weights():
                copy.start()
            sums_ref[...] = jnp.zeros_like(sums_ref)

        sent.fetch(sent_refs, block, arrived, step)

        @pl.when(step == 0)
        def _():
            for copy in weights():
                copy.wait()

        back_attn = dot_nt(grads_ref[...], qkv_whole[...])
        back_mlp = dot_nt(hidden_ref[...], fc_whole[...])
        token = block[step % 2].astype(f32)
        for at, back in enumerate((back_attn, back_mlp)):
            sums_ref[2 * at : 2 * at + 1, :] += jnp.sum(back * token, axis=0, keepdims=True)
            sums_ref[2 * at + 1 : 2 * at + 2, :] += jnp.sum(back, axis=0, keepdims=True)
        part = back_attn * gain_attn[...] + back_mlp * gain_mlp[...]
        store_half(send, keep, part.astype(bf16), step, groups)

    operands = [grads, hidden, *sent.arrays, *qkv_pack.arrays, *fc.arrays, gain_attn, gain_mlp]
    outs = [
        shaped(groups // 2, rows, model),
        shaped(groups // 2, rows, model),
        shaped(8, model, dtype=f32),
    ]
    return call(
        kernel,
        "norm_backward",
        (groups,),
        [ids],
        operands,
        [step_block(rows, columns), step_block(rows, units)]
        + sent.specs
        + qkv_pack.specs()
        + fc.specs()
        + [resident(x.shape) for x in operands[-2:]],
        outs,
        half_blocks(groups, rows, model) + [resident(x.shape) for x in outs[2:]],
        sent.scratch() + weight_scratch(qkv_pack) + weight_scratch(fc),
        2 * groups * rows * model * (units + columns),
        room=26,
    )


def taken(terms, block):
    return [
        pl.BlockSpec((pl.Squeezed(), block, x.shape[2]), lambda i, *_, at=at: (at, i, 0))
        for x, at in terms
    ]


def add_terms(terms, half):
    _, rows, columns = terms[0][0].shape
    block = max(x for x in (320, 128, 64) if rows % x == 0)

    def kernel(*refs):
        refs[-1][...] = sum(x[...].astype(f32) for x in refs[:-1]).astype(bf16)

    shape = (pl.Squeezed(), block, columns)
    out = shaped(half, rows, columns)
    return call(
        kernel,
        "add_terms",
        (half, rows // block),
        [],
        [x for x, _ in terms],
        [pl.BlockSpec(shape, lambda k, i, *_, at=at: (at + k, i, 0)) for _, at in terms],
        [out],
        [pl.BlockSpec(shape, lambda k, i, *_: (k, i, 0))],
        [],
        half * rows * columns * len(terms),
    )[0]


def whole_terms(terms, count):
    return [
        pl.BlockSpec((count, *x.shape[1:]), lambda *_, at=at: (at // count, 0, 0)) for x, at in terms
    ]


def add_stacks(stacks):
    counts = []
    for parts in stacks:
        parts.terms.append((parts.got, 0))
        counts.append(parts.got.shape[0] // 2)
    held = [len(parts.terms) for parts in stacks]
    operands = [x for parts in stacks for x, _ in parts.terms]

    def kernel(*refs):
        for at, half in enumerate(counts):
            first = sum(held[:at])
            total = sum(x[...].astype(f32) for x in refs[first : first + held[at]])
            refs[len(operands) + at][...] = total.astype(bf16)

    outs = [shaped(n, *parts.got.shape[1:]) for n, parts in zip(counts, stacks)]
    sends = call(
        kernel,
        "add_stacks",
        (1,),
        [],
        operands,
        [x for n, parts in zip(counts, stacks) for x in whole_terms(parts.terms, n)],
        outs,
        [resident(x.shape) for x in outs],
        [],
        sum(x.size for x in operands) // 2,
        room=16,
    )
    for n, parts, send in zip(counts, stacks, sends):
        parts.send = send
        parts.terms = [(x, at + n) for x, at in parts.terms]


def finish_mlp_weights(first, second):
    held, (_, rows, units) = len(first), first[0][0].shape
    half = units // 2

    def kernel(*refs):
        low = sum(x[0].astype(f32) for x in refs[:held])
        high = sum(x[0].astype(f32) for x in refs[held:-2])
        refs[-2][:, :half] = low[:, :half]
        refs[-2][:, half:] = high[:, :half]
        refs[-1][:half, :] = low[:, half:].T
        refs[-1][half:, :] = high[:, half:].T

    operands = [x for x, _ in [*first, *second]]
    outs = [shaped(rows, units, dtype=f32), shaped(units, rows, dtype=f32)]
    return call(
        kernel,
        "finish_mlp_weights",
        (1,),
        [],
        operands,
        whole_terms([*first, *second], 1),
        outs,
        [resident(x.shape) for x in outs],
        [],
        len(operands) * rows * units,
    )


def finish_attention_weights(first, second):
    held, (_, rows, columns) = len(first), first[0][0].shape
    width = columns // 2

    def kernel(*refs):
        low = sum(x[0].astype(f32) for x in refs[:held])
        high = sum(x[0].astype(f32) for x in refs[held:-2])
        for head in range(width // HD):
            for kind, (source, start) in enumerate(((low, 0), (low, width), (high, 0))):
                at = (3 * head + kind) * HD
                own = start + head * HD
                refs[-2][:, at : at + HD] = source[:, own : own + HD]
        refs[-1][...] = high[:, width:].T

    operands = [x for x, _ in [*first, *second]]
    outs = [shaped(rows, 3 * width, dtype=f32), shaped(width, rows, dtype=f32)]
    return call(
        kernel,
        "finish_attention_weights",
        (1,),
        [],
        operands,
        whole_terms([*first, *second], 1),
        outs,
        [resident(x.shape) for x in outs],
        [],
        len(operands) * rows * columns,
    )


def sum_rows(groups):
    return (12 + groups + 7) // 8 * 8


def finish_output(ids, stream, grad, attn_terms, mlp_terms, dense_bias, out_bias, norm_sums, fc_sums, qkv_sums, groups):
    rows, model = stream.shape
    block = 160
    first, second = len(attn_terms), len(mlp_terms)
    units, columns = fc_sums.shape[1], qkv_sums.shape[1]
    across = model // units

    def kernel(ids, stream_ref, grad_ref, *refs):
        attn_refs, refs = refs[:first], refs[first:]
        mlp_refs, refs = refs[:second], refs[second:]
        dense_bias, out_bias, norm_ref, fc_ref, qkv_ref, out_ref, sums_ref = refs

        @pl.when(pl.program_id(0) == 0)
        def _():
            sums_ref[...] = jnp.zeros_like(sums_ref)
            sums_ref[0:4, :] = norm_ref[0:4, :]
            own = jnp.concatenate([fc_ref[0:1, :]] * across, axis=1) if across > 1 else fc_ref[0:1, :]
            lane = lax.broadcasted_iota(jnp.int32, (1, model), 1) // units
            sums_ref[pl.ds(8 + ids[0] // across, 1), :] = jnp.where(lane == ids[0] % across, own, 0.0)
            sums_ref[pl.ds(12 + ids[0], 1), :columns] = qkv_ref[0:1, :]

        attn = sum(x[...].astype(f32) for x in attn_refs) + dense_bias[...]
        mlp = sum(x[...].astype(f32) for x in mlp_refs) + out_bias[...]
        output = stream_ref[...] + attn + mlp
        out_ref[...] = output
        for at, value in enumerate((output, attn, mlp)):
            sums_ref[4 + at : 5 + at, :] += jnp.sum(value * value, axis=0, keepdims=True)
        sums_ref[7:8, :] += jnp.sum(grad_ref[...].astype(f32), axis=0, keepdims=True)

    terms = [*attn_terms, *mlp_terms]
    operands = [stream, grad, *[x for x, _ in terms], dense_bias, out_bias, norm_sums, fc_sums, qkv_sums]
    outs = [shaped(rows, model, dtype=f32), shaped(sum_rows(groups), model, dtype=f32)]
    return call(
        kernel,
        "finish_output",
        (rows // block,),
        [ids],
        operands,
        [step_block(block, model), step_block(block, model)]
        + taken(terms, block)
        + [resident(x.shape) for x in operands[-5:]],
        outs,
        [step_block(block, model), resident(outs[1].shape)],
        [],
        rows * model * 16,
        room=16,
    )


def finish_grad(grad, normalized, inv_std, terms):
    rows, model = grad.shape
    block = 160

    def kernel(grad_ref, norm_ref, std_ref, *refs):
        term_refs, out_ref = refs[:-1], refs[-1]
        sent = sum(x[...].astype(f32) for x in term_refs)
        norm = norm_ref[...]
        mean = jnp.sum(sent, axis=1, keepdims=True) / model
        cross = jnp.sum(sent * norm, axis=1, keepdims=True) / model
        out_ref[...] = grad_ref[...].astype(f32) + std_ref[...] * (sent - mean - norm * cross)

    operands = [grad, normalized, inv_std, *[x for x, _ in terms]]
    return call(
        kernel,
        "finish_grad",
        (rows // block,),
        [],
        operands,
        [step_block(block, model), step_block(block, model), step_block(block, 1)]
        + taken(terms, block),
        [shaped(rows, model, dtype=f32)],
        [step_block(block, model)],
        [],
        rows * model * 12,
    )[0]


def tree_table(segment_ids, parent_ids):
    trees = segment_ids.shape[0] // TREE

    def kernel(segment, parent, table):
        for tree in range(trees):
            for block in range(NT):
                odd = block % 2
                row = (block - odd, block - odd + 1, SEG * odd, -SEG * (1 - odd), block)
                for at, value in enumerate(row):
                    table[tree, block, at] = value

            def place(block, carry):
                first = tree * TREE
                owner = parent[first + block * SEG]
                leaf = (owner != segment[first]).astype(jnp.int32)
                at = block
                for other in range(NT, NB):
                    at = jnp.where(segment[first + other * SEG] == owner, other, at)
                table[tree, block, 0] = block
                table[tree, block, 1] = at
                table[tree, block, 2] = 0
                table[tree, block, 3] = SEG * (2 * leaf - 1)
                table[tree, block, 4] = NT + leaf
                return carry

            lax.fori_loop(NT, NB, place, 0)

    smem = pl.BlockSpec(memory_space=pltpu.SMEM)
    return pl.pallas_call(
        kernel,
        in_specs=[smem, smem],
        out_specs=smem,
        out_shape=jax.ShapeDtypeStruct((trees, NB, 5), jnp.int32),
        name="tree_table",
    )(segment_ids, parent_ids)


def angle_tables(zero):
    places = TRUNK + 2 * SEG
    place = lax.broadcasted_iota(jnp.int32, (places, 2 * HD), 0).astype(f32)
    lane = lax.broadcasted_iota(jnp.int32, (places, 2 * HD), 1) % HD
    half = ROT // 2
    frequency = 10000.0 ** (-((lane % half).astype(f32) * 2.0 / ROT))
    angle = (place + zero) * frequency
    cosine = jnp.where(lane < ROT, jnp.cos(angle), 1.0)
    sine = jnp.where(lane < ROT, jnp.sin(angle), 0.0)
    return cosine, sine


def by_kind(array, heads):
    shape = array.shape[:-1]
    array = array.reshape(*shape, heads, 3, HD)
    return jnp.swapaxes(array, -3, -2).reshape(*shape, 3 * heads * HD)


def by_head(array, heads):
    shape = array.shape[:-1]
    array = array.reshape(*shape, 3, heads, HD)
    return jnp.swapaxes(array, -3, -2).reshape(*shape, 3 * heads * HD)


def local(
    stream_in,
    segment_ids,
    parent_ids,
    norm_gain_attn,
    norm_shift_attn,
    norm_gain_mlp,
    norm_shift_mlp,
    qkv_weight,
    qkv_bias,
    dense_weight,
    dense_bias,
    fc_weight,
    fc_bias,
    out_weight,
    out_bias,
    out_grad,
):
    tensor_rank = lax.axis_index("tensor")
    data_rank = lax.axis_index("dp")
    rows_local = stream_in.shape[0]
    model = stream_in.shape[1]
    qkv_width = qkv_weight.shape[1]
    heads = qkv_width // (3 * HD)
    width = heads * HD
    units = fc_weight.shape[1]
    groups = lax.axis_size("tensor")
    tensor_bits = bits_of(groups)
    far_first = tensor_bits[:0:-1] + tensor_bits[:1]
    order = halving_order(tensor_bits)
    ids = jnp.stack([tensor_rank, data_rank, *order]).astype(jnp.int32)
    data_bits = bits_of(lax.axis_size("dp"))
    rows_first = data_bits[:0:-1] + data_bits[:1]
    columns_first = data_bits[:1] + data_bits[:0:-1]
    near_bits = data_bits
    next_bits = data_bits[1:2] + data_bits[:1] + data_bits[2:]
    qkv_bits = [data_bits[:1] + data_bits[:0:-1], next_bits]

    blocks = prepare_weights(qkv_weight, dense_weight, fc_weight, out_weight)
    qkv_pack = Pack(blocks[0], "dp", rows_first)
    dense_pack = Pack(blocks[1], "dp", columns_first)
    fc_pack = Pack(blocks[2], "dp", rows_first)
    out_pack = Pack(blocks[3], "dp", rows_first)

    sent_norm, normalized, inv_std = normalize(stream_in)
    sent = gather_far(sent_norm, "tensor", tensor_bits)

    info = tree_table(segment_ids, parent_ids)
    gain_attn, shift_attn = norm_gain_attn[None, :], norm_shift_attn[None, :]
    gain_mlp, shift_mlp = norm_gain_mlp[None, :], norm_shift_mlp[None, :]
    sent_near, near = swap(sent[0], "tensor", 1), swap(out_grad, "tensor", 1)
    cut = rows_local * 3 // 5
    early, late = out_grad[:cut], out_grad[cut:]
    qkv_pack.double()
    dense_pack.double()
    zero = jnp.zeros((), f32)
    near, early, late, zero, qkv_bias, fc_bias, info = tie_packs(
        qkv_pack, dense_pack, fc_pack, beside=[near, early, late, zero, qkv_bias, fc_bias, info]
    )
    tables = angle_tables(zero)
    qkv_rows, fc_rows = qkv_bias.reshape(groups, qkv_width), fc_bias.reshape(groups, units)
    while len(qkv_pack.bits) > 1:
        qkv_pack.double()
        dense_pack.double()
    fc_pack.double()
    done = tie_packs(
        qkv_pack,
        dense_pack,
        out_pack,
        beside=[early, late, *tables, qkv_rows, fc_rows, sent_near, *sent],
    )
    early, late, *done = done
    tables, (qkv_rows, fc_rows, sent_near), sent = done[:2], done[2:5], done[5:]
    early_far = gather_far(early, "tensor", tensor_bits)[1:]
    sent_near = [sent_near] + [swap(x, "tensor", 1) for x in sent[1:]]
    sent = [x for pair in zip(sent, sent_near) for x in pair]
    qkv_pack.double()
    dense_pack.double()
    late, *done = tie_packs(
        qkv_pack, dense_pack, fc_pack, out_pack, beside=[late, *sent, *early_far]
    )
    sent, early_far = Tokens([(x,) for x in done[:groups]], order), done[groups:]
    late_far = gather_far(late, "tensor", tensor_bits)[1:]
    early_near = [swap(x, "tensor", 1) for x in early_far]
    out_pack.double()
    while len(fc_pack.bits) > 1:
        fc_pack.double()

    done = project_qkv(
        ids, info, sent, gain_attn, shift_attn, qkv_pack, qkv_rows, tables, width
    )
    done = tie_packs(fc_pack, out_pack, beside=[*done, *early_near, *late_far])
    (queries, keys, values), done = done[:3], done[3:]
    early_near, late_far = done[: groups // 2 - 1], done[groups // 2 - 1 :]
    late_near = [swap(x, "tensor", 1) for x in late_far]
    far = zip(zip(early_far, late_far), zip(early_near, late_near))
    grad = Tokens([(out_grad,), (near,), *[x for pair in far for x in pair]], order)
    while len(out_pack.bits) > 1:
        out_pack.double()
    (grad_context,) = tie_packs(out_pack, beside=[project_grad(ids, grad, dense_pack, width)])
    fc_pack.double()
    out_pack.double()
    done = attention(info, tables, queries, keys, values, grad_context)
    context, dq, dk, dv = tie_packs(fc_pack, out_pack, beside=done)
    dp_orders = [halving_order(near_bits), halving_order(next_bits)]
    qkv_orders = [halving_order(bits) for bits in qkv_bits]
    attn_parts = Halving(
        *project_context(ids, context, dense_pack, groups, model), "tensor", tensor_bits
    )
    while len(attn_parts.bits) > 2:
        attn_parts.swap()
        attn_parts.add()
    attn_parts.send, context = tie(attn_parts.send, context)
    attn_parts.swap()
    done = attention_weights(
        ids, info, tables, context, dq, dk, dv, sent, grad, gain_attn, shift_attn, qkv_orders
    )
    grads, qkv_bias_sums, *stacks = tie_halves(done, attn_parts)
    attn_parts.add()
    qkv_sums = [Halving(*stacks[:2], "dp", qkv_bits[0]), Halving(*stacks[2:], "dp", qkv_bits[1])]
    sent.arrays[0], attn_parts.send = tie(sent.arrays[0], attn_parts.send)
    attn_parts.swap()
    for parts in qkv_sums:
        parts.swap()
    done = mlp(
        ids, sent, grad, gain_mlp, shift_mlp, fc_pack, fc_rows, out_pack, dp_orders
    )
    done = tie_halves(done, attn_parts, *qkv_sums)
    mlp_send, mlp_keep, hidden, fc_bias_sums, *stacks = done
    attn_parts.add()
    mlp_parts = Halving(mlp_send, mlp_keep, "tensor", tensor_bits)
    mlp_sums = [Halving(*stacks[:2], "dp", near_bits), Halving(*stacks[2:], "dp", next_bits)]
    while len(mlp_parts.bits) > 2:
        mlp_parts.swap()
        mlp_parts.add()
    mlp_parts.swap()
    add_stacks(qkv_sums)
    mlp_parts.add()
    hidden, mlp_parts.send = tie(hidden, mlp_parts.send)
    mlp_parts.swap()
    for parts in qkv_sums + mlp_sums:
        parts.swap()
    done = norm_backward(ids, sent, grads, hidden, gain_attn, gain_mlp, qkv_pack, fc_pack)
    done = tie_halves(done, mlp_parts, *qkv_sums, *mlp_sums)
    back_send, back_keep, norm_sums = done
    mlp_parts.add()

    back_parts = Halving(back_send, back_keep, "tensor", tensor_bits)
    while len(back_parts.bits) > 2:
        back_parts.swap()
        back_parts.add()
    back_parts.swap()
    add_stacks(qkv_sums + mlp_sums)

    back_parts.add()
    stream_in, back_parts.send = tie(stream_in, back_parts.send)
    back_parts.swap()
    for parts in qkv_sums + mlp_sums:
        parts.swap()
    output, sums = finish_output(
        ids,
        stream_in,
        out_grad,
        attn_parts.terms,
        mlp_parts.terms,
        dense_bias[None, :],
        out_bias[None, :],
        norm_sums,
        fc_bias_sums,
        qkv_bias_sums,
        groups,
    )


    sums = sums + swap(sums, "tensor", 1)
    for bit in data_bits[3:]:
        sums = sums + swap(sums, "dp", bit)
    other, *_ = tie_halves([swap(sums, "dp", data_bits[2])], *mlp_sums, qkv_sums[1])
    sums = sums + other
    add_stacks(mlp_sums)
    sums, *sends = tie(sums, *[parts.send for parts in mlp_sums])
    for parts, send in zip(mlp_sums, sends):
        parts.send = send
    for bit in data_bits[:2]:
        sums = sums + swap(sums, "dp", bit)
    sums, back_parts.got = tie(sums, back_parts.got)
    back_parts.add()
    for bit in tensor_bits[1:]:
        sums = sums + swap(sums, "tensor", bit)
    stream_grad = finish_grad(out_grad, normalized, inv_std, back_parts.terms)

    fc_weight_grad, out_weight_grad = finish_mlp_weights(*[x.finish() for x in mlp_sums])
    for parts in qkv_sums:
        parts.add()
    qkv_weight_grad, dense_weight_grad = finish_attention_weights(*[x.finish() for x in qkv_sums])

    count_all = float(rows_local * lax.axis_size("dp") * groups * model)
    gain_attn_grad, shift_attn_grad, gain_mlp_grad, shift_mlp_grad = (sums[x] for x in range(4))
    root_squares = jnp.sqrt(jnp.sum(sums[4:7], axis=1) / count_all)
    residual_grad = sums[7]
    fc_bias_grad = sums[8:12].reshape(-1)
    qkv_bias_grad = by_head(sums[12 : 12 + groups, :qkv_width], heads).reshape(-1)
    return (
        output,
        stream_grad,
        gain_attn_grad,
        shift_attn_grad,
        gain_mlp_grad,
        shift_mlp_grad,
        qkv_weight_grad,
        qkv_bias_grad,
        dense_weight_grad,
        residual_grad,
        fc_weight_grad,
        fc_bias_grad,
        out_weight_grad,
        residual_grad,
        root_squares,
    )


def solution(mesh):
    tokens, weights, rows, whole = (
        P(("dp", "tensor"), None),
        P("dp", "tensor"),
        P("tensor", "dp"),
        P(),
    )
    return jax.shard_map(
        local,
        mesh=mesh,
        in_specs=(
            tokens,
            P("dp"),
            P("dp"),
            whole,
            whole,
            whole,
            whole,
            weights,
            whole,
            rows,
            whole,
            weights,
            whole,
            rows,
            whole,
            tokens,
        ),
        out_specs=(
            tokens,
            tokens,
            whole,
            whole,
            whole,
            whole,
            weights,
            whole,
            rows,
            whole,
            weights,
            whole,
            rows,
            whole,
            whole,
        ),
        check_vma=False,
    )
```

```python
import jax
import jax.numpy as jnp
from jax import lax
from jax.experimental import pallas as pl
from jax.experimental.pallas import tpu as pltpu
from jax.sharding import PartitionSpec as P

HD = 64
ROT = 16
TRUNK = 1024
SEG = 128
TREE = 2560
NB = TREE // SEG
NT = TRUNK // SEG

f32 = jnp.float32
bf16 = jnp.bfloat16
eps_norm = 1e-05
masked_score = -1e30


def dot_nn(left, right):
    return lax.dot_general(left, right, (((1,), (0,)), ((), ())), preferred_element_type=f32)


def dot_nt(left, right):
    return lax.dot_general(left, right, (((1,), (1,)), ((), ())), preferred_element_type=f32)


def dot_tn(left, right):
    return lax.dot_general(left, right, (((0,), (0,)), ((), ())), preferred_element_type=f32)


def bits_of(size):
    bits = []
    bit = 1
    while bit < size:
        bits.append(bit)
        bit *= 2
    return bits


def swap(block, axis, bit):
    size = lax.axis_size(axis)
    return lax.ppermute(block, axis, [(i, i ^ bit) for i in range(size)])


def tie(*values):
    return lax.optimization_barrier(values)


def gather_far(block, axis, bits):
    pieces = [block]
    for bit in bits[1:]:
        pieces = pieces + [swap(piece, axis, bit) for piece in pieces]
    return pieces


class Pack:
    def __init__(self, block, axis, bits):
        self.rows, self.axis, self.bits = block.shape[0], axis, list(bits)
        self.arrays, self.owners = [block], [[0]]

    def double(self):
        bit = self.bits.pop(0)
        held = self.arrays[0] if len(self.arrays) == 1 else jnp.concatenate(self.arrays, axis=0)
        self.owners.append([j ^ bit for owners in self.owners for j in owners])
        self.arrays.append(swap(held, self.axis, bit))

    def specs(self):
        return [pl.BlockSpec(memory_space=pltpu.HBM)] * len(self.arrays)

    def pieces(self):
        return sum(len(owners) for owners in self.owners)

    def copies(self, refs, where, number, done):
        started = []
        for ref, owners in zip(refs, self.owners):
            for at, j in enumerate(owners):
                rows = pl.ds(pl.multiple_of((number ^ j) * self.rows, self.rows), self.rows)
                source = ref.at[pl.ds(at * self.rows, self.rows), :]
                copy = pltpu.make_async_copy(source, where.at[rows, :], done.at[len(started)])
                started.append(copy)
        return started


def tie_packs(*packs, beside=()):
    flat = tie(*beside, *[x for pack in packs for x in pack.arrays])
    at = len(beside)
    for pack in packs:
        pack.arrays = list(flat[at : at + len(pack.arrays)])
        at += len(pack.arrays)
    return list(flat[: len(beside)])


def halving_order(bits):
    if not bits:
        return [0]
    rest = halving_order(bits[1:])
    return [bits[0] ^ j for j in rest] + rest


class Halving:
    def __init__(self, send, keep, axis, bits):
        self.send, self.axis, self.bits = send, axis, list(bits)
        self.terms = [(keep, 0)]

    def swap(self):
        self.got = swap(self.send, self.axis, self.bits.pop(0))

    def add(self):
        self.terms.append((self.got, 0))
        half = self.got.shape[0] // 2
        if half:
            self.send = add_terms(self.terms, half)
            self.terms = [(x, at + half) for x, at in self.terms]

    def most(self):
        while len(self.bits) > 1:
            self.swap()
            self.add()

    def finish(self):
        while self.bits:
            self.swap()
            self.add()
        return self.terms


def tie_halves(values, *halvings):
    flat = tie(*values, *[x.got for x in halvings])
    for x, got in zip(halvings, flat[len(values) :]):
        x.got = got
    return flat[: len(values)]


def resident(shape):
    zeros = (0,) * len(shape)
    return pl.BlockSpec(shape, lambda *_: zeros, pipeline_mode=pl.Buffered(1))


def own_block(rows, columns):
    return pl.BlockSpec((rows, columns), lambda i, ids, *_: (ids[0] ^ ids[2 + i], 0))


def step_block(rows, columns):
    return pl.BlockSpec((rows, columns), lambda i, *_: (i, 0))


def half_blocks(groups, rows, columns):
    half = groups // 2
    shape = (pl.Squeezed(), rows, columns)
    return [
        pl.BlockSpec(shape, lambda i, *_: (jnp.minimum(i, half - 1), 0, 0)),
        pl.BlockSpec(shape, lambda i, *_: (jnp.maximum(i - half, 0), 0, 0)),
    ]


def store_half(send, keep, value, step, groups):
    @pl.when(step < groups // 2)
    def _():
        send[...] = value

    @pl.when(step >= groups // 2)
    def _():
        keep[...] = value


class Tokens:
    def __init__(self, blocks, order):
        blocks = [blocks[j] for j in order]
        self.groups, self.counts = len(blocks), [len(block) for block in blocks]
        self.rows, self.model = sum(x.shape[0] for x in blocks[0]), blocks[0][0].shape[1]
        self.arrays = [x for block in blocks for x in block]
        self.specs = [pl.BlockSpec(memory_space=pltpu.HBM)] * len(self.arrays)

    def scratch(self):
        return [
            pltpu.VMEM((2, self.rows, self.model), bf16),
            pltpu.SemaphoreType.DMA((2, max(self.counts))),
        ]

    def fetch(self, refs, held, done, step):
        def copies(at):
            first, start, found = sum(self.counts[:at]), 0, []
            for k, ref in enumerate(refs[first : first + self.counts[at]]):
                where = held.at[at % 2, pl.ds(start, ref.shape[0]), :]
                found.append(pltpu.make_async_copy(ref, where, done.at[at % 2, k]))
                start += ref.shape[0]
            return found

        for at in range(self.groups):

            @pl.when(step == at)
            def _(at=at):
                ahead = copies(at) if at == 0 else []
                if at + 1 < self.groups:
                    ahead = ahead + copies(at + 1)
                for copy in ahead:
                    copy.start()
                for copy in copies(at):
                    copy.wait()


def store_halves(send, keep, total, number, order, columns=slice(None), source=slice(None)):
    half, rows = send.shape[0], send.shape[1]
    for at, j in enumerate(order):
        where = send if at < half else keep
        block = total[pl.ds(pl.multiple_of((number ^ j) * rows, rows), rows), source]
        where[at % half, :, columns] = block.astype(bf16)


def call(
    kernel, name, grid, prefetch, operands, specs, outs, out_specs, scratch, flops, extra=0, room=12, light=False
):
    size = 0 if light else sum(x.size * x.dtype.itemsize for x in [*operands, *outs])
    return pl.pallas_call(
        kernel,
        grid_spec=pltpu.PrefetchScalarGridSpec(
            num_scalar_prefetch=len(prefetch),
            grid=grid,
            in_specs=specs,
            out_specs=out_specs,
            scratch_shapes=scratch,
        ),
        out_shape=outs,
        compiler_params=pltpu.CompilerParams(
            dimension_semantics=("arbitrary",) * len(grid), vmem_limit_bytes=room << 20
        ),
        cost_estimate=pl.CostEstimate(
            flops=int(flops), bytes_accessed=int(size), transcendentals=int(extra)
        ),
        name=name,
    )(*prefetch, *operands)


def shaped(*shape, dtype=bf16):
    return jax.ShapeDtypeStruct(shape, dtype)


def shift_gain(block, gain, shift):
    return (block.astype(f32) * gain[...] + shift[...]).astype(bf16)


def turn(block, cosine, sine, sign):
    width = block.shape[1]
    step = min(width, 128)
    lane = lax.broadcasted_iota(jnp.int32, (block.shape[0], step), 1) % HD
    done = []
    for start in range(0, width, step):
        part = block[:, start : start + step]
        if step == 128:
            left = pltpu.roll(part, step - ROT // 2, 1)
            right = pltpu.roll(part, ROT // 2, 1)
        else:
            left = jnp.concatenate([part[:, ROT // 2 :], part[:, : ROT // 2]], axis=1)
            right = jnp.concatenate([part[:, -ROT // 2 :], part[:, : -ROT // 2]], axis=1)
        moved = jnp.where(lane < ROT // 2, -left, right) * sine[:, :step]
        done.append(part * cosine[:, :step] + moved * sign)
    return done[0] if len(done) == 1 else jnp.concatenate(done, axis=1)


def weight_scratch(pack):
    model = pack.rows * pack.pieces()
    columns = pack.arrays[0].shape[1]
    return [pltpu.VMEM((model, columns), bf16), pltpu.SemaphoreType.DMA((pack.pieces(),))]


def prepare_weights(qkv, dense, fc, out):
    rows, columns = qkv.shape
    width = columns // 3

    def kernel(qkv_ref, dense_ref, fc_ref, out_ref, qkv_to, dense_to, fc_to, out_to):
        for head in range(width // HD):
            for kind in range(3):
                at, own = (3 * head + kind) * HD, kind * width + head * HD
                qkv_to[:, own : own + HD] = qkv_ref[:, at : at + HD].astype(bf16)
        dense_to[...] = dense_ref[...].T.astype(bf16)
        fc_to[...] = fc_ref[...].astype(bf16)
        out_to[...] = out_ref[...].T.astype(bf16)

    operands = [qkv, dense, fc, out]
    outs = [shaped(*qkv.shape), shaped(*dense.shape[::-1]), shaped(*fc.shape), shaped(*out.shape[::-1])]
    return call(
        kernel,
        "prepare_weights",
        (1,),
        [],
        operands,
        [resident(x.shape) for x in operands],
        outs,
        [resident(x.shape) for x in outs],
        [],
        rows * columns,
    )


def normalize(stream):
    rows, model = stream.shape
    block = 160

    def kernel(stream_ref, sent_ref, norm_ref, std_ref):
        field = stream_ref[...]
        centred = field - jnp.sum(field, axis=1, keepdims=True) / model
        variance = jnp.sum(centred * centred, axis=1, keepdims=True) / model
        scale = lax.rsqrt(variance + eps_norm)
        norm = centred * scale
        norm_ref[...] = norm
        sent_ref[...] = norm.astype(bf16)
        std_ref[...] = scale

    return call(
        kernel,
        "normalize",
        (rows // block,),
        [],
        [stream],
        [step_block(block, model)],
        [shaped(rows, model), shaped(rows, model, dtype=f32), shaped(rows, 1, dtype=f32)],
        [step_block(block, model), step_block(block, model), step_block(block, 1)],
        [],
        rows * model * 8,
        room=62,
    )


def project_qkv(ids, info, sent, gain, shift, pack, bias, tables, width):
    groups, held, rows, model = sent.groups, len(sent.arrays), sent.rows, sent.model

    def kernel(ids, info, *refs):
        sent_refs, refs = refs[:held], refs[held:]
        weight_refs, refs = refs[: len(pack.arrays)], refs[len(pack.arrays) :]
        gain, shift, bias, cos, sine, q_out, k_out, v_out = refs[:8]
        block, arrived, whole, placed, added = refs[8:]
        step = pl.program_id(0)

        @pl.when(step == 0)
        def _():
            for copy in pack.copies(weight_refs, whole, ids[1], placed):
                copy.start()

        sent.fetch(sent_refs, block, arrived, step)

        @pl.when(step == 0)
        def _():
            for copy in pack.copies(weight_refs, whole, ids[1], placed):
                copy.wait()
            own = bias[pl.ds(ids[0], 1), :]
            for head in range(width // HD):
                for kind in range(3):
                    at, to = (3 * head + kind) * HD, kind * width + head * HD
                    added[:, to : to + HD] = own[:, at : at + HD]

        token = block[step % 2]
        qkv = dot_nn(shift_gain(token, gain, shift), whole[...]) + added[...]
        first = (ids[0] ^ ids[2 + step]) * (rows // SEG)
        for at in range(rows // SEG):
            number = first + at
            table = pl.ds(pl.multiple_of(info[number // NB, number % NB, 4] * SEG, SEG), SEG)
            tabs = (cos[table, :], sine[table, :])
            own = slice(at * SEG, (at + 1) * SEG)
            q_out[own, :] = (turn(qkv[own, :width], *tabs, 1.0) * HD**-0.5).astype(bf16)
            k_out[own, :] = turn(qkv[own, width : 2 * width], *tabs, 1.0).astype(bf16)
        v_out[...] = qkv[:, 2 * width :].astype(bf16)

    operands = [*sent.arrays, *pack.arrays, gain, shift, bias, *tables]
    out = shaped(groups * rows, width)
    return call(
        kernel,
        "project_qkv",
        (groups,),
        [ids, info],
        operands,
        sent.specs
        + pack.specs()
        + [resident(x.shape) for x in operands[held + len(pack.arrays) :]],
        [out] * 3,
        [own_block(rows, width)] * 3,
        sent.scratch() + weight_scratch(pack) + [pltpu.VMEM((1, 3 * width), f32)],
        2 * groups * rows * model * 3 * width,
        room=62,
    )


def project_grad(ids, grad, pack, width):
    groups, held, rows, model = grad.groups, len(grad.arrays), grad.rows, grad.model

    def kernel(ids, *refs):
        grad_refs, refs = refs[:held], refs[held:]
        weight_refs, (out, block, arrived, whole, placed) = refs[:-5], refs[-5:]
        step = pl.program_id(0)

        @pl.when(step == 0)
        def _():
            for copy in pack.copies(weight_refs, whole, ids[1], placed):
                copy.start()

        grad.fetch(grad_refs, block, arrived, step)

        @pl.when(step == 0)
        def _():
            for copy in pack.copies(weight_refs, whole, ids[1], placed):
                copy.wait()

        out[...] = dot_nn(block[step % 2], whole[...]).astype(bf16)

    operands = [*grad.arrays, *pack.arrays]
    return call(
        kernel,
        "project_grad",
        (groups,),
        [ids],
        operands,
        grad.specs + pack.specs(),
        [shaped(groups * rows, width)],
        [own_block(rows, width)],
        grad.scratch() + weight_scratch(pack),
        2 * groups * rows * model * width,
    )[0]


def attention_kernel(
    info, q_ref, do_ref, k_ref, v_ref, cos, sine, ctx_ref, dq_ref, dk_ref, dv_ref, dk_sum, dv_sum
):
    tree, step = pl.program_id(0), pl.program_id(1)
    width = q_ref.shape[1]
    heads = width // HD
    lane_head = lax.broadcasted_iota(jnp.int32, (SEG, width), 1) // HD

    @pl.when(step == 0)
    def _():
        dk_sum[...] = jnp.zeros_like(dk_sum)
        dv_sum[...] = jnp.zeros_like(dv_sum)

    first, second = info[tree, step, 0], info[tree, step, 1]
    first_rows = pl.ds(pl.multiple_of(first * SEG, SEG), SEG)
    second_rows = pl.ds(pl.multiple_of(second * SEG, SEG), SEG)
    queries, grads = q_ref[...], do_ref[...]
    zero = jnp.zeros_like(queries)
    q_rows = jnp.concatenate([jnp.where(lane_head == h, queries, zero) for h in range(heads)], axis=0)
    g_rows = jnp.concatenate([jnp.where(lane_head == h, grads, zero) for h in range(heads)], axis=0)
    q_turned, g_turned = queries.T, grads.T
    ahead = lax.broadcasted_iota(jnp.int32, (SEG, SEG), 1) - lax.broadcasted_iota(
        jnp.int32, (SEG, SEG), 0
    )
    seen = jnp.concatenate([ahead <= info[tree, step, 2], ahead <= info[tree, step, 3]], axis=1)
    seen = jnp.concatenate([seen] * heads, axis=0)
    k_near = jnp.concatenate([k_ref[first_rows, :], k_ref[second_rows, :]], axis=0)
    v_near = jnp.concatenate([v_ref[first_rows, :], v_ref[second_rows, :]], axis=0)

    def work(pairs):
        count = pairs * 2 * SEG
        near = jnp.where(seen, dot_nt(q_rows, k_near), masked_score)
        most = jnp.max(near, axis=1, keepdims=True)
        if count:
            k_far, v_far = k_ref[0:count, :], v_ref[0:count, :]
            far = dot_nt(q_rows, k_far)
            most = jnp.maximum(most, jnp.max(far, axis=1, keepdims=True))
        near = jnp.exp(near - most)
        total = jnp.sum(near, axis=1, keepdims=True)
        if count:
            far = jnp.exp(far - most)
            total = total + jnp.sum(far, axis=1, keepdims=True)
        scale = 1.0 / total
        near = near * scale
        near_low = near.astype(bf16)
        context = dot_nn(near_low, v_near)
        if count:
            far = far * scale
            far_low = far.astype(bf16)
            context = context + dot_nn(far_low, v_far)
        delta = jnp.sum(context * g_rows.astype(f32), axis=1, keepdims=True)
        near = (near * (dot_nt(g_rows, v_near) - delta)).astype(bf16)
        dq = dot_nn(near, k_near)
        if count:
            far = (far * (dot_nt(g_rows, v_far) - delta)).astype(bf16)
            dq = dq + dot_nn(far, k_far)
        ctx_own, dq_own = context[0:SEG], dq[0:SEG]
        for h in range(1, heads):
            ctx_own = jnp.where(lane_head == h, context[h * SEG : (h + 1) * SEG], ctx_own)
            dq_own = jnp.where(lane_head == h, dq[h * SEG : (h + 1) * SEG], dq_own)
        ctx_ref[...] = ctx_own.astype(bf16)
        dq_ref[...] = turn(dq_own * HD**-0.5, cos, sine, -1.0).astype(bf16)
        for h in range(heads):
            own = slice(h * SEG, (h + 1) * SEG)
            part = slice(h * HD, (h + 1) * HD)
            dk = dot_nn(q_turned[part], near[own])
            dv = dot_nn(g_turned[part], near_low[own])
            dk_sum[first, part, :] += dk[:, :SEG]
            dv_sum[first, part, :] += dv[:, :SEG]
            dk_sum[second, part, :] += dk[:, SEG:]
            dv_sum[second, part, :] += dv[:, SEG:]
            if count:
                dk = dot_nn(q_turned[part], far[own])
                dv = dot_nn(g_turned[part], far_low[own])
                for j in range(2 * pairs):
                    dk_sum[j, part, :] += dk[:, j * SEG : (j + 1) * SEG]
                    dv_sum[j, part, :] += dv[:, j * SEG : (j + 1) * SEG]

    for pairs in range(NT // 2):

        @pl.when(step // 2 == pairs)
        def _(pairs=pairs):
            work(pairs)

    @pl.when(step >= NT)
    def _():
        work(NT // 2)

    @pl.when(step == NB - 1)
    def _():
        def finish(j, carry):
            rows = pl.ds(pl.multiple_of(j * SEG, SEG), SEG)
            dv_ref[rows, :] = dv_sum[j].T.astype(bf16)
            dk_ref[rows, :] = dk_sum[j].T.astype(bf16)
            return carry

        lax.fori_loop(0, NB, finish, 0)


def attention(info, tables, queries, keys, values, grads):
    total, width = queries.shape
    trees = total // TREE
    table_width = tables[0].shape[1]
    block = pl.BlockSpec((SEG, width), lambda t, b, info: (t * NB + b, 0))
    whole = pl.BlockSpec((TREE, width), lambda t, b, info: (t, 0))
    table = pl.BlockSpec((SEG, table_width), lambda t, b, info: (info[t, b, 4], 0))
    scores = trees * (TREE - TRUNK) * (TRUNK + 2 * SEG) * (width // HD)
    return call(
        attention_kernel,
        "attention",
        (trees, NB),
        [info],
        [queries, grads, keys, values, *tables],
        [block, block, whole, whole, table, table],
        [shaped(total, width)] * 4,
        [block, block, whole, whole],
        [pltpu.VMEM((NB, width, SEG), f32), pltpu.VMEM((NB, width, SEG), f32)],
        scores * width * 2 * 6 * 1.3,
        scores,
        room=22,
    )


def project_context(ids, context, pack, groups, model):
    rows, width = context.shape[0] // groups, context.shape[1]

    def kernel(ids, ctx, *refs):
        weight_refs, (send, keep, whole, placed) = refs[:-4], refs[-4:]
        step = pl.program_id(0)

        @pl.when(step == 0)
        def _():
            copies = pack.copies(weight_refs, whole, ids[1], placed)
            for copy in copies:
                copy.start()
            for copy in copies:
                copy.wait()

        store_half(send, keep, dot_nt(ctx[...], whole[...]).astype(bf16), step, groups)

    operands = [context, *pack.arrays]
    half = shaped(groups // 2, rows, model)
    return call(
        kernel,
        "project_context",
        (groups,),
        [ids],
        operands,
        [own_block(rows, width)] + pack.specs(),
        [half] * 2,
        half_blocks(groups, rows, model),
        weight_scratch(pack),
        2 * groups * rows * model * width,
        room=14,
    )


def attention_weights(ids, info, tables, context, dq, dk, dv, sent, grad, gain, shift, orders):
    groups, held, rows, model = sent.groups, len(sent.arrays), sent.rows, sent.model
    width, count = dq.shape[1], len(orders[0])

    def kernel(ids, info, ctx_ref, dq_ref, dk_ref, dv_ref, *refs):
        sent_refs, refs = refs[:held], refs[held:]
        grad_refs, refs = refs[: len(grad.arrays)], refs[len(grad.arrays) :]
        gain, shift, cos, sine, grads, bias_ref, *stacks = refs[:10]
        block, arrived, grad_block, grad_arrived, total, dense_total = refs[10:]
        step = pl.program_id(0)

        @pl.when(step == 0)
        def _():
            total[...] = jnp.zeros_like(total)
            dense_total[...] = jnp.zeros_like(dense_total)
            bias_ref[...] = jnp.zeros_like(bias_ref)

        sent.fetch(sent_refs, block, arrived, step)
        grad.fetch(grad_refs, grad_block, grad_arrived, step)
        grads[:, :width] = dq_ref[...]
        first = (ids[0] ^ ids[2 + step]) * (rows // SEG)
        for at in range(rows // SEG):
            number = first + at
            table = pl.ds(pl.multiple_of(info[number // NB, number % NB, 4] * SEG, SEG), SEG)
            own = slice(at * SEG, (at + 1) * SEG)
            turned = turn(dk_ref[own, :], cos[table, :], sine[table, :], -1.0)
            grads[own, width : 2 * width] = turned.astype(bf16)
        grads[:, 2 * width :] = dv_ref[...]
        bias_ref[0:1, :] += jnp.sum(grads[...].astype(f32), axis=0, keepdims=True)
        total[...] += dot_tn(shift_gain(block[step % 2], gain, shift), grads[...])
        dense_total[...] += dot_tn(grad_block[step % 2], ctx_ref[...])

        @pl.when(step == groups - 1)
        def _():
            store_halves(*stacks[:2], total, ids[1], orders[0], source=slice(0, 2 * width))
            source = slice(2 * width, 3 * width)
            store_halves(*stacks[2:], total, ids[1], orders[1], slice(0, width), source)
            columns = slice(width, 2 * width)
            store_halves(*stacks[2:], dense_total, ids[1], orders[1], columns)

    operands = [context, dq, dk, dv, *sent.arrays, *grad.arrays, gain, shift, *tables]
    outs = [shaped(groups * rows, 3 * width), shaped(8, 3 * width, dtype=f32)]
    outs += [shaped(count // 2, model // count, 2 * width)] * 4
    return call(
        kernel,
        "attention_weights",
        (groups,),
        [ids, info],
        operands,
        [own_block(rows, width)] * 4
        + sent.specs
        + grad.specs
        + [resident(x.shape) for x in operands[-4:]],
        outs,
        [step_block(rows, 3 * width)] + [resident(x.shape) for x in outs[1:]],
        sent.scratch()
        + grad.scratch()
        + [pltpu.VMEM((model, 3 * width), f32), pltpu.VMEM((model, width), f32)],
        2 * groups * rows * model * 4 * width,
        room=24,
    )


def mlp(ids, sent, grad, gain, shift, fc, bias, out, orders):
    groups, held, rows, model = sent.groups, len(sent.arrays), sent.rows, sent.model
    pieces, units = len(fc.arrays), fc.arrays[0].shape[1]

    def kernel(ids, *refs):
        sent_refs, refs = refs[:held], refs[held:]
        grad_refs, refs = refs[: len(grad.arrays)], refs[len(grad.arrays) :]
        fc_refs, refs = refs[:pieces], refs[pieces:]
        out_refs, refs = refs[:pieces], refs[pieces:]
        gain, shift, bias, part_send, part_keep, hidden_ref, bias_ref = refs[:7]
        stacks, refs = refs[7:11], refs[11:]
        block, arrived, grad_block, grad_arrived, fc_whole, fc_placed, out_whole, out_placed = refs[:8]
        act_ref, fc_total, out_total = refs[8:]
        step = pl.program_id(0)

        def weights():
            copies = fc.copies(fc_refs, fc_whole, ids[1], fc_placed)
            return copies + out.copies(out_refs, out_whole, ids[1], out_placed)

        @pl.when(step == 0)
        def _():
            for copy in weights():
                copy.start()
            fc_total[...] = jnp.zeros_like(fc_total)
            out_total[...] = jnp.zeros_like(out_total)
            bias_ref[...] = jnp.zeros_like(bias_ref)

        sent.fetch(sent_refs, block, arrived, step)
        grad.fetch(grad_refs, grad_block, grad_arrived, step)

        @pl.when(step == 0)
        def _():
            for copy in weights():
                copy.wait()

        token, grads = block[step % 2], grad_block[step % 2]
        normed = shift_gain(token, gain, shift)
        count = 2
        parts = [slice(k * rows // count, (k + 1) * rows // count) for k in range(count)]
        added = bias[pl.ds(ids[0], 1), :]
        hidden = [dot_nn(normed[x], fc_whole[...]) + added for x in parts]
        back = [dot_nn(grads[x], out_whole[...]) for x in parts]
        for x, field, slope in zip(parts, hidden, back):
            chance = 0.5 + 0.5 * lax.erf(field * 0.7071067811865476)
            bell = jnp.exp(field * field * -0.5) * 0.3989422804014327
            act_ref[x, :] = (field * chance).astype(bf16)
            low = (slope * (chance + field * bell)).astype(bf16)
            hidden_ref[x, :] = low
            bias_ref[0:1, :] += jnp.sum(low.astype(f32), axis=0, keepdims=True)
        store_half(
            part_send, part_keep, dot_nt(act_ref[...], out_whole[...]).astype(bf16), step, groups
        )
        out_total[...] += dot_tn(grads, act_ref[...])
        fc_total[...] += dot_tn(normed, hidden_ref[...])

        @pl.when(step == groups - 1)
        def _():
            half = units // 2
            for at, order in enumerate(orders):
                stack = stacks[2 * at : 2 * at + 2]
                source = slice(at * half, (at + 1) * half)
                store_halves(*stack, fc_total, ids[1], order, slice(0, half), source)
                store_halves(*stack, out_total, ids[1], order, slice(half, units), source)

    operands = [*sent.arrays, *grad.arrays, *fc.arrays, *out.arrays, gain, shift, bias]
    count = model // fc.rows
    outs = [
        shaped(groups // 2, rows, model),
        shaped(groups // 2, rows, model),
        shaped(groups * rows, units),
        shaped(8, units, dtype=f32),
    ]
    outs += [shaped(count // 2, fc.rows, units)] * 4
    return call(
        kernel,
        "mlp",
        (groups,),
        [ids],
        operands,
        sent.specs
        + grad.specs
        + fc.specs()
        + out.specs()
        + [resident(x.shape) for x in operands[-3:]],
        outs,
        half_blocks(groups, rows, model)
        + [step_block(rows, units)]
        + [resident(x.shape) for x in outs[3:]],
        sent.scratch()
        + grad.scratch()
        + weight_scratch(fc)
        + weight_scratch(out)
        + [
            pltpu.VMEM((rows, units), bf16),
            pltpu.VMEM((model, units), f32),
            pltpu.VMEM((model, units), f32),
        ],
        10 * groups * rows * model * units,
        room=42,
    )


def norm_backward(ids, sent, grads, hidden, gain_attn, gain_mlp, qkv_pack, fc):
    groups, held, rows, model = sent.groups, len(sent.arrays), sent.rows, sent.model
    pieces, units, columns = len(fc.arrays), hidden.shape[1], grads.shape[1]

    def kernel(ids, grads_ref, hidden_ref, *refs):
        sent_refs, refs = refs[:held], refs[held:]
        qkv_refs, refs = refs[:pieces], refs[pieces:]
        fc_refs, refs = refs[:pieces], refs[pieces:]
        gain_attn, gain_mlp, send, keep, sums_ref = refs[:5]
        block, arrived, qkv_whole, qkv_placed, fc_whole, fc_placed = refs[5:]
        step = pl.program_id(0)

        def weights():
            copies = qkv_pack.copies(qkv_refs, qkv_whole, ids[1], qkv_placed)
            return copies + fc.copies(fc_refs, fc_whole, ids[1], fc_placed)

        @pl.when(step == 0)
        def _():
            for copy in weights():
                copy.start()
            sums_ref[...] = jnp.zeros_like(sums_ref)

        sent.fetch(sent_refs, block, arrived, step)

        @pl.when(step == 0)
        def _():
            for copy in weights():
                copy.wait()

        back_attn = dot_nt(grads_ref[...], qkv_whole[...])
        back_mlp = dot_nt(hidden_ref[...], fc_whole[...])
        token = block[step % 2].astype(f32)
        for at, back in enumerate((back_attn, back_mlp)):
            sums_ref[2 * at : 2 * at + 1, :] += jnp.sum(back * token, axis=0, keepdims=True)
            sums_ref[2 * at + 1 : 2 * at + 2, :] += jnp.sum(back, axis=0, keepdims=True)
        part = back_attn * gain_attn[...] + back_mlp * gain_mlp[...]
        store_half(send, keep, part.astype(bf16), step, groups)

    operands = [grads, hidden, *sent.arrays, *qkv_pack.arrays, *fc.arrays, gain_attn, gain_mlp]
    outs = [
        shaped(groups // 2, rows, model),
        shaped(groups // 2, rows, model),
        shaped(8, model, dtype=f32),
    ]
    return call(
        kernel,
        "norm_backward",
        (groups,),
        [ids],
        operands,
        [step_block(rows, columns), step_block(rows, units)]
        + sent.specs
        + qkv_pack.specs()
        + fc.specs()
        + [resident(x.shape) for x in operands[-2:]],
        outs,
        half_blocks(groups, rows, model) + [resident(x.shape) for x in outs[2:]],
        sent.scratch() + weight_scratch(qkv_pack) + weight_scratch(fc),
        2 * groups * rows * model * (units + columns),
        room=26,
    )


def taken(terms, block):
    return [
        pl.BlockSpec((pl.Squeezed(), block, x.shape[2]), lambda i, *_, at=at: (at, i, 0))
        for x, at in terms
    ]


def add_terms(terms, half):
    _, rows, columns = terms[0][0].shape
    block = max(x for x in (320, 128, 64) if rows % x == 0)

    def kernel(*refs):
        refs[-1][...] = sum(x[...].astype(f32) for x in refs[:-1]).astype(bf16)

    shape = (pl.Squeezed(), block, columns)
    out = shaped(half, rows, columns)
    return call(
        kernel,
        "add_terms",
        (half, rows // block),
        [],
        [x for x, _ in terms],
        [pl.BlockSpec(shape, lambda k, i, *_, at=at: (at + k, i, 0)) for _, at in terms],
        [out],
        [pl.BlockSpec(shape, lambda k, i, *_: (k, i, 0))],
        [],
        half * rows * columns * len(terms),
    )[0]


def whole_terms(terms, count):
    return [
        pl.BlockSpec((count, *x.shape[1:]), lambda *_, at=at: (at // count, 0, 0)) for x, at in terms
    ]


def add_stacks(stacks):
    counts = []
    for parts in stacks:
        parts.terms.append((parts.got, 0))
        counts.append(parts.got.shape[0] // 2)
    held = [len(parts.terms) for parts in stacks]
    operands = [x for parts in stacks for x, _ in parts.terms]

    def kernel(*refs):
        for at, half in enumerate(counts):
            first = sum(held[:at])
            total = sum(x[...].astype(f32) for x in refs[first : first + held[at]])
            refs[len(operands) + at][...] = total.astype(bf16)

    outs = [shaped(n, *parts.got.shape[1:]) for n, parts in zip(counts, stacks)]
    sends = call(
        kernel,
        "add_stacks",
        (1,),
        [],
        operands,
        [x for n, parts in zip(counts, stacks) for x in whole_terms(parts.terms, n)],
        outs,
        [resident(x.shape) for x in outs],
        [],
        sum(x.size for x in operands) // 2,
        room=16,
    )
    for n, parts, send in zip(counts, stacks, sends):
        parts.send = send
        parts.terms = [(x, at + n) for x, at in parts.terms]


def finish_mlp_weights(first, second):
    held, (_, rows, units) = len(first), first[0][0].shape
    half = units // 2

    def kernel(*refs):
        low = sum(x[0].astype(f32) for x in refs[:held])
        high = sum(x[0].astype(f32) for x in refs[held:-2])
        refs[-2][:, :half] = low[:, :half]
        refs[-2][:, half:] = high[:, :half]
        refs[-1][:half, :] = low[:, half:].T
        refs[-1][half:, :] = high[:, half:].T

    operands = [x for x, _ in [*first, *second]]
    outs = [shaped(rows, units, dtype=f32), shaped(units, rows, dtype=f32)]
    return call(
        kernel,
        "finish_mlp_weights",
        (1,),
        [],
        operands,
        whole_terms([*first, *second], 1),
        outs,
        [resident(x.shape) for x in outs],
        [],
        len(operands) * rows * units,
    )


def finish_attention_weights(first, second):
    held, (_, rows, columns) = len(first), first[0][0].shape
    width = columns // 2

    def kernel(*refs):
        low = sum(x[0].astype(f32) for x in refs[:held])
        high = sum(x[0].astype(f32) for x in refs[held:-2])
        for head in range(width // HD):
            for kind, (source, start) in enumerate(((low, 0), (low, width), (high, 0))):
                at = (3 * head + kind) * HD
                own = start + head * HD
                refs[-2][:, at : at + HD] = source[:, own : own + HD]
        refs[-1][...] = high[:, width:].T

    operands = [x for x, _ in [*first, *second]]
    outs = [shaped(rows, 3 * width, dtype=f32), shaped(width, rows, dtype=f32)]
    return call(
        kernel,
        "finish_attention_weights",
        (1,),
        [],
        operands,
        whole_terms([*first, *second], 1),
        outs,
        [resident(x.shape) for x in outs],
        [],
        len(operands) * rows * columns,
    )


def sum_rows(groups):
    return (12 + groups + 7) // 8 * 8


def finish_output(ids, stream, grad, attn_terms, mlp_terms, dense_bias, out_bias, norm_sums, fc_sums, qkv_sums, groups):
    rows, model = stream.shape
    block = 160
    first, second = len(attn_terms), len(mlp_terms)
    units, columns = fc_sums.shape[1], qkv_sums.shape[1]
    across = model // units

    def kernel(ids, stream_ref, grad_ref, *refs):
        attn_refs, refs = refs[:first], refs[first:]
        mlp_refs, refs = refs[:second], refs[second:]
        dense_bias, out_bias, norm_ref, fc_ref, qkv_ref, out_ref, sums_ref = refs

        @pl.when(pl.program_id(0) == 0)
        def _():
            sums_ref[...] = jnp.zeros_like(sums_ref)
            sums_ref[0:4, :] = norm_ref[0:4, :]
            own = jnp.concatenate([fc_ref[0:1, :]] * across, axis=1) if across > 1 else fc_ref[0:1, :]
            lane = lax.broadcasted_iota(jnp.int32, (1, model), 1) // units
            sums_ref[pl.ds(8 + ids[0] // across, 1), :] = jnp.where(lane == ids[0] % across, own, 0.0)
            sums_ref[pl.ds(12 + ids[0], 1), :columns] = qkv_ref[0:1, :]

        attn = sum(x[...].astype(f32) for x in attn_refs) + dense_bias[...]
        mlp = sum(x[...].astype(f32) for x in mlp_refs) + out_bias[...]
        output = stream_ref[...] + attn + mlp
        out_ref[...] = output
        for at, value in enumerate((output, attn, mlp)):
            sums_ref[4 + at : 5 + at, :] += jnp.sum(value * value, axis=0, keepdims=True)
        sums_ref[7:8, :] += jnp.sum(grad_ref[...].astype(f32), axis=0, keepdims=True)

    terms = [*attn_terms, *mlp_terms]
    operands = [stream, grad, *[x for x, _ in terms], dense_bias, out_bias, norm_sums, fc_sums, qkv_sums]
    outs = [shaped(rows, model, dtype=f32), shaped(sum_rows(groups), model, dtype=f32)]
    return call(
        kernel,
        "finish_output",
        (rows // block,),
        [ids],
        operands,
        [step_block(block, model), step_block(block, model)]
        + taken(terms, block)
        + [resident(x.shape) for x in operands[-5:]],
        outs,
        [step_block(block, model), resident(outs[1].shape)],
        [],
        rows * model * 16,
        room=16,
    )


def finish_grad(grad, normalized, inv_std, terms):
    rows, model = grad.shape
    block = 160

    def kernel(grad_ref, norm_ref, std_ref, *refs):
        term_refs, out_ref = refs[:-1], refs[-1]
        sent = sum(x[...].astype(f32) for x in term_refs)
        norm = norm_ref[...]
        mean = jnp.sum(sent, axis=1, keepdims=True) / model
        cross = jnp.sum(sent * norm, axis=1, keepdims=True) / model
        out_ref[...] = grad_ref[...].astype(f32) + std_ref[...] * (sent - mean - norm * cross)

    operands = [grad, normalized, inv_std, *[x for x, _ in terms]]
    return call(
        kernel,
        "finish_grad",
        (rows // block,),
        [],
        operands,
        [step_block(block, model), step_block(block, model), step_block(block, 1)]
        + taken(terms, block),
        [shaped(rows, model, dtype=f32)],
        [step_block(block, model)],
        [],
        0,
        light=True,
    )[0]


def tree_table(segment_ids, parent_ids):
    trees = segment_ids.shape[0] // TREE

    def kernel(segment, parent, table):
        for tree in range(trees):
            for block in range(NT):
                odd = block % 2
                row = (block - odd, block - odd + 1, SEG * odd, -SEG * (1 - odd), block)
                for at, value in enumerate(row):
                    table[tree, block, at] = value

            def place(block, carry):
                first = tree * TREE
                owner = parent[first + block * SEG]
                leaf = (owner != segment[first]).astype(jnp.int32)
                at = block
                for other in range(NT, NB):
                    at = jnp.where(segment[first + other * SEG] == owner, other, at)
                table[tree, block, 0] = block
                table[tree, block, 1] = at
                table[tree, block, 2] = 0
                table[tree, block, 3] = SEG * (2 * leaf - 1)
                table[tree, block, 4] = NT + leaf
                return carry

            lax.fori_loop(NT, NB, place, 0)

    smem = pl.BlockSpec(memory_space=pltpu.SMEM)
    return pl.pallas_call(
        kernel,
        in_specs=[smem, smem],
        out_specs=smem,
        out_shape=jax.ShapeDtypeStruct((trees, NB, 5), jnp.int32),
        name="tree_table",
    )(segment_ids, parent_ids)


def angle_tables(zero):
    places = TRUNK + 2 * SEG
    place = lax.broadcasted_iota(jnp.int32, (places, 2 * HD), 0).astype(f32)
    lane = lax.broadcasted_iota(jnp.int32, (places, 2 * HD), 1) % HD
    half = ROT // 2
    frequency = 10000.0 ** (-((lane % half).astype(f32) * 2.0 / ROT))
    angle = (place + zero) * frequency
    cosine = jnp.where(lane < ROT, jnp.cos(angle), 1.0)
    sine = jnp.where(lane < ROT, jnp.sin(angle), 0.0)
    return cosine, sine


def by_kind(array, heads):
    shape = array.shape[:-1]
    array = array.reshape(*shape, heads, 3, HD)
    return jnp.swapaxes(array, -3, -2).reshape(*shape, 3 * heads * HD)


def by_head(array, heads):
    shape = array.shape[:-1]
    array = array.reshape(*shape, 3, heads, HD)
    return jnp.swapaxes(array, -3, -2).reshape(*shape, 3 * heads * HD)


def local(
    stream_in,
    segment_ids,
    parent_ids,
    norm_gain_attn,
    norm_shift_attn,
    norm_gain_mlp,
    norm_shift_mlp,
    qkv_weight,
    qkv_bias,
    dense_weight,
    dense_bias,
    fc_weight,
    fc_bias,
    out_weight,
    out_bias,
    out_grad,
):
    tensor_rank = lax.axis_index("tensor")
    data_rank = lax.axis_index("dp")
    rows_local = stream_in.shape[0]
    model = stream_in.shape[1]
    qkv_width = qkv_weight.shape[1]
    heads = qkv_width // (3 * HD)
    width = heads * HD
    units = fc_weight.shape[1]
    groups = lax.axis_size("tensor")
    tensor_bits = bits_of(groups)
    far_first = tensor_bits[:0:-1] + tensor_bits[:1]
    order = halving_order(tensor_bits)
    ids = jnp.stack([tensor_rank, data_rank, *order]).astype(jnp.int32)
    data_bits = bits_of(lax.axis_size("dp"))
    rows_first = data_bits[:0:-1] + data_bits[:1]
    columns_first = data_bits[:1] + data_bits[:0:-1]
    near_bits = data_bits
    next_bits = data_bits[1:2] + data_bits[:1] + data_bits[2:]
    qkv_bits = [data_bits[:1] + data_bits[:0:-1], next_bits]

    blocks = prepare_weights(qkv_weight, dense_weight, fc_weight, out_weight)
    qkv_pack = Pack(blocks[0], "dp", rows_first)
    dense_pack = Pack(blocks[1], "dp", columns_first)
    fc_pack = Pack(blocks[2], "dp", rows_first)
    out_pack = Pack(blocks[3], "dp", rows_first)

    sent_norm, normalized, inv_std = normalize(stream_in)
    sent = gather_far(sent_norm, "tensor", tensor_bits)

    info = tree_table(segment_ids, parent_ids)
    gain_attn, shift_attn = norm_gain_attn[None, :], norm_shift_attn[None, :]
    gain_mlp, shift_mlp = norm_gain_mlp[None, :], norm_shift_mlp[None, :]
    sent_near, near = swap(sent[0], "tensor", 1), swap(out_grad, "tensor", 1)
    cut = rows_local * 3 // 5
    early, late = out_grad[:cut], out_grad[cut:]
    qkv_pack.double()
    dense_pack.double()
    zero = jnp.zeros((), f32)
    near, early, late, zero, qkv_bias, fc_bias, info = tie_packs(
        qkv_pack, dense_pack, fc_pack, beside=[near, early, late, zero, qkv_bias, fc_bias, info]
    )
    tables = angle_tables(zero)
    qkv_rows, fc_rows = qkv_bias.reshape(groups, qkv_width), fc_bias.reshape(groups, units)
    while len(qkv_pack.bits) > 1:
        qkv_pack.double()
        dense_pack.double()
    fc_pack.double()
    done = tie_packs(
        qkv_pack,
        dense_pack,
        out_pack,
        beside=[early, late, *tables, qkv_rows, fc_rows, sent_near, *sent],
    )
    early, late, *done = done
    tables, (qkv_rows, fc_rows, sent_near), sent = done[:2], done[2:5], done[5:]
    early_far = gather_far(early, "tensor", tensor_bits)[1:]
    sent_near = [sent_near] + [swap(x, "tensor", 1) for x in sent[1:]]
    sent = [x for pair in zip(sent, sent_near) for x in pair]
    qkv_pack.double()
    dense_pack.double()
    late, *done = tie_packs(
        qkv_pack, dense_pack, fc_pack, out_pack, beside=[late, *sent, *early_far]
    )
    sent, early_far = Tokens([(x,) for x in done[:groups]], order), done[groups:]
    late_far = gather_far(late, "tensor", tensor_bits)[1:]
    early_near = [swap(x, "tensor", 1) for x in early_far]
    out_pack.double()
    while len(fc_pack.bits) > 1:
        fc_pack.double()

    done = project_qkv(
        ids, info, sent, gain_attn, shift_attn, qkv_pack, qkv_rows, tables, width
    )
    done = tie_packs(fc_pack, out_pack, beside=[*done, *early_near, *late_far])
    (queries, keys, values), done = done[:3], done[3:]
    early_near, late_far = done[: groups // 2 - 1], done[groups // 2 - 1 :]
    late_near = [swap(x, "tensor", 1) for x in late_far]
    far = zip(zip(early_far, late_far), zip(early_near, late_near))
    grad = Tokens([(out_grad,), (near,), *[x for pair in far for x in pair]], order)
    while len(out_pack.bits) > 1:
        out_pack.double()
    (grad_context,) = tie_packs(out_pack, beside=[project_grad(ids, grad, dense_pack, width)])
    fc_pack.double()
    out_pack.double()
    done = attention(info, tables, queries, keys, values, grad_context)
    context, dq, dk, dv = tie_packs(fc_pack, out_pack, beside=done)
    dp_orders = [halving_order(near_bits), halving_order(next_bits)]
    qkv_orders = [halving_order(bits) for bits in qkv_bits]
    attn_parts = Halving(
        *project_context(ids, context, dense_pack, groups, model), "tensor", tensor_bits
    )
    while len(attn_parts.bits) > 2:
        attn_parts.swap()
        attn_parts.add()
    attn_parts.send, context = tie(attn_parts.send, context)
    attn_parts.swap()
    done = attention_weights(
        ids, info, tables, context, dq, dk, dv, sent, grad, gain_attn, shift_attn, qkv_orders
    )
    grads, qkv_bias_sums, *stacks = tie_halves(done, attn_parts)
    attn_parts.add()
    qkv_sums = [Halving(*stacks[:2], "dp", qkv_bits[0]), Halving(*stacks[2:], "dp", qkv_bits[1])]
    sent.arrays[0], attn_parts.send = tie(sent.arrays[0], attn_parts.send)
    attn_parts.swap()
    for parts in qkv_sums:
        parts.swap()
    done = mlp(
        ids, sent, grad, gain_mlp, shift_mlp, fc_pack, fc_rows, out_pack, dp_orders
    )
    done = tie_halves(done, attn_parts, *qkv_sums)
    mlp_send, mlp_keep, hidden, fc_bias_sums, *stacks = done
    attn_parts.add()
    mlp_parts = Halving(mlp_send, mlp_keep, "tensor", tensor_bits)
    mlp_sums = [Halving(*stacks[:2], "dp", near_bits), Halving(*stacks[2:], "dp", next_bits)]
    while len(mlp_parts.bits) > 2:
        mlp_parts.swap()
        mlp_parts.add()
    mlp_parts.swap()
    add_stacks(qkv_sums)
    mlp_parts.add()
    hidden, mlp_parts.send = tie(hidden, mlp_parts.send)
    mlp_parts.swap()
    for parts in qkv_sums + mlp_sums:
        parts.swap()
    done = norm_backward(ids, sent, grads, hidden, gain_attn, gain_mlp, qkv_pack, fc_pack)
    done = tie_halves(done, mlp_parts, *qkv_sums, *mlp_sums)
    back_send, back_keep, norm_sums = done
    mlp_parts.add()

    back_parts = Halving(back_send, back_keep, "tensor", tensor_bits)
    while len(back_parts.bits) > 2:
        back_parts.swap()
        back_parts.add()
    back_parts.swap()
    add_stacks(qkv_sums + mlp_sums)

    back_parts.add()
    stream_in, back_parts.send = tie(stream_in, back_parts.send)
    back_parts.swap()
    for parts in qkv_sums + mlp_sums:
        parts.swap()
    output, sums = finish_output(
        ids,
        stream_in,
        out_grad,
        attn_parts.terms,
        mlp_parts.terms,
        dense_bias[None, :],
        out_bias[None, :],
        norm_sums,
        fc_bias_sums,
        qkv_bias_sums,
        groups,
    )


    sums = sums + swap(sums, "tensor", 1)
    for bit in data_bits[3:]:
        sums = sums + swap(sums, "dp", bit)
    other, *_ = tie_halves([swap(sums, "dp", data_bits[2])], *mlp_sums, qkv_sums[1])
    sums = sums + other
    add_stacks(mlp_sums)
    sums, *sends = tie(sums, *[parts.send for parts in mlp_sums])
    for parts, send in zip(mlp_sums, sends):
        parts.send = send
    for bit in data_bits[:2]:
        sums = sums + swap(sums, "dp", bit)
    sums, back_parts.got = tie(sums, back_parts.got)
    back_parts.add()
    stream_grad = finish_grad(out_grad, normalized, inv_std, back_parts.terms)
    sums, stream_grad = tie(sums, stream_grad)
    for bit in tensor_bits[1:]:
        sums = sums + swap(sums, "tensor", bit)

    fc_weight_grad, out_weight_grad = finish_mlp_weights(*[x.finish() for x in mlp_sums])
    for parts in qkv_sums:
        parts.add()
    qkv_weight_grad, dense_weight_grad = finish_attention_weights(*[x.finish() for x in qkv_sums])

    count_all = float(rows_local * lax.axis_size("dp") * groups * model)
    gain_attn_grad, shift_attn_grad, gain_mlp_grad, shift_mlp_grad = (sums[x] for x in range(4))
    root_squares = jnp.sqrt(jnp.sum(sums[4:7], axis=1) / count_all)
    residual_grad = sums[7]
    fc_bias_grad = sums[8:12].reshape(-1)
    qkv_bias_grad = by_head(sums[12 : 12 + groups, :qkv_width], heads).reshape(-1)
    return (
        output,
        stream_grad,
        gain_attn_grad,
        shift_attn_grad,
        gain_mlp_grad,
        shift_mlp_grad,
        qkv_weight_grad,
        qkv_bias_grad,
        dense_weight_grad,
        residual_grad,
        fc_weight_grad,
        fc_bias_grad,
        out_weight_grad,
        residual_grad,
        root_squares,
    )


def solution(mesh):
    tokens, weights, rows, whole = (
        P(("dp", "tensor"), None),
        P("dp", "tensor"),
        P("tensor", "dp"),
        P(),
    )
    return jax.shard_map(
        local,
        mesh=mesh,
        in_specs=(
            tokens,
            P("dp"),
            P("dp"),
            whole,
            whole,
            whole,
            whole,
            weights,
            whole,
            rows,
            whole,
            weights,
            whole,
            rows,
            whole,
            tokens,
        ),
        out_specs=(
            tokens,
            tokens,
            whole,
            whole,
            whole,
            whole,
            weights,
            whole,
            rows,
            whole,
            weights,
            whole,
            rows,
            whole,
            whole,
        ),
        check_vma=False,
    )
```

```python
import jax
import jax.numpy as jnp
from jax import lax
from jax.experimental import pallas as pl
from jax.experimental.pallas import tpu as pltpu
from jax.sharding import PartitionSpec as P

HD = 64
ROT = 16
TRUNK = 1024
SEG = 128
TREE = 2560
NB = TREE // SEG
NT = TRUNK // SEG

f32 = jnp.float32
bf16 = jnp.bfloat16
eps_norm = 1e-05
masked_score = -1e30


def dot_nn(left, right):
    return lax.dot_general(left, right, (((1,), (0,)), ((), ())), preferred_element_type=f32)


def dot_nt(left, right):
    return lax.dot_general(left, right, (((1,), (1,)), ((), ())), preferred_element_type=f32)


def dot_tn(left, right):
    return lax.dot_general(left, right, (((0,), (0,)), ((), ())), preferred_element_type=f32)


def bits_of(size):
    bits = []
    bit = 1
    while bit < size:
        bits.append(bit)
        bit *= 2
    return bits


def swap(block, axis, bit):
    size = lax.axis_size(axis)
    return lax.ppermute(block, axis, [(i, i ^ bit) for i in range(size)])


def tie(*values):
    return lax.optimization_barrier(values)


def gather_far(block, axis, bits):
    pieces = [block]
    for bit in bits[1:]:
        pieces = pieces + [swap(piece, axis, bit) for piece in pieces]
    return pieces


class Pack:
    def __init__(self, block, axis, bits):
        self.rows, self.axis, self.bits = block.shape[0], axis, list(bits)
        self.arrays, self.owners = [block], [[0]]

    def double(self):
        bit = self.bits.pop(0)
        held = self.arrays[0] if len(self.arrays) == 1 else jnp.concatenate(self.arrays, axis=0)
        self.owners.append([j ^ bit for owners in self.owners for j in owners])
        self.arrays.append(swap(held, self.axis, bit))

    def specs(self):
        return [pl.BlockSpec(memory_space=pltpu.HBM)] * len(self.arrays)

    def pieces(self):
        return sum(len(owners) for owners in self.owners)

    def copies(self, refs, where, number, done):
        started = []
        for ref, owners in zip(refs, self.owners):
            for at, j in enumerate(owners):
                rows = pl.ds(pl.multiple_of((number ^ j) * self.rows, self.rows), self.rows)
                source = ref.at[pl.ds(at * self.rows, self.rows), :]
                copy = pltpu.make_async_copy(source, where.at[rows, :], done.at[len(started)])
                started.append(copy)
        return started


def tie_packs(*packs, beside=()):
    flat = tie(*beside, *[x for pack in packs for x in pack.arrays])
    at = len(beside)
    for pack in packs:
        pack.arrays = list(flat[at : at + len(pack.arrays)])
        at += len(pack.arrays)
    return list(flat[: len(beside)])


def halving_order(bits):
    if not bits:
        return [0]
    rest = halving_order(bits[1:])
    return [bits[0] ^ j for j in rest] + rest


class Halving:
    def __init__(self, send, keep, axis, bits):
        self.send, self.axis, self.bits = send, axis, list(bits)
        self.terms = [(keep, 0)]

    def swap(self):
        self.got = swap(self.send, self.axis, self.bits.pop(0))

    def add(self):
        self.terms.append((self.got, 0))
        half = self.got.shape[0] // 2
        if half:
            self.send = add_terms(self.terms, half)
            self.terms = [(x, at + half) for x, at in self.terms]

    def most(self):
        while len(self.bits) > 1:
            self.swap()
            self.add()

    def finish(self):
        while self.bits:
            self.swap()
            self.add()
        return self.terms


class Parts(Halving):
    def __init__(self, first, second, keep, axis, bits):
        super().__init__(first, keep, axis, bits)
        self.second = second

    def begin(self):
        bit = self.bits.pop(0)
        self.got, self.other = swap(self.send, self.axis, bit), swap(self.second, self.axis, bit)

    def middle(self):
        half = self.got.shape[0]
        self.send = add_terms([*self.terms, (self.got, 0)], half)
        self.terms = [(self.terms[0][0], half), (self.other, 0)]
        while len(self.bits) > 1:
            self.swap()
            self.add()


def tie_halves(values, *halvings):
    flat = tie(*values, *[x.got for x in halvings])
    for x, got in zip(halvings, flat[len(values) :]):
        x.got = got
    return flat[: len(values)]


def resident(shape):
    zeros = (0,) * len(shape)
    return pl.BlockSpec(shape, lambda *_: zeros, pipeline_mode=pl.Buffered(1))


def own_block(rows, columns):
    return pl.BlockSpec((rows, columns), lambda i, ids, *_: (ids[0] ^ ids[2 + i], 0))


def step_block(rows, columns):
    return pl.BlockSpec((rows, columns), lambda i, *_: (i, 0))


def part_shapes(groups, rows, columns):
    quarter = max(groups // 4, 1)
    return [shaped(n, rows, columns) for n in (quarter, quarter, groups - 2 * quarter)]


def part_blocks(groups, rows, columns):
    quarter = max(groups // 4, 1)
    shape = (pl.Squeezed(), rows, columns)
    return [
        pl.BlockSpec(shape, lambda i, *_: (jnp.minimum(i, quarter - 1), 0, 0)),
        pl.BlockSpec(shape, lambda i, *_: (jnp.clip(i - quarter, 0, quarter - 1), 0, 0)),
        pl.BlockSpec(shape, lambda i, *_: (jnp.maximum(i - 2 * quarter, 0), 0, 0)),
    ]


def store_part(stacks, value, step, groups):
    quarter = max(groups // 4, 1)
    turn_of = jnp.minimum(step // quarter, 2)
    for at, stack in enumerate(stacks):

        @pl.when(turn_of == at)
        def _(stack=stack):
            stack[...] = value


class Tokens:
    def __init__(self, blocks, order):
        blocks = [blocks[j] for j in order]
        self.groups, self.counts = len(blocks), [len(block) for block in blocks]
        self.rows, self.model = sum(x.shape[0] for x in blocks[0]), blocks[0][0].shape[1]
        self.arrays = [x for block in blocks for x in block]
        self.specs = [pl.BlockSpec(memory_space=pltpu.HBM)] * len(self.arrays)

    def scratch(self):
        return [
            pltpu.VMEM((2, self.rows, self.model), bf16),
            pltpu.SemaphoreType.DMA((2, max(self.counts))),
        ]

    def fetch(self, refs, held, done, step):
        def copies(at):
            first, start, found = sum(self.counts[:at]), 0, []
            for k, ref in enumerate(refs[first : first + self.counts[at]]):
                where = held.at[at % 2, pl.ds(start, ref.shape[0]), :]
                found.append(pltpu.make_async_copy(ref, where, done.at[at % 2, k]))
                start += ref.shape[0]
            return found

        for at in range(self.groups):

            @pl.when(step == at)
            def _(at=at):
                ahead = copies(at) if at == 0 else []
                if at + 1 < self.groups:
                    ahead = ahead + copies(at + 1)
                for copy in ahead:
                    copy.start()
                for copy in copies(at):
                    copy.wait()


def store_halves(send, keep, total, number, order, columns=slice(None), source=slice(None)):
    half, rows = send.shape[0], send.shape[1]
    for at, j in enumerate(order):
        where = send if at < half else keep
        block = total[pl.ds(pl.multiple_of((number ^ j) * rows, rows), rows), source]
        where[at % half, :, columns] = block.astype(bf16)


def call(
    kernel, name, grid, prefetch, operands, specs, outs, out_specs, scratch, flops, extra=0, room=12, light=False
):
    size = 0 if light else sum(x.size * x.dtype.itemsize for x in [*operands, *outs])
    return pl.pallas_call(
        kernel,
        grid_spec=pltpu.PrefetchScalarGridSpec(
            num_scalar_prefetch=len(prefetch),
            grid=grid,
            in_specs=specs,
            out_specs=out_specs,
            scratch_shapes=scratch,
        ),
        out_shape=outs,
        compiler_params=pltpu.CompilerParams(
            dimension_semantics=("arbitrary",) * len(grid), vmem_limit_bytes=room << 20
        ),
        cost_estimate=pl.CostEstimate(
            flops=int(flops), bytes_accessed=int(size), transcendentals=int(extra)
        ),
        name=name,
    )(*prefetch, *operands)


def shaped(*shape, dtype=bf16):
    return jax.ShapeDtypeStruct(shape, dtype)


def shift_gain(block, gain, shift):
    return (block.astype(f32) * gain[...] + shift[...]).astype(bf16)


def turn(block, cosine, sine, sign):
    width = block.shape[1]
    step = min(width, 128)
    lane = lax.broadcasted_iota(jnp.int32, (block.shape[0], step), 1) % HD
    done = []
    for start in range(0, width, step):
        part = block[:, start : start + step]
        if step == 128:
            left = pltpu.roll(part, step - ROT // 2, 1)
            right = pltpu.roll(part, ROT // 2, 1)
        else:
            left = jnp.concatenate([part[:, ROT // 2 :], part[:, : ROT // 2]], axis=1)
            right = jnp.concatenate([part[:, -ROT // 2 :], part[:, : -ROT // 2]], axis=1)
        moved = jnp.where(lane < ROT // 2, -left, right) * sine[:, :step]
        done.append(part * cosine[:, :step] + moved * sign)
    return done[0] if len(done) == 1 else jnp.concatenate(done, axis=1)


def weight_scratch(pack):
    model = pack.rows * pack.pieces()
    columns = pack.arrays[0].shape[1]
    return [pltpu.VMEM((model, columns), bf16), pltpu.SemaphoreType.DMA((pack.pieces(),))]


def prepare_weights(qkv, dense, fc, out):
    rows, columns = qkv.shape
    width = columns // 3

    def kernel(qkv_ref, dense_ref, fc_ref, out_ref, qkv_to, dense_to, fc_to, out_to):
        for head in range(width // HD):
            for kind in range(3):
                at, own = (3 * head + kind) * HD, kind * width + head * HD
                qkv_to[:, own : own + HD] = qkv_ref[:, at : at + HD].astype(bf16)
        dense_to[...] = dense_ref[...].T.astype(bf16)
        fc_to[...] = fc_ref[...].astype(bf16)
        out_to[...] = out_ref[...].T.astype(bf16)

    operands = [qkv, dense, fc, out]
    outs = [shaped(*qkv.shape), shaped(*dense.shape[::-1]), shaped(*fc.shape), shaped(*out.shape[::-1])]
    return call(
        kernel,
        "prepare_weights",
        (1,),
        [],
        operands,
        [resident(x.shape) for x in operands],
        outs,
        [resident(x.shape) for x in outs],
        [],
        rows * columns,
    )


def normalize(stream):
    rows, model = stream.shape
    block = 160

    def kernel(stream_ref, sent_ref, norm_ref, std_ref):
        field = stream_ref[...]
        centred = field - jnp.sum(field, axis=1, keepdims=True) / model
        variance = jnp.sum(centred * centred, axis=1, keepdims=True) / model
        scale = lax.rsqrt(variance + eps_norm)
        norm = centred * scale
        norm_ref[...] = norm
        sent_ref[...] = norm.astype(bf16)
        std_ref[...] = scale

    return call(
        kernel,
        "normalize",
        (rows // block,),
        [],
        [stream],
        [step_block(block, model)],
        [shaped(rows, model), shaped(rows, model, dtype=f32), shaped(rows, 1, dtype=f32)],
        [step_block(block, model), step_block(block, model), step_block(block, 1)],
        [],
        rows * model * 8,
        room=62,
    )


def project_qkv(ids, info, sent, gain, shift, pack, bias, tables, width):
    groups, held, rows, model = sent.groups, len(sent.arrays), sent.rows, sent.model

    def kernel(ids, info, *refs):
        sent_refs, refs = refs[:held], refs[held:]
        weight_refs, refs = refs[: len(pack.arrays)], refs[len(pack.arrays) :]
        gain, shift, bias, cos, sine, q_out, k_out, v_out = refs[:8]
        block, arrived, whole, placed, added = refs[8:]
        step = pl.program_id(0)

        @pl.when(step == 0)
        def _():
            for copy in pack.copies(weight_refs, whole, ids[1], placed):
                copy.start()

        sent.fetch(sent_refs, block, arrived, step)

        @pl.when(step == 0)
        def _():
            for copy in pack.copies(weight_refs, whole, ids[1], placed):
                copy.wait()
            own = bias[pl.ds(ids[0], 1), :]
            for head in range(width // HD):
                for kind in range(3):
                    at, to = (3 * head + kind) * HD, kind * width + head * HD
                    added[:, to : to + HD] = own[:, at : at + HD]

        token = block[step % 2]
        normed = shift_gain(token, gain, shift)
        blocks = rows // SEG
        cut = (blocks + 1) // 2
        both = [dot_nn(normed[x], whole[...]) + added[...] for x in (slice(0, cut * SEG), slice(cut * SEG, rows))]
        first = (ids[0] ^ ids[2 + step]) * blocks
        for at in range(blocks):
            number = first + at
            table = pl.ds(pl.multiple_of(info[number // NB, number % NB, 4] * SEG, SEG), SEG)
            tabs = (cos[table, :], sine[table, :])
            own = slice(at * SEG, (at + 1) * SEG)
            here = at * SEG if at < cut else (at - cut) * SEG
            qkv = both[at >= cut][here : here + SEG]
            q_out[own, :] = (turn(qkv[:, :width], *tabs, 1.0) * HD**-0.5).astype(bf16)
            k_out[own, :] = turn(qkv[:, width : 2 * width], *tabs, 1.0).astype(bf16)
            v_out[own, :] = qkv[:, 2 * width :].astype(bf16)

    operands = [*sent.arrays, *pack.arrays, gain, shift, bias, *tables]
    out = shaped(groups * rows, width)
    return call(
        kernel,
        "project_qkv",
        (groups,),
        [ids, info],
        operands,
        sent.specs
        + pack.specs()
        + [resident(x.shape) for x in operands[held + len(pack.arrays) :]],
        [out] * 3,
        [own_block(rows, width)] * 3,
        sent.scratch() + weight_scratch(pack) + [pltpu.VMEM((1, 3 * width), f32)],
        2 * groups * rows * model * 3 * width,
        room=62,
    )


def project_grad(ids, grad, pack, width):
    groups, held, rows, model = grad.groups, len(grad.arrays), grad.rows, grad.model

    def kernel(ids, *refs):
        grad_refs, refs = refs[:held], refs[held:]
        weight_refs, (out, block, arrived, whole, placed) = refs[:-5], refs[-5:]
        step = pl.program_id(0)

        @pl.when(step == 0)
        def _():
            for copy in pack.copies(weight_refs, whole, ids[1], placed):
                copy.start()

        grad.fetch(grad_refs, block, arrived, step)

        @pl.when(step == 0)
        def _():
            for copy in pack.copies(weight_refs, whole, ids[1], placed):
                copy.wait()

        out[...] = dot_nn(block[step % 2], whole[...]).astype(bf16)

    operands = [*grad.arrays, *pack.arrays]
    return call(
        kernel,
        "project_grad",
        (groups,),
        [ids],
        operands,
        grad.specs + pack.specs(),
        [shaped(groups * rows, width)],
        [own_block(rows, width)],
        grad.scratch() + weight_scratch(pack),
        2 * groups * rows * model * width,
    )[0]


def attention_kernel(
    info, q_ref, do_ref, k_ref, v_ref, cos, sine, ctx_ref, dq_ref, dk_ref, dv_ref, dk_sum, dv_sum
):
    tree, step = pl.program_id(0), pl.program_id(1)
    width = q_ref.shape[1]
    heads = width // HD
    lane_head = lax.broadcasted_iota(jnp.int32, (SEG, width), 1) // HD

    @pl.when(step == 0)
    def _():
        dk_sum[...] = jnp.zeros_like(dk_sum)
        dv_sum[...] = jnp.zeros_like(dv_sum)

    first, second = info[tree, step, 0], info[tree, step, 1]
    first_rows = pl.ds(pl.multiple_of(first * SEG, SEG), SEG)
    second_rows = pl.ds(pl.multiple_of(second * SEG, SEG), SEG)
    queries, grads = q_ref[...], do_ref[...]
    zero = jnp.zeros_like(queries)
    q_rows = jnp.concatenate([jnp.where(lane_head == h, queries, zero) for h in range(heads)], axis=0)
    g_rows = jnp.concatenate([jnp.where(lane_head == h, grads, zero) for h in range(heads)], axis=0)
    q_turned, g_turned = queries.T, grads.T
    ahead = lax.broadcasted_iota(jnp.int32, (SEG, SEG), 1) - lax.broadcasted_iota(
        jnp.int32, (SEG, SEG), 0
    )
    seen = jnp.concatenate([ahead <= info[tree, step, 2], ahead <= info[tree, step, 3]], axis=1)
    seen = jnp.concatenate([seen] * heads, axis=0)
    k_near = jnp.concatenate([k_ref[first_rows, :], k_ref[second_rows, :]], axis=0)
    v_near = jnp.concatenate([v_ref[first_rows, :], v_ref[second_rows, :]], axis=0)

    def work(pairs):
        count = pairs * 2 * SEG
        near = jnp.where(seen, dot_nt(q_rows, k_near), masked_score)
        most = jnp.max(near, axis=1, keepdims=True)
        if count:
            k_far, v_far = k_ref[0:count, :], v_ref[0:count, :]
            far = dot_nt(q_rows, k_far)
            most = jnp.maximum(most, jnp.max(far, axis=1, keepdims=True))
        near = jnp.exp(near - most)
        total = jnp.sum(near, axis=1, keepdims=True)
        if count:
            far = jnp.exp(far - most)
            total = total + jnp.sum(far, axis=1, keepdims=True)
        scale = 1.0 / total
        near = near * scale
        near_low = near.astype(bf16)
        context = dot_nn(near_low, v_near)
        if count:
            far = far * scale
            far_low = far.astype(bf16)
            context = context + dot_nn(far_low, v_far)
        delta = jnp.sum(context * g_rows.astype(f32), axis=1, keepdims=True)
        near = (near * (dot_nt(g_rows, v_near) - delta)).astype(bf16)
        dq = dot_nn(near, k_near)
        if count:
            far = (far * (dot_nt(g_rows, v_far) - delta)).astype(bf16)
            dq = dq + dot_nn(far, k_far)
        ctx_own, dq_own = context[0:SEG], dq[0:SEG]
        for h in range(1, heads):
            ctx_own = jnp.where(lane_head == h, context[h * SEG : (h + 1) * SEG], ctx_own)
            dq_own = jnp.where(lane_head == h, dq[h * SEG : (h + 1) * SEG], dq_own)
        ctx_ref[...] = ctx_own.astype(bf16)
        dq_ref[...] = turn(dq_own * HD**-0.5, cos, sine, -1.0).astype(bf16)
        for h in range(heads):
            own = slice(h * SEG, (h + 1) * SEG)
            part = slice(h * HD, (h + 1) * HD)
            dk = dot_nn(q_turned[part], near[own])
            dv = dot_nn(g_turned[part], near_low[own])
            dk_sum[first, part, :] += dk[:, :SEG]
            dv_sum[first, part, :] += dv[:, :SEG]
            dk_sum[second, part, :] += dk[:, SEG:]
            dv_sum[second, part, :] += dv[:, SEG:]
            if count:
                dk = dot_nn(q_turned[part], far[own])
                dv = dot_nn(g_turned[part], far_low[own])
                for j in range(2 * pairs):
                    dk_sum[j, part, :] += dk[:, j * SEG : (j + 1) * SEG]
                    dv_sum[j, part, :] += dv[:, j * SEG : (j + 1) * SEG]

    for pairs in range(NT // 2):

        @pl.when(step // 2 == pairs)
        def _(pairs=pairs):
            work(pairs)

    @pl.when(step >= NT)
    def _():
        work(NT // 2)

    @pl.when(step == NB - 1)
    def _():
        def finish(j, carry):
            rows = pl.ds(pl.multiple_of(j * SEG, SEG), SEG)
            dv_ref[rows, :] = dv_sum[j].T.astype(bf16)
            dk_ref[rows, :] = dk_sum[j].T.astype(bf16)
            return carry

        lax.fori_loop(0, NB, finish, 0)


def attention(info, tables, queries, keys, values, grads):
    total, width = queries.shape
    trees = total // TREE
    table_width = tables[0].shape[1]
    block = pl.BlockSpec((SEG, width), lambda t, b, info: (t * NB + b, 0))
    whole = pl.BlockSpec((TREE, width), lambda t, b, info: (t, 0))
    table = pl.BlockSpec((SEG, table_width), lambda t, b, info: (info[t, b, 4], 0))
    scores = trees * (TREE - TRUNK) * (TRUNK + 2 * SEG) * (width // HD)
    return call(
        attention_kernel,
        "attention",
        (trees, NB),
        [info],
        [queries, grads, keys, values, *tables],
        [block, block, whole, whole, table, table],
        [shaped(total, width)] * 4,
        [block, block, whole, whole],
        [pltpu.VMEM((NB, width, SEG), f32), pltpu.VMEM((NB, width, SEG), f32)],
        scores * width * 2 * 6 * 1.3,
        scores,
        room=22,
    )


def project_context(ids, context, pack, groups, model):
    rows, width = context.shape[0] // groups, context.shape[1]

    def kernel(ids, ctx, *refs):
        weight_refs, stacks, (whole, placed) = refs[:-5], refs[-5:-2], refs[-2:]
        step = pl.program_id(0)

        @pl.when(step == 0)
        def _():
            copies = pack.copies(weight_refs, whole, ids[1], placed)
            for copy in copies:
                copy.start()
            for copy in copies:
                copy.wait()

        store_part(stacks, dot_nt(ctx[...], whole[...]).astype(bf16), step, groups)

    operands = [context, *pack.arrays]
    return call(
        kernel,
        "project_context",
        (groups,),
        [ids],
        operands,
        [own_block(rows, width)] + pack.specs(),
        part_shapes(groups, rows, model),
        part_blocks(groups, rows, model),
        weight_scratch(pack),
        2 * groups * rows * model * width,
        room=14,
    )


def attention_weights(ids, info, tables, context, dq, dk, dv, sent, grad, gain, shift, orders):
    groups, held, rows, model = sent.groups, len(sent.arrays), sent.rows, sent.model
    width, count = dq.shape[1], len(orders[0])

    def kernel(ids, info, ctx_ref, dq_ref, dk_ref, dv_ref, *refs):
        sent_refs, refs = refs[:held], refs[held:]
        grad_refs, refs = refs[: len(grad.arrays)], refs[len(grad.arrays) :]
        gain, shift, cos, sine, grads, bias_ref, *stacks = refs[:10]
        block, arrived, grad_block, grad_arrived, total, dense_total = refs[10:]
        step = pl.program_id(0)

        @pl.when(step == 0)
        def _():
            total[...] = jnp.zeros_like(total)
            dense_total[...] = jnp.zeros_like(dense_total)
            bias_ref[...] = jnp.zeros_like(bias_ref)

        sent.fetch(sent_refs, block, arrived, step)
        grad.fetch(grad_refs, grad_block, grad_arrived, step)
        grads[:, :width] = dq_ref[...]
        first = (ids[0] ^ ids[2 + step]) * (rows // SEG)
        for at in range(rows // SEG):
            number = first + at
            table = pl.ds(pl.multiple_of(info[number // NB, number % NB, 4] * SEG, SEG), SEG)
            own = slice(at * SEG, (at + 1) * SEG)
            turned = turn(dk_ref[own, :], cos[table, :], sine[table, :], -1.0)
            grads[own, width : 2 * width] = turned.astype(bf16)
        grads[:, 2 * width :] = dv_ref[...]
        bias_ref[0:1, :] += jnp.sum(grads[...].astype(f32), axis=0, keepdims=True)
        total[...] += dot_tn(shift_gain(block[step % 2], gain, shift), grads[...])
        dense_total[...] += dot_tn(grad_block[step % 2], ctx_ref[...])

        @pl.when(step == groups - 1)
        def _():
            store_halves(*stacks[:2], total, ids[1], orders[0], source=slice(0, 2 * width))
            source = slice(2 * width, 3 * width)
            store_halves(*stacks[2:], total, ids[1], orders[1], slice(0, width), source)
            columns = slice(width, 2 * width)
            store_halves(*stacks[2:], dense_total, ids[1], orders[1], columns)

    operands = [context, dq, dk, dv, *sent.arrays, *grad.arrays, gain, shift, *tables]
    outs = [shaped(groups * rows, 3 * width), shaped(8, 3 * width, dtype=f32)]
    outs += [shaped(count // 2, model // count, 2 * width)] * 4
    return call(
        kernel,
        "attention_weights",
        (groups,),
        [ids, info],
        operands,
        [own_block(rows, width)] * 4
        + sent.specs
        + grad.specs
        + [resident(x.shape) for x in operands[-4:]],
        outs,
        [step_block(rows, 3 * width)] + [resident(x.shape) for x in outs[1:]],
        sent.scratch()
        + grad.scratch()
        + [pltpu.VMEM((model, 3 * width), f32), pltpu.VMEM((model, width), f32)],
        2 * groups * rows * model * 4 * width,
        room=24,
    )


def mlp(ids, sent, grad, gain, shift, fc, bias, out, orders):
    groups, held, rows, model = sent.groups, len(sent.arrays), sent.rows, sent.model
    pieces, units = len(fc.arrays), fc.arrays[0].shape[1]

    def kernel(ids, *refs):
        sent_refs, refs = refs[:held], refs[held:]
        grad_refs, refs = refs[: len(grad.arrays)], refs[len(grad.arrays) :]
        fc_refs, refs = refs[:pieces], refs[pieces:]
        out_refs, refs = refs[:pieces], refs[pieces:]
        gain, shift, bias, *parts_out = refs[:6]
        hidden_ref, bias_ref = refs[6:8]
        stacks, refs = refs[8:12], refs[12:]
        block, arrived, grad_block, grad_arrived, fc_whole, fc_placed, out_whole, out_placed = refs[:8]
        act_ref, fc_total, out_total = refs[8:]
        step = pl.program_id(0)

        def weights():
            copies = fc.copies(fc_refs, fc_whole, ids[1], fc_placed)
            return copies + out.copies(out_refs, out_whole, ids[1], out_placed)

        @pl.when(step == 0)
        def _():
            for copy in weights():
                copy.start()
            fc_total[...] = jnp.zeros_like(fc_total)
            out_total[...] = jnp.zeros_like(out_total)
            bias_ref[...] = jnp.zeros_like(bias_ref)

        sent.fetch(sent_refs, block, arrived, step)
        grad.fetch(grad_refs, grad_block, grad_arrived, step)

        @pl.when(step == 0)
        def _():
            for copy in weights():
                copy.wait()

        token, grads = block[step % 2], grad_block[step % 2]
        normed = shift_gain(token, gain, shift)
        count = 2
        parts = [slice(k * rows // count, (k + 1) * rows // count) for k in range(count)]
        added = bias[pl.ds(ids[0], 1), :]
        hidden = [dot_nn(normed[x], fc_whole[...]) + added for x in parts]
        back = [dot_nn(grads[x], out_whole[...]) for x in parts]
        for x, field, slope in zip(parts, hidden, back):
            chance = 0.5 + 0.5 * lax.erf(field * 0.7071067811865476)
            bell = jnp.exp(field * field * -0.5) * 0.3989422804014327
            act_ref[x, :] = (field * chance).astype(bf16)
            low = (slope * (chance + field * bell)).astype(bf16)
            hidden_ref[x, :] = low
            bias_ref[0:1, :] += jnp.sum(low.astype(f32), axis=0, keepdims=True)
        store_part(parts_out, dot_nt(act_ref[...], out_whole[...]).astype(bf16), step, groups)
        out_total[...] += dot_tn(grads, act_ref[...])
        fc_total[...] += dot_tn(normed, hidden_ref[...])

        @pl.when(step == groups - 1)
        def _():
            half = units // 2
            for at, order in enumerate(orders):
                stack = stacks[2 * at : 2 * at + 2]
                source = slice(at * half, (at + 1) * half)
                store_halves(*stack, fc_total, ids[1], order, slice(0, half), source)
                store_halves(*stack, out_total, ids[1], order, slice(half, units), source)

    operands = [*sent.arrays, *grad.arrays, *fc.arrays, *out.arrays, gain, shift, bias]
    count = model // fc.rows
    outs = part_shapes(groups, rows, model)
    outs += [shaped(groups * rows, units), shaped(8, units, dtype=f32)]
    outs += [shaped(count // 2, fc.rows, units)] * 4
    return call(
        kernel,
        "mlp",
        (groups,),
        [ids],
        operands,
        sent.specs
        + grad.specs
        + fc.specs()
        + out.specs()
        + [resident(x.shape) for x in operands[-3:]],
        outs,
        part_blocks(groups, rows, model)
        + [step_block(rows, units)]
        + [resident(x.shape) for x in outs[4:]],
        sent.scratch()
        + grad.scratch()
        + weight_scratch(fc)
        + weight_scratch(out)
        + [
            pltpu.VMEM((rows, units), bf16),
            pltpu.VMEM((model, units), f32),
            pltpu.VMEM((model, units), f32),
        ],
        10 * groups * rows * model * units,
        room=42,
    )


def norm_backward(ids, sent, grads, hidden, gain_attn, gain_mlp, qkv_pack, fc):
    groups, held, rows, model = sent.groups, len(sent.arrays), sent.rows, sent.model
    pieces, units, columns = len(fc.arrays), hidden.shape[1], grads.shape[1]

    def kernel(ids, grads_ref, hidden_ref, *refs):
        sent_refs, refs = refs[:held], refs[held:]
        qkv_refs, refs = refs[:pieces], refs[pieces:]
        fc_refs, refs = refs[:pieces], refs[pieces:]
        gain_attn, gain_mlp, *stacks = refs[:5]
        sums_ref, block, arrived, qkv_whole, qkv_placed, fc_whole, fc_placed = refs[5:]
        step = pl.program_id(0)

        def weights():
            copies = qkv_pack.copies(qkv_refs, qkv_whole, ids[1], qkv_placed)
            return copies + fc.copies(fc_refs, fc_whole, ids[1], fc_placed)

        @pl.when(step == 0)
        def _():
            for copy in weights():
                copy.start()
            sums_ref[...] = jnp.zeros_like(sums_ref)

        sent.fetch(sent_refs, block, arrived, step)

        @pl.when(step == 0)
        def _():
            for copy in weights():
                copy.wait()

        back_attn = dot_nt(grads_ref[...], qkv_whole[...])
        back_mlp = dot_nt(hidden_ref[...], fc_whole[...])
        token = block[step % 2].astype(f32)
        for at, back in enumerate((back_attn, back_mlp)):
            sums_ref[2 * at : 2 * at + 1, :] += jnp.sum(back * token, axis=0, keepdims=True)
            sums_ref[2 * at + 1 : 2 * at + 2, :] += jnp.sum(back, axis=0, keepdims=True)
        part = back_attn * gain_attn[...] + back_mlp * gain_mlp[...]
        store_part(stacks, part.astype(bf16), step, groups)

    operands = [grads, hidden, *sent.arrays, *qkv_pack.arrays, *fc.arrays, gain_attn, gain_mlp]
    outs = part_shapes(groups, rows, model) + [shaped(8, model, dtype=f32)]
    return call(
        kernel,
        "norm_backward",
        (groups,),
        [ids],
        operands,
        [step_block(rows, columns), step_block(rows, units)]
        + sent.specs
        + qkv_pack.specs()
        + fc.specs()
        + [resident(x.shape) for x in operands[-2:]],
        outs,
        part_blocks(groups, rows, model) + [resident(x.shape) for x in outs[3:]],
        sent.scratch() + weight_scratch(qkv_pack) + weight_scratch(fc),
        2 * groups * rows * model * (units + columns),
        room=26,
    )


def taken(terms, block):
    return [
        pl.BlockSpec((pl.Squeezed(), block, x.shape[2]), lambda i, *_, at=at: (at, i, 0))
        for x, at in terms
    ]


def add_terms(terms, half):
    _, rows, columns = terms[0][0].shape
    block = max(x for x in (320, 128, 64) if rows % x == 0)

    def kernel(*refs):
        refs[-1][...] = sum(x[...].astype(f32) for x in refs[:-1]).astype(bf16)

    shape = (pl.Squeezed(), block, columns)
    out = shaped(half, rows, columns)
    return call(
        kernel,
        "add_terms",
        (half, rows // block),
        [],
        [x for x, _ in terms],
        [pl.BlockSpec(shape, lambda k, i, *_, at=at: (at + k, i, 0)) for _, at in terms],
        [out],
        [pl.BlockSpec(shape, lambda k, i, *_: (k, i, 0))],
        [],
        half * rows * columns * len(terms),
    )[0]


def whole_terms(terms, count):
    return [
        pl.BlockSpec((count, *x.shape[1:]), lambda *_, at=at: (at // count, 0, 0)) for x, at in terms
    ]


def add_stacks(stacks):
    counts = []
    for parts in stacks:
        parts.terms.append((parts.got, 0))
        counts.append(parts.got.shape[0] // 2)
    held = [len(parts.terms) for parts in stacks]
    operands = [x for parts in stacks for x, _ in parts.terms]

    def kernel(*refs):
        for at, half in enumerate(counts):
            first = sum(held[:at])
            total = sum(x[...].astype(f32) for x in refs[first : first + held[at]])
            refs[len(operands) + at][...] = total.astype(bf16)

    outs = [shaped(n, *parts.got.shape[1:]) for n, parts in zip(counts, stacks)]
    sends = call(
        kernel,
        "add_stacks",
        (1,),
        [],
        operands,
        [x for n, parts in zip(counts, stacks) for x in whole_terms(parts.terms, n)],
        outs,
        [resident(x.shape) for x in outs],
        [],
        sum(x.size for x in operands) // 2,
        room=16,
    )
    for n, parts, send in zip(counts, stacks, sends):
        parts.send = send
        parts.terms = [(x, at + n) for x, at in parts.terms]


def finish_mlp_weights(first, second):
    held, (_, rows, units) = len(first), first[0][0].shape
    half = units // 2

    def kernel(*refs):
        low = sum(x[0].astype(f32) for x in refs[:held])
        high = sum(x[0].astype(f32) for x in refs[held:-2])
        refs[-2][:, :half] = low[:, :half]
        refs[-2][:, half:] = high[:, :half]
        refs[-1][:half, :] = low[:, half:].T
        refs[-1][half:, :] = high[:, half:].T

    operands = [x for x, _ in [*first, *second]]
    outs = [shaped(rows, units, dtype=f32), shaped(units, rows, dtype=f32)]
    return call(
        kernel,
        "finish_mlp_weights",
        (1,),
        [],
        operands,
        whole_terms([*first, *second], 1),
        outs,
        [resident(x.shape) for x in outs],
        [],
        len(operands) * rows * units,
    )


def finish_attention_weights(first, second):
    held, (_, rows, columns) = len(first), first[0][0].shape
    width = columns // 2

    def kernel(*refs):
        low = sum(x[0].astype(f32) for x in refs[:held])
        high = sum(x[0].astype(f32) for x in refs[held:-2])
        for head in range(width // HD):
            for kind, (source, start) in enumerate(((low, 0), (low, width), (high, 0))):
                at = (3 * head + kind) * HD
                own = start + head * HD
                refs[-2][:, at : at + HD] = source[:, own : own + HD]
        refs[-1][...] = high[:, width:].T

    operands = [x for x, _ in [*first, *second]]
    outs = [shaped(rows, 3 * width, dtype=f32), shaped(width, rows, dtype=f32)]
    return call(
        kernel,
        "finish_attention_weights",
        (1,),
        [],
        operands,
        whole_terms([*first, *second], 1),
        outs,
        [resident(x.shape) for x in outs],
        [],
        len(operands) * rows * columns,
    )


def sum_rows(groups):
    return (12 + groups + 7) // 8 * 8


def finish_output(ids, stream, grad, attn_terms, mlp_terms, dense_bias, out_bias, norm_sums, fc_sums, qkv_sums, groups):
    rows, model = stream.shape
    block = 160
    first, second = len(attn_terms), len(mlp_terms)
    units, columns = fc_sums.shape[1], qkv_sums.shape[1]
    across = model // units

    def kernel(ids, stream_ref, grad_ref, *refs):
        attn_refs, refs = refs[:first], refs[first:]
        mlp_refs, refs = refs[:second], refs[second:]
        dense_bias, out_bias, norm_ref, fc_ref, qkv_ref, out_ref, sums_ref = refs

        @pl.when(pl.program_id(0) == 0)
        def _():
            sums_ref[...] = jnp.zeros_like(sums_ref)
            sums_ref[0:4, :] = norm_ref[0:4, :]
            own = jnp.concatenate([fc_ref[0:1, :]] * across, axis=1) if across > 1 else fc_ref[0:1, :]
            lane = lax.broadcasted_iota(jnp.int32, (1, model), 1) // units
            sums_ref[pl.ds(8 + ids[0] // across, 1), :] = jnp.where(lane == ids[0] % across, own, 0.0)
            sums_ref[pl.ds(12 + ids[0], 1), :columns] = qkv_ref[0:1, :]

        attn = sum(x[...].astype(f32) for x in attn_refs) + dense_bias[...]
        mlp = sum(x[...].astype(f32) for x in mlp_refs) + out_bias[...]
        output = stream_ref[...] + attn + mlp
        out_ref[...] = output
        for at, value in enumerate((output, attn, mlp)):
            sums_ref[4 + at : 5 + at, :] += jnp.sum(value * value, axis=0, keepdims=True)
        sums_ref[7:8, :] += jnp.sum(grad_ref[...].astype(f32), axis=0, keepdims=True)

    terms = [*attn_terms, *mlp_terms]
    operands = [stream, grad, *[x for x, _ in terms], dense_bias, out_bias, norm_sums, fc_sums, qkv_sums]
    outs = [shaped(rows, model, dtype=f32), shaped(sum_rows(groups), model, dtype=f32)]
    return call(
        kernel,
        "finish_output",
        (rows // block,),
        [ids],
        operands,
        [step_block(block, model), step_block(block, model)]
        + taken(terms, block)
        + [resident(x.shape) for x in operands[-5:]],
        outs,
        [step_block(block, model), resident(outs[1].shape)],
        [],
        rows * model * 16,
        room=16,
    )


def finish_grad(grad, normalized, inv_std, terms):
    rows, model = grad.shape
    block = 160

    def kernel(grad_ref, norm_ref, std_ref, *refs):
        term_refs, out_ref = refs[:-1], refs[-1]
        sent = sum(x[...].astype(f32) for x in term_refs)
        norm = norm_ref[...]
        mean = jnp.sum(sent, axis=1, keepdims=True) / model
        cross = jnp.sum(sent * norm, axis=1, keepdims=True) / model
        out_ref[...] = grad_ref[...].astype(f32) + std_ref[...] * (sent - mean - norm * cross)

    operands = [grad, normalized, inv_std, *[x for x, _ in terms]]
    return call(
        kernel,
        "finish_grad",
        (rows // block,),
        [],
        operands,
        [step_block(block, model), step_block(block, model), step_block(block, 1)]
        + taken(terms, block),
        [shaped(rows, model, dtype=f32)],
        [step_block(block, model)],
        [],
        0,
        light=True,
    )[0]


def tree_table(segment_ids, parent_ids):
    trees = segment_ids.shape[0] // TREE

    def kernel(segment, parent, table):
        for tree in range(trees):
            for block in range(NT):
                odd = block % 2
                row = (block - odd, block - odd + 1, SEG * odd, -SEG * (1 - odd), block)
                for at, value in enumerate(row):
                    table[tree, block, at] = value

            def place(block, carry):
                first = tree * TREE
                owner = parent[first + block * SEG]
                leaf = (owner != segment[first]).astype(jnp.int32)
                at = block
                for other in range(NT, NB):
                    at = jnp.where(segment[first + other * SEG] == owner, other, at)
                table[tree, block, 0] = block
                table[tree, block, 1] = at
                table[tree, block, 2] = 0
                table[tree, block, 3] = SEG * (2 * leaf - 1)
                table[tree, block, 4] = NT + leaf
                return carry

            lax.fori_loop(NT, NB, place, 0)

    smem = pl.BlockSpec(memory_space=pltpu.SMEM)
    return pl.pallas_call(
        kernel,
        in_specs=[smem, smem],
        out_specs=smem,
        out_shape=jax.ShapeDtypeStruct((trees, NB, 5), jnp.int32),
        name="tree_table",
    )(segment_ids, parent_ids)


def angle_tables(zero):
    places = TRUNK + 2 * SEG
    place = lax.broadcasted_iota(jnp.int32, (places, 2 * HD), 0).astype(f32)
    lane = lax.broadcasted_iota(jnp.int32, (places, 2 * HD), 1) % HD
    half = ROT // 2
    frequency = 10000.0 ** (-((lane % half).astype(f32) * 2.0 / ROT))
    angle = (place + zero) * frequency
    cosine = jnp.where(lane < ROT, jnp.cos(angle), 1.0)
    sine = jnp.where(lane < ROT, jnp.sin(angle), 0.0)
    return cosine, sine


def by_kind(array, heads):
    shape = array.shape[:-1]
    array = array.reshape(*shape, heads, 3, HD)
    return jnp.swapaxes(array, -3, -2).reshape(*shape, 3 * heads * HD)


def by_head(array, heads):
    shape = array.shape[:-1]
    array = array.reshape(*shape, 3, heads, HD)
    return jnp.swapaxes(array, -3, -2).reshape(*shape, 3 * heads * HD)


def local(
    stream_in,
    segment_ids,
    parent_ids,
    norm_gain_attn,
    norm_shift_attn,
    norm_gain_mlp,
    norm_shift_mlp,
    qkv_weight,
    qkv_bias,
    dense_weight,
    dense_bias,
    fc_weight,
    fc_bias,
    out_weight,
    out_bias,
    out_grad,
):
    tensor_rank = lax.axis_index("tensor")
    data_rank = lax.axis_index("dp")
    rows_local = stream_in.shape[0]
    model = stream_in.shape[1]
    qkv_width = qkv_weight.shape[1]
    heads = qkv_width // (3 * HD)
    width = heads * HD
    units = fc_weight.shape[1]
    groups = lax.axis_size("tensor")
    tensor_bits = bits_of(groups)
    far_first = tensor_bits[:0:-1] + tensor_bits[:1]
    order = halving_order(tensor_bits)
    ids = jnp.stack([tensor_rank, data_rank, *order]).astype(jnp.int32)
    data_bits = bits_of(lax.axis_size("dp"))
    rows_first = data_bits[:0:-1] + data_bits[:1]
    columns_first = data_bits[:1] + data_bits[:0:-1]
    near_bits = data_bits
    next_bits = data_bits[1:2] + data_bits[:1] + data_bits[2:]
    qkv_bits = [data_bits[:1] + data_bits[:0:-1], next_bits]

    blocks = prepare_weights(qkv_weight, dense_weight, fc_weight, out_weight)
    qkv_pack = Pack(blocks[0], "dp", rows_first)
    dense_pack = Pack(blocks[1], "dp", columns_first)
    fc_pack = Pack(blocks[2], "dp", rows_first)
    out_pack = Pack(blocks[3], "dp", rows_first)

    sent_norm, normalized, inv_std = normalize(stream_in)
    sent = gather_far(sent_norm, "tensor", tensor_bits)

    info = tree_table(segment_ids, parent_ids)
    gain_attn, shift_attn = norm_gain_attn[None, :], norm_shift_attn[None, :]
    gain_mlp, shift_mlp = norm_gain_mlp[None, :], norm_shift_mlp[None, :]
    sent_near, near = swap(sent[0], "tensor", 1), swap(out_grad, "tensor", 1)
    cut = rows_local * 3 // 5
    early, late = out_grad[:cut], out_grad[cut:]
    qkv_pack.double()
    dense_pack.double()
    zero = jnp.zeros((), f32)
    near, early, late, zero, qkv_bias, fc_bias, info = tie_packs(
        qkv_pack, dense_pack, fc_pack, beside=[near, early, late, zero, qkv_bias, fc_bias, info]
    )
    tables = angle_tables(zero)
    qkv_rows, fc_rows = qkv_bias.reshape(groups, qkv_width), fc_bias.reshape(groups, units)
    while len(qkv_pack.bits) > 1:
        qkv_pack.double()
        dense_pack.double()
    fc_pack.double()
    done = tie_packs(
        qkv_pack,
        dense_pack,
        out_pack,
        beside=[early, late, *tables, qkv_rows, fc_rows, sent_near, *sent],
    )
    early, late, *done = done
    tables, (qkv_rows, fc_rows, sent_near), sent = done[:2], done[2:5], done[5:]
    early_far = gather_far(early, "tensor", tensor_bits)[1:]
    sent_near = [sent_near] + [swap(x, "tensor", 1) for x in sent[1:]]
    sent = [x for pair in zip(sent, sent_near) for x in pair]
    qkv_pack.double()
    dense_pack.double()
    late, *done = tie_packs(
        qkv_pack, dense_pack, fc_pack, out_pack, beside=[late, *sent, *early_far]
    )
    sent, early_far = Tokens([(x,) for x in done[:groups]], order), done[groups:]
    late_far = gather_far(late, "tensor", tensor_bits)[1:]
    early_near = [swap(x, "tensor", 1) for x in early_far]
    out_pack.double()
    while len(fc_pack.bits) > 1:
        fc_pack.double()

    done = project_qkv(
        ids, info, sent, gain_attn, shift_attn, qkv_pack, qkv_rows, tables, width
    )
    done = tie_packs(fc_pack, out_pack, beside=[*done, *early_near, *late_far])
    (queries, keys, values), done = done[:3], done[3:]
    early_near, late_far = done[: groups // 2 - 1], done[groups // 2 - 1 :]
    late_near = [swap(x, "tensor", 1) for x in late_far]
    far = zip(zip(early_far, late_far), zip(early_near, late_near))
    grad = Tokens([(out_grad,), (near,), *[x for pair in far for x in pair]], order)
    while len(out_pack.bits) > 1:
        out_pack.double()
    (grad_context,) = tie_packs(out_pack, beside=[project_grad(ids, grad, dense_pack, width)])
    fc_pack.double()
    out_pack.double()
    done = attention(info, tables, queries, keys, values, grad_context)
    context, dq, dk, dv = tie_packs(fc_pack, out_pack, beside=done)
    dp_orders = [halving_order(near_bits), halving_order(next_bits)]
    qkv_orders = [halving_order(bits) for bits in qkv_bits]
    attn_parts = Parts(
        *project_context(ids, context, dense_pack, groups, model), "tensor", tensor_bits
    )
    attn_parts.begin()
    done = attention_weights(
        ids, info, tables, context, dq, dk, dv, sent, grad, gain_attn, shift_attn, qkv_orders
    )
    *done, attn_parts.other = tie_halves([*done, attn_parts.other], attn_parts)
    grads, qkv_bias_sums, *stacks = done
    attn_parts.middle()
    qkv_sums = [Halving(*stacks[:2], "dp", qkv_bits[0]), Halving(*stacks[2:], "dp", qkv_bits[1])]
    sent.arrays[0], attn_parts.send = tie(sent.arrays[0], attn_parts.send)
    attn_parts.swap()
    for parts in qkv_sums:
        parts.swap()
    done = mlp(
        ids, sent, grad, gain_mlp, shift_mlp, fc_pack, fc_rows, out_pack, dp_orders
    )
    done = tie_halves(done, attn_parts, *qkv_sums)
    *mlp_stacks, hidden, fc_bias_sums = done[:5]
    stacks = done[5:]
    attn_parts.add()
    mlp_parts = Parts(*mlp_stacks, "tensor", tensor_bits)
    mlp_sums = [Halving(*stacks[:2], "dp", near_bits), Halving(*stacks[2:], "dp", next_bits)]
    mlp_parts.begin()
    add_stacks(qkv_sums)
    mlp_parts.middle()
    hidden, mlp_parts.send = tie(hidden, mlp_parts.send)
    hidden, other = tie(hidden, mlp_parts.terms[1][0])
    mlp_parts.terms[1] = (other, 0)
    mlp_parts.swap()
    for parts in qkv_sums + mlp_sums:
        parts.swap()
    done = norm_backward(ids, sent, grads, hidden, gain_attn, gain_mlp, qkv_pack, fc_pack)
    done = tie_halves(done, mlp_parts, *qkv_sums, *mlp_sums)
    *back_stacks, norm_sums = done
    mlp_parts.add()

    back_parts = Parts(*back_stacks, "tensor", tensor_bits)
    back_parts.begin()
    add_stacks(qkv_sums + mlp_sums)
    back_parts.middle()

    stream_in, back_parts.send = tie(stream_in, back_parts.send)
    stream_in, other = tie(stream_in, back_parts.terms[1][0])
    back_parts.terms[1] = (other, 0)
    back_parts.swap()
    for parts in qkv_sums + mlp_sums:
        parts.swap()
    output, sums = finish_output(
        ids,
        stream_in,
        out_grad,
        attn_parts.terms,
        mlp_parts.terms,
        dense_bias[None, :],
        out_bias[None, :],
        norm_sums,
        fc_bias_sums,
        qkv_bias_sums,
        groups,
    )


    sums = sums + swap(sums, "tensor", 1)
    for bit in data_bits[3:]:
        sums = sums + swap(sums, "dp", bit)
    other, *_ = tie_halves([swap(sums, "dp", data_bits[2])], *mlp_sums, qkv_sums[1])
    sums = sums + other
    add_stacks(mlp_sums)
    sums, *sends = tie(sums, *[parts.send for parts in mlp_sums])
    for parts, send in zip(mlp_sums, sends):
        parts.send = send
    for bit in data_bits[:2]:
        sums = sums + swap(sums, "dp", bit)
    sums, back_parts.got = tie(sums, back_parts.got)
    back_parts.add()
    stream_grad = finish_grad(out_grad, normalized, inv_std, back_parts.terms)
    sums, stream_grad = tie(sums, stream_grad)
    for bit in tensor_bits[1:]:
        sums = sums + swap(sums, "tensor", bit)

    fc_weight_grad, out_weight_grad = finish_mlp_weights(*[x.finish() for x in mlp_sums])
    for parts in qkv_sums:
        parts.add()
    qkv_weight_grad, dense_weight_grad = finish_attention_weights(*[x.finish() for x in qkv_sums])

    count_all = float(rows_local * lax.axis_size("dp") * groups * model)
    gain_attn_grad, shift_attn_grad, gain_mlp_grad, shift_mlp_grad = (sums[x] for x in range(4))
    root_squares = jnp.sqrt(jnp.sum(sums[4:7], axis=1) / count_all)
    residual_grad = sums[7]
    fc_bias_grad = sums[8:12].reshape(-1)
    qkv_bias_grad = by_head(sums[12 : 12 + groups, :qkv_width], heads).reshape(-1)
    return (
        output,
        stream_grad,
        gain_attn_grad,
        shift_attn_grad,
        gain_mlp_grad,
        shift_mlp_grad,
        qkv_weight_grad,
        qkv_bias_grad,
        dense_weight_grad,
        residual_grad,
        fc_weight_grad,
        fc_bias_grad,
        out_weight_grad,
        residual_grad,
        root_squares,
    )


def solution(mesh):
    tokens, weights, rows, whole = (
        P(("dp", "tensor"), None),
        P("dp", "tensor"),
        P("tensor", "dp"),
        P(),
    )
    return jax.shard_map(
        local,
        mesh=mesh,
        in_specs=(
            tokens,
            P("dp"),
            P("dp"),
            whole,
            whole,
            whole,
            whole,
            weights,
            whole,
            rows,
            whole,
            weights,
            whole,
            rows,
            whole,
            tokens,
        ),
        out_specs=(
            tokens,
            tokens,
            whole,
            whole,
            whole,
            whole,
            weights,
            whole,
            rows,
            whole,
            weights,
            whole,
            rows,
            whole,
            whole,
        ),
        check_vma=False,
    )
```

```python
import jax
import jax.numpy as jnp
from jax import lax
from jax.experimental import pallas as pl
from jax.experimental.pallas import tpu as pltpu
from jax.sharding import PartitionSpec as P

HD = 64
ROT = 16
TRUNK = 1024
SEG = 128
TREE = 2560
NB = TREE // SEG
NT = TRUNK // SEG

f32 = jnp.float32
bf16 = jnp.bfloat16
eps_norm = 1e-05
masked_score = -1e30


def dot_nn(left, right):
    return lax.dot_general(left, right, (((1,), (0,)), ((), ())), preferred_element_type=f32)


def dot_nt(left, right):
    return lax.dot_general(left, right, (((1,), (1,)), ((), ())), preferred_element_type=f32)


def dot_tn(left, right):
    return lax.dot_general(left, right, (((0,), (0,)), ((), ())), preferred_element_type=f32)


def bits_of(size):
    bits = []
    bit = 1
    while bit < size:
        bits.append(bit)
        bit *= 2
    return bits


def swap(block, axis, bit):
    size = lax.axis_size(axis)
    return lax.ppermute(block, axis, [(i, i ^ bit) for i in range(size)])


def tie(*values):
    return lax.optimization_barrier(values)


def gather_far(block, axis, bits):
    pieces = [block]
    for bit in bits[1:]:
        pieces = pieces + [swap(piece, axis, bit) for piece in pieces]
    return pieces


class Pack:
    def __init__(self, block, axis, bits):
        self.rows, self.axis, self.bits = block.shape[0], axis, list(bits)
        self.arrays, self.owners = [block], [[0]]

    def double(self):
        bit = self.bits.pop(0)
        held = self.arrays[0] if len(self.arrays) == 1 else jnp.concatenate(self.arrays, axis=0)
        self.owners.append([j ^ bit for owners in self.owners for j in owners])
        self.arrays.append(swap(held, self.axis, bit))

    def specs(self):
        return [pl.BlockSpec(memory_space=pltpu.HBM)] * len(self.arrays)

    def pieces(self):
        return sum(len(owners) for owners in self.owners)

    def copies(self, refs, where, number, done):
        started = []
        for ref, owners in zip(refs, self.owners):
            for at, j in enumerate(owners):
                rows = pl.ds(pl.multiple_of((number ^ j) * self.rows, self.rows), self.rows)
                source = ref.at[pl.ds(at * self.rows, self.rows), :]
                copy = pltpu.make_async_copy(source, where.at[rows, :], done.at[len(started)])
                started.append(copy)
        return started


def tie_packs(*packs, beside=()):
    flat = tie(*beside, *[x for pack in packs for x in pack.arrays])
    at = len(beside)
    for pack in packs:
        pack.arrays = list(flat[at : at + len(pack.arrays)])
        at += len(pack.arrays)
    return list(flat[: len(beside)])


def halving_order(bits):
    if not bits:
        return [0]
    rest = halving_order(bits[1:])
    return [bits[0] ^ j for j in rest] + rest


class Halving:
    def __init__(self, send, keep, axis, bits):
        self.send, self.axis, self.bits = send, axis, list(bits)
        self.terms = [(keep, 0)]

    def swap(self):
        self.got = swap(self.send, self.axis, self.bits.pop(0))

    def add(self):
        self.terms.append((self.got, 0))
        half = self.got.shape[0] // 2
        if half:
            self.send = add_terms(self.terms, half)
            self.terms = [(x, at + half) for x, at in self.terms]

    def most(self):
        while len(self.bits) > 1:
            self.swap()
            self.add()

    def finish(self):
        while self.bits:
            self.swap()
            self.add()
        return self.terms


class Parts(Halving):
    def __init__(self, first, second, keep, axis, bits):
        super().__init__(first, keep, axis, bits)
        self.second = second

    def begin(self):
        bit = self.bits.pop(0)
        self.got, self.other = swap(self.send, self.axis, bit), swap(self.second, self.axis, bit)

    def middle(self):
        half = self.got.shape[0]
        self.send = add_terms([*self.terms, (self.got, 0)], half)
        self.terms = [(self.terms[0][0], half), (self.other, 0)]
        while len(self.bits) > 1:
            self.swap()
            self.add()


def tie_halves(values, *halvings):
    flat = tie(*values, *[x.got for x in halvings])
    for x, got in zip(halvings, flat[len(values) :]):
        x.got = got
    return flat[: len(values)]


def resident(shape):
    zeros = (0,) * len(shape)
    return pl.BlockSpec(shape, lambda *_: zeros, pipeline_mode=pl.Buffered(1))


def own_block(rows, columns):
    return pl.BlockSpec((rows, columns), lambda i, ids, *_: (ids[0] ^ ids[2 + i], 0))


def step_block(rows, columns):
    return pl.BlockSpec((rows, columns), lambda i, *_: (i, 0))


def part_shapes(groups, rows, columns):
    quarter = max(groups // 4, 1)
    return [shaped(n, rows, columns) for n in (quarter, quarter, groups - 2 * quarter)]


def part_blocks(groups, rows, columns):
    quarter = max(groups // 4, 1)
    shape = (pl.Squeezed(), rows, columns)
    return [
        pl.BlockSpec(shape, lambda i, *_: (jnp.minimum(i, quarter - 1), 0, 0)),
        pl.BlockSpec(shape, lambda i, *_: (jnp.clip(i - quarter, 0, quarter - 1), 0, 0)),
        pl.BlockSpec(shape, lambda i, *_: (jnp.maximum(i - 2 * quarter, 0), 0, 0)),
    ]


def store_part(stacks, value, step, groups):
    quarter = max(groups // 4, 1)
    turn_of = jnp.minimum(step // quarter, 2)
    for at, stack in enumerate(stacks):

        @pl.when(turn_of == at)
        def _(stack=stack):
            stack[...] = value


class Tokens:
    def __init__(self, blocks, order):
        blocks = [blocks[j] for j in order]
        self.groups, self.counts = len(blocks), [len(block) for block in blocks]
        self.rows, self.model = sum(x.shape[0] for x in blocks[0]), blocks[0][0].shape[1]
        self.arrays = [x for block in blocks for x in block]
        self.specs = [pl.BlockSpec(memory_space=pltpu.HBM)] * len(self.arrays)

    def scratch(self):
        return [
            pltpu.VMEM((2, self.rows, self.model), bf16),
            pltpu.SemaphoreType.DMA((2, max(self.counts))),
        ]

    def fetch(self, refs, held, done, step):
        def copies(at):
            first, start, found = sum(self.counts[:at]), 0, []
            for k, ref in enumerate(refs[first : first + self.counts[at]]):
                where = held.at[at % 2, pl.ds(start, ref.shape[0]), :]
                found.append(pltpu.make_async_copy(ref, where, done.at[at % 2, k]))
                start += ref.shape[0]
            return found

        for at in range(self.groups):

            @pl.when(step == at)
            def _(at=at):
                ahead = copies(at) if at == 0 else []
                if at + 1 < self.groups:
                    ahead = ahead + copies(at + 1)
                for copy in ahead:
                    copy.start()
                for copy in copies(at):
                    copy.wait()


def store_halves(send, keep, total, number, order, columns=slice(None), source=slice(None)):
    half, rows = send.shape[0], send.shape[1]
    for at, j in enumerate(order):
        where = send if at < half else keep
        block = total[pl.ds(pl.multiple_of((number ^ j) * rows, rows), rows), source]
        where[at % half, :, columns] = block.astype(bf16)


def call(
    kernel, name, grid, prefetch, operands, specs, outs, out_specs, scratch, flops, extra=0, room=12, light=False
):
    size = 0 if light else sum(x.size * x.dtype.itemsize for x in [*operands, *outs])
    return pl.pallas_call(
        kernel,
        grid_spec=pltpu.PrefetchScalarGridSpec(
            num_scalar_prefetch=len(prefetch),
            grid=grid,
            in_specs=specs,
            out_specs=out_specs,
            scratch_shapes=scratch,
        ),
        out_shape=outs,
        compiler_params=pltpu.CompilerParams(
            dimension_semantics=("arbitrary",) * len(grid), vmem_limit_bytes=room << 20
        ),
        cost_estimate=pl.CostEstimate(
            flops=int(flops), bytes_accessed=int(size), transcendentals=int(extra)
        ),
        name=name,
    )(*prefetch, *operands)


def shaped(*shape, dtype=bf16):
    return jax.ShapeDtypeStruct(shape, dtype)


def shift_gain(block, gain, shift):
    return (block.astype(f32) * gain[...] + shift[...]).astype(bf16)


def turn(block, cosine, sine, sign):
    width = block.shape[1]
    step = min(width, 128)
    lane = lax.broadcasted_iota(jnp.int32, (block.shape[0], step), 1) % HD
    done = []
    for start in range(0, width, step):
        part = block[:, start : start + step]
        if step == 128:
            left = pltpu.roll(part, step - ROT // 2, 1)
            right = pltpu.roll(part, ROT // 2, 1)
        else:
            left = jnp.concatenate([part[:, ROT // 2 :], part[:, : ROT // 2]], axis=1)
            right = jnp.concatenate([part[:, -ROT // 2 :], part[:, : -ROT // 2]], axis=1)
        moved = jnp.where(lane < ROT // 2, -left, right) * sine[:, :step]
        done.append(part * cosine[:, :step] + moved * sign)
    return done[0] if len(done) == 1 else jnp.concatenate(done, axis=1)


def weight_scratch(pack):
    model = pack.rows * pack.pieces()
    columns = pack.arrays[0].shape[1]
    return [pltpu.VMEM((model, columns), bf16), pltpu.SemaphoreType.DMA((pack.pieces(),))]


def prepare_weights(qkv, dense, fc, out):
    rows, columns = qkv.shape
    width = columns // 3

    def kernel(qkv_ref, dense_ref, fc_ref, out_ref, qkv_to, dense_to, fc_to, out_to):
        for head in range(width // HD):
            for kind in range(3):
                at, own = (3 * head + kind) * HD, kind * width + head * HD
                qkv_to[:, own : own + HD] = qkv_ref[:, at : at + HD].astype(bf16)
        dense_to[...] = dense_ref[...].T.astype(bf16)
        fc_to[...] = fc_ref[...].astype(bf16)
        out_to[...] = out_ref[...].T.astype(bf16)

    operands = [qkv, dense, fc, out]
    outs = [shaped(*qkv.shape), shaped(*dense.shape[::-1]), shaped(*fc.shape), shaped(*out.shape[::-1])]
    return call(
        kernel,
        "prepare_weights",
        (1,),
        [],
        operands,
        [resident(x.shape) for x in operands],
        outs,
        [resident(x.shape) for x in outs],
        [],
        rows * columns,
    )


def normalize(stream):
    rows, model = stream.shape
    block = 160

    def kernel(stream_ref, sent_ref, mean_ref, std_ref):
        field = stream_ref[...]
        mean = jnp.sum(field, axis=1, keepdims=True) / model
        centred = field - mean
        variance = jnp.sum(centred * centred, axis=1, keepdims=True) / model
        scale = lax.rsqrt(variance + eps_norm)
        sent_ref[...] = (centred * scale).astype(bf16)
        mean_ref[...] = mean
        std_ref[...] = scale

    return call(
        kernel,
        "normalize",
        (rows // block,),
        [],
        [stream],
        [step_block(block, model)],
        [shaped(rows, model), shaped(rows, 1, dtype=f32), shaped(rows, 1, dtype=f32)],
        [step_block(block, model), step_block(block, 1), step_block(block, 1)],
        [],
        rows * model * 8,
        room=62,
    )


def project_qkv(ids, info, sent, gain, shift, pack, bias, tables, width):
    groups, held, rows, model = sent.groups, len(sent.arrays), sent.rows, sent.model

    def kernel(ids, info, *refs):
        sent_refs, refs = refs[:held], refs[held:]
        weight_refs, refs = refs[: len(pack.arrays)], refs[len(pack.arrays) :]
        gain, shift, bias, cos, sine, q_out, k_out, v_out = refs[:8]
        block, arrived, whole, placed, added = refs[8:]
        step = pl.program_id(0)

        @pl.when(step == 0)
        def _():
            for copy in pack.copies(weight_refs, whole, ids[1], placed):
                copy.start()

        sent.fetch(sent_refs, block, arrived, step)

        @pl.when(step == 0)
        def _():
            for copy in pack.copies(weight_refs, whole, ids[1], placed):
                copy.wait()
            own = bias[pl.ds(ids[0], 1), :]
            for head in range(width // HD):
                for kind in range(3):
                    at, to = (3 * head + kind) * HD, kind * width + head * HD
                    added[:, to : to + HD] = own[:, at : at + HD]

        token = block[step % 2]
        normed = shift_gain(token, gain, shift)
        blocks = rows // SEG
        cut = (blocks + 1) // 2
        both = [dot_nn(normed[x], whole[...]) + added[...] for x in (slice(0, cut * SEG), slice(cut * SEG, rows))]
        first = (ids[0] ^ ids[2 + step]) * blocks
        for at in range(blocks):
            number = first + at
            table = pl.ds(pl.multiple_of(info[number // NB, number % NB, 4] * SEG, SEG), SEG)
            tabs = (cos[table, :], sine[table, :])
            own = slice(at * SEG, (at + 1) * SEG)
            here = at * SEG if at < cut else (at - cut) * SEG
            qkv = both[at >= cut][here : here + SEG]
            q_out[own, :] = (turn(qkv[:, :width], *tabs, 1.0) * HD**-0.5).astype(bf16)
            k_out[own, :] = turn(qkv[:, width : 2 * width], *tabs, 1.0).astype(bf16)
            v_out[own, :] = qkv[:, 2 * width :].astype(bf16)

    operands = [*sent.arrays, *pack.arrays, gain, shift, bias, *tables]
    out = shaped(groups * rows, width)
    return call(
        kernel,
        "project_qkv",
        (groups,),
        [ids, info],
        operands,
        sent.specs
        + pack.specs()
        + [resident(x.shape) for x in operands[held + len(pack.arrays) :]],
        [out] * 3,
        [own_block(rows, width)] * 3,
        sent.scratch() + weight_scratch(pack) + [pltpu.VMEM((1, 3 * width), f32)],
        2 * groups * rows * model * 3 * width,
        room=62,
    )


def project_grad(ids, grad, pack, width):
    groups, held, rows, model = grad.groups, len(grad.arrays), grad.rows, grad.model

    def kernel(ids, *refs):
        grad_refs, refs = refs[:held], refs[held:]
        weight_refs, (out, block, arrived, whole, placed) = refs[:-5], refs[-5:]
        step = pl.program_id(0)

        @pl.when(step == 0)
        def _():
            for copy in pack.copies(weight_refs, whole, ids[1], placed):
                copy.start()

        grad.fetch(grad_refs, block, arrived, step)

        @pl.when(step == 0)
        def _():
            for copy in pack.copies(weight_refs, whole, ids[1], placed):
                copy.wait()

        out[...] = dot_nn(block[step % 2], whole[...]).astype(bf16)

    operands = [*grad.arrays, *pack.arrays]
    return call(
        kernel,
        "project_grad",
        (groups,),
        [ids],
        operands,
        grad.specs + pack.specs(),
        [shaped(groups * rows, width)],
        [own_block(rows, width)],
        grad.scratch() + weight_scratch(pack),
        2 * groups * rows * model * width,
    )[0]


def attention_kernel(
    info, q_ref, do_ref, k_ref, v_ref, cos, sine, ctx_ref, dq_ref, dk_ref, dv_ref, dk_sum, dv_sum
):
    tree, step = pl.program_id(0), pl.program_id(1)
    width = q_ref.shape[1]
    heads = width // HD
    both = 2 * SEG
    lane_head = lax.broadcasted_iota(jnp.int32, (both, width), 1) // HD

    @pl.when(step == 0)
    def _():
        dk_sum[...] = jnp.zeros_like(dk_sum)
        dv_sum[...] = jnp.zeros_like(dv_sum)

    queries, grads = q_ref[...], do_ref[...]
    zero = jnp.zeros_like(queries)
    q_rows = jnp.concatenate([jnp.where(lane_head == h, queries, zero) for h in range(heads)], axis=0)
    g_rows = jnp.concatenate([jnp.where(lane_head == h, grads, zero) for h in range(heads)], axis=0)
    q_turned, g_turned = queries.T, grads.T
    ahead = lax.broadcasted_iota(jnp.int32, (SEG, SEG), 1) - lax.broadcasted_iota(
        jnp.int32, (SEG, SEG), 0
    )
    blocks = []
    for at in range(2):
        number = step * 2 + at
        first, second = info[tree, number, 0], info[tree, number, 1]
        rows = [pl.ds(pl.multiple_of(x * SEG, SEG), SEG) for x in (first, second)]
        seen = [ahead <= info[tree, number, 2], ahead <= info[tree, number, 3]]
        seen = jnp.concatenate([jnp.concatenate(seen, axis=1)] * heads, axis=0)
        k_near = jnp.concatenate([k_ref[x, :] for x in rows], axis=0)
        v_near = jnp.concatenate([v_ref[x, :] for x in rows], axis=0)
        blocks.append((first, second, seen, k_near, v_near))

    def of_block(stack, at):
        cuts = [stack[h * both + at * SEG : h * both + (at + 1) * SEG] for h in range(heads)]
        return jnp.concatenate(cuts, axis=0)

    def by_block(parts):
        cuts = [x[h * SEG : (h + 1) * SEG] for h in range(heads) for x in parts]
        return jnp.concatenate(cuts, axis=0)

    def work(pairs):
        count = pairs * both
        near = [
            jnp.where(seen, dot_nt(of_block(q_rows, at), k_near), masked_score)
            for at, (_, _, seen, k_near, _) in enumerate(blocks)
        ]
        near = by_block(near)
        most = jnp.max(near, axis=1, keepdims=True)
        if count:
            k_far, v_far = k_ref[0:count, :], v_ref[0:count, :]
            far = dot_nt(q_rows, k_far)
            most = jnp.maximum(most, jnp.max(far, axis=1, keepdims=True))
        near = jnp.exp(near - most)
        total = jnp.sum(near, axis=1, keepdims=True)
        if count:
            far = jnp.exp(far - most)
            total = total + jnp.sum(far, axis=1, keepdims=True)
        scale = 1.0 / total
        near = near * scale
        near_low = near.astype(bf16)
        context = by_block([dot_nn(of_block(near_low, at), x[4]) for at, x in enumerate(blocks)])
        if count:
            far = far * scale
            far_low = far.astype(bf16)
            context = context + dot_nn(far_low, v_far)
        delta = jnp.sum(context * g_rows.astype(f32), axis=1, keepdims=True)
        slope = by_block([dot_nt(of_block(g_rows, at), x[4]) for at, x in enumerate(blocks)])
        near = (near * (slope - delta)).astype(bf16)
        dq = by_block([dot_nn(of_block(near, at), x[3]) for at, x in enumerate(blocks)])
        if count:
            far = (far * (dot_nt(g_rows, v_far) - delta)).astype(bf16)
            dq = dq + dot_nn(far, k_far)
        ctx_own, dq_own = context[0:both], dq[0:both]
        for h in range(1, heads):
            ctx_own = jnp.where(lane_head == h, context[h * both : (h + 1) * both], ctx_own)
            dq_own = jnp.where(lane_head == h, dq[h * both : (h + 1) * both], dq_own)
        ctx_ref[...] = ctx_own.astype(bf16)
        for at in range(2):
            table = pl.ds(pl.multiple_of(info[tree, step * 2 + at, 4] * SEG, SEG), SEG)
            own = slice(at * SEG, (at + 1) * SEG)
            turned = turn(dq_own[own] * HD**-0.5, cos[table, :], sine[table, :], -1.0)
            dq_ref[own, :] = turned.astype(bf16)
        for h in range(heads):
            part = slice(h * HD, (h + 1) * HD)
            for at, (first, second, *_) in enumerate(blocks):
                own = slice(h * both + at * SEG, h * both + (at + 1) * SEG)
                columns = slice(at * SEG, (at + 1) * SEG)
                dk = dot_nn(q_turned[part, columns], near[own])
                dv = dot_nn(g_turned[part, columns], near_low[own])
                dk_sum[first, part, :] += dk[:, :SEG]
                dv_sum[first, part, :] += dv[:, :SEG]
                dk_sum[second, part, :] += dk[:, SEG:]
                dv_sum[second, part, :] += dv[:, SEG:]
            if count:
                own = slice(h * both, (h + 1) * both)
                dk = dot_nn(q_turned[part], far[own])
                dv = dot_nn(g_turned[part], far_low[own])
                for j in range(2 * pairs):
                    dk_sum[j, part, :] += dk[:, j * SEG : (j + 1) * SEG]
                    dv_sum[j, part, :] += dv[:, j * SEG : (j + 1) * SEG]

    for pairs in range(NT // 2):

        @pl.when(step == pairs)
        def _(pairs=pairs):
            work(pairs)

    @pl.when(step >= NT // 2)
    def _():
        work(NT // 2)

    @pl.when(step == NB // 2 - 1)
    def _():
        def finish(j, carry):
            rows = pl.ds(pl.multiple_of(j * SEG, SEG), SEG)
            dv_ref[rows, :] = dv_sum[j].T.astype(bf16)
            dk_ref[rows, :] = dk_sum[j].T.astype(bf16)
            return carry

        lax.fori_loop(0, NB, finish, 0)


def attention(info, tables, queries, keys, values, grads):
    total, width = queries.shape
    trees = total // TREE
    block = pl.BlockSpec((2 * SEG, width), lambda t, b, info: (t * NB // 2 + b, 0))
    whole = pl.BlockSpec((TREE, width), lambda t, b, info: (t, 0))
    scores = trees * (TREE - TRUNK) * (TRUNK + 2 * SEG) * (width // HD)
    return call(
        attention_kernel,
        "attention",
        (trees, NB // 2),
        [info],
        [queries, grads, keys, values, *tables],
        [block, block, whole, whole] + [resident(x.shape) for x in tables],
        [shaped(total, width)] * 4,
        [block, block, whole, whole],
        [pltpu.VMEM((NB, width, SEG), f32), pltpu.VMEM((NB, width, SEG), f32)],
        scores * width * 2 * 6 * 1.3,
        scores,
        room=20,
    )


def project_context(ids, context, pack, groups, model):
    rows, width = context.shape[0] // groups, context.shape[1]

    def kernel(ids, ctx, *refs):
        weight_refs, stacks, (whole, placed) = refs[:-5], refs[-5:-2], refs[-2:]
        step = pl.program_id(0)

        @pl.when(step == 0)
        def _():
            copies = pack.copies(weight_refs, whole, ids[1], placed)
            for copy in copies:
                copy.start()
            for copy in copies:
                copy.wait()

        store_part(stacks, dot_nt(ctx[...], whole[...]).astype(bf16), step, groups)

    operands = [context, *pack.arrays]
    return call(
        kernel,
        "project_context",
        (groups,),
        [ids],
        operands,
        [own_block(rows, width)] + pack.specs(),
        part_shapes(groups, rows, model),
        part_blocks(groups, rows, model),
        weight_scratch(pack),
        2 * groups * rows * model * width,
        room=14,
    )


def attention_weights(ids, info, tables, context, dq, dk, dv, sent, grad, gain, shift, orders):
    groups, held, rows, model = sent.groups, len(sent.arrays), sent.rows, sent.model
    width, count = dq.shape[1], len(orders[0])

    def kernel(ids, info, ctx_ref, dq_ref, dk_ref, dv_ref, *refs):
        sent_refs, refs = refs[:held], refs[held:]
        grad_refs, refs = refs[: len(grad.arrays)], refs[len(grad.arrays) :]
        gain, shift, cos, sine, grads, bias_ref, *stacks = refs[:10]
        block, arrived, grad_block, grad_arrived, total, dense_total = refs[10:]
        step = pl.program_id(0)

        @pl.when(step == 0)
        def _():
            total[...] = jnp.zeros_like(total)
            dense_total[...] = jnp.zeros_like(dense_total)
            bias_ref[...] = jnp.zeros_like(bias_ref)

        sent.fetch(sent_refs, block, arrived, step)
        grad.fetch(grad_refs, grad_block, grad_arrived, step)
        grads[:, :width] = dq_ref[...]
        first = (ids[0] ^ ids[2 + step]) * (rows // SEG)
        for at in range(rows // SEG):
            number = first + at
            table = pl.ds(pl.multiple_of(info[number // NB, number % NB, 4] * SEG, SEG), SEG)
            own = slice(at * SEG, (at + 1) * SEG)
            turned = turn(dk_ref[own, :], cos[table, :], sine[table, :], -1.0)
            grads[own, width : 2 * width] = turned.astype(bf16)
        grads[:, 2 * width :] = dv_ref[...]
        bias_ref[0:1, :] += jnp.sum(grads[...].astype(f32), axis=0, keepdims=True)
        total[...] += dot_tn(shift_gain(block[step % 2], gain, shift), grads[...])
        dense_total[...] += dot_tn(grad_block[step % 2], ctx_ref[...])

        @pl.when(step == groups - 1)
        def _():
            store_halves(*stacks[:2], total, ids[1], orders[0], source=slice(0, 2 * width))
            source = slice(2 * width, 3 * width)
            store_halves(*stacks[2:], total, ids[1], orders[1], slice(0, width), source)
            columns = slice(width, 2 * width)
            store_halves(*stacks[2:], dense_total, ids[1], orders[1], columns)

    operands = [context, dq, dk, dv, *sent.arrays, *grad.arrays, gain, shift, *tables]
    outs = [shaped(groups * rows, 3 * width), shaped(8, 3 * width, dtype=f32)]
    outs += [shaped(count // 2, model // count, 2 * width)] * 4
    return call(
        kernel,
        "attention_weights",
        (groups,),
        [ids, info],
        operands,
        [own_block(rows, width)] * 4
        + sent.specs
        + grad.specs
        + [resident(x.shape) for x in operands[-4:]],
        outs,
        [step_block(rows, 3 * width)] + [resident(x.shape) for x in outs[1:]],
        sent.scratch()
        + grad.scratch()
        + [pltpu.VMEM((model, 3 * width), f32), pltpu.VMEM((model, width), f32)],
        2 * groups * rows * model * 4 * width,
        room=24,
    )


def mlp(ids, sent, grad, gain, shift, fc, bias, out, orders):
    groups, held, rows, model = sent.groups, len(sent.arrays), sent.rows, sent.model
    pieces, units = len(fc.arrays), fc.arrays[0].shape[1]

    def kernel(ids, *refs):
        sent_refs, refs = refs[:held], refs[held:]
        grad_refs, refs = refs[: len(grad.arrays)], refs[len(grad.arrays) :]
        fc_refs, refs = refs[:pieces], refs[pieces:]
        out_refs, refs = refs[:pieces], refs[pieces:]
        gain, shift, bias, *parts_out = refs[:6]
        hidden_ref, bias_ref = refs[6:8]
        stacks, refs = refs[8:12], refs[12:]
        block, arrived, grad_block, grad_arrived, fc_whole, fc_placed, out_whole, out_placed = refs[:8]
        act_ref, fc_total, out_total = refs[8:]
        step = pl.program_id(0)

        def weights():
            copies = fc.copies(fc_refs, fc_whole, ids[1], fc_placed)
            return copies + out.copies(out_refs, out_whole, ids[1], out_placed)

        @pl.when(step == 0)
        def _():
            for copy in weights():
                copy.start()
            fc_total[...] = jnp.zeros_like(fc_total)
            out_total[...] = jnp.zeros_like(out_total)
            bias_ref[...] = jnp.zeros_like(bias_ref)

        sent.fetch(sent_refs, block, arrived, step)
        grad.fetch(grad_refs, grad_block, grad_arrived, step)

        @pl.when(step == 0)
        def _():
            for copy in weights():
                copy.wait()

        token, grads = block[step % 2], grad_block[step % 2]
        normed = shift_gain(token, gain, shift)
        count = 2
        parts = [slice(k * rows // count, (k + 1) * rows // count) for k in range(count)]
        added = bias[pl.ds(ids[0], 1), :]
        hidden = [dot_nn(normed[x], fc_whole[...]) + added for x in parts]
        back = [dot_nn(grads[x], out_whole[...]) for x in parts]
        for x, field, slope in zip(parts, hidden, back):
            chance = 0.5 + 0.5 * lax.erf(field * 0.7071067811865476)
            bell = jnp.exp(field * field * -0.5) * 0.3989422804014327
            act_ref[x, :] = (field * chance).astype(bf16)
            low = (slope * (chance + field * bell)).astype(bf16)
            hidden_ref[x, :] = low
            bias_ref[0:1, :] += jnp.sum(low.astype(f32), axis=0, keepdims=True)
        store_part(parts_out, dot_nt(act_ref[...], out_whole[...]).astype(bf16), step, groups)
        out_total[...] += dot_tn(grads, act_ref[...])
        fc_total[...] += dot_tn(normed, hidden_ref[...])

        @pl.when(step == groups - 1)
        def _():
            half = units // 2
            for at, order in enumerate(orders):
                stack = stacks[2 * at : 2 * at + 2]
                source = slice(at * half, (at + 1) * half)
                store_halves(*stack, fc_total, ids[1], order, slice(0, half), source)
                store_halves(*stack, out_total, ids[1], order, slice(half, units), source)

    operands = [*sent.arrays, *grad.arrays, *fc.arrays, *out.arrays, gain, shift, bias]
    count = model // fc.rows
    outs = part_shapes(groups, rows, model)
    outs += [shaped(groups * rows, units), shaped(8, units, dtype=f32)]
    outs += [shaped(count // 2, fc.rows, units)] * 4
    return call(
        kernel,
        "mlp",
        (groups,),
        [ids],
        operands,
        sent.specs
        + grad.specs
        + fc.specs()
        + out.specs()
        + [resident(x.shape) for x in operands[-3:]],
        outs,
        part_blocks(groups, rows, model)
        + [step_block(rows, units)]
        + [resident(x.shape) for x in outs[4:]],
        sent.scratch()
        + grad.scratch()
        + weight_scratch(fc)
        + weight_scratch(out)
        + [
            pltpu.VMEM((rows, units), bf16),
            pltpu.VMEM((model, units), f32),
            pltpu.VMEM((model, units), f32),
        ],
        10 * groups * rows * model * units,
        room=42,
    )


def norm_backward(ids, sent, grads, hidden, gain_attn, gain_mlp, qkv_pack, fc):
    groups, held, rows, model = sent.groups, len(sent.arrays), sent.rows, sent.model
    pieces, units, columns = len(fc.arrays), hidden.shape[1], grads.shape[1]

    def kernel(ids, grads_ref, hidden_ref, *refs):
        sent_refs, refs = refs[:held], refs[held:]
        qkv_refs, refs = refs[:pieces], refs[pieces:]
        fc_refs, refs = refs[:pieces], refs[pieces:]
        gain_attn, gain_mlp, *stacks = refs[:5]
        sums_ref, block, arrived, qkv_whole, qkv_placed, fc_whole, fc_placed = refs[5:]
        step = pl.program_id(0)

        def weights():
            copies = qkv_pack.copies(qkv_refs, qkv_whole, ids[1], qkv_placed)
            return copies + fc.copies(fc_refs, fc_whole, ids[1], fc_placed)

        @pl.when(step == 0)
        def _():
            for copy in weights():
                copy.start()
            sums_ref[...] = jnp.zeros_like(sums_ref)

        sent.fetch(sent_refs, block, arrived, step)

        @pl.when(step == 0)
        def _():
            for copy in weights():
                copy.wait()

        back_attn = dot_nt(grads_ref[...], qkv_whole[...])
        back_mlp = dot_nt(hidden_ref[...], fc_whole[...])
        token = block[step % 2].astype(f32)
        for at, back in enumerate((back_attn, back_mlp)):
            sums_ref[2 * at : 2 * at + 1, :] += jnp.sum(back * token, axis=0, keepdims=True)
            sums_ref[2 * at + 1 : 2 * at + 2, :] += jnp.sum(back, axis=0, keepdims=True)
        part = back_attn * gain_attn[...] + back_mlp * gain_mlp[...]
        store_part(stacks, part.astype(bf16), step, groups)

    operands = [grads, hidden, *sent.arrays, *qkv_pack.arrays, *fc.arrays, gain_attn, gain_mlp]
    outs = part_shapes(groups, rows, model) + [shaped(8, model, dtype=f32)]
    return call(
        kernel,
        "norm_backward",
        (groups,),
        [ids],
        operands,
        [step_block(rows, columns), step_block(rows, units)]
        + sent.specs
        + qkv_pack.specs()
        + fc.specs()
        + [resident(x.shape) for x in operands[-2:]],
        outs,
        part_blocks(groups, rows, model) + [resident(x.shape) for x in outs[3:]],
        sent.scratch() + weight_scratch(qkv_pack) + weight_scratch(fc),
        2 * groups * rows * model * (units + columns),
        room=26,
    )


def taken(terms, block):
    return [
        pl.BlockSpec((pl.Squeezed(), block, x.shape[2]), lambda i, *_, at=at: (at, i, 0))
        for x, at in terms
    ]


def add_terms(terms, half):
    _, rows, columns = terms[0][0].shape
    block = max(x for x in (320, 128, 64) if rows % x == 0)

    def kernel(*refs):
        refs[-1][...] = sum(x[...].astype(f32) for x in refs[:-1]).astype(bf16)

    shape = (pl.Squeezed(), block, columns)
    out = shaped(half, rows, columns)
    return call(
        kernel,
        "add_terms",
        (half, rows // block),
        [],
        [x for x, _ in terms],
        [pl.BlockSpec(shape, lambda k, i, *_, at=at: (at + k, i, 0)) for _, at in terms],
        [out],
        [pl.BlockSpec(shape, lambda k, i, *_: (k, i, 0))],
        [],
        half * rows * columns * len(terms),
    )[0]


def whole_terms(terms, count):
    return [
        pl.BlockSpec((count, *x.shape[1:]), lambda *_, at=at: (at // count, 0, 0)) for x, at in terms
    ]


def add_stacks(stacks):
    counts = []
    for parts in stacks:
        parts.terms.append((parts.got, 0))
        counts.append(parts.got.shape[0] // 2)
    held = [len(parts.terms) for parts in stacks]
    operands = [x for parts in stacks for x, _ in parts.terms]

    def kernel(*refs):
        for at, half in enumerate(counts):
            first = sum(held[:at])
            total = sum(x[...].astype(f32) for x in refs[first : first + held[at]])
            refs[len(operands) + at][...] = total.astype(bf16)

    outs = [shaped(n, *parts.got.shape[1:]) for n, parts in zip(counts, stacks)]
    sends = call(
        kernel,
        "add_stacks",
        (1,),
        [],
        operands,
        [x for n, parts in zip(counts, stacks) for x in whole_terms(parts.terms, n)],
        outs,
        [resident(x.shape) for x in outs],
        [],
        sum(x.size for x in operands) // 2,
        room=16,
    )
    for n, parts, send in zip(counts, stacks, sends):
        parts.send = send
        parts.terms = [(x, at + n) for x, at in parts.terms]


def finish_mlp_weights(first, second):
    held, (_, rows, units) = len(first), first[0][0].shape
    half = units // 2

    def kernel(*refs):
        low = sum(x[0].astype(f32) for x in refs[:held])
        high = sum(x[0].astype(f32) for x in refs[held:-2])
        refs[-2][:, :half] = low[:, :half]
        refs[-2][:, half:] = high[:, :half]
        refs[-1][:half, :] = low[:, half:].T
        refs[-1][half:, :] = high[:, half:].T

    operands = [x for x, _ in [*first, *second]]
    outs = [shaped(rows, units, dtype=f32), shaped(units, rows, dtype=f32)]
    return call(
        kernel,
        "finish_mlp_weights",
        (1,),
        [],
        operands,
        whole_terms([*first, *second], 1),
        outs,
        [resident(x.shape) for x in outs],
        [],
        len(operands) * rows * units,
    )


def finish_attention_weights(first, second):
    held, (_, rows, columns) = len(first), first[0][0].shape
    width = columns // 2

    def kernel(*refs):
        low = sum(x[0].astype(f32) for x in refs[:held])
        high = sum(x[0].astype(f32) for x in refs[held:-2])
        for head in range(width // HD):
            for kind, (source, start) in enumerate(((low, 0), (low, width), (high, 0))):
                at = (3 * head + kind) * HD
                own = start + head * HD
                refs[-2][:, at : at + HD] = source[:, own : own + HD]
        refs[-1][...] = high[:, width:].T

    operands = [x for x, _ in [*first, *second]]
    outs = [shaped(rows, 3 * width, dtype=f32), shaped(width, rows, dtype=f32)]
    return call(
        kernel,
        "finish_attention_weights",
        (1,),
        [],
        operands,
        whole_terms([*first, *second], 1),
        outs,
        [resident(x.shape) for x in outs],
        [],
        len(operands) * rows * columns,
    )


def sum_rows(groups):
    return (12 + groups + 7) // 8 * 8


def finish_output(ids, stream, grad, attn_terms, mlp_terms, dense_bias, out_bias, norm_sums, fc_sums, qkv_sums, groups):
    rows, model = stream.shape
    block = 160
    first, second = len(attn_terms), len(mlp_terms)
    units, columns = fc_sums.shape[1], qkv_sums.shape[1]
    across = model // units

    def kernel(ids, stream_ref, grad_ref, *refs):
        attn_refs, refs = refs[:first], refs[first:]
        mlp_refs, refs = refs[:second], refs[second:]
        dense_bias, out_bias, norm_ref, fc_ref, qkv_ref, out_ref, sums_ref = refs

        @pl.when(pl.program_id(0) == 0)
        def _():
            sums_ref[...] = jnp.zeros_like(sums_ref)
            sums_ref[0:4, :] = norm_ref[0:4, :]
            own = jnp.concatenate([fc_ref[0:1, :]] * across, axis=1) if across > 1 else fc_ref[0:1, :]
            lane = lax.broadcasted_iota(jnp.int32, (1, model), 1) // units
            sums_ref[pl.ds(8 + ids[0] // across, 1), :] = jnp.where(lane == ids[0] % across, own, 0.0)
            sums_ref[pl.ds(12 + ids[0], 1), :columns] = qkv_ref[0:1, :]

        attn = sum(x[...].astype(f32) for x in attn_refs) + dense_bias[...]
        mlp = sum(x[...].astype(f32) for x in mlp_refs) + out_bias[...]
        output = stream_ref[...] + attn + mlp
        out_ref[...] = output
        for at, value in enumerate((output, attn, mlp)):
            sums_ref[4 + at : 5 + at, :] += jnp.sum(value * value, axis=0, keepdims=True)
        sums_ref[7:8, :] += jnp.sum(grad_ref[...].astype(f32), axis=0, keepdims=True)

    terms = [*attn_terms, *mlp_terms]
    operands = [stream, grad, *[x for x, _ in terms], dense_bias, out_bias, norm_sums, fc_sums, qkv_sums]
    outs = [shaped(rows, model, dtype=f32), shaped(sum_rows(groups), model, dtype=f32)]
    return call(
        kernel,
        "finish_output",
        (rows // block,),
        [ids],
        operands,
        [step_block(block, model), step_block(block, model)]
        + taken(terms, block)
        + [resident(x.shape) for x in operands[-5:]],
        outs,
        [step_block(block, model), resident(outs[1].shape)],
        [],
        rows * model * 16,
        room=16,
    )


def finish_grad(grad, stream, row_mean, inv_std, terms):
    rows, model = grad.shape
    block = 160

    def kernel(grad_ref, stream_ref, mean_ref, std_ref, *refs):
        term_refs, out_ref = refs[:-1], refs[-1]
        sent = sum(x[...].astype(f32) for x in term_refs)
        norm = (stream_ref[...] - mean_ref[...]) * std_ref[...]
        mean = jnp.sum(sent, axis=1, keepdims=True) / model
        cross = jnp.sum(sent * norm, axis=1, keepdims=True) / model
        out_ref[...] = grad_ref[...].astype(f32) + std_ref[...] * (sent - mean - norm * cross)

    operands = [grad, stream, row_mean, inv_std, *[x for x, _ in terms]]
    return call(
        kernel,
        "finish_grad",
        (rows // block,),
        [],
        operands,
        [step_block(block, model)] * 2
        + [step_block(block, 1)] * 2
        + taken(terms, block),
        [shaped(rows, model, dtype=f32)],
        [step_block(block, model)],
        [],
        0,
        light=True,
    )[0]


def tree_table(segment_ids, parent_ids):
    trees = segment_ids.shape[0] // TREE

    def kernel(segment, parent, table):
        for tree in range(trees):
            for block in range(NT):
                odd = block % 2
                row = (block - odd, block - odd + 1, SEG * odd, -SEG * (1 - odd), block)
                for at, value in enumerate(row):
                    table[tree, block, at] = value

            def place(block, carry):
                first = tree * TREE
                owner = parent[first + block * SEG]
                leaf = (owner != segment[first]).astype(jnp.int32)
                at = block
                for other in range(NT, NB):
                    at = jnp.where(segment[first + other * SEG] == owner, other, at)
                table[tree, block, 0] = block
                table[tree, block, 1] = at
                table[tree, block, 2] = 0
                table[tree, block, 3] = SEG * (2 * leaf - 1)
                table[tree, block, 4] = NT + leaf
                return carry

            lax.fori_loop(NT, NB, place, 0)

    smem = pl.BlockSpec(memory_space=pltpu.SMEM)
    return pl.pallas_call(
        kernel,
        in_specs=[smem, smem],
        out_specs=smem,
        out_shape=jax.ShapeDtypeStruct((trees, NB, 5), jnp.int32),
        name="tree_table",
    )(segment_ids, parent_ids)


def angle_tables(zero):
    places = TRUNK + 2 * SEG
    place = lax.broadcasted_iota(jnp.int32, (places, 2 * HD), 0).astype(f32)
    lane = lax.broadcasted_iota(jnp.int32, (places, 2 * HD), 1) % HD
    half = ROT // 2
    frequency = 10000.0 ** (-((lane % half).astype(f32) * 2.0 / ROT))
    angle = (place + zero) * frequency
    cosine = jnp.where(lane < ROT, jnp.cos(angle), 1.0)
    sine = jnp.where(lane < ROT, jnp.sin(angle), 0.0)
    return cosine, sine


def by_kind(array, heads):
    shape = array.shape[:-1]
    array = array.reshape(*shape, heads, 3, HD)
    return jnp.swapaxes(array, -3, -2).reshape(*shape, 3 * heads * HD)


def by_head(array, heads):
    shape = array.shape[:-1]
    array = array.reshape(*shape, 3, heads, HD)
    return jnp.swapaxes(array, -3, -2).reshape(*shape, 3 * heads * HD)


def local(
    stream_in,
    segment_ids,
    parent_ids,
    norm_gain_attn,
    norm_shift_attn,
    norm_gain_mlp,
    norm_shift_mlp,
    qkv_weight,
    qkv_bias,
    dense_weight,
    dense_bias,
    fc_weight,
    fc_bias,
    out_weight,
    out_bias,
    out_grad,
):
    tensor_rank = lax.axis_index("tensor")
    data_rank = lax.axis_index("dp")
    rows_local = stream_in.shape[0]
    model = stream_in.shape[1]
    qkv_width = qkv_weight.shape[1]
    heads = qkv_width // (3 * HD)
    width = heads * HD
    units = fc_weight.shape[1]
    groups = lax.axis_size("tensor")
    tensor_bits = bits_of(groups)
    far_first = tensor_bits[:0:-1] + tensor_bits[:1]
    order = halving_order(tensor_bits)
    ids = jnp.stack([tensor_rank, data_rank, *order]).astype(jnp.int32)
    data_bits = bits_of(lax.axis_size("dp"))
    rows_first = data_bits[:0:-1] + data_bits[:1]
    columns_first = data_bits[:1] + data_bits[:0:-1]
    near_bits = data_bits
    next_bits = data_bits[1:2] + data_bits[:1] + data_bits[2:]
    qkv_bits = [data_bits[:1] + data_bits[:0:-1], next_bits]

    blocks = prepare_weights(qkv_weight, dense_weight, fc_weight, out_weight)
    qkv_pack = Pack(blocks[0], "dp", rows_first)
    dense_pack = Pack(blocks[1], "dp", columns_first)
    fc_pack = Pack(blocks[2], "dp", rows_first)
    out_pack = Pack(blocks[3], "dp", rows_first)

    sent_norm, row_mean, inv_std = normalize(stream_in)
    sent = gather_far(sent_norm, "tensor", tensor_bits)

    info = tree_table(segment_ids, parent_ids)
    gain_attn, shift_attn = norm_gain_attn[None, :], norm_shift_attn[None, :]
    gain_mlp, shift_mlp = norm_gain_mlp[None, :], norm_shift_mlp[None, :]
    sent_near, near = swap(sent[0], "tensor", 1), swap(out_grad, "tensor", 1)
    cut = rows_local * 3 // 5
    early, late = out_grad[:cut], out_grad[cut:]
    qkv_pack.double()
    dense_pack.double()
    zero = jnp.zeros((), f32)
    near, early, late, zero, qkv_bias, fc_bias, info = tie_packs(
        qkv_pack, dense_pack, fc_pack, beside=[near, early, late, zero, qkv_bias, fc_bias, info]
    )
    tables = angle_tables(zero)
    qkv_rows, fc_rows = qkv_bias.reshape(groups, qkv_width), fc_bias.reshape(groups, units)
    while len(qkv_pack.bits) > 1:
        qkv_pack.double()
        dense_pack.double()
    fc_pack.double()
    done = tie_packs(
        qkv_pack,
        dense_pack,
        out_pack,
        beside=[early, late, *tables, qkv_rows, fc_rows, sent_near, *sent],
    )
    early, late, *done = done
    tables, (qkv_rows, fc_rows, sent_near), sent = done[:2], done[2:5], done[5:]
    early_far = gather_far(early, "tensor", tensor_bits)[1:]
    sent_near = [sent_near] + [swap(x, "tensor", 1) for x in sent[1:]]
    sent = [x for pair in zip(sent, sent_near) for x in pair]
    qkv_pack.double()
    dense_pack.double()
    late, *done = tie_packs(
        qkv_pack, dense_pack, fc_pack, out_pack, beside=[late, *sent, *early_far]
    )
    sent, early_far = Tokens([(x,) for x in done[:groups]], order), done[groups:]
    late_far = gather_far(late, "tensor", tensor_bits)[1:]
    early_near = [swap(x, "tensor", 1) for x in early_far]
    out_pack.double()
    while len(fc_pack.bits) > 1:
        fc_pack.double()

    done = project_qkv(
        ids, info, sent, gain_attn, shift_attn, qkv_pack, qkv_rows, tables, width
    )
    done = tie_packs(fc_pack, out_pack, beside=[*done, *early_near, *late_far])
    (queries, keys, values), done = done[:3], done[3:]
    early_near, late_far = done[: groups // 2 - 1], done[groups // 2 - 1 :]
    late_near = [swap(x, "tensor", 1) for x in late_far]
    far = zip(zip(early_far, late_far), zip(early_near, late_near))
    grad = Tokens([(out_grad,), (near,), *[x for pair in far for x in pair]], order)
    while len(out_pack.bits) > 1:
        out_pack.double()
    (grad_context,) = tie_packs(out_pack, beside=[project_grad(ids, grad, dense_pack, width)])
    fc_pack.double()
    out_pack.double()
    done = attention(info, tables, queries, keys, values, grad_context)
    context, dq, dk, dv = tie_packs(fc_pack, out_pack, beside=done)
    dp_orders = [halving_order(near_bits), halving_order(next_bits)]
    qkv_orders = [halving_order(bits) for bits in qkv_bits]
    attn_parts = Parts(
        *project_context(ids, context, dense_pack, groups, model), "tensor", tensor_bits
    )
    attn_parts.begin()
    done = attention_weights(
        ids, info, tables, context, dq, dk, dv, sent, grad, gain_attn, shift_attn, qkv_orders
    )
    *done, attn_parts.other = tie_halves([*done, attn_parts.other], attn_parts)
    grads, qkv_bias_sums, *stacks = done
    attn_parts.middle()
    qkv_sums = [Halving(*stacks[:2], "dp", qkv_bits[0]), Halving(*stacks[2:], "dp", qkv_bits[1])]
    sent.arrays[0], attn_parts.send = tie(sent.arrays[0], attn_parts.send)
    attn_parts.swap()
    for parts in qkv_sums:
        parts.swap()
    done = mlp(
        ids, sent, grad, gain_mlp, shift_mlp, fc_pack, fc_rows, out_pack, dp_orders
    )
    done = tie_halves(done, attn_parts, *qkv_sums)
    *mlp_stacks, hidden, fc_bias_sums = done[:5]
    stacks = done[5:]
    attn_parts.add()
    mlp_parts = Parts(*mlp_stacks, "tensor", tensor_bits)
    mlp_sums = [Halving(*stacks[:2], "dp", near_bits), Halving(*stacks[2:], "dp", next_bits)]
    mlp_parts.begin()
    add_stacks(qkv_sums)
    mlp_parts.middle()
    hidden, mlp_parts.send = tie(hidden, mlp_parts.send)
    hidden, other = tie(hidden, mlp_parts.terms[1][0])
    mlp_parts.terms[1] = (other, 0)
    mlp_parts.swap()
    for parts in qkv_sums + mlp_sums:
        parts.swap()
    done = norm_backward(ids, sent, grads, hidden, gain_attn, gain_mlp, qkv_pack, fc_pack)
    done = tie_halves(done, mlp_parts, *qkv_sums, *mlp_sums)
    *back_stacks, norm_sums = done
    mlp_parts.add()

    back_parts = Parts(*back_stacks, "tensor", tensor_bits)
    back_parts.begin()
    add_stacks(qkv_sums + mlp_sums)
    back_parts.middle()

    stream_in, back_parts.send = tie(stream_in, back_parts.send)
    stream_in, other = tie(stream_in, back_parts.terms[1][0])
    back_parts.terms[1] = (other, 0)
    back_parts.swap()
    for parts in qkv_sums + mlp_sums:
        parts.swap()
    output, sums = finish_output(
        ids,
        stream_in,
        out_grad,
        attn_parts.terms,
        mlp_parts.terms,
        dense_bias[None, :],
        out_bias[None, :],
        norm_sums,
        fc_bias_sums,
        qkv_bias_sums,
        groups,
    )


    sums = sums + swap(sums, "tensor", 1)
    for bit in data_bits[3:]:
        sums = sums + swap(sums, "dp", bit)
    other, *_ = tie_halves([swap(sums, "dp", data_bits[2])], *mlp_sums, qkv_sums[1])
    sums = sums + other
    add_stacks(mlp_sums)
    sums, *sends = tie(sums, *[parts.send for parts in mlp_sums])
    for parts, send in zip(mlp_sums, sends):
        parts.send = send
    for bit in data_bits[:2]:
        sums = sums + swap(sums, "dp", bit)
    sums, back_parts.got = tie(sums, back_parts.got)
    back_parts.add()
    stream_grad = finish_grad(out_grad, stream_in, row_mean, inv_std, back_parts.terms)
    sums, stream_grad = tie(sums, stream_grad)
    for bit in tensor_bits[1:]:
        sums = sums + swap(sums, "tensor", bit)

    fc_weight_grad, out_weight_grad = finish_mlp_weights(*[x.finish() for x in mlp_sums])
    for parts in qkv_sums:
        parts.add()
    qkv_weight_grad, dense_weight_grad = finish_attention_weights(*[x.finish() for x in qkv_sums])

    count_all = float(rows_local * lax.axis_size("dp") * groups * model)
    gain_attn_grad, shift_attn_grad, gain_mlp_grad, shift_mlp_grad = (sums[x] for x in range(4))
    root_squares = jnp.sqrt(jnp.sum(sums[4:7], axis=1) / count_all)
    residual_grad = sums[7]
    fc_bias_grad = sums[8:12].reshape(-1)
    qkv_bias_grad = by_head(sums[12 : 12 + groups, :qkv_width], heads).reshape(-1)
    return (
        output,
        stream_grad,
        gain_attn_grad,
        shift_attn_grad,
        gain_mlp_grad,
        shift_mlp_grad,
        qkv_weight_grad,
        qkv_bias_grad,
        dense_weight_grad,
        residual_grad,
        fc_weight_grad,
        fc_bias_grad,
        out_weight_grad,
        residual_grad,
        root_squares,
    )


def solution(mesh):
    tokens, weights, rows, whole = (
        P(("dp", "tensor"), None),
        P("dp", "tensor"),
        P("tensor", "dp"),
        P(),
    )
    return jax.shard_map(
        local,
        mesh=mesh,
        in_specs=(
            tokens,
            P("dp"),
            P("dp"),
            whole,
            whole,
            whole,
            whole,
            weights,
            whole,
            rows,
            whole,
            weights,
            whole,
            rows,
            whole,
            tokens,
        ),
        out_specs=(
            tokens,
            tokens,
            whole,
            whole,
            whole,
            whole,
            weights,
            whole,
            rows,
            whole,
            weights,
            whole,
            rows,
            whole,
            whole,
        ),
        check_vma=False,
    )
```

```python
import jax
import jax.numpy as jnp
from jax import lax
from jax.experimental import pallas as pl
from jax.experimental.pallas import tpu as pltpu
from jax.sharding import PartitionSpec as P

HD = 64
ROT = 16
TRUNK = 1024
SEG = 128
TREE = 2560
NB = TREE // SEG
NT = TRUNK // SEG

f32 = jnp.float32
bf16 = jnp.bfloat16
eps_norm = 1e-05
masked_score = -1e30


def dot_nn(left, right):
    return lax.dot_general(left, right, (((1,), (0,)), ((), ())), preferred_element_type=f32)


def dot_nt(left, right):
    return lax.dot_general(left, right, (((1,), (1,)), ((), ())), preferred_element_type=f32)


def dot_tn(left, right):
    return lax.dot_general(left, right, (((0,), (0,)), ((), ())), preferred_element_type=f32)


def bits_of(size):
    bits = []
    bit = 1
    while bit < size:
        bits.append(bit)
        bit *= 2
    return bits


def swap(block, axis, bit):
    size = lax.axis_size(axis)
    return lax.ppermute(block, axis, [(i, i ^ bit) for i in range(size)])


def tie(*values):
    return lax.optimization_barrier(values)


def gather_far(block, axis, bits):
    pieces = [block]
    for bit in bits[1:]:
        pieces = pieces + [swap(piece, axis, bit) for piece in pieces]
    return pieces


class Pack:
    def __init__(self, block, axis, bits):
        self.rows, self.axis, self.bits = block.shape[0], axis, list(bits)
        self.arrays, self.owners = [block], [[0]]

    def double(self):
        bit = self.bits.pop(0)
        held = self.arrays[0] if len(self.arrays) == 1 else jnp.concatenate(self.arrays, axis=0)
        self.owners.append([j ^ bit for owners in self.owners for j in owners])
        self.arrays.append(swap(held, self.axis, bit))

    def specs(self):
        return [pl.BlockSpec(memory_space=pltpu.HBM)] * len(self.arrays)

    def pieces(self):
        return sum(len(owners) for owners in self.owners)

    def copies(self, refs, where, number, done):
        started = []
        for ref, owners in zip(refs, self.owners):
            for at, j in enumerate(owners):
                rows = pl.ds(pl.multiple_of((number ^ j) * self.rows, self.rows), self.rows)
                source = ref.at[pl.ds(at * self.rows, self.rows), :]
                copy = pltpu.make_async_copy(source, where.at[rows, :], done.at[len(started)])
                started.append(copy)
        return started


def tie_packs(*packs, beside=()):
    flat = tie(*beside, *[x for pack in packs for x in pack.arrays])
    at = len(beside)
    for pack in packs:
        pack.arrays = list(flat[at : at + len(pack.arrays)])
        at += len(pack.arrays)
    return list(flat[: len(beside)])


def halving_order(bits):
    if not bits:
        return [0]
    rest = halving_order(bits[1:])
    return [bits[0] ^ j for j in rest] + rest


class Halving:
    def __init__(self, send, keep, axis, bits):
        self.send, self.axis, self.bits = send, axis, list(bits)
        self.terms = [(keep, 0)]

    def swap(self):
        self.got = swap(self.send, self.axis, self.bits.pop(0))

    def add(self):
        self.terms.append((self.got, 0))
        half = self.got.shape[0] // 2
        if half:
            self.send = add_terms(self.terms, half)
            self.terms = [(x, at + half) for x, at in self.terms]

    def most(self):
        while len(self.bits) > 1:
            self.swap()
            self.add()

    def finish(self):
        while self.bits:
            self.swap()
            self.add()
        return self.terms


class Parts(Halving):
    def __init__(self, first, second, keep, axis, bits):
        super().__init__(first, keep, axis, bits)
        self.second = second

    def begin(self):
        bit = self.bits.pop(0)
        self.got, self.other = swap(self.send, self.axis, bit), swap(self.second, self.axis, bit)

    def middle(self):
        half = self.got.shape[0]
        self.send = add_terms([*self.terms, (self.got, 0)], half)
        self.terms = [(self.terms[0][0], half), (self.other, 0)]
        while len(self.bits) > 1:
            self.swap()
            self.add()


def tie_halves(values, *halvings):
    flat = tie(*values, *[x.got for x in halvings])
    for x, got in zip(halvings, flat[len(values) :]):
        x.got = got
    return flat[: len(values)]


def resident(shape):
    zeros = (0,) * len(shape)
    return pl.BlockSpec(shape, lambda *_: zeros, pipeline_mode=pl.Buffered(1))


def own_block(rows, columns):
    return pl.BlockSpec((rows, columns), lambda i, ids, *_: (ids[0] ^ ids[2 + i], 0))


def step_block(rows, columns):
    return pl.BlockSpec((rows, columns), lambda i, *_: (i, 0))


def part_shapes(groups, rows, columns):
    quarter = max(groups // 4, 1)
    return [shaped(n, rows, columns) for n in (quarter, quarter, groups - 2 * quarter)]


def part_blocks(groups, rows, columns):
    quarter = max(groups // 4, 1)
    shape = (pl.Squeezed(), rows, columns)
    return [
        pl.BlockSpec(shape, lambda i, *_: (jnp.minimum(i, quarter - 1), 0, 0)),
        pl.BlockSpec(shape, lambda i, *_: (jnp.clip(i - quarter, 0, quarter - 1), 0, 0)),
        pl.BlockSpec(shape, lambda i, *_: (jnp.maximum(i - 2 * quarter, 0), 0, 0)),
    ]


def store_part(stacks, value, step, groups):
    quarter = max(groups // 4, 1)
    turn_of = jnp.minimum(step // quarter, 2)
    for at, stack in enumerate(stacks):

        @pl.when(turn_of == at)
        def _(stack=stack):
            stack[...] = value


class Tokens:
    def __init__(self, blocks, order):
        blocks = [blocks[j] for j in order]
        self.groups, self.counts = len(blocks), [len(block) for block in blocks]
        self.rows, self.model = sum(x.shape[0] for x in blocks[0]), blocks[0][0].shape[1]
        self.arrays = [x for block in blocks for x in block]
        self.specs = [pl.BlockSpec(memory_space=pltpu.HBM)] * len(self.arrays)

    def scratch(self):
        return [
            pltpu.VMEM((2, self.rows, self.model), bf16),
            pltpu.SemaphoreType.DMA((2, max(self.counts))),
        ]

    def fetch(self, refs, held, done, step):
        def copies(at):
            first, start, found = sum(self.counts[:at]), 0, []
            for k, ref in enumerate(refs[first : first + self.counts[at]]):
                where = held.at[at % 2, pl.ds(start, ref.shape[0]), :]
                found.append(pltpu.make_async_copy(ref, where, done.at[at % 2, k]))
                start += ref.shape[0]
            return found

        for at in range(self.groups):

            @pl.when(step == at)
            def _(at=at):
                ahead = copies(at) if at == 0 else []
                if at + 1 < self.groups:
                    ahead = ahead + copies(at + 1)
                for copy in ahead:
                    copy.start()
                for copy in copies(at):
                    copy.wait()


def store_halves(send, keep, total, number, order, columns=slice(None), source=slice(None)):
    half, rows = send.shape[0], send.shape[1]
    for at, j in enumerate(order):
        where = send if at < half else keep
        block = total[pl.ds(pl.multiple_of((number ^ j) * rows, rows), rows), source]
        where[at % half, :, columns] = block.astype(bf16)


def call(
    kernel, name, grid, prefetch, operands, specs, outs, out_specs, scratch, flops, extra=0, room=12, light=False
):
    size = 0 if light else sum(x.size * x.dtype.itemsize for x in [*operands, *outs])
    return pl.pallas_call(
        kernel,
        grid_spec=pltpu.PrefetchScalarGridSpec(
            num_scalar_prefetch=len(prefetch),
            grid=grid,
            in_specs=specs,
            out_specs=out_specs,
            scratch_shapes=scratch,
        ),
        out_shape=outs,
        compiler_params=pltpu.CompilerParams(
            dimension_semantics=("arbitrary",) * len(grid), vmem_limit_bytes=room << 20
        ),
        cost_estimate=pl.CostEstimate(
            flops=int(flops), bytes_accessed=int(size), transcendentals=int(extra)
        ),
        name=name,
    )(*prefetch, *operands)


def shaped(*shape, dtype=bf16):
    return jax.ShapeDtypeStruct(shape, dtype)


def shift_gain(block, gain, shift):
    return (block.astype(f32) * gain[...] + shift[...]).astype(bf16)


def turn(block, cosine, sine, sign):
    width = block.shape[1]
    step = min(width, 128)
    lane = lax.broadcasted_iota(jnp.int32, (block.shape[0], step), 1) % HD
    done = []
    for start in range(0, width, step):
        part = block[:, start : start + step]
        if step == 128:
            left = pltpu.roll(part, step - ROT // 2, 1)
            right = pltpu.roll(part, ROT // 2, 1)
        else:
            left = jnp.concatenate([part[:, ROT // 2 :], part[:, : ROT // 2]], axis=1)
            right = jnp.concatenate([part[:, -ROT // 2 :], part[:, : -ROT // 2]], axis=1)
        moved = jnp.where(lane < ROT // 2, -left, right) * sine[:, :step]
        done.append(part * cosine[:, :step] + moved * sign)
    return done[0] if len(done) == 1 else jnp.concatenate(done, axis=1)


def weight_scratch(pack):
    model = pack.rows * pack.pieces()
    columns = pack.arrays[0].shape[1]
    return [pltpu.VMEM((model, columns), bf16), pltpu.SemaphoreType.DMA((pack.pieces(),))]


def prepare_weights(qkv, dense, fc, out):
    rows, columns = qkv.shape
    width = columns // 3

    def kernel(qkv_ref, dense_ref, fc_ref, out_ref, qkv_to, dense_to, fc_to, out_to):
        for head in range(width // HD):
            for kind in range(3):
                at, own = (3 * head + kind) * HD, kind * width + head * HD
                qkv_to[:, own : own + HD] = qkv_ref[:, at : at + HD].astype(bf16)
        dense_to[...] = dense_ref[...].T.astype(bf16)
        fc_to[...] = fc_ref[...].astype(bf16)
        out_to[...] = out_ref[...].T.astype(bf16)

    operands = [qkv, dense, fc, out]
    outs = [shaped(*qkv.shape), shaped(*dense.shape[::-1]), shaped(*fc.shape), shaped(*out.shape[::-1])]
    return call(
        kernel,
        "prepare_weights",
        (1,),
        [],
        operands,
        [resident(x.shape) for x in operands],
        outs,
        [resident(x.shape) for x in outs],
        [],
        rows * columns,
        room=62,
    )


def normalize(stream):
    rows, model = stream.shape
    block = 160

    def kernel(stream_ref, sent_ref, mean_ref, std_ref):
        field = stream_ref[...]
        mean = jnp.sum(field, axis=1, keepdims=True) / model
        centred = field - mean
        variance = jnp.sum(centred * centred, axis=1, keepdims=True) / model
        scale = lax.rsqrt(variance + eps_norm)
        sent_ref[...] = (centred * scale).astype(bf16)
        mean_ref[...] = mean
        std_ref[...] = scale

    return call(
        kernel,
        "normalize",
        (rows // block,),
        [],
        [stream],
        [step_block(block, model)],
        [shaped(rows, model), shaped(rows, 1, dtype=f32), shaped(rows, 1, dtype=f32)],
        [step_block(block, model), step_block(block, 1), step_block(block, 1)],
        [],
        rows * model * 8,
        room=62,
    )


def project_qkv(ids, info, sent, gain, shift, pack, bias, tables, width):
    groups, held, rows, model = sent.groups, len(sent.arrays), sent.rows, sent.model

    def kernel(ids, info, *refs):
        sent_refs, refs = refs[:held], refs[held:]
        weight_refs, refs = refs[: len(pack.arrays)], refs[len(pack.arrays) :]
        gain, shift, bias, cos, sine, q_out, k_out, v_out = refs[:8]
        block, arrived, whole, placed, added = refs[8:]
        step = pl.program_id(0)

        @pl.when(step == 0)
        def _():
            for copy in pack.copies(weight_refs, whole, ids[1], placed):
                copy.start()

        sent.fetch(sent_refs, block, arrived, step)

        @pl.when(step == 0)
        def _():
            for copy in pack.copies(weight_refs, whole, ids[1], placed):
                copy.wait()
            own = bias[pl.ds(ids[0], 1), :]
            for head in range(width // HD):
                for kind in range(3):
                    at, to = (3 * head + kind) * HD, kind * width + head * HD
                    added[:, to : to + HD] = own[:, at : at + HD]

        token = block[step % 2]
        normed = shift_gain(token, gain, shift)
        blocks = rows // SEG
        cut = (blocks + 1) // 2
        both = [dot_nn(normed[x], whole[...]) + added[...] for x in (slice(0, cut * SEG), slice(cut * SEG, rows))]
        first = (ids[0] ^ ids[2 + step]) * blocks
        for at in range(blocks):
            number = first + at
            table = pl.ds(pl.multiple_of(info[number // NB, number % NB, 4] * SEG, SEG), SEG)
            tabs = (cos[table, :], sine[table, :])
            own = slice(at * SEG, (at + 1) * SEG)
            here = at * SEG if at < cut else (at - cut) * SEG
            qkv = both[at >= cut][here : here + SEG]
            q_out[own, :] = (turn(qkv[:, :width], *tabs, 1.0) * HD**-0.5).astype(bf16)
            k_out[own, :] = turn(qkv[:, width : 2 * width], *tabs, 1.0).astype(bf16)
            v_out[own, :] = qkv[:, 2 * width :].astype(bf16)

    operands = [*sent.arrays, *pack.arrays, gain, shift, bias, *tables]
    out = shaped(groups * rows, width)
    return call(
        kernel,
        "project_qkv",
        (groups,),
        [ids, info],
        operands,
        sent.specs
        + pack.specs()
        + [resident(x.shape) for x in operands[held + len(pack.arrays) :]],
        [out] * 3,
        [own_block(rows, width)] * 3,
        sent.scratch() + weight_scratch(pack) + [pltpu.VMEM((1, 3 * width), f32)],
        2 * groups * rows * model * 3 * width,
        room=62,
    )


def project_grad(ids, grad, pack, width):
    groups, held, rows, model = grad.groups, len(grad.arrays), grad.rows, grad.model

    def kernel(ids, *refs):
        grad_refs, refs = refs[:held], refs[held:]
        weight_refs, (out, block, arrived, whole, placed) = refs[:-5], refs[-5:]
        step = pl.program_id(0)

        @pl.when(step == 0)
        def _():
            for copy in pack.copies(weight_refs, whole, ids[1], placed):
                copy.start()

        grad.fetch(grad_refs, block, arrived, step)

        @pl.when(step == 0)
        def _():
            for copy in pack.copies(weight_refs, whole, ids[1], placed):
                copy.wait()

        out[...] = dot_nn(block[step % 2], whole[...]).astype(bf16)

    operands = [*grad.arrays, *pack.arrays]
    return call(
        kernel,
        "project_grad",
        (groups,),
        [ids],
        operands,
        grad.specs + pack.specs(),
        [shaped(groups * rows, width)],
        [own_block(rows, width)],
        grad.scratch() + weight_scratch(pack),
        2 * groups * rows * model * width,
    )[0]


def attention_kernel(
    info, q_ref, do_ref, k_ref, v_ref, cos, sine, ctx_ref, dq_ref, dk_ref, dv_ref, dk_sum, dv_sum
):
    tree, step = pl.program_id(0), pl.program_id(1)
    width = q_ref.shape[1]
    heads = width // HD
    lane_head = lax.broadcasted_iota(jnp.int32, (SEG, width), 1) // HD

    @pl.when(step == 0)
    def _():
        dk_sum[...] = jnp.zeros_like(dk_sum)
        dv_sum[...] = jnp.zeros_like(dv_sum)

    first, second = info[tree, step, 0], info[tree, step, 1]
    first_rows = pl.ds(pl.multiple_of(first * SEG, SEG), SEG)
    second_rows = pl.ds(pl.multiple_of(second * SEG, SEG), SEG)
    queries, grads = q_ref[...], do_ref[...]
    zero = jnp.zeros_like(queries)
    q_rows = jnp.concatenate([jnp.where(lane_head == h, queries, zero) for h in range(heads)], axis=0)
    g_rows = jnp.concatenate([jnp.where(lane_head == h, grads, zero) for h in range(heads)], axis=0)
    q_turned, g_turned = queries.T, grads.T
    ahead = lax.broadcasted_iota(jnp.int32, (SEG, SEG), 1) - lax.broadcasted_iota(
        jnp.int32, (SEG, SEG), 0
    )
    seen = jnp.concatenate([ahead <= info[tree, step, 2], ahead <= info[tree, step, 3]], axis=1)
    seen = jnp.concatenate([seen] * heads, axis=0)
    k_near = jnp.concatenate([k_ref[first_rows, :], k_ref[second_rows, :]], axis=0)
    v_near = jnp.concatenate([v_ref[first_rows, :], v_ref[second_rows, :]], axis=0)

    def work(pairs):
        count = pairs * 2 * SEG
        near = jnp.where(seen, dot_nt(q_rows, k_near), masked_score)
        most = jnp.max(near, axis=1, keepdims=True)
        if count:
            k_far, v_far = k_ref[0:count, :], v_ref[0:count, :]
            far = dot_nt(q_rows, k_far)
            most = jnp.maximum(most, jnp.max(far, axis=1, keepdims=True))
        near = jnp.exp(near - most)
        total = jnp.sum(near, axis=1, keepdims=True)
        if count:
            far = jnp.exp(far - most)
            total = total + jnp.sum(far, axis=1, keepdims=True)
        scale = 1.0 / total
        near = near * scale
        near_low = near.astype(bf16)
        context = dot_nn(near_low, v_near)
        if count:
            far = far * scale
            far_low = far.astype(bf16)
            context = context + dot_nn(far_low, v_far)
        delta = jnp.sum(context * g_rows.astype(f32), axis=1, keepdims=True)
        near = (near * (dot_nt(g_rows, v_near) - delta)).astype(bf16)
        dq = dot_nn(near, k_near)
        if count:
            far = (far * (dot_nt(g_rows, v_far) - delta)).astype(bf16)
            dq = dq + dot_nn(far, k_far)
        ctx_own, dq_own = context[0:SEG], dq[0:SEG]
        for h in range(1, heads):
            ctx_own = jnp.where(lane_head == h, context[h * SEG : (h + 1) * SEG], ctx_own)
            dq_own = jnp.where(lane_head == h, dq[h * SEG : (h + 1) * SEG], dq_own)
        ctx_ref[...] = ctx_own.astype(bf16)
        dq_ref[...] = turn(dq_own * HD**-0.5, cos, sine, -1.0).astype(bf16)
        for h in range(heads):
            own = slice(h * SEG, (h + 1) * SEG)
            part = slice(h * HD, (h + 1) * HD)
            dk = dot_nn(q_turned[part], near[own])
            dv = dot_nn(g_turned[part], near_low[own])
            dk_sum[first, part, :] += dk[:, :SEG]
            dv_sum[first, part, :] += dv[:, :SEG]
            dk_sum[second, part, :] += dk[:, SEG:]
            dv_sum[second, part, :] += dv[:, SEG:]
            if count:
                dk = dot_nn(q_turned[part], far[own])
                dv = dot_nn(g_turned[part], far_low[own])
                for j in range(2 * pairs):
                    dk_sum[j, part, :] += dk[:, j * SEG : (j + 1) * SEG]
                    dv_sum[j, part, :] += dv[:, j * SEG : (j + 1) * SEG]

    for pairs in range(NT // 2):

        @pl.when(step // 2 == pairs)
        def _(pairs=pairs):
            work(pairs)

    @pl.when(step >= NT)
    def _():
        work(NT // 2)

    @pl.when(step == NB - 1)
    def _():
        def finish(j, carry):
            rows = pl.ds(pl.multiple_of(j * SEG, SEG), SEG)
            dv_ref[rows, :] = dv_sum[j].T.astype(bf16)
            dk_ref[rows, :] = dk_sum[j].T.astype(bf16)
            return carry

        lax.fori_loop(0, NB, finish, 0)


def attention(info, tables, queries, keys, values, grads):
    total, width = queries.shape
    trees = total // TREE
    table_width = tables[0].shape[1]
    block = pl.BlockSpec((SEG, width), lambda t, b, info: (t * NB + b, 0))
    whole = pl.BlockSpec((TREE, width), lambda t, b, info: (t, 0))
    table = pl.BlockSpec((SEG, table_width), lambda t, b, info: (info[t, b, 4], 0))
    scores = trees * (TREE - TRUNK) * (TRUNK + 2 * SEG) * (width // HD)
    return call(
        attention_kernel,
        "attention",
        (trees, NB),
        [info],
        [queries, grads, keys, values, *tables],
        [block, block, whole, whole, table, table],
        [shaped(total, width)] * 4,
        [block, block, whole, whole],
        [pltpu.VMEM((NB, width, SEG), f32), pltpu.VMEM((NB, width, SEG), f32)],
        scores * width * 2 * 6 * 1.3,
        scores,
        room=22,
    )


def project_context(ids, context, pack, groups, model):
    rows, width = context.shape[0] // groups, context.shape[1]

    def kernel(ids, ctx, *refs):
        weight_refs, stacks, (whole, placed) = refs[:-5], refs[-5:-2], refs[-2:]
        step = pl.program_id(0)

        @pl.when(step == 0)
        def _():
            copies = pack.copies(weight_refs, whole, ids[1], placed)
            for copy in copies:
                copy.start()
            for copy in copies:
                copy.wait()

        store_part(stacks, dot_nt(ctx[...], whole[...]).astype(bf16), step, groups)

    operands = [context, *pack.arrays]
    return call(
        kernel,
        "project_context",
        (groups,),
        [ids],
        operands,
        [own_block(rows, width)] + pack.specs(),
        part_shapes(groups, rows, model),
        part_blocks(groups, rows, model),
        weight_scratch(pack),
        2 * groups * rows * model * width,
        room=14,
    )


def attention_weights(ids, info, tables, context, dq, dk, dv, sent, grad, gain, shift, orders):
    groups, held, rows, model = sent.groups, len(sent.arrays), sent.rows, sent.model
    width, count = dq.shape[1], len(orders[0])

    def kernel(ids, info, ctx_ref, dq_ref, dk_ref, dv_ref, *refs):
        sent_refs, refs = refs[:held], refs[held:]
        grad_refs, refs = refs[: len(grad.arrays)], refs[len(grad.arrays) :]
        gain, shift, cos, sine, grads, bias_ref, *stacks = refs[:10]
        block, arrived, grad_block, grad_arrived, total, dense_total = refs[10:]
        step = pl.program_id(0)

        @pl.when(step == 0)
        def _():
            total[...] = jnp.zeros_like(total)
            dense_total[...] = jnp.zeros_like(dense_total)
            bias_ref[...] = jnp.zeros_like(bias_ref)

        sent.fetch(sent_refs, block, arrived, step)
        grad.fetch(grad_refs, grad_block, grad_arrived, step)
        grads[:, :width] = dq_ref[...]
        first = (ids[0] ^ ids[2 + step]) * (rows // SEG)
        for at in range(rows // SEG):
            number = first + at
            table = pl.ds(pl.multiple_of(info[number // NB, number % NB, 4] * SEG, SEG), SEG)
            own = slice(at * SEG, (at + 1) * SEG)
            turned = turn(dk_ref[own, :], cos[table, :], sine[table, :], -1.0)
            grads[own, width : 2 * width] = turned.astype(bf16)
        grads[:, 2 * width :] = dv_ref[...]
        bias_ref[0:1, :] += jnp.sum(grads[...].astype(f32), axis=0, keepdims=True)
        total[...] += dot_tn(shift_gain(block[step % 2], gain, shift), grads[...])
        dense_total[...] += dot_tn(grad_block[step % 2], ctx_ref[...])

        @pl.when(step == groups - 1)
        def _():
            store_halves(*stacks[:2], total, ids[1], orders[0], source=slice(0, 2 * width))
            source = slice(2 * width, 3 * width)
            store_halves(*stacks[2:], total, ids[1], orders[1], slice(0, width), source)
            columns = slice(width, 2 * width)
            store_halves(*stacks[2:], dense_total, ids[1], orders[1], columns)

    operands = [context, dq, dk, dv, *sent.arrays, *grad.arrays, gain, shift, *tables]
    outs = [shaped(groups * rows, 3 * width), shaped(8, 3 * width, dtype=f32)]
    outs += [shaped(count // 2, model // count, 2 * width)] * 4
    return call(
        kernel,
        "attention_weights",
        (groups,),
        [ids, info],
        operands,
        [own_block(rows, width)] * 4
        + sent.specs
        + grad.specs
        + [resident(x.shape) for x in operands[-4:]],
        outs,
        [step_block(rows, 3 * width)] + [resident(x.shape) for x in outs[1:]],
        sent.scratch()
        + grad.scratch()
        + [pltpu.VMEM((model, 3 * width), f32), pltpu.VMEM((model, width), f32)],
        2 * groups * rows * model * 4 * width,
        room=24,
    )


def mlp(ids, sent, grad, gain, shift, fc, bias, out, orders):
    groups, held, rows, model = sent.groups, len(sent.arrays), sent.rows, sent.model
    pieces, units = len(fc.arrays), fc.arrays[0].shape[1]

    def kernel(ids, *refs):
        sent_refs, refs = refs[:held], refs[held:]
        grad_refs, refs = refs[: len(grad.arrays)], refs[len(grad.arrays) :]
        fc_refs, refs = refs[:pieces], refs[pieces:]
        out_refs, refs = refs[:pieces], refs[pieces:]
        gain, shift, bias, *parts_out = refs[:6]
        hidden_ref, bias_ref = refs[6:8]
        stacks, refs = refs[8:12], refs[12:]
        block, arrived, grad_block, grad_arrived, fc_whole, fc_placed, out_whole, out_placed = refs[:8]
        act_ref, fc_total, out_total = refs[8:]
        step = pl.program_id(0)

        def weights():
            copies = fc.copies(fc_refs, fc_whole, ids[1], fc_placed)
            return copies + out.copies(out_refs, out_whole, ids[1], out_placed)

        @pl.when(step == 0)
        def _():
            for copy in weights():
                copy.start()
            fc_total[...] = jnp.zeros_like(fc_total)
            out_total[...] = jnp.zeros_like(out_total)
            bias_ref[...] = jnp.zeros_like(bias_ref)

        sent.fetch(sent_refs, block, arrived, step)
        grad.fetch(grad_refs, grad_block, grad_arrived, step)

        @pl.when(step == 0)
        def _():
            for copy in weights():
                copy.wait()

        token, grads = block[step % 2], grad_block[step % 2]
        normed = shift_gain(token, gain, shift)
        count = 1
        parts = [slice(k * rows // count, (k + 1) * rows // count) for k in range(count)]
        added = bias[pl.ds(ids[0], 1), :]
        hidden = [dot_nn(normed[x], fc_whole[...]) + added for x in parts]
        back = [dot_nn(grads[x], out_whole[...]) for x in parts]
        for x, field, slope in zip(parts, hidden, back):
            chance = 0.5 + 0.5 * lax.erf(field * 0.7071067811865476)
            bell = jnp.exp(field * field * -0.5) * 0.3989422804014327
            act_ref[x, :] = (field * chance).astype(bf16)
            low = (slope * (chance + field * bell)).astype(bf16)
            hidden_ref[x, :] = low
            bias_ref[0:1, :] += jnp.sum(low.astype(f32), axis=0, keepdims=True)
        store_part(parts_out, dot_nt(act_ref[...], out_whole[...]).astype(bf16), step, groups)
        out_total[...] += dot_tn(grads, act_ref[...])
        fc_total[...] += dot_tn(normed, hidden_ref[...])

        @pl.when(step == groups - 1)
        def _():
            half = units // 2
            for at, order in enumerate(orders):
                stack = stacks[2 * at : 2 * at + 2]
                source = slice(at * half, (at + 1) * half)
                store_halves(*stack, fc_total, ids[1], order, slice(0, half), source)
                store_halves(*stack, out_total, ids[1], order, slice(half, units), source)

    operands = [*sent.arrays, *grad.arrays, *fc.arrays, *out.arrays, gain, shift, bias]
    count = model // fc.rows
    outs = part_shapes(groups, rows, model)
    outs += [shaped(groups * rows, units), shaped(8, units, dtype=f32)]
    outs += [shaped(count // 2, fc.rows, units)] * 4
    return call(
        kernel,
        "mlp",
        (groups,),
        [ids],
        operands,
        sent.specs
        + grad.specs
        + fc.specs()
        + out.specs()
        + [resident(x.shape) for x in operands[-3:]],
        outs,
        part_blocks(groups, rows, model)
        + [step_block(rows, units)]
        + [resident(x.shape) for x in outs[4:]],
        sent.scratch()
        + grad.scratch()
        + weight_scratch(fc)
        + weight_scratch(out)
        + [
            pltpu.VMEM((rows, units), bf16),
            pltpu.VMEM((model, units), f32),
            pltpu.VMEM((model, units), f32),
        ],
        10 * groups * rows * model * units,
        room=42,
    )


def norm_backward(ids, sent, grads, hidden, gain_attn, gain_mlp, qkv_pack, fc):
    groups, held, rows, model = sent.groups, len(sent.arrays), sent.rows, sent.model
    pieces, units, columns = len(fc.arrays), hidden.shape[1], grads.shape[1]

    def kernel(ids, grads_ref, hidden_ref, *refs):
        sent_refs, refs = refs[:held], refs[held:]
        qkv_refs, refs = refs[:pieces], refs[pieces:]
        fc_refs, refs = refs[:pieces], refs[pieces:]
        gain_attn, gain_mlp, *stacks = refs[:5]
        sums_ref, block, arrived, qkv_whole, qkv_placed, fc_whole, fc_placed = refs[5:]
        step = pl.program_id(0)

        def weights():
            copies = qkv_pack.copies(qkv_refs, qkv_whole, ids[1], qkv_placed)
            return copies + fc.copies(fc_refs, fc_whole, ids[1], fc_placed)

        @pl.when(step == 0)
        def _():
            for copy in weights():
                copy.start()
            sums_ref[...] = jnp.zeros_like(sums_ref)

        sent.fetch(sent_refs, block, arrived, step)

        @pl.when(step == 0)
        def _():
            for copy in weights():
                copy.wait()

        back_attn = dot_nt(grads_ref[...], qkv_whole[...])
        back_mlp = dot_nt(hidden_ref[...], fc_whole[...])
        token = block[step % 2].astype(f32)
        for at, back in enumerate((back_attn, back_mlp)):
            sums_ref[2 * at : 2 * at + 1, :] += jnp.sum(back * token, axis=0, keepdims=True)
            sums_ref[2 * at + 1 : 2 * at + 2, :] += jnp.sum(back, axis=0, keepdims=True)
        part = back_attn * gain_attn[...] + back_mlp * gain_mlp[...]
        store_part(stacks, part.astype(bf16), step, groups)

    operands = [grads, hidden, *sent.arrays, *qkv_pack.arrays, *fc.arrays, gain_attn, gain_mlp]
    outs = part_shapes(groups, rows, model) + [shaped(8, model, dtype=f32)]
    return call(
        kernel,
        "norm_backward",
        (groups,),
        [ids],
        operands,
        [step_block(rows, columns), step_block(rows, units)]
        + sent.specs
        + qkv_pack.specs()
        + fc.specs()
        + [resident(x.shape) for x in operands[-2:]],
        outs,
        part_blocks(groups, rows, model) + [resident(x.shape) for x in outs[3:]],
        sent.scratch() + weight_scratch(qkv_pack) + weight_scratch(fc),
        2 * groups * rows * model * (units + columns),
        room=26,
    )


def taken(terms, block):
    return [
        pl.BlockSpec((pl.Squeezed(), block, x.shape[2]), lambda i, *_, at=at: (at, i, 0))
        for x, at in terms
    ]


def add_terms(terms, half):
    _, rows, columns = terms[0][0].shape
    block = max(x for x in (320, 128, 64) if rows % x == 0)

    def kernel(*refs):
        refs[-1][...] = sum(x[...].astype(f32) for x in refs[:-1]).astype(bf16)

    shape = (pl.Squeezed(), block, columns)
    out = shaped(half, rows, columns)
    return call(
        kernel,
        "add_terms",
        (half, rows // block),
        [],
        [x for x, _ in terms],
        [pl.BlockSpec(shape, lambda k, i, *_, at=at: (at + k, i, 0)) for _, at in terms],
        [out],
        [pl.BlockSpec(shape, lambda k, i, *_: (k, i, 0))],
        [],
        half * rows * columns * len(terms),
    )[0]


def whole_terms(terms, count):
    return [
        pl.BlockSpec((count, *x.shape[1:]), lambda *_, at=at: (at // count, 0, 0)) for x, at in terms
    ]


def add_stacks(stacks):
    counts = []
    for parts in stacks:
        parts.terms.append((parts.got, 0))
        counts.append(parts.got.shape[0] // 2)
    held = [len(parts.terms) for parts in stacks]
    operands = [x for parts in stacks for x, _ in parts.terms]

    def kernel(*refs):
        for at, half in enumerate(counts):
            first = sum(held[:at])
            total = sum(x[...].astype(f32) for x in refs[first : first + held[at]])
            refs[len(operands) + at][...] = total.astype(bf16)

    outs = [shaped(n, *parts.got.shape[1:]) for n, parts in zip(counts, stacks)]
    sends = call(
        kernel,
        "add_stacks",
        (1,),
        [],
        operands,
        [x for n, parts in zip(counts, stacks) for x in whole_terms(parts.terms, n)],
        outs,
        [resident(x.shape) for x in outs],
        [],
        sum(x.size for x in operands) // 2,
        room=16,
    )
    for n, parts, send in zip(counts, stacks, sends):
        parts.send = send
        parts.terms = [(x, at + n) for x, at in parts.terms]


def finish_mlp_weights(first, second):
    held, (_, rows, units) = len(first), first[0][0].shape
    half = units // 2

    def kernel(*refs):
        low = sum(x[0].astype(f32) for x in refs[:held])
        high = sum(x[0].astype(f32) for x in refs[held:-2])
        refs[-2][:, :half] = low[:, :half]
        refs[-2][:, half:] = high[:, :half]
        refs[-1][:half, :] = low[:, half:].T
        refs[-1][half:, :] = high[:, half:].T

    operands = [x for x, _ in [*first, *second]]
    outs = [shaped(rows, units, dtype=f32), shaped(units, rows, dtype=f32)]
    return call(
        kernel,
        "finish_mlp_weights",
        (1,),
        [],
        operands,
        whole_terms([*first, *second], 1),
        outs,
        [resident(x.shape) for x in outs],
        [],
        len(operands) * rows * units,
    )


def finish_attention_weights(first, second):
    held, (_, rows, columns) = len(first), first[0][0].shape
    width = columns // 2

    def kernel(*refs):
        low = sum(x[0].astype(f32) for x in refs[:held])
        high = sum(x[0].astype(f32) for x in refs[held:-2])
        for head in range(width // HD):
            for kind, (source, start) in enumerate(((low, 0), (low, width), (high, 0))):
                at = (3 * head + kind) * HD
                own = start + head * HD
                refs[-2][:, at : at + HD] = source[:, own : own + HD]
        refs[-1][...] = high[:, width:].T

    operands = [x for x, _ in [*first, *second]]
    outs = [shaped(rows, 3 * width, dtype=f32), shaped(width, rows, dtype=f32)]
    return call(
        kernel,
        "finish_attention_weights",
        (1,),
        [],
        operands,
        whole_terms([*first, *second], 1),
        outs,
        [resident(x.shape) for x in outs],
        [],
        len(operands) * rows * columns,
    )


def sum_rows(groups):
    return (12 + groups + 7) // 8 * 8


def finish_output(ids, stream, grad, attn_terms, mlp_terms, dense_bias, out_bias, norm_sums, fc_sums, qkv_sums, groups):
    rows, model = stream.shape
    block = 160
    first, second = len(attn_terms), len(mlp_terms)
    units, columns = fc_sums.shape[1], qkv_sums.shape[1]
    across = model // units

    def kernel(ids, stream_ref, grad_ref, *refs):
        attn_refs, refs = refs[:first], refs[first:]
        mlp_refs, refs = refs[:second], refs[second:]
        dense_bias, out_bias, norm_ref, fc_ref, qkv_ref, out_ref, sums_ref = refs

        @pl.when(pl.program_id(0) == 0)
        def _():
            sums_ref[...] = jnp.zeros_like(sums_ref)
            sums_ref[0:4, :] = norm_ref[0:4, :]
            own = jnp.concatenate([fc_ref[0:1, :]] * across, axis=1) if across > 1 else fc_ref[0:1, :]
            lane = lax.broadcasted_iota(jnp.int32, (1, model), 1) // units
            sums_ref[pl.ds(8 + ids[0] // across, 1), :] = jnp.where(lane == ids[0] % across, own, 0.0)
            sums_ref[pl.ds(12 + ids[0], 1), :columns] = qkv_ref[0:1, :]

        attn = sum(x[...].astype(f32) for x in attn_refs) + dense_bias[...]
        mlp = sum(x[...].astype(f32) for x in mlp_refs) + out_bias[...]
        output = stream_ref[...] + attn + mlp
        out_ref[...] = output
        for at, value in enumerate((output, attn, mlp)):
            sums_ref[4 + at : 5 + at, :] += jnp.sum(value * value, axis=0, keepdims=True)
        sums_ref[7:8, :] += jnp.sum(grad_ref[...].astype(f32), axis=0, keepdims=True)

    terms = [*attn_terms, *mlp_terms]
    operands = [stream, grad, *[x for x, _ in terms], dense_bias, out_bias, norm_sums, fc_sums, qkv_sums]
    outs = [shaped(rows, model, dtype=f32), shaped(sum_rows(groups), model, dtype=f32)]
    return call(
        kernel,
        "finish_output",
        (rows // block,),
        [ids],
        operands,
        [step_block(block, model), step_block(block, model)]
        + taken(terms, block)
        + [resident(x.shape) for x in operands[-5:]],
        outs,
        [step_block(block, model), resident(outs[1].shape)],
        [],
        rows * model * 16,
        room=16,
    )


def finish_grad(grad, stream, row_mean, inv_std, terms):
    rows, model = grad.shape
    block = 160

    def kernel(grad_ref, stream_ref, mean_ref, std_ref, *refs):
        term_refs, out_ref = refs[:-1], refs[-1]
        sent = sum(x[...].astype(f32) for x in term_refs)
        norm = (stream_ref[...] - mean_ref[...]) * std_ref[...]
        mean = jnp.sum(sent, axis=1, keepdims=True) / model
        cross = jnp.sum(sent * norm, axis=1, keepdims=True) / model
        out_ref[...] = grad_ref[...].astype(f32) + std_ref[...] * (sent - mean - norm * cross)

    operands = [grad, stream, row_mean, inv_std, *[x for x, _ in terms]]
    return call(
        kernel,
        "finish_grad",
        (rows // block,),
        [],
        operands,
        [step_block(block, model)] * 2
        + [step_block(block, 1)] * 2
        + taken(terms, block),
        [shaped(rows, model, dtype=f32)],
        [step_block(block, model)],
        [],
        0,
        light=True,
    )[0]


def tree_table(segment_ids, parent_ids):
    trees = segment_ids.shape[0] // TREE

    def kernel(segment, parent, table):
        for tree in range(trees):
            for block in range(NT):
                odd = block % 2
                row = (block - odd, block - odd + 1, SEG * odd, -SEG * (1 - odd), block)
                for at, value in enumerate(row):
                    table[tree, block, at] = value

            def place(block, carry):
                first = tree * TREE
                owner = parent[first + block * SEG]
                leaf = (owner != segment[first]).astype(jnp.int32)
                at = block
                for other in range(NT, NB):
                    at = jnp.where(segment[first + other * SEG] == owner, other, at)
                table[tree, block, 0] = block
                table[tree, block, 1] = at
                table[tree, block, 2] = 0
                table[tree, block, 3] = SEG * (2 * leaf - 1)
                table[tree, block, 4] = NT + leaf
                return carry

            lax.fori_loop(NT, NB, place, 0)

    smem = pl.BlockSpec(memory_space=pltpu.SMEM)
    return pl.pallas_call(
        kernel,
        in_specs=[smem, smem],
        out_specs=smem,
        out_shape=jax.ShapeDtypeStruct((trees, NB, 5), jnp.int32),
        name="tree_table",
    )(segment_ids, parent_ids)


def angle_tables(zero):
    places = TRUNK + 2 * SEG
    place = lax.broadcasted_iota(jnp.int32, (places, 2 * HD), 0).astype(f32)
    lane = lax.broadcasted_iota(jnp.int32, (places, 2 * HD), 1) % HD
    half = ROT // 2
    frequency = 10000.0 ** (-((lane % half).astype(f32) * 2.0 / ROT))
    angle = (place + zero) * frequency
    cosine = jnp.where(lane < ROT, jnp.cos(angle), 1.0)
    sine = jnp.where(lane < ROT, jnp.sin(angle), 0.0)
    return cosine, sine


def by_kind(array, heads):
    shape = array.shape[:-1]
    array = array.reshape(*shape, heads, 3, HD)
    return jnp.swapaxes(array, -3, -2).reshape(*shape, 3 * heads * HD)


def by_head(array, heads):
    shape = array.shape[:-1]
    array = array.reshape(*shape, 3, heads, HD)
    return jnp.swapaxes(array, -3, -2).reshape(*shape, 3 * heads * HD)


def local(
    stream_in,
    segment_ids,
    parent_ids,
    norm_gain_attn,
    norm_shift_attn,
    norm_gain_mlp,
    norm_shift_mlp,
    qkv_weight,
    qkv_bias,
    dense_weight,
    dense_bias,
    fc_weight,
    fc_bias,
    out_weight,
    out_bias,
    out_grad,
):
    tensor_rank = lax.axis_index("tensor")
    data_rank = lax.axis_index("dp")
    rows_local = stream_in.shape[0]
    model = stream_in.shape[1]
    qkv_width = qkv_weight.shape[1]
    heads = qkv_width // (3 * HD)
    width = heads * HD
    units = fc_weight.shape[1]
    groups = lax.axis_size("tensor")
    tensor_bits = bits_of(groups)
    far_first = tensor_bits[:0:-1] + tensor_bits[:1]
    order = halving_order(tensor_bits)
    ids = jnp.stack([tensor_rank, data_rank, *order]).astype(jnp.int32)
    data_bits = bits_of(lax.axis_size("dp"))
    rows_first = data_bits[:0:-1] + data_bits[:1]
    columns_first = data_bits[:1] + data_bits[:0:-1]
    near_bits = data_bits
    next_bits = data_bits[1:2] + data_bits[:1] + data_bits[2:]
    qkv_bits = [data_bits[:1] + data_bits[:0:-1], next_bits]

    blocks = prepare_weights(qkv_weight, dense_weight, fc_weight, out_weight)
    qkv_pack = Pack(blocks[0], "dp", rows_first)
    dense_pack = Pack(blocks[1], "dp", columns_first)
    fc_pack = Pack(blocks[2], "dp", rows_first)
    out_pack = Pack(blocks[3], "dp", rows_first)

    sent_norm, row_mean, inv_std = normalize(stream_in)
    sent = gather_far(sent_norm, "tensor", tensor_bits)

    info = tree_table(segment_ids, parent_ids)
    gain_attn, shift_attn = norm_gain_attn[None, :], norm_shift_attn[None, :]
    gain_mlp, shift_mlp = norm_gain_mlp[None, :], norm_shift_mlp[None, :]
    sent_near, near = swap(sent[0], "tensor", 1), swap(out_grad, "tensor", 1)
    cut = rows_local * 3 // 5
    early, late = out_grad[:cut], out_grad[cut:]
    qkv_pack.double()
    dense_pack.double()
    zero = jnp.zeros((), f32)
    near, early, late, zero, qkv_bias, fc_bias, info = tie_packs(
        qkv_pack, dense_pack, fc_pack, beside=[near, early, late, zero, qkv_bias, fc_bias, info]
    )
    tables = angle_tables(zero)
    qkv_rows, fc_rows = qkv_bias.reshape(groups, qkv_width), fc_bias.reshape(groups, units)
    while len(qkv_pack.bits) > 1:
        qkv_pack.double()
        dense_pack.double()
    fc_pack.double()
    done = tie_packs(
        qkv_pack,
        dense_pack,
        out_pack,
        beside=[early, late, *tables, qkv_rows, fc_rows, sent_near, *sent],
    )
    early, late, *done = done
    tables, (qkv_rows, fc_rows, sent_near), sent = done[:2], done[2:5], done[5:]
    early_far = gather_far(early, "tensor", tensor_bits)[1:]
    sent_near = [sent_near] + [swap(x, "tensor", 1) for x in sent[1:]]
    sent = [x for pair in zip(sent, sent_near) for x in pair]
    qkv_pack.double()
    dense_pack.double()
    late, *done = tie_packs(
        qkv_pack, dense_pack, fc_pack, out_pack, beside=[late, *sent, *early_far]
    )
    sent, early_far = Tokens([(x,) for x in done[:groups]], order), done[groups:]
    late_far = gather_far(late, "tensor", tensor_bits)[1:]
    early_near = [swap(x, "tensor", 1) for x in early_far]
    out_pack.double()
    while len(fc_pack.bits) > 1:
        fc_pack.double()

    done = project_qkv(
        ids, info, sent, gain_attn, shift_attn, qkv_pack, qkv_rows, tables, width
    )
    done = tie_packs(fc_pack, out_pack, beside=[*done, *early_near, *late_far])
    (queries, keys, values), done = done[:3], done[3:]
    early_near, late_far = done[: groups // 2 - 1], done[groups // 2 - 1 :]
    late_near = [swap(x, "tensor", 1) for x in late_far]
    far = zip(zip(early_far, late_far), zip(early_near, late_near))
    grad = Tokens([(out_grad,), (near,), *[x for pair in far for x in pair]], order)
    while len(out_pack.bits) > 1:
        out_pack.double()
    (grad_context,) = tie_packs(out_pack, beside=[project_grad(ids, grad, dense_pack, width)])
    fc_pack.double()
    out_pack.double()
    done = attention(info, tables, queries, keys, values, grad_context)
    context, dq, dk, dv = tie_packs(fc_pack, out_pack, beside=done)
    dp_orders = [halving_order(near_bits), halving_order(next_bits)]
    qkv_orders = [halving_order(bits) for bits in qkv_bits]
    attn_parts = Parts(
        *project_context(ids, context, dense_pack, groups, model), "tensor", tensor_bits
    )
    attn_parts.begin()
    done = attention_weights(
        ids, info, tables, context, dq, dk, dv, sent, grad, gain_attn, shift_attn, qkv_orders
    )
    *done, attn_parts.other = tie_halves([*done, attn_parts.other], attn_parts)
    grads, qkv_bias_sums, *stacks = done
    attn_parts.middle()
    qkv_sums = [Halving(*stacks[:2], "dp", qkv_bits[0]), Halving(*stacks[2:], "dp", qkv_bits[1])]
    sent.arrays[0], attn_parts.send = tie(sent.arrays[0], attn_parts.send)
    attn_parts.swap()
    for parts in qkv_sums:
        parts.swap()
    done = mlp(
        ids, sent, grad, gain_mlp, shift_mlp, fc_pack, fc_rows, out_pack, dp_orders
    )
    done = tie_halves(done, attn_parts, *qkv_sums)
    *mlp_stacks, hidden, fc_bias_sums = done[:5]
    stacks = done[5:]
    attn_parts.add()
    mlp_parts = Parts(*mlp_stacks, "tensor", tensor_bits)
    mlp_sums = [Halving(*stacks[:2], "dp", near_bits), Halving(*stacks[2:], "dp", next_bits)]
    mlp_parts.begin()
    add_stacks(qkv_sums)
    mlp_parts.middle()
    hidden, mlp_parts.send = tie(hidden, mlp_parts.send)
    hidden, other = tie(hidden, mlp_parts.terms[1][0])
    mlp_parts.terms[1] = (other, 0)
    mlp_parts.swap()
    for parts in qkv_sums + mlp_sums:
        parts.swap()
    done = norm_backward(ids, sent, grads, hidden, gain_attn, gain_mlp, qkv_pack, fc_pack)
    done = tie_halves(done, mlp_parts, *qkv_sums, *mlp_sums)
    *back_stacks, norm_sums = done
    mlp_parts.add()

    back_parts = Parts(*back_stacks, "tensor", tensor_bits)
    back_parts.begin()
    add_stacks(qkv_sums + mlp_sums)
    back_parts.middle()

    stream_in, back_parts.send = tie(stream_in, back_parts.send)
    stream_in, other = tie(stream_in, back_parts.terms[1][0])
    back_parts.terms[1] = (other, 0)
    back_parts.swap()
    for parts in qkv_sums + mlp_sums:
        parts.swap()
    output, sums = finish_output(
        ids,
        stream_in,
        out_grad,
        attn_parts.terms,
        mlp_parts.terms,
        dense_bias[None, :],
        out_bias[None, :],
        norm_sums,
        fc_bias_sums,
        qkv_bias_sums,
        groups,
    )


    sums = sums + swap(sums, "tensor", 1)
    for bit in data_bits[3:]:
        sums = sums + swap(sums, "dp", bit)
    other, *_ = tie_halves([swap(sums, "dp", data_bits[2])], *mlp_sums, qkv_sums[1])
    sums = sums + other
    add_stacks(mlp_sums)
    sums, *sends = tie(sums, *[parts.send for parts in mlp_sums])
    for parts, send in zip(mlp_sums, sends):
        parts.send = send
    for bit in data_bits[:2]:
        sums = sums + swap(sums, "dp", bit)
    sums, back_parts.got = tie(sums, back_parts.got)
    back_parts.add()
    stream_grad = finish_grad(out_grad, stream_in, row_mean, inv_std, back_parts.terms)
    sums, stream_grad = tie(sums, stream_grad)
    for bit in tensor_bits[1:]:
        sums = sums + swap(sums, "tensor", bit)

    fc_weight_grad, out_weight_grad = finish_mlp_weights(*[x.finish() for x in mlp_sums])
    for parts in qkv_sums:
        parts.add()
    qkv_weight_grad, dense_weight_grad = finish_attention_weights(*[x.finish() for x in qkv_sums])

    count_all = float(rows_local * lax.axis_size("dp") * groups * model)
    gain_attn_grad, shift_attn_grad, gain_mlp_grad, shift_mlp_grad = (sums[x] for x in range(4))
    root_squares = jnp.sqrt(jnp.sum(sums[4:7], axis=1) / count_all)
    residual_grad = sums[7]
    fc_bias_grad = sums[8:12].reshape(-1)
    qkv_bias_grad = by_head(sums[12 : 12 + groups, :qkv_width], heads).reshape(-1)
    return (
        output,
        stream_grad,
        gain_attn_grad,
        shift_attn_grad,
        gain_mlp_grad,
        shift_mlp_grad,
        qkv_weight_grad,
        qkv_bias_grad,
        dense_weight_grad,
        residual_grad,
        fc_weight_grad,
        fc_bias_grad,
        out_weight_grad,
        residual_grad,
        root_squares,
    )


def solution(mesh):
    tokens, weights, rows, whole = (
        P(("dp", "tensor"), None),
        P("dp", "tensor"),
        P("tensor", "dp"),
        P(),
    )
    return jax.shard_map(
        local,
        mesh=mesh,
        in_specs=(
            tokens,
            P("dp"),
            P("dp"),
            whole,
            whole,
            whole,
            whole,
            weights,
            whole,
            rows,
            whole,
            weights,
            whole,
            rows,
            whole,
            tokens,
        ),
        out_specs=(
            tokens,
            tokens,
            whole,
            whole,
            whole,
            whole,
            weights,
            whole,
            rows,
            whole,
            weights,
            whole,
            rows,
            whole,
            whole,
        ),
        check_vma=False,
    )
```

```python
import jax
import jax.numpy as jnp
from jax import lax
from jax.experimental import pallas as pl
from jax.experimental.pallas import tpu as pltpu
from jax.sharding import PartitionSpec as P

HD = 64
ROT = 16
TRUNK = 1024
SEG = 128
TREE = 2560
NB = TREE // SEG
NT = TRUNK // SEG

f32 = jnp.float32
bf16 = jnp.bfloat16
eps_norm = 1e-05
masked_score = -1e30


def dot_nn(left, right):
    return lax.dot_general(left, right, (((1,), (0,)), ((), ())), preferred_element_type=f32)


def dot_nt(left, right):
    return lax.dot_general(left, right, (((1,), (1,)), ((), ())), preferred_element_type=f32)


def dot_tn(left, right):
    return lax.dot_general(left, right, (((0,), (0,)), ((), ())), preferred_element_type=f32)


def bits_of(size):
    bits = []
    bit = 1
    while bit < size:
        bits.append(bit)
        bit *= 2
    return bits


def swap(block, axis, bit):
    size = lax.axis_size(axis)
    return lax.ppermute(block, axis, [(i, i ^ bit) for i in range(size)])


def tie(*values):
    return lax.optimization_barrier(values)


def gather_far(block, axis, bits):
    pieces = [block]
    for bit in bits[1:]:
        pieces = pieces + [swap(piece, axis, bit) for piece in pieces]
    return pieces


class Pack:
    def __init__(self, block, axis, bits):
        self.rows, self.axis, self.bits = block.shape[0], axis, list(bits)
        self.arrays, self.owners = [block], [[0]]

    def double(self):
        bit = self.bits.pop(0)
        held = self.arrays[0] if len(self.arrays) == 1 else jnp.concatenate(self.arrays, axis=0)
        self.owners.append([j ^ bit for owners in self.owners for j in owners])
        self.arrays.append(swap(held, self.axis, bit))

    def specs(self):
        return [pl.BlockSpec(memory_space=pltpu.HBM)] * len(self.arrays)

    def pieces(self):
        return sum(len(owners) for owners in self.owners)

    def copies(self, refs, where, number, done):
        started = []
        for ref, owners in zip(refs, self.owners):
            for at, j in enumerate(owners):
                rows = pl.ds(pl.multiple_of((number ^ j) * self.rows, self.rows), self.rows)
                source = ref.at[pl.ds(at * self.rows, self.rows), :]
                copy = pltpu.make_async_copy(source, where.at[rows, :], done.at[len(started)])
                started.append(copy)
        return started


def tie_packs(*packs, beside=()):
    flat = tie(*beside, *[x for pack in packs for x in pack.arrays])
    at = len(beside)
    for pack in packs:
        pack.arrays = list(flat[at : at + len(pack.arrays)])
        at += len(pack.arrays)
    return list(flat[: len(beside)])


def halving_order(bits):
    if not bits:
        return [0]
    rest = halving_order(bits[1:])
    return [bits[0] ^ j for j in rest] + rest


class Halving:
    def __init__(self, send, keep, axis, bits):
        self.send, self.axis, self.bits = send, axis, list(bits)
        self.terms = [(keep, 0)]

    def swap(self):
        self.got = swap(self.send, self.axis, self.bits.pop(0))

    def add(self):
        self.terms.append((self.got, 0))
        half = self.got.shape[0] // 2
        if half:
            self.send = add_terms(self.terms, half)
            self.terms = [(x, at + half) for x, at in self.terms]

    def most(self):
        while len(self.bits) > 1:
            self.swap()
            self.add()

    def finish(self):
        while self.bits:
            self.swap()
            self.add()
        return self.terms


class Parts(Halving):
    def __init__(self, first, second, keep, axis, bits):
        super().__init__(first, keep, axis, bits)
        self.second = second

    def begin(self):
        bit = self.bits.pop(0)
        self.got, self.other = swap(self.send, self.axis, bit), swap(self.second, self.axis, bit)

    def middle(self):
        half = self.got.shape[0]
        self.send = add_terms([*self.terms, (self.got, 0)], half)
        self.terms = [(self.terms[0][0], half), (self.other, 0)]
        while len(self.bits) > 1:
            self.swap()
            self.add()


def tie_halves(values, *halvings):
    flat = tie(*values, *[x.got for x in halvings])
    for x, got in zip(halvings, flat[len(values) :]):
        x.got = got
    return flat[: len(values)]


def resident(shape):
    zeros = (0,) * len(shape)
    return pl.BlockSpec(shape, lambda *_: zeros, pipeline_mode=pl.Buffered(1))


def own_block(rows, columns):
    return pl.BlockSpec((rows, columns), lambda i, ids, *_: (ids[0] ^ ids[2 + i], 0))


def step_block(rows, columns):
    return pl.BlockSpec((rows, columns), lambda i, *_: (i, 0))


def part_shapes(groups, rows, columns):
    quarter = max(groups // 4, 1)
    return [shaped(n, rows, columns) for n in (quarter, quarter, groups - 2 * quarter)]


def part_blocks(groups, rows, columns):
    quarter = max(groups // 4, 1)
    shape = (pl.Squeezed(), rows, columns)
    return [
        pl.BlockSpec(shape, lambda i, *_: (jnp.minimum(i, quarter - 1), 0, 0)),
        pl.BlockSpec(shape, lambda i, *_: (jnp.clip(i - quarter, 0, quarter - 1), 0, 0)),
        pl.BlockSpec(shape, lambda i, *_: (jnp.maximum(i - 2 * quarter, 0), 0, 0)),
    ]


def store_part(stacks, value, step, groups):
    quarter = max(groups // 4, 1)
    turn_of = jnp.minimum(step // quarter, 2)
    for at, stack in enumerate(stacks):

        @pl.when(turn_of == at)
        def _(stack=stack):
            stack[...] = value


class Tokens:
    def __init__(self, blocks, order):
        blocks = [blocks[j] for j in order]
        self.groups, self.counts = len(blocks), [len(block) for block in blocks]
        self.rows, self.model = sum(x.shape[0] for x in blocks[0]), blocks[0][0].shape[1]
        self.arrays = [x for block in blocks for x in block]
        self.specs = [pl.BlockSpec(memory_space=pltpu.HBM)] * len(self.arrays)

    def scratch(self):
        return [
            pltpu.VMEM((2, self.rows, self.model), bf16),
            pltpu.SemaphoreType.DMA((2, max(self.counts))),
        ]

    def fetch(self, refs, held, done, step):
        def copies(at):
            first, start, found = sum(self.counts[:at]), 0, []
            for k, ref in enumerate(refs[first : first + self.counts[at]]):
                where = held.at[at % 2, pl.ds(start, ref.shape[0]), :]
                found.append(pltpu.make_async_copy(ref, where, done.at[at % 2, k]))
                start += ref.shape[0]
            return found

        for at in range(self.groups):

            @pl.when(step == at)
            def _(at=at):
                ahead = copies(at) if at == 0 else []
                if at + 1 < self.groups:
                    ahead = ahead + copies(at + 1)
                for copy in ahead:
                    copy.start()
                for copy in copies(at):
                    copy.wait()


def store_halves(send, keep, total, number, order, columns=slice(None), source=slice(None)):
    half, rows = send.shape[0], send.shape[1]
    for at, j in enumerate(order):
        where = send if at < half else keep
        block = total[pl.ds(pl.multiple_of((number ^ j) * rows, rows), rows), source]
        where[at % half, :, columns] = block.astype(bf16)


def call(
    kernel, name, grid, prefetch, operands, specs, outs, out_specs, scratch, flops, extra=0, room=12, light=False
):
    size = 0 if light else sum(x.size * x.dtype.itemsize for x in [*operands, *outs])
    return pl.pallas_call(
        kernel,
        grid_spec=pltpu.PrefetchScalarGridSpec(
            num_scalar_prefetch=len(prefetch),
            grid=grid,
            in_specs=specs,
            out_specs=out_specs,
            scratch_shapes=scratch,
        ),
        out_shape=outs,
        compiler_params=pltpu.CompilerParams(
            dimension_semantics=("arbitrary",) * len(grid), vmem_limit_bytes=room << 20
        ),
        cost_estimate=pl.CostEstimate(
            flops=int(flops), bytes_accessed=int(size), transcendentals=int(extra)
        ),
        name=name,
    )(*prefetch, *operands)


def shaped(*shape, dtype=bf16):
    return jax.ShapeDtypeStruct(shape, dtype)


def shift_gain(block, gain, shift):
    return (block.astype(f32) * gain[...] + shift[...]).astype(bf16)


def turn(block, cosine, sine, sign):
    width = block.shape[1]
    step = min(width, 128)
    lane = lax.broadcasted_iota(jnp.int32, (block.shape[0], step), 1) % HD
    done = []
    for start in range(0, width, step):
        part = block[:, start : start + step]
        if step == 128:
            left = pltpu.roll(part, step - ROT // 2, 1)
            right = pltpu.roll(part, ROT // 2, 1)
        else:
            left = jnp.concatenate([part[:, ROT // 2 :], part[:, : ROT // 2]], axis=1)
            right = jnp.concatenate([part[:, -ROT // 2 :], part[:, : -ROT // 2]], axis=1)
        moved = jnp.where(lane < ROT // 2, -left, right) * sine[:, :step]
        done.append(part * cosine[:, :step] + moved * sign)
    return done[0] if len(done) == 1 else jnp.concatenate(done, axis=1)


def weight_scratch(pack):
    model = pack.rows * pack.pieces()
    columns = pack.arrays[0].shape[1]
    return [pltpu.VMEM((model, columns), bf16), pltpu.SemaphoreType.DMA((pack.pieces(),))]


def prepare_weights(qkv, dense, fc, out):
    rows, columns = qkv.shape
    width = columns // 3

    def kernel(qkv_ref, dense_ref, fc_ref, out_ref, qkv_to, dense_to, fc_to, out_to):
        for head in range(width // HD):
            for kind in range(3):
                at, own = (3 * head + kind) * HD, kind * width + head * HD
                qkv_to[:, own : own + HD] = qkv_ref[:, at : at + HD].astype(bf16)
        dense_to[...] = dense_ref[...].T.astype(bf16)
        fc_to[...] = fc_ref[...].astype(bf16)
        out_to[...] = out_ref[...].T.astype(bf16)

    operands = [qkv, dense, fc, out]
    outs = [shaped(*qkv.shape), shaped(*dense.shape[::-1]), shaped(*fc.shape), shaped(*out.shape[::-1])]
    return call(
        kernel,
        "prepare_weights",
        (1,),
        [],
        operands,
        [resident(x.shape) for x in operands],
        outs,
        [resident(x.shape) for x in outs],
        [],
        rows * columns,
        room=62,
    )


def normalize(stream):
    rows, model = stream.shape
    block = 160

    def kernel(stream_ref, sent_ref, mean_ref, std_ref):
        field = stream_ref[...]
        mean = jnp.sum(field, axis=1, keepdims=True) / model
        centred = field - mean
        variance = jnp.sum(centred * centred, axis=1, keepdims=True) / model
        scale = lax.rsqrt(variance + eps_norm)
        sent_ref[...] = (centred * scale).astype(bf16)
        mean_ref[...] = mean
        std_ref[...] = scale

    return call(
        kernel,
        "normalize",
        (rows // block,),
        [],
        [stream],
        [step_block(block, model)],
        [shaped(rows, model), shaped(rows, 1, dtype=f32), shaped(rows, 1, dtype=f32)],
        [step_block(block, model), step_block(block, 1), step_block(block, 1)],
        [],
        rows * model * 8,
        room=62,
    )


def project_qkv(ids, info, sent, gain, shift, pack, bias, tables, width):
    groups, held, rows, model = sent.groups, len(sent.arrays), sent.rows, sent.model

    def kernel(ids, info, *refs):
        sent_refs, refs = refs[:held], refs[held:]
        weight_refs, refs = refs[: len(pack.arrays)], refs[len(pack.arrays) :]
        gain, shift, bias, cos, sine, q_out, k_out, v_out = refs[:8]
        block, arrived, whole, placed, added = refs[8:]
        step = pl.program_id(0)

        @pl.when(step == 0)
        def _():
            for copy in pack.copies(weight_refs, whole, ids[1], placed):
                copy.start()

        sent.fetch(sent_refs, block, arrived, step)

        @pl.when(step == 0)
        def _():
            for copy in pack.copies(weight_refs, whole, ids[1], placed):
                copy.wait()
            own = bias[pl.ds(ids[0], 1), :]
            for head in range(width // HD):
                for kind in range(3):
                    at, to = (3 * head + kind) * HD, kind * width + head * HD
                    added[:, to : to + HD] = own[:, at : at + HD]

        token = block[step % 2]
        normed = shift_gain(token, gain, shift)
        blocks = rows // SEG
        cut = (blocks + 1) // 2
        both = [dot_nn(normed[x], whole[...]) + added[...] for x in (slice(0, cut * SEG), slice(cut * SEG, rows))]
        first = (ids[0] ^ ids[2 + step]) * blocks
        for at in range(blocks):
            number = first + at
            table = pl.ds(pl.multiple_of(info[number // NB, number % NB, 4] * SEG, SEG), SEG)
            tabs = (cos[table, :], sine[table, :])
            own = slice(at * SEG, (at + 1) * SEG)
            here = at * SEG if at < cut else (at - cut) * SEG
            qkv = both[at >= cut][here : here + SEG]
            q_out[own, :] = (turn(qkv[:, :width], *tabs, 1.0) * HD**-0.5).astype(bf16)
            k_out[own, :] = turn(qkv[:, width : 2 * width], *tabs, 1.0).astype(bf16)
            v_out[own, :] = qkv[:, 2 * width :].astype(bf16)

    operands = [*sent.arrays, *pack.arrays, gain, shift, bias, *tables]
    out = shaped(groups * rows, width)
    return call(
        kernel,
        "project_qkv",
        (groups,),
        [ids, info],
        operands,
        sent.specs
        + pack.specs()
        + [resident(x.shape) for x in operands[held + len(pack.arrays) :]],
        [out] * 3,
        [own_block(rows, width)] * 3,
        sent.scratch() + weight_scratch(pack) + [pltpu.VMEM((1, 3 * width), f32)],
        2 * groups * rows * model * 3 * width,
        room=62,
    )


def project_grad(ids, grad, pack, width):
    groups, held, rows, model = grad.groups, len(grad.arrays), grad.rows, grad.model

    def kernel(ids, *refs):
        grad_refs, refs = refs[:held], refs[held:]
        weight_refs, (out, block, arrived, whole, placed) = refs[:-5], refs[-5:]
        step = pl.program_id(0)

        @pl.when(step == 0)
        def _():
            for copy in pack.copies(weight_refs, whole, ids[1], placed):
                copy.start()

        grad.fetch(grad_refs, block, arrived, step)

        @pl.when(step == 0)
        def _():
            for copy in pack.copies(weight_refs, whole, ids[1], placed):
                copy.wait()

        out[...] = dot_nn(block[step % 2], whole[...]).astype(bf16)

    operands = [*grad.arrays, *pack.arrays]
    return call(
        kernel,
        "project_grad",
        (groups,),
        [ids],
        operands,
        grad.specs + pack.specs(),
        [shaped(groups * rows, width)],
        [own_block(rows, width)],
        grad.scratch() + weight_scratch(pack),
        2 * groups * rows * model * width,
    )[0]


def attention_kernel(
    info, q_ref, do_ref, k_ref, v_ref, cos, sine, ctx_ref, dq_ref, dk_ref, dv_ref, dk_sum, dv_sum
):
    tree, step = pl.program_id(0), pl.program_id(1)
    width = q_ref.shape[1]
    heads = width // HD
    lane_head = lax.broadcasted_iota(jnp.int32, (SEG, width), 1) // HD

    @pl.when(step == 0)
    def _():
        dk_sum[...] = jnp.zeros_like(dk_sum)
        dv_sum[...] = jnp.zeros_like(dv_sum)

    first, second = info[tree, step, 0], info[tree, step, 1]
    first_rows = pl.ds(pl.multiple_of(first * SEG, SEG), SEG)
    second_rows = pl.ds(pl.multiple_of(second * SEG, SEG), SEG)
    queries, grads = q_ref[...], do_ref[...]
    zero = jnp.zeros_like(queries)
    q_rows = jnp.concatenate([jnp.where(lane_head == h, queries, zero) for h in range(heads)], axis=0)
    g_rows = jnp.concatenate([jnp.where(lane_head == h, grads, zero) for h in range(heads)], axis=0)
    q_turned, g_turned = queries.T, grads.T
    ahead = lax.broadcasted_iota(jnp.int32, (SEG, SEG), 1) - lax.broadcasted_iota(
        jnp.int32, (SEG, SEG), 0
    )
    seen = jnp.concatenate([ahead <= info[tree, step, 2], ahead <= info[tree, step, 3]], axis=1)
    seen = jnp.concatenate([seen] * heads, axis=0)
    k_near = jnp.concatenate([k_ref[first_rows, :], k_ref[second_rows, :]], axis=0)
    v_near = jnp.concatenate([v_ref[first_rows, :], v_ref[second_rows, :]], axis=0)

    def work(pairs):
        count = pairs * 2 * SEG
        near = jnp.where(seen, dot_nt(q_rows, k_near), masked_score)
        most = jnp.max(near, axis=1, keepdims=True)
        if count:
            k_far, v_far = k_ref[0:count, :], v_ref[0:count, :]
            far = dot_nt(q_rows, k_far)
            most = jnp.maximum(most, jnp.max(far, axis=1, keepdims=True))
        near = jnp.exp(near - most)
        total = jnp.sum(near, axis=1, keepdims=True)
        if count:
            far = jnp.exp(far - most)
            total = total + jnp.sum(far, axis=1, keepdims=True)
        scale = 1.0 / total
        near = near * scale
        near_low = near.astype(bf16)
        context = dot_nn(near_low, v_near)
        if count:
            far = far * scale
            far_low = far.astype(bf16)
            context = context + dot_nn(far_low, v_far)
        delta = jnp.sum(context * g_rows.astype(f32), axis=1, keepdims=True)
        near = (near * (dot_nt(g_rows, v_near) - delta)).astype(bf16)
        dq = dot_nn(near, k_near)
        if count:
            far = (far * (dot_nt(g_rows, v_far) - delta)).astype(bf16)
            dq = dq + dot_nn(far, k_far)
        ctx_own, dq_own = context[0:SEG], dq[0:SEG]
        for h in range(1, heads):
            ctx_own = jnp.where(lane_head == h, context[h * SEG : (h + 1) * SEG], ctx_own)
            dq_own = jnp.where(lane_head == h, dq[h * SEG : (h + 1) * SEG], dq_own)
        ctx_ref[...] = ctx_own.astype(bf16)
        dq_ref[...] = turn(dq_own * HD**-0.5, cos, sine, -1.0).astype(bf16)
        for h in range(heads):
            own = slice(h * SEG, (h + 1) * SEG)
            part = slice(h * HD, (h + 1) * HD)
            dk = dot_nn(q_turned[part], near[own])
            dv = dot_nn(g_turned[part], near_low[own])
            dk_sum[first, part, :] += dk[:, :SEG]
            dv_sum[first, part, :] += dv[:, :SEG]
            dk_sum[second, part, :] += dk[:, SEG:]
            dv_sum[second, part, :] += dv[:, SEG:]
            if count:
                dk = dot_nn(q_turned[part], far[own])
                dv = dot_nn(g_turned[part], far_low[own])
                for j in range(2 * pairs):
                    dk_sum[j, part, :] += dk[:, j * SEG : (j + 1) * SEG]
                    dv_sum[j, part, :] += dv[:, j * SEG : (j + 1) * SEG]

    for pairs in range(NT // 2):

        @pl.when(step // 2 == pairs)
        def _(pairs=pairs):
            work(pairs)

    @pl.when(step >= NT)
    def _():
        work(NT // 2)

    @pl.when(step == NB - 1)
    def _():
        def finish(j, carry):
            rows = pl.ds(pl.multiple_of(j * SEG, SEG), SEG)
            dv_ref[rows, :] = dv_sum[j].T.astype(bf16)
            dk_ref[rows, :] = dk_sum[j].T.astype(bf16)
            return carry

        lax.fori_loop(0, NB, finish, 0)


def attention(info, tables, queries, keys, values, grads):
    total, width = queries.shape
    trees = total // TREE
    table_width = tables[0].shape[1]
    block = pl.BlockSpec((SEG, width), lambda t, b, info: (t * NB + b, 0))
    whole = pl.BlockSpec((TREE, width), lambda t, b, info: (t, 0))
    table = pl.BlockSpec((SEG, table_width), lambda t, b, info: (info[t, b, 4], 0))
    scores = trees * (TREE - TRUNK) * (TRUNK + 2 * SEG) * (width // HD)
    return call(
        attention_kernel,
        "attention",
        (trees, NB),
        [info],
        [queries, grads, keys, values, *tables],
        [block, block, whole, whole, table, table],
        [shaped(total, width)] * 4,
        [block, block, whole, whole],
        [pltpu.VMEM((NB, width, SEG), f32), pltpu.VMEM((NB, width, SEG), f32)],
        scores * width * 2 * 6 * 1.3,
        scores,
        room=22,
    )


def project_context(ids, context, pack, groups, model):
    rows, width = context.shape[0] // groups, context.shape[1]

    def kernel(ids, ctx, *refs):
        weight_refs, stacks, (whole, placed) = refs[:-5], refs[-5:-2], refs[-2:]
        step = pl.program_id(0)

        @pl.when(step == 0)
        def _():
            copies = pack.copies(weight_refs, whole, ids[1], placed)
            for copy in copies:
                copy.start()
            for copy in copies:
                copy.wait()

        store_part(stacks, dot_nt(ctx[...], whole[...]).astype(bf16), step, groups)

    operands = [context, *pack.arrays]
    return call(
        kernel,
        "project_context",
        (groups,),
        [ids],
        operands,
        [own_block(rows, width)] + pack.specs(),
        part_shapes(groups, rows, model),
        part_blocks(groups, rows, model),
        weight_scratch(pack),
        2 * groups * rows * model * width,
        room=14,
    )


def attention_weights(ids, info, tables, context, dq, dk, dv, sent, grad, gain, shift, orders):
    groups, held, rows, model = sent.groups, len(sent.arrays), sent.rows, sent.model
    width, count = dq.shape[1], len(orders[0])

    def kernel(ids, info, ctx_ref, dq_ref, dk_ref, dv_ref, *refs):
        sent_refs, refs = refs[:held], refs[held:]
        grad_refs, refs = refs[: len(grad.arrays)], refs[len(grad.arrays) :]
        gain, shift, cos, sine, grads, bias_ref, *stacks = refs[:10]
        block, arrived, grad_block, grad_arrived, total, dense_total = refs[10:]
        step = pl.program_id(0)

        @pl.when(step == 0)
        def _():
            total[...] = jnp.zeros_like(total)
            dense_total[...] = jnp.zeros_like(dense_total)
            bias_ref[...] = jnp.zeros_like(bias_ref)

        sent.fetch(sent_refs, block, arrived, step)
        grad.fetch(grad_refs, grad_block, grad_arrived, step)
        grads[:, :width] = dq_ref[...]
        first = (ids[0] ^ ids[2 + step]) * (rows // SEG)
        for at in range(rows // SEG):
            number = first + at
            table = pl.ds(pl.multiple_of(info[number // NB, number % NB, 4] * SEG, SEG), SEG)
            own = slice(at * SEG, (at + 1) * SEG)
            turned = turn(dk_ref[own, :], cos[table, :], sine[table, :], -1.0)
            grads[own, width : 2 * width] = turned.astype(bf16)
        grads[:, 2 * width :] = dv_ref[...]
        bias_ref[0:1, :] += jnp.sum(grads[...].astype(f32), axis=0, keepdims=True)
        total[...] += dot_tn(shift_gain(block[step % 2], gain, shift), grads[...])
        dense_total[...] += dot_tn(grad_block[step % 2], ctx_ref[...])

        @pl.when(step == groups - 1)
        def _():
            store_halves(*stacks[:2], total, ids[1], orders[0], source=slice(0, 2 * width))
            source = slice(2 * width, 3 * width)
            store_halves(*stacks[2:], total, ids[1], orders[1], slice(0, width), source)
            columns = slice(width, 2 * width)
            store_halves(*stacks[2:], dense_total, ids[1], orders[1], columns)

    operands = [context, dq, dk, dv, *sent.arrays, *grad.arrays, gain, shift, *tables]
    outs = [shaped(groups * rows, 3 * width), shaped(8, 3 * width, dtype=f32)]
    outs += [shaped(count // 2, model // count, 2 * width)] * 4
    return call(
        kernel,
        "attention_weights",
        (groups,),
        [ids, info],
        operands,
        [own_block(rows, width)] * 4
        + sent.specs
        + grad.specs
        + [resident(x.shape) for x in operands[-4:]],
        outs,
        [step_block(rows, 3 * width)] + [resident(x.shape) for x in outs[1:]],
        sent.scratch()
        + grad.scratch()
        + [pltpu.VMEM((model, 3 * width), f32), pltpu.VMEM((model, width), f32)],
        2 * groups * rows * model * 4 * width,
        room=24,
    )


def mlp(ids, sent, grad, gain, shift, fc, bias, out, orders):
    groups, held, rows, model = sent.groups, len(sent.arrays), sent.rows, sent.model
    pieces, units = len(fc.arrays), fc.arrays[0].shape[1]

    def kernel(ids, *refs):
        sent_refs, refs = refs[:held], refs[held:]
        grad_refs, refs = refs[: len(grad.arrays)], refs[len(grad.arrays) :]
        fc_refs, refs = refs[:pieces], refs[pieces:]
        out_refs, refs = refs[:pieces], refs[pieces:]
        gain, shift, bias, *parts_out = refs[:6]
        hidden_ref, bias_ref = refs[6:8]
        stacks, refs = refs[8:12], refs[12:]
        block, arrived, grad_block, grad_arrived, fc_whole, fc_placed, out_whole, out_placed = refs[:8]
        act_ref, fc_total, out_total = refs[8:]
        step = pl.program_id(0)

        def weights():
            copies = fc.copies(fc_refs, fc_whole, ids[1], fc_placed)
            return copies + out.copies(out_refs, out_whole, ids[1], out_placed)

        @pl.when(step == 0)
        def _():
            for copy in weights():
                copy.start()
            fc_total[...] = jnp.zeros_like(fc_total)
            out_total[...] = jnp.zeros_like(out_total)
            bias_ref[...] = jnp.zeros_like(bias_ref)

        sent.fetch(sent_refs, block, arrived, step)
        grad.fetch(grad_refs, grad_block, grad_arrived, step)

        @pl.when(step == 0)
        def _():
            for copy in weights():
                copy.wait()

        token, grads = block[step % 2], grad_block[step % 2]
        normed = shift_gain(token, gain, shift)
        count = 1
        parts = [slice(k * rows // count, (k + 1) * rows // count) for k in range(count)]
        added = bias[pl.ds(ids[0], 1), :]
        hidden = [dot_nn(normed[x], fc_whole[...]) + added for x in parts]
        back = [dot_nn(grads[x], out_whole[...]) for x in parts]
        for x, field, slope in zip(parts, hidden, back):
            chance = 0.5 + 0.5 * lax.erf(field * 0.7071067811865476)
            bell = jnp.exp(field * field * -0.5) * 0.3989422804014327
            act_ref[x, :] = (field * chance).astype(bf16)
            low = (slope * (chance + field * bell)).astype(bf16)
            hidden_ref[x, :] = low
            bias_ref[0:1, :] += jnp.sum(low.astype(f32), axis=0, keepdims=True)
        store_part(parts_out, dot_nt(act_ref[...], out_whole[...]).astype(bf16), step, groups)
        out_total[...] += dot_tn(grads, act_ref[...])
        fc_total[...] += dot_tn(normed, hidden_ref[...])

        @pl.when(step == groups - 1)
        def _():
            half = units // 2
            for at, order in enumerate(orders):
                stack = stacks[2 * at : 2 * at + 2]
                source = slice(at * half, (at + 1) * half)
                store_halves(*stack, fc_total, ids[1], order, slice(0, half), source)
                store_halves(*stack, out_total, ids[1], order, slice(half, units), source)

    operands = [*sent.arrays, *grad.arrays, *fc.arrays, *out.arrays, gain, shift, bias]
    count = model // fc.rows
    outs = part_shapes(groups, rows, model)
    outs += [shaped(groups * rows, units), shaped(8, units, dtype=f32)]
    outs += [shaped(count // 2, fc.rows, units)] * 4
    return call(
        kernel,
        "mlp",
        (groups,),
        [ids],
        operands,
        sent.specs
        + grad.specs
        + fc.specs()
        + out.specs()
        + [resident(x.shape) for x in operands[-3:]],
        outs,
        part_blocks(groups, rows, model)
        + [step_block(rows, units)]
        + [resident(x.shape) for x in outs[4:]],
        sent.scratch()
        + grad.scratch()
        + weight_scratch(fc)
        + weight_scratch(out)
        + [
            pltpu.VMEM((rows, units), bf16),
            pltpu.VMEM((model, units), f32),
            pltpu.VMEM((model, units), f32),
        ],
        10 * groups * rows * model * units,
        room=42,
    )


def norm_backward(ids, sent, grads, hidden, gain_attn, gain_mlp, qkv_pack, fc):
    groups, held, rows, model = sent.groups, len(sent.arrays), sent.rows, sent.model
    pieces, units, columns = len(fc.arrays), hidden.shape[1], grads.shape[1]

    def kernel(ids, grads_ref, hidden_ref, *refs):
        sent_refs, refs = refs[:held], refs[held:]
        qkv_refs, refs = refs[:pieces], refs[pieces:]
        fc_refs, refs = refs[:pieces], refs[pieces:]
        gain_attn, gain_mlp, *stacks = refs[:5]
        sums_ref, block, arrived, qkv_whole, qkv_placed, fc_whole, fc_placed = refs[5:]
        step = pl.program_id(0)

        def weights():
            copies = qkv_pack.copies(qkv_refs, qkv_whole, ids[1], qkv_placed)
            return copies + fc.copies(fc_refs, fc_whole, ids[1], fc_placed)

        @pl.when(step == 0)
        def _():
            for copy in weights():
                copy.start()
            sums_ref[...] = jnp.zeros_like(sums_ref)

        sent.fetch(sent_refs, block, arrived, step)

        @pl.when(step == 0)
        def _():
            for copy in weights():
                copy.wait()

        back_attn = dot_nt(grads_ref[...], qkv_whole[...])
        back_mlp = dot_nt(hidden_ref[...], fc_whole[...])
        token = block[step % 2].astype(f32)
        for at, back in enumerate((back_attn, back_mlp)):
            sums_ref[2 * at : 2 * at + 1, :] += jnp.sum(back * token, axis=0, keepdims=True)
            sums_ref[2 * at + 1 : 2 * at + 2, :] += jnp.sum(back, axis=0, keepdims=True)
        part = back_attn * gain_attn[...] + back_mlp * gain_mlp[...]
        store_part(stacks, part.astype(bf16), step, groups)

    operands = [grads, hidden, *sent.arrays, *qkv_pack.arrays, *fc.arrays, gain_attn, gain_mlp]
    outs = part_shapes(groups, rows, model) + [shaped(8, model, dtype=f32)]
    return call(
        kernel,
        "norm_backward",
        (groups,),
        [ids],
        operands,
        [step_block(rows, columns), step_block(rows, units)]
        + sent.specs
        + qkv_pack.specs()
        + fc.specs()
        + [resident(x.shape) for x in operands[-2:]],
        outs,
        part_blocks(groups, rows, model) + [resident(x.shape) for x in outs[3:]],
        sent.scratch() + weight_scratch(qkv_pack) + weight_scratch(fc),
        2 * groups * rows * model * (units + columns),
        room=26,
    )


def taken(terms, block):
    return [
        pl.BlockSpec((pl.Squeezed(), block, x.shape[2]), lambda i, *_, at=at: (at, i, 0))
        for x, at in terms
    ]


def add_terms(terms, half):
    _, rows, columns = terms[0][0].shape
    block = max(x for x in (320, 128, 64) if rows % x == 0)

    def kernel(*refs):
        refs[-1][...] = sum(x[...].astype(f32) for x in refs[:-1]).astype(bf16)

    shape = (pl.Squeezed(), block, columns)
    out = shaped(half, rows, columns)
    return call(
        kernel,
        "add_terms",
        (half, rows // block),
        [],
        [x for x, _ in terms],
        [pl.BlockSpec(shape, lambda k, i, *_, at=at: (at + k, i, 0)) for _, at in terms],
        [out],
        [pl.BlockSpec(shape, lambda k, i, *_: (k, i, 0))],
        [],
        half * rows * columns * len(terms),
    )[0]


def whole_terms(terms, count):
    return [
        pl.BlockSpec((count, *x.shape[1:]), lambda *_, at=at: (at // count, 0, 0)) for x, at in terms
    ]


def add_stacks(stacks):
    counts = []
    for parts in stacks:
        parts.terms.append((parts.got, 0))
        counts.append(parts.got.shape[0] // 2)
    held = [len(parts.terms) for parts in stacks]
    operands = [x for parts in stacks for x, _ in parts.terms]

    def kernel(*refs):
        for at, half in enumerate(counts):
            first = sum(held[:at])
            total = sum(x[...].astype(f32) for x in refs[first : first + held[at]])
            refs[len(operands) + at][...] = total.astype(bf16)

    outs = [shaped(n, *parts.got.shape[1:]) for n, parts in zip(counts, stacks)]
    sends = call(
        kernel,
        "add_stacks",
        (1,),
        [],
        operands,
        [x for n, parts in zip(counts, stacks) for x in whole_terms(parts.terms, n)],
        outs,
        [resident(x.shape) for x in outs],
        [],
        sum(x.size for x in operands) // 2,
        room=16,
    )
    for n, parts, send in zip(counts, stacks, sends):
        parts.send = send
        parts.terms = [(x, at + n) for x, at in parts.terms]


def finish_mlp_weights(first, second):
    held, (_, rows, units) = len(first), first[0][0].shape
    half = units // 2

    def kernel(*refs):
        low = sum(x[0].astype(f32) for x in refs[:held])
        high = sum(x[0].astype(f32) for x in refs[held:-2])
        refs[-2][:, :half] = low[:, :half]
        refs[-2][:, half:] = high[:, :half]
        refs[-1][:half, :] = low[:, half:].T
        refs[-1][half:, :] = high[:, half:].T

    operands = [x for x, _ in [*first, *second]]
    outs = [shaped(rows, units, dtype=f32), shaped(units, rows, dtype=f32)]
    return call(
        kernel,
        "finish_mlp_weights",
        (1,),
        [],
        operands,
        whole_terms([*first, *second], 1),
        outs,
        [resident(x.shape) for x in outs],
        [],
        len(operands) * rows * units,
    )


def finish_attention_weights(first, second):
    held, (_, rows, columns) = len(first), first[0][0].shape
    width = columns // 2

    def kernel(*refs):
        low = sum(x[0].astype(f32) for x in refs[:held])
        high = sum(x[0].astype(f32) for x in refs[held:-2])
        for head in range(width // HD):
            for kind, (source, start) in enumerate(((low, 0), (low, width), (high, 0))):
                at = (3 * head + kind) * HD
                own = start + head * HD
                refs[-2][:, at : at + HD] = source[:, own : own + HD]
        refs[-1][...] = high[:, width:].T

    operands = [x for x, _ in [*first, *second]]
    outs = [shaped(rows, 3 * width, dtype=f32), shaped(width, rows, dtype=f32)]
    return call(
        kernel,
        "finish_attention_weights",
        (1,),
        [],
        operands,
        whole_terms([*first, *second], 1),
        outs,
        [resident(x.shape) for x in outs],
        [],
        len(operands) * rows * columns,
    )


def sum_rows(groups):
    return (12 + groups + 7) // 8 * 8


def finish_output(ids, stream, grad, attn_terms, mlp_terms, dense_bias, out_bias, norm_sums, fc_sums, qkv_sums, groups):
    rows, model = stream.shape
    block = 160
    first, second = len(attn_terms), len(mlp_terms)
    units, columns = fc_sums.shape[1], qkv_sums.shape[1]
    across = model // units

    def kernel(ids, stream_ref, grad_ref, *refs):
        attn_refs, refs = refs[:first], refs[first:]
        mlp_refs, refs = refs[:second], refs[second:]
        dense_bias, out_bias, norm_ref, fc_ref, qkv_ref, out_ref, sums_ref = refs

        @pl.when(pl.program_id(0) == 0)
        def _():
            sums_ref[...] = jnp.zeros_like(sums_ref)
            sums_ref[0:4, :] = norm_ref[0:4, :]
            own = jnp.concatenate([fc_ref[0:1, :]] * across, axis=1) if across > 1 else fc_ref[0:1, :]
            lane = lax.broadcasted_iota(jnp.int32, (1, model), 1) // units
            sums_ref[pl.ds(8 + ids[0] // across, 1), :] = jnp.where(lane == ids[0] % across, own, 0.0)
            sums_ref[pl.ds(12 + ids[0], 1), :columns] = qkv_ref[0:1, :]

        attn = sum(x[...].astype(f32) for x in attn_refs) + dense_bias[...]
        mlp = sum(x[...].astype(f32) for x in mlp_refs) + out_bias[...]
        output = stream_ref[...] + attn + mlp
        out_ref[...] = output
        for at, value in enumerate((output, attn, mlp)):
            sums_ref[4 + at : 5 + at, :] += jnp.sum(value * value, axis=0, keepdims=True)
        sums_ref[7:8, :] += jnp.sum(grad_ref[...].astype(f32), axis=0, keepdims=True)

    terms = [*attn_terms, *mlp_terms]
    operands = [stream, grad, *[x for x, _ in terms], dense_bias, out_bias, norm_sums, fc_sums, qkv_sums]
    outs = [shaped(rows, model, dtype=f32), shaped(sum_rows(groups), model, dtype=f32)]
    return call(
        kernel,
        "finish_output",
        (rows // block,),
        [ids],
        operands,
        [step_block(block, model), step_block(block, model)]
        + taken(terms, block)
        + [resident(x.shape) for x in operands[-5:]],
        outs,
        [step_block(block, model), resident(outs[1].shape)],
        [],
        rows * model * 16,
        room=16,
    )


def finish_grad(grad, stream, row_mean, inv_std, terms):
    rows, model = grad.shape
    block = 160

    def kernel(grad_ref, stream_ref, mean_ref, std_ref, *refs):
        term_refs, out_ref = refs[:-1], refs[-1]
        sent = sum(x[...].astype(f32) for x in term_refs)
        norm = (stream_ref[...] - mean_ref[...]) * std_ref[...]
        mean = jnp.sum(sent, axis=1, keepdims=True) / model
        cross = jnp.sum(sent * norm, axis=1, keepdims=True) / model
        out_ref[...] = grad_ref[...].astype(f32) + std_ref[...] * (sent - mean - norm * cross)

    operands = [grad, stream, row_mean, inv_std, *[x for x, _ in terms]]
    return call(
        kernel,
        "finish_grad",
        (rows // block,),
        [],
        operands,
        [step_block(block, model)] * 2
        + [step_block(block, 1)] * 2
        + taken(terms, block),
        [shaped(rows, model, dtype=f32)],
        [step_block(block, model)],
        [],
        0,
        light=True,
    )[0]


def tree_table(segment_ids, parent_ids):
    trees = segment_ids.shape[0] // TREE

    def kernel(segment, parent, table):
        for tree in range(trees):
            for block in range(NT):
                odd = block % 2
                row = (block - odd, block - odd + 1, SEG * odd, -SEG * (1 - odd), block)
                for at, value in enumerate(row):
                    table[tree, block, at] = value

            def place(block, carry):
                first = tree * TREE
                owner = parent[first + block * SEG]
                leaf = (owner != segment[first]).astype(jnp.int32)
                at = block
                for other in range(NT, NB):
                    at = jnp.where(segment[first + other * SEG] == owner, other, at)
                table[tree, block, 0] = block
                table[tree, block, 1] = at
                table[tree, block, 2] = 0
                table[tree, block, 3] = SEG * (2 * leaf - 1)
                table[tree, block, 4] = NT + leaf
                return carry

            lax.fori_loop(NT, NB, place, 0)

    smem = pl.BlockSpec(memory_space=pltpu.SMEM)
    return pl.pallas_call(
        kernel,
        in_specs=[smem, smem],
        out_specs=smem,
        out_shape=jax.ShapeDtypeStruct((trees, NB, 5), jnp.int32),
        name="tree_table",
    )(segment_ids, parent_ids)


def angle_tables(zero):
    places = TRUNK + 2 * SEG
    place = lax.broadcasted_iota(jnp.int32, (places, 2 * HD), 0).astype(f32)
    lane = lax.broadcasted_iota(jnp.int32, (places, 2 * HD), 1) % HD
    half = ROT // 2
    frequency = 10000.0 ** (-((lane % half).astype(f32) * 2.0 / ROT))
    angle = (place + zero) * frequency
    cosine = jnp.where(lane < ROT, jnp.cos(angle), 1.0)
    sine = jnp.where(lane < ROT, jnp.sin(angle), 0.0)
    return cosine, sine


def by_kind(array, heads):
    shape = array.shape[:-1]
    array = array.reshape(*shape, heads, 3, HD)
    return jnp.swapaxes(array, -3, -2).reshape(*shape, 3 * heads * HD)


def by_head(array, heads):
    shape = array.shape[:-1]
    array = array.reshape(*shape, 3, heads, HD)
    return jnp.swapaxes(array, -3, -2).reshape(*shape, 3 * heads * HD)


def local(
    stream_in,
    segment_ids,
    parent_ids,
    norm_gain_attn,
    norm_shift_attn,
    norm_gain_mlp,
    norm_shift_mlp,
    qkv_weight,
    qkv_bias,
    dense_weight,
    dense_bias,
    fc_weight,
    fc_bias,
    out_weight,
    out_bias,
    out_grad,
):
    tensor_rank = lax.axis_index("tensor")
    data_rank = lax.axis_index("dp")
    rows_local = stream_in.shape[0]
    model = stream_in.shape[1]
    qkv_width = qkv_weight.shape[1]
    heads = qkv_width // (3 * HD)
    width = heads * HD
    units = fc_weight.shape[1]
    groups = lax.axis_size("tensor")
    tensor_bits = bits_of(groups)
    far_first = tensor_bits[:0:-1] + tensor_bits[:1]
    order = halving_order(tensor_bits)
    ids = jnp.stack([tensor_rank, data_rank, *order]).astype(jnp.int32)
    data_bits = bits_of(lax.axis_size("dp"))
    rows_first = data_bits[:0:-1] + data_bits[:1]
    columns_first = data_bits[:1] + data_bits[:0:-1]
    near_bits = data_bits
    next_bits = data_bits[1:2] + data_bits[:1] + data_bits[2:]
    qkv_bits = [data_bits[:1] + data_bits[:0:-1], next_bits]

    blocks = prepare_weights(qkv_weight, dense_weight, fc_weight, out_weight)
    qkv_pack = Pack(blocks[0], "dp", rows_first)
    dense_pack = Pack(blocks[1], "dp", columns_first)
    fc_pack = Pack(blocks[2], "dp", rows_first)
    out_pack = Pack(blocks[3], "dp", rows_first)

    sent_norm, row_mean, inv_std = normalize(stream_in)
    sent = gather_far(sent_norm, "tensor", tensor_bits)

    info = tree_table(segment_ids, parent_ids)
    gain_attn, shift_attn = norm_gain_attn[None, :], norm_shift_attn[None, :]
    gain_mlp, shift_mlp = norm_gain_mlp[None, :], norm_shift_mlp[None, :]
    sent_near, near = swap(sent[0], "tensor", 1), swap(out_grad, "tensor", 1)
    cut = rows_local * 3 // 5
    early, late = out_grad[:cut], out_grad[cut:]
    qkv_pack.double()
    dense_pack.double()
    zero = jnp.zeros((), f32)
    near, early, late, zero, qkv_bias, fc_bias, info = tie_packs(
        qkv_pack, dense_pack, fc_pack, beside=[near, early, late, zero, qkv_bias, fc_bias, info]
    )
    tables = angle_tables(zero)
    qkv_rows, fc_rows = qkv_bias.reshape(groups, qkv_width), fc_bias.reshape(groups, units)
    while len(qkv_pack.bits) > 1:
        qkv_pack.double()
        dense_pack.double()
    fc_pack.double()
    done = tie_packs(
        qkv_pack,
        dense_pack,
        out_pack,
        beside=[early, late, *tables, qkv_rows, fc_rows, sent_near, *sent],
    )
    early, late, *done = done
    tables, (qkv_rows, fc_rows, sent_near), sent = done[:2], done[2:5], done[5:]
    early_far = gather_far(early, "tensor", tensor_bits)[1:]
    sent_near = [sent_near] + [swap(x, "tensor", 1) for x in sent[1:]]
    sent = [x for pair in zip(sent, sent_near) for x in pair]
    qkv_pack.double()
    dense_pack.double()
    late, *done = tie_packs(
        qkv_pack, dense_pack, fc_pack, out_pack, beside=[late, *sent, *early_far]
    )
    sent, early_far = Tokens([(x,) for x in done[:groups]], order), done[groups:]
    late_far = gather_far(late, "tensor", tensor_bits)[1:]
    early_near = [swap(x, "tensor", 1) for x in early_far]
    out_pack.double()
    while len(fc_pack.bits) > 1:
        fc_pack.double()

    done = project_qkv(
        ids, info, sent, gain_attn, shift_attn, qkv_pack, qkv_rows, tables, width
    )
    done = tie_packs(fc_pack, out_pack, beside=[*done, *early_near, *late_far])
    (queries, keys, values), done = done[:3], done[3:]
    early_near, late_far = done[: groups // 2 - 1], done[groups // 2 - 1 :]
    late_near = [swap(x, "tensor", 1) for x in late_far]
    far = zip(zip(early_far, late_far), zip(early_near, late_near))
    grad = Tokens([(out_grad,), (near,), *[x for pair in far for x in pair]], order)
    grad_context = project_grad(ids, grad, dense_pack, width)
    fc_pack.double()
    while len(out_pack.bits) > 1:
        out_pack.double()
    done = attention(info, tables, queries, keys, values, grad_context)
    context, dq, dk, dv = tie_packs(fc_pack, out_pack, beside=done)
    dp_orders = [halving_order(near_bits), halving_order(next_bits)]
    qkv_orders = [halving_order(bits) for bits in qkv_bits]
    attn_parts = Parts(
        *project_context(ids, context, dense_pack, groups, model), "tensor", tensor_bits
    )
    attn_parts.begin()
    out_pack.double()
    done = attention_weights(
        ids, info, tables, context, dq, dk, dv, sent, grad, gain_attn, shift_attn, qkv_orders
    )
    *done, attn_parts.other = tie_halves([*done, attn_parts.other], attn_parts)
    grads, qkv_bias_sums, *stacks = done
    attn_parts.middle()
    qkv_sums = [Halving(*stacks[:2], "dp", qkv_bits[0]), Halving(*stacks[2:], "dp", qkv_bits[1])]
    sent.arrays[0], attn_parts.send = tie_packs(
        out_pack, beside=[sent.arrays[0], attn_parts.send]
    )
    attn_parts.swap()
    for parts in qkv_sums:
        parts.swap()
    done = mlp(
        ids, sent, grad, gain_mlp, shift_mlp, fc_pack, fc_rows, out_pack, dp_orders
    )
    done = tie_halves(done, attn_parts, *qkv_sums)
    *mlp_stacks, hidden, fc_bias_sums = done[:5]
    stacks = done[5:]
    attn_parts.add()
    mlp_parts = Parts(*mlp_stacks, "tensor", tensor_bits)
    mlp_sums = [Halving(*stacks[:2], "dp", near_bits), Halving(*stacks[2:], "dp", next_bits)]
    mlp_parts.begin()
    add_stacks(qkv_sums)
    mlp_parts.middle()
    hidden, mlp_parts.send = tie(hidden, mlp_parts.send)
    hidden, other = tie(hidden, mlp_parts.terms[1][0])
    mlp_parts.terms[1] = (other, 0)
    mlp_parts.swap()
    for parts in qkv_sums + mlp_sums:
        parts.swap()
    done = norm_backward(ids, sent, grads, hidden, gain_attn, gain_mlp, qkv_pack, fc_pack)
    done = tie_halves(done, mlp_parts, *qkv_sums, *mlp_sums)
    *back_stacks, norm_sums = done
    mlp_parts.add()

    back_parts = Parts(*back_stacks, "tensor", tensor_bits)
    back_parts.begin()
    add_stacks(qkv_sums + mlp_sums)
    back_parts.middle()

    stream_in, back_parts.send = tie(stream_in, back_parts.send)
    stream_in, other = tie(stream_in, back_parts.terms[1][0])
    back_parts.terms[1] = (other, 0)
    back_parts.swap()
    for parts in qkv_sums + mlp_sums:
        parts.swap()
    output, sums = finish_output(
        ids,
        stream_in,
        out_grad,
        attn_parts.terms,
        mlp_parts.terms,
        dense_bias[None, :],
        out_bias[None, :],
        norm_sums,
        fc_bias_sums,
        qkv_bias_sums,
        groups,
    )


    sums = sums + swap(sums, "tensor", 1)
    for bit in data_bits[3:]:
        sums = sums + swap(sums, "dp", bit)
    other, *_ = tie_halves([swap(sums, "dp", data_bits[2])], *mlp_sums, qkv_sums[1])
    sums = sums + other
    add_stacks(mlp_sums)
    sums, *sends = tie(sums, *[parts.send for parts in mlp_sums])
    for parts, send in zip(mlp_sums, sends):
        parts.send = send
    for bit in data_bits[:2]:
        sums = sums + swap(sums, "dp", bit)
    sums, back_parts.got = tie(sums, back_parts.got)
    back_parts.add()
    stream_grad = finish_grad(out_grad, stream_in, row_mean, inv_std, back_parts.terms)
    sums, stream_grad = tie(sums, stream_grad)
    for bit in tensor_bits[1:]:
        sums = sums + swap(sums, "tensor", bit)

    fc_weight_grad, out_weight_grad = finish_mlp_weights(*[x.finish() for x in mlp_sums])
    for parts in qkv_sums:
        parts.add()
    qkv_weight_grad, dense_weight_grad = finish_attention_weights(*[x.finish() for x in qkv_sums])

    count_all = float(rows_local * lax.axis_size("dp") * groups * model)
    gain_attn_grad, shift_attn_grad, gain_mlp_grad, shift_mlp_grad = (sums[x] for x in range(4))
    root_squares = jnp.sqrt(jnp.sum(sums[4:7], axis=1) / count_all)
    residual_grad = sums[7]
    fc_bias_grad = sums[8:12].reshape(-1)
    qkv_bias_grad = by_head(sums[12 : 12 + groups, :qkv_width], heads).reshape(-1)
    return (
        output,
        stream_grad,
        gain_attn_grad,
        shift_attn_grad,
        gain_mlp_grad,
        shift_mlp_grad,
        qkv_weight_grad,
        qkv_bias_grad,
        dense_weight_grad,
        residual_grad,
        fc_weight_grad,
        fc_bias_grad,
        out_weight_grad,
        residual_grad,
        root_squares,
    )


def solution(mesh):
    tokens, weights, rows, whole = (
        P(("dp", "tensor"), None),
        P("dp", "tensor"),
        P("tensor", "dp"),
        P(),
    )
    return jax.shard_map(
        local,
        mesh=mesh,
        in_specs=(
            tokens,
            P("dp"),
            P("dp"),
            whole,
            whole,
            whole,
            whole,
            weights,
            whole,
            rows,
            whole,
            weights,
            whole,
            rows,
            whole,
            tokens,
        ),
        out_specs=(
            tokens,
            tokens,
            whole,
            whole,
            whole,
            whole,
            weights,
            whole,
            rows,
            whole,
            weights,
            whole,
            rows,
            whole,
            whole,
        ),
        check_vma=False,
    )
```
